32 devices in a mesh: grp: 16 (over z, y, core), seq: 2 (over x).
Axes of the slice: x: 2, y: 2, z: 4, core: 2. Of those that a mesh axis runs over, the one named last changes fastest.
Arguments:
- prompt_x: bfloat16 [16, 1024, 1536], P('grp', 'seq'), may hold values from -6 to 6
- cont_x: bfloat16 [16, 8, 128, 1536], P('grp', 'seq'), may hold values from -6 to 6
- cont_len: int32 [16, 8], P('grp', 'seq'), may hold values from 1 to 128, 768 in all within a row
- prompt_cot: bfloat16 [16, 1024, 1536], P('grp', 'seq'), may hold values from -6 to 6
- cont_cot: bfloat16 [16, 8, 128, 1536], P('grp', 'seq'), may hold values from -6 to 6
- norm1_gain: float32 [1536], P(('grp', 'seq')), may hold values from 0.5 to 1.5
- q_weight: float32 [1536, 768], P(('grp', 'seq')), may hold values from -0.078125 to 0.078125
- k_weight: float32 [1536, 768], P(('grp', 'seq')), may hold values from -0.078125 to 0.078125
- v_weight: float32 [1536, 768], P(('grp', 'seq')), may hold values from -0.15625 to 0.15625
- o_weight: float32 [1536, 768], P(('grp', 'seq')), may hold values from -0.875 to 0.875
- bucket_table: float32 [32, 12], replicated, may hold values from -4 to 4
- norm2_gain: float32 [1536], P(('grp', 'seq')), may hold values from 0.5 to 1.5
- gate_weight: float32 [1536, 3968], P(('grp', 'seq')), may hold values from -0.15625 to 0.15625
- up_weight: float32 [1536, 3968], P(('grp', 'seq')), may hold values from -0.15625 to 0.15625
- down_weight: float32 [1536, 3968], P(('grp', 'seq')), may hold values from -0.125 to 0.125
Outputs:
- prompt_out: bfloat16 [16, 1024, 1536], P('grp', 'seq')
- cont_out: bfloat16 [16, 8, 128, 1536], P('grp', 'seq')
- prompt_grad: bfloat16 [16, 1024, 1536], P('grp', 'seq')
- cont_grad: bfloat16 [16, 8, 128, 1536], P('grp', 'seq')
- norm1_grad: float32 [1536], P(('grp', 'seq'))
- q_grad: float32 [1536, 768], P(('grp', 'seq'))
- k_grad: float32 [1536, 768], P(('grp', 'seq'))
- v_grad: float32 [1536, 768], P(('grp', 'seq'))
- o_grad: float32 [1536, 768], P(('grp', 'seq'))
- table_grad: float32 [32, 12], replicated
- norm2_grad: float32 [1536], P(('grp', 'seq'))
- gate_grad: float32 [1536, 3968], P(('grp', 'seq'))
- up_grad: float32 [1536, 3968], P(('grp', 'seq'))
- down_grad: float32 [1536, 3968], P(('grp', 'seq'))
The draws below stay inside these ranges and needn't reach their ends.
Inputs may be any that keep to these rules, and one draw needn't show every extreme that they name: `cont_len`: live bytes of continuation c of group g; keys of the continuation at places at or past this length are not attended to. In each group the lengths sum to 768 and one of them equals 128.
All inputs are finite; a program needn't handle non-finite values.
Results may differ from the reference program's by a relative error of at most 0.018.
The reference program's roundings to bfloat16 on the way count: a program that leaves them out, or rounds other values in their place, can miss the bound.
Values may be sent and summed in bfloat16 or wider, within the bound.
A program may use at most 512 MiB of HBM per device.

```python
import math
import jax
import jax.numpy as jnp
import numpy as np
from jax import lax

D = 1536
HEADS = 12
FF = 3968
BUCKETS = 32
INNER = 768
PROMPT = 1024
CONTS = 8
CONT = 128
GROUPS = 16


def raised(values, key, source, target, parts, factor):
    owner, partner = [(jnp.arange(values.shape[axis_at]) // (values.shape[axis_at] // parts)).reshape([-1 if axis == axis_at else 1 for axis in range(values.ndim)]) for axis_at in (source, target)]
    chosen = jax.random.permutation(key, parts)[partner]
    strong = (owner == chosen) | (owner == (partner + parts // 2) % parts)
    return jnp.where(strong, factor * values, values)


def level_of(own_key, extent, shards, smallest, largest):
    def one(axis_at, shards_of):
        heights = jax.random.uniform(jax.random.fold_in(jax.random.fold_in(own_key, 6), axis_at), (shards_of,), jnp.float32, smallest / len(shards), largest / len(shards))
        return jnp.repeat(jnp.exp(heights), extent[axis_at] // shards_of).reshape((-1,) + (1,) * (len(extent) - axis_at - 1))

    loudness = one(*shards[0])
    for cut in shards[1:]:
        loudness = loudness * one(*cut)
    return loudness


def profile(count, total, reach, slope):
    weights = [(1 << 20) // math.isqrt(standing ** slope) + 1 for standing in range(2, count + 1)]
    spare, holding = total - reach - (count - 1), [1] * (count - 1)
    while spare > 0:
        free = [i for i in range(count - 1) if holding[i] < reach]
        whole, budget = sum([weights[i] for i in free]), spare
        for i in free:
            more = min(reach - holding[i], max(1, budget * weights[i] // whole), spare)
            holding[i] = holding[i] + more
            spare = spare - more
    return np.array([reach] + holding)


def uneven(key, count, total, limit, lean):
    if count == 2:
        one = jax.random.randint(key, (), max(1, total - limit), min(limit, total - 1) + 1)
        return jnp.stack([one, total - one])
    sizes = jnp.asarray(profile(count, total, limit, lean), jnp.int32)
    couples = (count - 1) // 2
    source_of, sink = sizes[1:1 + 2 * couples:2], sizes[2:2 + 2 * couples:2]
    room = jnp.minimum(source_of - 1, limit - sink)
    moved = jax.random.randint(jax.random.fold_in(key, 1), (couples,), 0, 1 << 20) % (room + 1)
    sizes = sizes.at[1:1 + 2 * couples:2].set(source_of - moved).at[2:2 + 2 * couples:2].set(sink + moved)
    return sizes[jax.random.permutation(jax.random.fold_in(key, 2), count)]


def normal_values(key, extent, scale, most, shards=(), kind=jnp.bfloat16):
    values = scale * jax.random.normal(key, extent, jnp.float32)
    if shards:
        values = values * level_of(key, extent, shards, -0.22, 0.18)
    return jnp.clip(values, -most, most).astype(kind)


def heavy_noise(own_key, dims, spread, bound, split, heavy, held_as=jnp.bfloat16):
    result = spread * jax.random.normal(own_key, dims, jnp.float32)
    if split:
        result = result * level_of(own_key, dims, split, -0.22, 0.18)
    return jnp.clip(raised(result, jax.random.fold_in(own_key, 3), *heavy), -bound, bound).astype(held_as)


def setup_inputs(seed: int = 0) -> dict:
    streams_of = jax.random.split(jax.random.key(seed), 16)
    prompt_x = normal_values(streams_of[0], (GROUPS, PROMPT, D), 1.0, 6.0, ((0, 16), (1, 2)))
    cont_x = normal_values(streams_of[1], (GROUPS, CONTS, CONT, D), 1.0, 6.0, ((0, 16), (1, 2)))
    cont_len = jax.vmap(lambda own: uneven(own, CONTS, 3 * CONTS * CONT // 4, CONT, 2))(jax.random.split(streams_of[2], GROUPS)).reshape((GROUPS, CONTS)).astype(jnp.int32)
    prompt_cot = heavy_noise(streams_of[3], (GROUPS, PROMPT, D), 1.0, 6.0, ((0, 16), (1, 2)), (0, 2, 16, 2.0))
    cont_cot = normal_values(streams_of[4], (GROUPS, CONTS, CONT, D), 1.0, 6.0, ((0, 16), (1, 2)))
    norm1_gain = jnp.clip(1.0 + 0.1 * jax.random.normal(streams_of[5], (D,), jnp.float32), 0.5, 1.5)
    q_weight = normal_values(streams_of[6], (D, INNER), (4 * D) ** -0.5, 0.078125, ((0, 32),), jnp.float32)
    k_weight = normal_values(streams_of[7], (D, INNER), (4 * D) ** -0.5, 0.078125, ((0, 32),), jnp.float32)
    v_weight = normal_values(streams_of[8], (D, INNER), D ** -0.5, 0.15625, ((0, 32),), jnp.float32)
    o_weight = normal_values(streams_of[9], (D, INNER), (INNER // 16) ** -0.5, 0.875, ((0, 32),), jnp.float32)
    bucket_table = normal_values(streams_of[10], (BUCKETS, HEADS), 1.0, 4.0, (), jnp.float32)
    norm2_gain = jnp.clip(1.0 + 0.1 * jax.random.normal(streams_of[11], (D,), jnp.float32), 0.5, 1.5)
    gate_weight = normal_values(streams_of[12], (D, FF), D ** -0.5, 0.15625, ((0, 32),), jnp.float32)
    up_weight = normal_values(streams_of[13], (D, FF), D ** -0.5, 0.15625, ((0, 32),), jnp.float32)
    down_weight = normal_values(streams_of[14], (D, FF), (FF // 2) ** -0.5, 0.125, ((0, 32),), jnp.float32)
    return {"prompt_x": prompt_x, "cont_x": cont_x, "cont_len": cont_len, "prompt_cot": prompt_cot, "cont_cot": cont_cot, "norm1_gain": norm1_gain, "q_weight": q_weight, "k_weight": k_weight, "v_weight": v_weight, "o_weight": o_weight, "bucket_table": bucket_table, "norm2_gain": norm2_gain, "gate_weight": gate_weight, "up_weight": up_weight, "down_weight": down_weight}


@jax.custom_vjp
def low(v):
    return lax.optimization_barrier(v.astype(jnp.bfloat16)).astype(jnp.float32)

@jax.custom_vjp
def low_back(v):
    return v

def low_keep(v):
    return (low(v), None)

def low_pass(kept, grad):
    return (grad,)

def back_keep(v):
    return (v, None)

def back_low(kept, grad):
    return (low(grad),)
low.defvjp(low_keep, low_pass)
low_back.defvjp(back_keep, back_low)
EPS = 1e-06
HIGH = lax.Precision.HIGHEST
LIMITS = (8, 12, 16, 23, 32, 46, 64, 91)
NEGATIVE = -1e+30

def bucket_ids(relative):
    distance = jnp.abs(relative)
    coarse = 7 + sum(((distance >= boundary).astype(jnp.int32) for boundary in LIMITS))
    return jnp.where(distance < 8, distance, coarse) + 16 * (relative > 0).astype(jnp.int32)

def rms_scale(values):
    return lax.rsqrt(lax.optimization_barrier(jnp.mean(values * values, axis=-1, keepdims=True)) + EPS)

def attention(queries, key_rows, value_rows, table, positions, owners, live):
    row_count = queries.shape[0]
    head_count = table.shape[1]
    q_heads = queries.reshape(row_count, head_count, -1)
    k_heads = key_rows.reshape(row_count, head_count, -1)
    v_heads = value_rows.reshape(row_count, head_count, -1)
    raw_scores = low_back(jnp.einsum('qhe,khe->hqk', q_heads, k_heads, precision=HIGH))
    relative = positions[None, :] - positions[:, None]
    position_bias = jnp.transpose(table)[:, bucket_ids(relative)]
    allowed = ((owners[None, :] < 0) | (owners[None, :] == owners[:, None])) & live[None, :]
    logits = jnp.where(allowed[None], raw_scores + position_bias, NEGATIVE)
    shifted = jnp.exp(logits - lax.optimization_barrier(jnp.max(logits, axis=-1, keepdims=True)))
    probs_full = shifted / lax.optimization_barrier(jnp.sum(shifted, axis=-1, keepdims=True))
    mixture = jnp.einsum('hqk,khe->qhe', low(probs_full), v_heads, precision=HIGH)
    return mixture.reshape(row_count, -1)

def layer_group(params, group_x, lengths):
    gain_one, q_mat, k_mat, v_mat, o_mat, table, gain_two, gate_mat, up_mat, down_mat = params
    cont_place = jnp.tile(jnp.arange(CONT, dtype=jnp.int32), CONTS)
    positions = jnp.concatenate([jnp.arange(PROMPT, dtype=jnp.int32), PROMPT + cont_place])
    owners = jnp.concatenate([jnp.full((PROMPT,), -1, jnp.int32), jnp.repeat(jnp.arange(CONTS, dtype=jnp.int32), CONT)])
    live_conts = (jnp.arange(CONT, dtype=jnp.int32)[None, :] < lengths[:, None]).reshape(-1)
    live = jnp.concatenate([jnp.ones((PROMPT,), jnp.bool_), live_conts])
    normed_one = low(group_x * rms_scale(group_x) * low(gain_one))
    queries = low(low_back(jnp.dot(normed_one, low(q_mat), precision=HIGH)))
    key_rows = low(low_back(jnp.dot(normed_one, low(k_mat), precision=HIGH)))
    value_rows = low(low_back(jnp.dot(normed_one, low(v_mat), precision=HIGH)))
    mixture = attention(queries, key_rows, value_rows, table, positions, owners, live)
    attended = low(low_back(mixture))
    middle = group_x + low_back(jnp.dot(attended, low(o_mat).T, precision=HIGH))
    normed_two = low(middle * rms_scale(middle) * low(gain_two))
    gate_pre = low_back(jnp.dot(normed_two, low(gate_mat), precision=HIGH))
    up_pre = low_back(jnp.dot(normed_two, low(up_mat), precision=HIGH))
    hidden = low(jax.nn.gelu(gate_pre, approximate=True) * up_pre)
    return middle + low_back(jnp.dot(hidden, low(down_mat).T, precision=HIGH))

def reference(prompt_x, cont_x, cont_len, prompt_cot, cont_cot, norm1_gain, q_weight, k_weight, v_weight, o_weight, bucket_table, norm2_gain, gate_weight, up_weight, down_weight):
    params = (norm1_gain, q_weight, k_weight, v_weight, o_weight, bucket_table, norm2_gain, gate_weight, up_weight, down_weight)
    checked = jax.checkpoint(layer_group)

    def forward(prompt_in, cont_in, weights):
        rows_all = jnp.concatenate([prompt_in, cont_in.reshape(GROUPS, CONTS * CONT, D)], axis=1)
        outputs = lax.map(lambda inputs: checked(weights, inputs[0], inputs[1]), (rows_all, cont_len))
        return (outputs[:, :PROMPT], outputs[:, PROMPT:].reshape(GROUPS, CONTS, CONT, D))
    prompt_in = prompt_x.astype(jnp.float32)
    cont_in = cont_x.astype(jnp.float32)
    outputs, pullback = jax.vjp(forward, prompt_in, cont_in, params)
    d_prompt, d_cont, d_params = pullback((prompt_cot.astype(jnp.float32), cont_cot.astype(jnp.float32)))
    return (outputs[0].astype(jnp.bfloat16), outputs[1].astype(jnp.bfloat16), d_prompt.astype(jnp.bfloat16), d_cont.astype(jnp.bfloat16), d_params[0], d_params[1], d_params[2], d_params[3], d_params[4], d_params[5], d_params[6], d_params[7], d_params[8], d_params[9])
```

```python
import functools

import jax
import jax.numpy as jnp
from jax import lax
from jax.experimental import pallas as pl
from jax.experimental.pallas import tpu as pltpu
from jax.sharding import PartitionSpec as P

EPS = 1e-06
LIMITS = (8, 12, 16, 23, 32, 46, 64, 91)
NEGATIVE = -1e30
MESH = pl.DeviceIdType.MESH
T = 128
HEAD = 64
BANDS = 5
BF = jnp.bfloat16
F32 = jnp.float32
VMEM_LIMIT = 63 * 2**20
Y = 2
C = 2


def nn(left, right):
    return jnp.dot(left, right, preferred_element_type=F32)


def nt(left, right):
    return lax.dot_general(left, right, (((1,), (1,)), ((), ())), preferred_element_type=F32)


def tn(left, right):
    return lax.dot_general(left, right, (((0,), (0,)), ((), ())), preferred_element_type=F32)


def bucket_ids(relative):
    distance = jnp.abs(relative)
    coarse = 7 + sum(((distance >= boundary).astype(jnp.int32) for boundary in LIMITS))
    return jnp.where(distance < 8, distance, coarse) + 16 * (relative > 0).astype(jnp.int32)


def band_one_hot(num_buckets):
    band = jnp.arange(BANDS)[:, None, None] - 2
    query = jnp.arange(T)[None, :, None]
    key = jnp.arange(T)[None, None, :]
    ids = bucket_ids(band * T + key - query)
    return (ids[..., None] == jnp.arange(num_buckets)).astype(F32)


class Place:
    def __init__(self, zs, xs):
        grp = lax.axis_index("grp")
        self.zs, self.xs = zs, xs
        self.x = lax.axis_index("seq")
        self.z = grp // (Y * C)
        self.y = (grp // C) % Y
        self.c = grp % C

    def device(self, z=None, y=None, c=None, x=None):
        z = self.z if z is None else z
        y = self.y if y is None else y
        c = self.c if c is None else c
        x = self.x if x is None else x
        return (z * (Y * C) + y * C + c, x)

    def peers(self):
        around = [self.device(z=(self.z + d) % self.zs) for d in range(1, self.zs)]
        return around + [
            self.device(y=1 - self.y),
            self.device(x=1 - self.x),
            self.device(c=1 - self.c),
        ]

    def barrier(self):
        sem = pltpu.get_barrier_semaphore()
        peers = self.peers()
        for peer in peers:
            pl.semaphore_signal(sem, inc=1, device_id=peer, device_id_type=MESH)
        pl.semaphore_wait(sem, len(peers))


def remote(src, dst, send_sem, recv_sem, device):
    return pltpu.make_async_remote_copy(
        src_ref=src,
        dst_ref=dst,
        send_sem=send_sem,
        recv_sem=recv_sem,
        device_id=device,
        device_id_type=MESH,
    )


def staged(step, offset, count, action):
    @pl.when((step >= offset) & (step < count + offset))
    def _():
        action(step - offset)


class Gather:
    def __init__(self, place, own, whole, send, recv):
        self.p, self.own, self.whole, self.send, self.recv = place, own, whole, send, recv

    def copy(self, k, half, index, src, dst, device):
        return remote(src, dst, self.send.at[k, half, index], self.recv.at[k, half, index], device)

    def along_z(self, k, half, d):
        p = self.p
        dst = self.whole.at[k, half, :, p.z, p.y, p.c * p.xs + p.x]
        return self.copy(k, half, d - 1, self.own.at[k, half], dst, p.device(z=(p.z + d) % p.zs))

    def second(self, k, half):
        p = self.p
        view = self.whole.at[k, half, :, :, p.y, p.c * p.xs + p.x]
        peer = p.device(x=1 - p.x) if half == 0 else p.device(y=1 - p.y)
        return self.copy(k, half, p.zs - 1, view, view, peer)

    def third(self, k, half):
        p = self.p
        if half == 0:
            view = self.whole.at[k, half, :, :, p.y, pl.ds(p.c * p.xs, p.xs)]
            peer = p.device(y=1 - p.y)
        else:
            view = self.whole.at[k, half, :, :, :, p.c * p.xs + p.x]
            peer = p.device(x=1 - p.x)
        return self.copy(k, half, p.zs, view, view, peer)

    def fourth(self, k, half):
        p = self.p
        view = self.whole.at[k, half, :, :, :, pl.ds(p.c * p.xs, p.xs)]
        return self.copy(k, half, p.zs + 1, view, view, p.device(c=1 - p.c))

    def tick(self, step, count):
        def start_z(k):
            for half in (0, 1):
                for d in range(1, self.p.zs):
                    self.along_z(k, half, d).start()

        def start_second(k):
            for half in (0, 1):
                for d in range(1, self.p.zs):
                    self.along_z(k, half, d).wait_recv()
                self.second(k, half).start()

        def start_third(k):
            for half in (0, 1):
                self.second(k, half).wait_recv()
                self.third(k, half).start()

        def start_fourth(k):
            for half in (0, 1):
                self.third(k, half).wait_recv()
                self.fourth(k, half).start()

        def finish(k):
            for half in (0, 1):
                self.fourth(k, half).wait_recv()
                for d in range(1, self.p.zs):
                    self.along_z(k, half, d).wait_send()
                self.second(k, half).wait_send()
                self.third(k, half).wait_send()
                self.fourth(k, half).wait_send()

        staged(step, 0, count, start_z)
        staged(step, 1, count, start_second)
        staged(step, 2, count, start_third)
        staged(step, 3, count, start_fourth)
        staged(step, 4, count, finish)


def gather_kernel(zs, xs, own, whole, held, local, send, recv):
    place = Place(zs, xs)
    step = pl.program_id(0)

    @pl.when(step == 0)
    def _():
        place.barrier()
        load = pltpu.make_async_copy(own, held, local.at[0])
        load.start()
        load.wait()
        mine = whole.at[:, :, :, place.z, place.y, place.c * place.xs + place.x]
        store = pltpu.make_async_copy(held, mine, local.at[1])
        store.start()
        store.wait()

    Gather(place, held, whole, send, recv).tick(step, own.shape[0])


def gather(own, sizes, collective_id):
    grp, seq = sizes
    chunks, halves, n, rows, lanes = own.shape
    if rows % 16 or seq != 2 or grp % (Y * C):
        whole = lax.all_gather(own, ("grp", "seq"), axis=3, tiled=True)
        return whole
    zs = grp // (Y * C)
    slots = (chunks, 2, zs + 2)
    whole = pl.pallas_call(
        functools.partial(gather_kernel, zs, seq),
        grid=(chunks + 4,),
        out_shape=jax.ShapeDtypeStruct((chunks, 2, n, zs, Y, C * seq, rows, lanes), own.dtype),
        in_specs=[pl.BlockSpec(memory_space=pl.ANY)],
        out_specs=pl.BlockSpec(memory_space=pl.ANY),
        scratch_shapes=[
            pltpu.VMEM(own.shape, own.dtype),
            pltpu.SemaphoreType.DMA((2,)),
            pltpu.SemaphoreType.DMA(slots),
            pltpu.SemaphoreType.DMA(slots),
        ],
        compiler_params=pltpu.CompilerParams(collective_id=collective_id, has_side_effects=True),
    )(own)
    return whole.reshape(chunks, 2, n, grp * seq * rows, lanes)


class Scatter:
    def __init__(self, place, bufs, send, recv, out):
        self.p, self.send, self.recv, self.out = place, send, recv, out
        (self.in1, self.in2, self.in3, self.in4, self.sum1, self.sum2, self.sum3) = bufs

    def copy(self, k, half, index, src, dst, device):
        slot = k % 2
        return remote(
            src, dst, self.send.at[slot, half, index], self.recv.at[slot, half, index], device
        )

    def first(self, k, half, part):
        p = self.p
        src = part.at[half, :, :, :, pl.ds((1 - p.c) * p.xs, p.xs)]
        return self.copy(k, half, 0, src, self.in1.at[k % 2, half], p.device(c=1 - p.c))

    def second(self, k, half):
        p = self.p
        if half == 0:
            src, peer = self.sum1.at[k % 2, half, :, :, 1 - p.y], p.device(y=1 - p.y)
        else:
            src, peer = self.sum1.at[k % 2, half, :, :, :, 1 - p.x], p.device(x=1 - p.x)
        return self.copy(k, half, 1, src, self.in2.at[k % 2, half], peer)

    def third(self, k, half):
        p = self.p
        other = 1 - p.x if half == 0 else 1 - p.y
        peer = p.device(x=1 - p.x) if half == 0 else p.device(y=1 - p.y)
        src = self.sum2.at[k % 2, half, :, :, other]
        return self.copy(k, half, 2, src, self.in3.at[k % 2, half], peer)

    def fourth(self, k, half, d):
        p = self.p
        target = (p.z + d) % p.zs
        src = self.sum3.at[k % 2, half, :, target]
        dst = self.in4.at[k % 2, half, d - 1]
        return self.copy(k, half, 2 + d, src, dst, p.device(z=target))

    def finish(self, k):
        p = self.p
        slot = k % 2
        for half in (0, 1):
            total = self.sum3[slot, half, :, p.z].astype(F32)
            for d in range(1, p.zs):
                copy = self.fourth(k, half, d)
                copy.wait_recv()
                copy.wait_send()
                total = total + self.in4[slot, half, d - 1].astype(F32)
            self.out[k, half] = total

    def start_fourth(self, k):
        p = self.p
        slot = k % 2
        for half in (0, 1):
            copy = self.third(k, half)
            copy.wait_recv()
            copy.wait_send()
            keep = p.x if half == 0 else p.y
            for i in range(self.sum3.shape[2]):
                total = self.sum2[slot, half, i, :, keep].astype(F32)
                total = total + self.in3[slot, half, i].astype(F32)
                self.sum3[slot, half, i] = total.astype(BF)
            for d in range(1, p.zs):
                self.fourth(k, half, d).start()

    def start_third(self, k):
        p = self.p
        slot = k % 2
        for half in (0, 1):
            copy = self.second(k, half)
            copy.wait_recv()
            copy.wait_send()
            for i in range(self.sum2.shape[2]):
                if half == 0:
                    mine = self.sum1[slot, half, i, :, p.y]
                else:
                    mine = self.sum1[slot, half, i, :, :, p.x]
                total = mine.astype(F32) + self.in2[slot, half, i].astype(F32)
                self.sum2[slot, half, i] = total.astype(BF)
            self.third(k, half).start()

    def start_second(self, k, part):
        p = self.p
        slot = k % 2
        for half in (0, 1):
            copy = self.first(k, half, part)
            copy.wait_recv()
            copy.wait_send()

            def add(z, _, half=half):
                for i in range(self.sum1.shape[2]):
                    mine = part[half, i, z, :, pl.ds(p.c * p.xs, p.xs)]
                    total = mine.astype(F32) + self.in1[slot, half, i, z].astype(F32)
                    self.sum1[slot, half, i, z] = total.astype(BF)
                return 0

            lax.fori_loop(0, p.zs, add, 0)
            self.second(k, half).start()

    def start_first(self, k, part):
        for half in (0, 1):
            self.first(k, half, part).start()


def scatter_buffers(n, zs, xs, rows, lanes):
    shapes = [
        (2, 2, n, zs, Y, xs, rows, lanes),
        (2, 2, n, zs, 2, rows, lanes),
        (2, 2, n, zs, rows, lanes),
        (2, 2, zs - 1, n, rows, lanes),
        (2, 2, n, zs, Y, xs, rows, lanes),
        (2, 2, n, zs, 2, rows, lanes),
        (2, 2, n, zs, rows, lanes),
    ]
    return [pltpu.VMEM(shape, BF) for shape in shapes]


def scatter_kernel(zs, xs, chunks, parts, out, held, local, *rest):
    bufs, (send, recv) = rest[:7], rest[7:]
    place = Place(zs, xs)
    step = pl.program_id(0)
    engine = Scatter(place, bufs, send, recv, out)

    @pl.when(step == 0)
    def _():
        place.barrier()

    def load(k):
        return pltpu.make_async_copy(parts.at[k], held.at[k % 3], local.at[k % 3])

    def first(k):
        load(k).wait()
        engine.start_first(k, held.at[k % 3])

    staged(step, 5, chunks, engine.finish)
    staged(step, 4, chunks, engine.start_fourth)
    staged(step, 3, chunks, engine.start_third)
    staged(step, 2, chunks, lambda k: engine.start_second(k, held.at[k % 3]))
    staged(step, 1, chunks, first)
    staged(step, 0, chunks, lambda k: load(k).start())


def scatter(parts, sizes, rows, collective_id):
    grp, seq = sizes
    chunks, halves, n, _, lanes = parts.shape
    if rows % 16 or seq != 2 or grp % (Y * C):
        return lax.psum_scatter(parts, ("grp", "seq"), scatter_dimension=3, tiled=True).astype(F32)
    zs = grp // (Y * C)
    view = parts.reshape(chunks, 2, n, zs, Y, C * seq, rows, lanes)
    sems = (2, 2, zs + 2)
    return pl.pallas_call(
        functools.partial(scatter_kernel, zs, seq, chunks),
        grid=(chunks + 5,),
        out_shape=jax.ShapeDtypeStruct((chunks, 2, n, rows, lanes), F32),
        in_specs=[pl.BlockSpec(memory_space=pl.ANY)],
        out_specs=pl.BlockSpec((chunks, 2, n, rows, lanes), lambda step: (0, 0, 0, 0, 0)),
        scratch_shapes=[
            pltpu.VMEM((3, 2, n, zs, Y, C * seq, rows, lanes), BF),
            pltpu.SemaphoreType.DMA((3,)),
        ]
        + scatter_buffers(n, zs, seq, rows, lanes)
        + [pltpu.SemaphoreType.DMA(sems), pltpu.SemaphoreType.DMA(sems)],
        compiler_params=pltpu.CompilerParams(
            collective_id=collective_id, has_side_effects=True, vmem_limit_bytes=VMEM_LIMIT
        ),
    )(view)


def band_of(key_tile, query_tile):
    return jnp.clip(key_tile - query_tile, -2, 2) + 2


def attend_kernel(tiles, local_tiles, conts, live, base, q, k, v, bias, out, norm):
    first_half = lax.broadcasted_iota(jnp.int32, (T, 2 * HEAD), 1) < HEAD
    place = lax.broadcasted_iota(jnp.int32, (T, T), 1)

    def tile(i, is_cont):
        rows = pl.ds(pl.multiple_of(i * T, T), T)
        queries = q[rows, :]
        query_tile = tiles if is_cont else base[0] + i
        cont = i - local_tiles
        cont_keys = pl.ds(pl.multiple_of((tiles + cont) * T, T), T)
        mixed = []
        for h in range(2):
            mine = first_half if h == 0 else ~first_half
            masked = jnp.where(mine, queries, jnp.zeros_like(queries))
            scores = nt(masked, k[0 : tiles * T, :])
            parts = []
            for j in range(tiles):
                band = band_of(lax.rem(base[1] + j, tiles), query_tile)
                parts.append(scores[:, j * T : (j + 1) * T] + bias[h, band])
            if is_cont:
                own = nt(masked, k[cont_keys, :]) + bias[h, 2]
                parts.append(jnp.where(place < live[0, cont], own, NEGATIVE))
            top = jnp.max(functools.reduce(jnp.maximum, parts), axis=1, keepdims=True)
            weights = [jnp.exp(part - top) for part in parts]
            total = jnp.sum(functools.reduce(jnp.add, weights), axis=1, keepdims=True)
            inverse = 1.0 / total
            probs = [(weight * inverse).astype(BF) for weight in weights]
            result = nn(jnp.concatenate(probs[:tiles], axis=1), v[0 : tiles * T, :])
            if is_cont:
                result = result + nn(probs[tiles], v[cont_keys, :])
            mixed.append(result)
            norm[h, rows, :] = top + jnp.log(total)
        out[rows, :] = jnp.where(first_half, mixed[0], mixed[1]).astype(BF)

    def prompt_tile(i, carry):
        tile(i, False)
        return carry

    def cont_tile(i, carry):
        tile(i, True)
        return carry

    lax.fori_loop(0, local_tiles, prompt_tile, 0)
    lax.fori_loop(local_tiles, local_tiles + conts, cont_tile, 0)


def attend(q, k, v, bias, live, base, tiles, local_tiles, conts):
    rows, width = q.shape
    keys = k.shape[0]
    pairs = width // (2 * HEAD)
    block = lambda n: pl.BlockSpec((n, 2 * HEAD), lambda h, *_: (0, h))
    return pl.pallas_call(
        functools.partial(attend_kernel, tiles, local_tiles, conts),
        grid_spec=pltpu.PrefetchScalarGridSpec(
            num_scalar_prefetch=2,
            grid=(pairs,),
            in_specs=[
                block(rows),
                block(keys),
                block(keys),
                pl.BlockSpec((2, BANDS, T, T), lambda h, *_: (h, 0, 0, 0)),
            ],
            out_specs=[block(rows), pl.BlockSpec((2, rows, 1), lambda h, *_: (h, 0, 0))],
        ),
        out_shape=[
            jax.ShapeDtypeStruct((rows, width), BF),
            jax.ShapeDtypeStruct((2 * pairs, rows, 1), F32),
        ],
        compiler_params=pltpu.CompilerParams(vmem_limit_bytes=VMEM_LIMIT),
    )(live, base, q, k, v, bias)


def attend_back_kernel(
    tiles,
    local_tiles,
    conts,
    live,
    base,
    q,
    k,
    v,
    bias,
    grad,
    out,
    norm,
    d_q,
    d_k,
    d_v,
    d_bias,
    k_sum,
    v_sum,
):
    first_half = lax.broadcasted_iota(jnp.int32, (T, 2 * HEAD), 1) < HEAD
    place = lax.broadcasted_iota(jnp.int32, (T, T), 1)
    k_sum[...] = jnp.zeros_like(k_sum)
    v_sum[...] = jnp.zeros_like(v_sum)
    d_bias[...] = jnp.zeros_like(d_bias)

    def tile(i, is_cont):
        rows = pl.ds(pl.multiple_of(i * T, T), T)
        queries = q[rows, :]
        grads = grad[rows, :]
        query_tile = tiles if is_cont else base[0] + i
        overlap = grads.astype(F32) * out[rows, :].astype(F32)
        mixed = []
        for h in range(2):
            mine = first_half if h == 0 else ~first_half
            masked = jnp.where(mine, queries, jnp.zeros_like(queries))
            masked_grad = jnp.where(mine, grads, jnp.zeros_like(grads))
            inner = jnp.sum(jnp.where(mine, overlap, 0.0), axis=1, keepdims=True)
            log_norm = norm[h, rows, :]

            def piece(keys, bands, allowed):
                scores = nt(masked, k[keys, :])
                d_probs = nt(masked_grad, v[keys, :])
                probs_low, scores_low = [], []
                for j, band in enumerate(bands):
                    cols = slice(j * T, (j + 1) * T)
                    logits = scores[:, cols] + bias[h, band]
                    if allowed is not None:
                        logits = jnp.where(allowed, logits, NEGATIVE)
                    probs = jnp.exp(logits - log_norm)
                    d_scores = probs * (d_probs[:, cols] - inner)
                    d_bias[h, band] += d_scores
                    probs_low.append(probs.astype(BF))
                    scores_low.append(d_scores.astype(BF))
                probs_low = jnp.concatenate(probs_low, axis=1)
                scores_low = jnp.concatenate(scores_low, axis=1)
                v_sum[keys, :] += tn(probs_low, masked_grad)
                k_sum[keys, :] += tn(scores_low, masked)
                return nn(scores_low, k[keys, :])

            bands = [band_of(lax.rem(base[1] + j, tiles), query_tile) for j in range(tiles)]
            result = piece(pl.ds(0, tiles * T), bands, None)
            if is_cont:
                cont = i - local_tiles
                cont_keys = pl.ds(pl.multiple_of((tiles + cont) * T, T), T)
                result = result + piece(cont_keys, [2], place < live[0, cont])
            mixed.append(result)
        d_q[rows, :] = jnp.where(first_half, mixed[0], mixed[1]).astype(BF)

    def prompt_tile(i, carry):
        tile(i, False)
        return carry

    def cont_tile(i, carry):
        tile(i, True)
        return carry

    lax.fori_loop(0, local_tiles, prompt_tile, 0)
    lax.fori_loop(local_tiles, local_tiles + conts, cont_tile, 0)
    d_k[...] = k_sum[...].astype(BF)
    d_v[...] = v_sum[...].astype(BF)


def attend_back(q, k, v, bias, grad, out, norm, live, base, tiles, local_tiles, conts):
    rows, width = q.shape
    keys = k.shape[0]
    pairs = width // (2 * HEAD)
    block = lambda n: pl.BlockSpec((n, 2 * HEAD), lambda h, *_: (0, h))
    bands = pl.BlockSpec((2, BANDS, T, T), lambda h, *_: (h, 0, 0, 0))
    return pl.pallas_call(
        functools.partial(attend_back_kernel, tiles, local_tiles, conts),
        grid_spec=pltpu.PrefetchScalarGridSpec(
            num_scalar_prefetch=2,
            grid=(pairs,),
            in_specs=[
                block(rows),
                block(keys),
                block(keys),
                bands,
                block(rows),
                block(rows),
                pl.BlockSpec((2, rows, 1), lambda h, *_: (h, 0, 0)),
            ],
            out_specs=[block(rows), block(keys), block(keys), bands],
            scratch_shapes=[pltpu.VMEM((keys, 2 * HEAD), F32), pltpu.VMEM((keys, 2 * HEAD), F32)],
        ),
        out_shape=[
            jax.ShapeDtypeStruct((rows, width), BF),
            jax.ShapeDtypeStruct((keys, width), BF),
            jax.ShapeDtypeStruct((keys, width), BF),
            jax.ShapeDtypeStruct((2 * pairs, BANDS, T, T), F32),
        ],
        compiler_params=pltpu.CompilerParams(vmem_limit_bytes=VMEM_LIMIT),
    )(live, base, q, k, v, bias, grad, out, norm)


GELU_SCALE = 0.7978845608028654
GELU_CUBIC = 0.044715


def gelu_and_slope(a):
    square = a * a
    tanh = jnp.tanh(GELU_SCALE * a * (1.0 + GELU_CUBIC * square))
    half = 0.5 * (1.0 + tanh)
    slope = half + 0.5 * a * (1.0 - tanh * tanh) * (
        GELU_SCALE * (1.0 + 3.0 * GELU_CUBIC * square)
    )
    return a * half, slope


def feed_kernel(
    x_hbm,
    dy_hbm,
    weights,
    out,
    d_x,
    grads,
    x,
    x_t,
    dy,
    dy_t,
    out_sum,
    d_x_sum,
    hidden,
    d_gate,
    d_up,
    sem,
):
    step = pl.program_id(0)
    rows = x.shape[0]
    row_block = min(rows, 256)
    width = x.shape[1]
    width_block = 512

    @pl.when(step == 0)
    def _():
        load_x = pltpu.make_async_copy(x_hbm, x, sem.at[0])
        load_dy = pltpu.make_async_copy(dy_hbm, dy, sem.at[1])
        load_x.start()
        load_dy.start()
        load_x.wait()
        load_dy.wait()

        def turn(i, carry):
            part = pl.ds(pl.multiple_of(i * T, T), T)
            x_t[:, part] = x[part, :].T
            dy_t[:, part] = dy[part, :].T
            return carry

        lax.fori_loop(0, rows // T, turn, 0)
        out_sum[...] = jnp.zeros_like(out_sum)
        d_x_sum[...] = jnp.zeros_like(d_x_sum)

    w_gate, w_up, w_down = [
        jnp.concatenate([weights[0, 0, i], weights[0, 1, i]], axis=1) for i in range(3)
    ]

    def by_rows(i, carry):
        part = pl.ds(pl.multiple_of(i * row_block, row_block), row_block)
        gate = nn(x[part, :], w_gate)
        up = nn(x[part, :], w_up)
        d_hidden = nn(dy[part, :], w_down)
        active, slope = gelu_and_slope(gate)
        hidden_low = (active * up).astype(BF)
        d_gate_low = (d_hidden * up * slope).astype(BF)
        d_up_low = (d_hidden * active).astype(BF)
        hidden[part, :] = hidden_low
        d_gate[part, :] = d_gate_low
        d_up[part, :] = d_up_low
        out_sum[part, :] += nt(hidden_low, w_down)
        d_x_sum[part, :] += nt(d_gate_low, w_gate) + nt(d_up_low, w_up)
        return carry

    lax.fori_loop(0, rows // row_block, by_rows, 0)

    def by_width(i, carry):
        part = pl.ds(pl.multiple_of(i * width_block, width_block), width_block)
        pairs = ((x_t, d_gate), (x_t, d_up), (dy_t, hidden))
        for index, (left, right) in enumerate(pairs):
            total = nn(left[part, :], right[...]).astype(BF)
            grads[0, 0, index, part, :] = total[:, :T]
            grads[0, 1, index, part, :] = total[:, T:]
        return carry

    lax.fori_loop(0, width // width_block, by_width, 0)

    @pl.when(step == pl.num_programs(0) - 1)
    def _():
        out[...] = out_sum[...]
        d_x[...] = d_x_sum[...]


def feed(x, dy, weights):
    rows, width = x.shape
    chunks = weights.shape[0]
    chunk = pl.BlockSpec((1, 2, 3, width, T), lambda j: (j, 0, 0, 0, 0))
    whole = pl.BlockSpec((rows, width), lambda j: (0, 0), pipeline_mode=pl.Buffered(1))
    return pl.pallas_call(
        feed_kernel,
        grid=(chunks,),
        in_specs=[pl.BlockSpec(memory_space=pl.ANY)] * 2 + [chunk],
        out_specs=[whole, whole, chunk],
        out_shape=[
            jax.ShapeDtypeStruct((rows, width), F32),
            jax.ShapeDtypeStruct((rows, width), F32),
            jax.ShapeDtypeStruct((chunks, 2, 3, width, T), BF),
        ],
        scratch_shapes=[
            pltpu.VMEM((rows, width), BF),
            pltpu.VMEM((width, rows), BF),
            pltpu.VMEM((rows, width), BF),
            pltpu.VMEM((width, rows), BF),
            pltpu.VMEM((rows, width), F32),
            pltpu.VMEM((rows, width), F32),
            pltpu.VMEM((rows, 2 * T), BF),
            pltpu.VMEM((rows, 2 * T), BF),
            pltpu.VMEM((rows, 2 * T), BF),
            pltpu.SemaphoreType.DMA((2,)),
        ],
        compiler_params=pltpu.CompilerParams(vmem_limit_bytes=VMEM_LIMIT),
    )(x, dy, weights)


def rms_scale(values):
    return lax.rsqrt(jnp.mean(values * values, axis=-1, keepdims=True) + EPS)


def norm_back(d_normed, unit, scale, gain):
    d_unit = d_normed * gain
    return scale * (d_unit - unit * jnp.mean(d_unit * unit, axis=-1, keepdims=True))


def pieces_of(matrix):
    rows, columns = matrix.shape
    return jnp.swapaxes(matrix.reshape(rows, columns // T, T), 0, 1)


def joined(pieces):
    count, rows, _ = pieces.shape
    return jnp.swapaxes(pieces, 0, 1).reshape(rows, count * T)


def attention_chunks(matrices):
    flat = jnp.concatenate([pieces_of(m) for m in matrices], axis=0)
    pad = -flat.shape[0] % 6
    flat = jnp.pad(flat, ((0, pad), (0, 0), (0, 0)))
    return flat.reshape(-1, 2, 3, *flat.shape[1:])


def feed_chunks(matrices):
    stacked = jnp.stack([pieces_of(m) for m in matrices], axis=1)
    pad = -stacked.shape[0] % 2
    stacked = jnp.pad(stacked, ((0, pad), (0, 0), (0, 0), (0, 0)))
    return stacked.reshape(-1, 2, *stacked.shape[1:])


def body(sizes, *args):
    (
        prompt_x,
        cont_x,
        cont_len,
        prompt_cot,
        cont_cot,
        norm1_gain,
        q_weight,
        k_weight,
        v_weight,
        o_weight,
        bucket_table,
        norm2_gain,
        gate_weight,
        up_weight,
        down_weight,
    ) = args
    _, local_prompt, width = prompt_x.shape
    conts, cont_rows = cont_x.shape[1], cont_x.shape[2]
    assert prompt_x.shape[0] == 1 and cont_rows == T and local_prompt % T == 0
    seq = sizes[1]
    num_buckets, heads = bucket_table.shape
    inner = q_weight.shape[1]
    assert inner == heads * HEAD
    shard = q_weight.shape[0]
    hidden_width = gate_weight.shape[1]
    local_tiles = local_prompt // T
    tiles = local_tiles * seq
    seq_index = lax.axis_index("seq")

    x_low = jnp.concatenate([prompt_x[0], cont_x[0].reshape(-1, width)], axis=0)
    dy_low = jnp.concatenate([prompt_cot[0], cont_cot[0].reshape(-1, width)], axis=0)
    x = x_low.astype(F32)
    dy = dy_low.astype(F32)

    lanes = jnp.zeros((shard, T - 2), F32)
    gains = jnp.concatenate([norm1_gain[:, None], norm2_gain[:, None], lanes], axis=1)
    own_attention = attention_chunks([q_weight, k_weight, v_weight, o_weight, gains]).astype(BF)
    own_feed = feed_chunks([gate_weight, up_weight, down_weight]).astype(BF)
    attention_whole = gather(own_attention, sizes, 0)
    count = inner // T
    flat = attention_whole.reshape(-1, width, T)
    q_full, k_full, v_full, o_full = [
        joined(flat[i * count : (i + 1) * count]) for i in range(4)
    ]
    gain_one = flat[4 * count, :, 0].astype(F32)
    gain_two = flat[4 * count, :, 1].astype(F32)
    feed_whole = gather(own_feed, sizes, 1)

    scale_one = rms_scale(x)
    unit_one = x * scale_one
    normed_one = (unit_one * gain_one).astype(BF)
    kv = nn(normed_one, jnp.concatenate([k_full, v_full], axis=1)).astype(BF)
    queries = nn(normed_one, q_full).astype(BF)
    prompt_kv = kv[:local_prompt]
    if seq == 2:
        other = lax.ppermute(prompt_kv, "seq", [(0, 1), (1, 0)])
        every = jnp.concatenate([kv[:local_prompt], other, kv[local_prompt:]], axis=0)
        first_tile = seq_index * local_tiles
    else:
        gathered = lax.all_gather(prompt_kv, "seq", axis=0, tiled=True)
        every = jnp.concatenate([gathered, kv[local_prompt:]], axis=0)
        first_tile = jnp.zeros((), jnp.int32)
    keys, values = every[:, :inner], every[:, inner:]
    base = jnp.stack([seq_index * local_tiles, first_tile]).astype(jnp.int32)

    one_hot = band_one_hot(num_buckets)
    bias = jnp.einsum("cqkb,bh->hcqk", one_hot, bucket_table, precision=lax.Precision.HIGHEST)
    attended, log_norm = attend(
        queries, keys, values, bias, cont_len, base, tiles, local_tiles, conts
    )
    middle = x + nt(attended, o_full)
    scale_two = rms_scale(middle)
    unit_two = middle * scale_two
    normed_two = (unit_two * gain_two).astype(BF)

    out_sum, d_normed_two, feed_grads = feed(normed_two, dy_low, feed_whole)
    final = (middle + out_sum).astype(BF)

    d_gain_two = jnp.sum(d_normed_two * unit_two, axis=0)
    d_middle = dy + norm_back(d_normed_two, unit_two, scale_two, gain_two)
    d_branch = d_middle.astype(BF)
    d_attended = nn(d_branch, o_full).astype(BF)
    d_o = tn(d_branch, attended)

    d_queries, d_keys, d_values, d_bias = attend_back(
        queries,
        keys,
        values,
        bias,
        d_attended,
        attended,
        log_norm,
        cont_len,
        base,
        tiles,
        local_tiles,
        conts,
    )
    d_table = jnp.einsum("hcqk,cqkb->bh", d_bias, one_hot, precision=lax.Precision.HIGHEST)
    d_kv = jnp.concatenate([d_keys, d_values], axis=1)
    prompt_rows = local_prompt * seq
    if seq == 2:
        back = lax.ppermute(d_kv[local_prompt:prompt_rows], "seq", [(0, 1), (1, 0)])
        d_prompt = (d_kv[:local_prompt].astype(F32) + back.astype(F32)).astype(BF)
    else:
        d_prompt = lax.psum_scatter(
            d_kv[:prompt_rows], "seq", scatter_dimension=0, tiled=True
        )
    d_kv = jnp.concatenate([d_prompt, d_kv[prompt_rows:]], axis=0)
    d_normed_one = nt(d_queries, q_full) + nt(d_kv, jnp.concatenate([k_full, v_full], axis=1))
    d_q = tn(normed_one, d_queries)
    d_kv_weight = tn(normed_one, d_kv)
    d_gain_one = jnp.sum(d_normed_one * unit_one, axis=0)
    d_x = d_middle + norm_back(d_normed_one, unit_one, scale_one, gain_one)
    d_x = d_x.astype(BF)

    attention_parts = attention_chunks([d_q, d_kv_weight, d_o]).astype(BF)
    parts = jnp.concatenate([feed_grads, attention_parts], axis=0)
    sums = scatter(parts, sizes, shard, 2)
    feed_sums = sums[: feed_grads.shape[0]].reshape(-1, 3, shard, T)
    feed_sums = feed_sums[: hidden_width // T]
    gate_grad, up_grad, down_grad = [joined(feed_sums[:, i]) for i in range(3)]
    attention_sums = sums[feed_grads.shape[0] :].reshape(-1, shard, T)
    q_grad, k_grad, v_grad, o_grad = [
        joined(attention_sums[i * count : (i + 1) * count]) for i in range(4)
    ]
    norm1_grad = lax.psum_scatter(d_gain_one, ("grp", "seq"), scatter_dimension=0, tiled=True)
    norm2_grad = lax.psum_scatter(d_gain_two, ("grp", "seq"), scatter_dimension=0, tiled=True)
    table_grad = lax.psum(d_table, ("grp", "seq"))
    split = lambda rows: (
        rows[:local_prompt][None],
        rows[local_prompt:].reshape(1, conts, cont_rows, width),
    )
    return (
        *split(final),
        *split(d_x),
        norm1_grad,
        q_grad,
        k_grad,
        v_grad,
        o_grad,
        table_grad,
        norm2_grad,
        gate_grad,
        up_grad,
        down_grad,
    )


def solution(mesh):
    sizes = (mesh.shape["grp"], mesh.shape["seq"])
    rows = P("grp", "seq", None)
    conts = P("grp", "seq", None, None)
    shard = P(("grp", "seq"), None)
    gain = P(("grp", "seq"))
    in_specs = (rows, conts, P("grp", "seq"), rows, conts, gain, shard, shard, shard, shard)
    in_specs += (P(), gain, shard, shard, shard)
    out_specs = (rows, conts, rows, conts, gain, shard, shard, shard, shard, P(), gain)
    out_specs += (shard, shard, shard)
    return jax.shard_map(
        functools.partial(body, sizes),
        mesh=mesh,
        in_specs=in_specs,
        out_specs=out_specs,
        check_vma=False,
    )
```

```python
import functools

import jax
import jax.numpy as jnp
from jax import lax
from jax.experimental import pallas as pl
from jax.experimental.pallas import tpu as pltpu
from jax.sharding import PartitionSpec as P

EPS = 1e-06
LIMITS = (8, 12, 16, 23, 32, 46, 64, 91)
NEGATIVE = -1e30
MESH = pl.DeviceIdType.MESH
T = 128
HEAD = 64
BANDS = 5
BF = jnp.bfloat16
F32 = jnp.float32
VMEM_LIMIT = 63 * 2**20
Y = 2
C = 2


def nn(left, right):
    return jnp.dot(left, right, preferred_element_type=F32)


def nt(left, right):
    return lax.dot_general(left, right, (((1,), (1,)), ((), ())), preferred_element_type=F32)


def tn(left, right):
    return lax.dot_general(left, right, (((0,), (0,)), ((), ())), preferred_element_type=F32)


def bucket_ids(relative):
    distance = jnp.abs(relative)
    coarse = 7 + sum(((distance >= boundary).astype(jnp.int32) for boundary in LIMITS))
    return jnp.where(distance < 8, distance, coarse) + 16 * (relative > 0).astype(jnp.int32)


def band_one_hot(num_buckets):
    band = jnp.arange(BANDS)[:, None, None] - 2
    query = jnp.arange(T)[None, :, None]
    key = jnp.arange(T)[None, None, :]
    ids = bucket_ids(band * T + key - query)
    return (ids[..., None] == jnp.arange(num_buckets)).astype(F32)


def can_move(sizes, rows):
    return rows % 16 == 0 and sizes[1] == 2 and sizes[0] % (Y * C) == 0 and sizes[0] > Y * C


class Place:
    def __init__(self, zs, xs):
        grp = lax.axis_index("grp")
        self.zs, self.xs = zs, xs
        self.x = lax.axis_index("seq")
        self.z = grp // (Y * C)
        self.y = (grp // C) % Y
        self.c = grp % C

    def device(self, z=None, y=None, c=None, x=None):
        z = self.z if z is None else z
        y = self.y if y is None else y
        c = self.c if c is None else c
        x = self.x if x is None else x
        return (z * (Y * C) + y * C + c, x)

    def peers(self):
        around = [self.device(z=(self.z + d) % self.zs) for d in range(1, self.zs)]
        return around + [
            self.device(y=1 - self.y),
            self.device(x=1 - self.x),
            self.device(c=1 - self.c),
        ]

    def barrier(self):
        sem = pltpu.get_barrier_semaphore()
        peers = self.peers()
        for peer in peers:
            pl.semaphore_signal(sem, inc=1, device_id=peer, device_id_type=MESH)
        pl.semaphore_wait(sem, len(peers))


def remote(src, dst, send_sem, recv_sem, device):
    return pltpu.make_async_remote_copy(
        src_ref=src,
        dst_ref=dst,
        send_sem=send_sem,
        recv_sem=recv_sem,
        device_id=device,
        device_id_type=MESH,
    )


def staged(step, offset, count, action):
    @pl.when((step >= offset) & (step < count + offset))
    def _():
        action(step - offset)


class Gather:
    def __init__(self, place, own, whole, send, recv):
        self.p, self.own, self.whole, self.send, self.recv = place, own, whole, send, recv

    def copy(self, k, half, index, src, dst, device):
        return remote(src, dst, self.send.at[k, half, index], self.recv.at[k, half, index], device)

    def along_z(self, k, half, d):
        p = self.p
        dst = self.whole.at[k, half, :, p.z, p.y, p.c * p.xs + p.x]
        return self.copy(k, half, d - 1, self.own.at[k, half], dst, p.device(z=(p.z + d) % p.zs))

    def second(self, k, half):
        p = self.p
        view = self.whole.at[k, half, :, :, p.y, p.c * p.xs + p.x]
        peer = p.device(x=1 - p.x) if half == 0 else p.device(y=1 - p.y)
        return self.copy(k, half, p.zs - 1, view, view, peer)

    def third(self, k, half):
        p = self.p
        if half == 0:
            view = self.whole.at[k, half, :, :, p.y, pl.ds(p.c * p.xs, p.xs)]
            peer = p.device(y=1 - p.y)
        else:
            view = self.whole.at[k, half, :, :, :, p.c * p.xs + p.x]
            peer = p.device(x=1 - p.x)
        return self.copy(k, half, p.zs, view, view, peer)

    def fourth(self, k, half):
        p = self.p
        view = self.whole.at[k, half, :, :, :, pl.ds(p.c * p.xs, p.xs)]
        return self.copy(k, half, p.zs + 1, view, view, p.device(c=1 - p.c))

    def tick(self, step, first, end):
        def start_z(k):
            for half in (0, 1):
                for d in range(1, self.p.zs):
                    self.along_z(k, half, d).start()

        def start_second(k):
            for half in (0, 1):
                for d in range(1, self.p.zs):
                    self.along_z(k, half, d).wait_recv()
                self.second(k, half).start()

        def start_third(k):
            for half in (0, 1):
                self.second(k, half).wait_recv()
                self.third(k, half).start()

        def start_fourth(k):
            for half in (0, 1):
                self.third(k, half).wait_recv()
                self.fourth(k, half).start()

        def finish(k):
            for half in (0, 1):
                self.fourth(k, half).wait_recv()
                for d in range(1, self.p.zs):
                    self.along_z(k, half, d).wait_send()
                self.second(k, half).wait_send()
                self.third(k, half).wait_send()
                self.fourth(k, half).wait_send()

        for offset, action in enumerate((start_z, start_second, start_third, start_fourth, finish)):
            staged(step, offset, end - first, lambda k, action=action: action(first + k))


def gather_kernel(zs, xs, own, whole, held, local, send, recv):
    place = Place(zs, xs)
    step = pl.program_id(0)

    @pl.when(step == 0)
    def _():
        place.barrier()
        load = pltpu.make_async_copy(own, held, local.at[0])
        load.start()
        load.wait()
        mine = whole.at[:, :, :, place.z, place.y, place.c * place.xs + place.x]
        store = pltpu.make_async_copy(held, mine, local.at[1])
        store.start()
        store.wait()

    Gather(place, held, whole, send, recv).tick(step, 0, own.shape[0])


def gather(own, sizes, collective_id):
    grp, seq = sizes
    chunks, halves, n, rows, lanes = own.shape
    if not can_move(sizes, rows):
        whole = lax.all_gather(own, ("grp", "seq"), axis=3, tiled=True)
        return whole
    zs = grp // (Y * C)
    slots = (chunks, 2, zs + 2)
    whole = pl.pallas_call(
        functools.partial(gather_kernel, zs, seq),
        grid=(chunks + 4,),
        out_shape=jax.ShapeDtypeStruct((chunks, 2, n, zs, Y, C * seq, rows, lanes), own.dtype),
        in_specs=[pl.BlockSpec(memory_space=pl.ANY)],
        out_specs=pl.BlockSpec(memory_space=pl.ANY),
        scratch_shapes=[
            pltpu.VMEM(own.shape, own.dtype),
            pltpu.SemaphoreType.DMA((2,)),
            pltpu.SemaphoreType.DMA(slots),
            pltpu.SemaphoreType.DMA(slots),
        ],
        compiler_params=pltpu.CompilerParams(collective_id=collective_id, has_side_effects=True),
    )(own)
    return whole.reshape(chunks, 2, n, grp * seq * rows, lanes)


class Scatter:
    def __init__(self, place, bufs, send, recv, out):
        self.p, self.send, self.recv, self.out = place, send, recv, out
        (self.in1, self.in2, self.in3, self.in4, self.sum1, self.sum2, self.sum3) = bufs

    def copy(self, k, half, index, src, dst, device):
        slot = k % 2
        return remote(
            src, dst, self.send.at[slot, half, index], self.recv.at[slot, half, index], device
        )

    def first(self, k, half, part):
        p = self.p
        src = part.at[half, :, :, :, pl.ds((1 - p.c) * p.xs, p.xs)]
        return self.copy(k, half, 0, src, self.in1.at[k % 2, half], p.device(c=1 - p.c))

    def second(self, k, half):
        p = self.p
        if half == 0:
            src, peer = self.sum1.at[k % 2, half, :, :, 1 - p.y], p.device(y=1 - p.y)
        else:
            src, peer = self.sum1.at[k % 2, half, :, :, :, 1 - p.x], p.device(x=1 - p.x)
        return self.copy(k, half, 1, src, self.in2.at[k % 2, half], peer)

    def third(self, k, half):
        p = self.p
        other = 1 - p.x if half == 0 else 1 - p.y
        peer = p.device(x=1 - p.x) if half == 0 else p.device(y=1 - p.y)
        src = self.sum2.at[k % 2, half, :, :, other]
        return self.copy(k, half, 2, src, self.in3.at[k % 2, half], peer)

    def fourth(self, k, half, d):
        p = self.p
        target = (p.z + d) % p.zs
        src = self.sum3.at[k % 2, half, :, target]
        dst = self.in4.at[k % 2, half, d - 1]
        return self.copy(k, half, 2 + d, src, dst, p.device(z=target))

    def finish(self, k):
        p = self.p
        slot = k % 2
        for half in (0, 1):
            total = self.sum3[slot, half, :, p.z].astype(F32)
            for d in range(1, p.zs):
                copy = self.fourth(k, half, d)
                copy.wait_recv()
                copy.wait_send()
                total = total + self.in4[slot, half, d - 1].astype(F32)
            self.out[k, half] = total

    def start_fourth(self, k):
        p = self.p
        slot = k % 2
        for half in (0, 1):
            copy = self.third(k, half)
            copy.wait_recv()
            copy.wait_send()
            keep = p.x if half == 0 else p.y
            for i in range(self.sum3.shape[2]):
                total = self.sum2[slot, half, i, :, keep].astype(F32)
                total = total + self.in3[slot, half, i].astype(F32)
                self.sum3[slot, half, i] = total.astype(BF)
            for d in range(1, p.zs):
                self.fourth(k, half, d).start()

    def start_third(self, k):
        p = self.p
        slot = k % 2
        for half in (0, 1):
            copy = self.second(k, half)
            copy.wait_recv()
            copy.wait_send()
            for i in range(self.sum2.shape[2]):
                if half == 0:
                    mine = self.sum1[slot, half, i, :, p.y]
                else:
                    mine = self.sum1[slot, half, i, :, :, p.x]
                total = mine.astype(F32) + self.in2[slot, half, i].astype(F32)
                self.sum2[slot, half, i] = total.astype(BF)
            self.third(k, half).start()

    def start_second(self, k, part):
        p = self.p
        slot = k % 2
        for half in (0, 1):
            copy = self.first(k, half, part)
            copy.wait_recv()
            copy.wait_send()

            def add(z, _, half=half):
                for i in range(self.sum1.shape[2]):
                    mine = part[half, i, z, :, pl.ds(p.c * p.xs, p.xs)]
                    total = mine.astype(F32) + self.in1[slot, half, i, z].astype(F32)
                    self.sum1[slot, half, i, z] = total.astype(BF)
                return 0

            lax.fori_loop(0, p.zs, add, 0)
            self.second(k, half).start()

    def start_first(self, k, part):
        for half in (0, 1):
            self.first(k, half, part).start()


def scatter_buffers(n, zs, xs, rows, lanes):
    shapes = [
        (2, 2, n, zs, Y, xs, rows, lanes),
        (2, 2, n, zs, 2, rows, lanes),
        (2, 2, n, zs, rows, lanes),
        (2, 2, zs - 1, n, rows, lanes),
        (2, 2, n, zs, Y, xs, rows, lanes),
        (2, 2, n, zs, 2, rows, lanes),
        (2, 2, n, zs, rows, lanes),
    ]
    return [pltpu.VMEM(shape, BF) for shape in shapes]


def scatter_kernel(zs, xs, chunks, parts, out, held, local, *rest):
    bufs, (send, recv) = rest[:7], rest[7:]
    place = Place(zs, xs)
    step = pl.program_id(0)
    engine = Scatter(place, bufs, send, recv, out)

    @pl.when(step == 0)
    def _():
        place.barrier()

    def load(k):
        return pltpu.make_async_copy(parts.at[k], held.at[k % 3], local.at[k % 3])

    def first(k):
        load(k).wait()
        engine.start_first(k, held.at[k % 3])

    staged(step, 5, chunks, engine.finish)
    staged(step, 4, chunks, engine.start_fourth)
    staged(step, 3, chunks, engine.start_third)
    staged(step, 2, chunks, lambda k: engine.start_second(k, held.at[k % 3]))
    staged(step, 1, chunks, first)
    staged(step, 0, chunks, lambda k: load(k).start())


def scatter(parts, sizes, rows, collective_id):
    grp, seq = sizes
    chunks, halves, n, _, lanes = parts.shape
    if not can_move(sizes, rows):
        return lax.psum_scatter(parts, ("grp", "seq"), scatter_dimension=3, tiled=True).astype(F32)
    zs = grp // (Y * C)
    view = parts.reshape(chunks, 2, n, zs, Y, C * seq, rows, lanes)
    sems = (2, 2, zs + 2)
    return pl.pallas_call(
        functools.partial(scatter_kernel, zs, seq, chunks),
        grid=(chunks + 5,),
        out_shape=jax.ShapeDtypeStruct((chunks, 2, n, rows, lanes), F32),
        in_specs=[pl.BlockSpec(memory_space=pl.ANY)],
        out_specs=pl.BlockSpec((chunks, 2, n, rows, lanes), lambda step: (0, 0, 0, 0, 0)),
        scratch_shapes=[
            pltpu.VMEM((3, 2, n, zs, Y, C * seq, rows, lanes), BF),
            pltpu.SemaphoreType.DMA((3,)),
        ]
        + scatter_buffers(n, zs, seq, rows, lanes)
        + [pltpu.SemaphoreType.DMA(sems), pltpu.SemaphoreType.DMA(sems)],
        compiler_params=pltpu.CompilerParams(
            collective_id=collective_id, has_side_effects=True, vmem_limit_bytes=VMEM_LIMIT
        ),
    )(view)


def band_of(key_tile, query_tile):
    return jnp.clip(key_tile - query_tile, -2, 2) + 2


def attend_kernel(tiles, local_tiles, conts, live, base, q, k, v, bias, out, norm):
    first_half = lax.broadcasted_iota(jnp.int32, (T, 2 * HEAD), 1) < HEAD
    place = lax.broadcasted_iota(jnp.int32, (T, T), 1)

    def tile(i, is_cont):
        rows = pl.ds(pl.multiple_of(i * T, T), T)
        queries = q[rows, :]
        query_tile = tiles if is_cont else base[0] + i
        cont = i - local_tiles
        cont_keys = pl.ds(pl.multiple_of((tiles + cont) * T, T), T)
        mixed = []
        for h in range(2):
            mine = first_half if h == 0 else ~first_half
            masked = jnp.where(mine, queries, jnp.zeros_like(queries))
            scores = nt(masked, k[0 : tiles * T, :])
            parts = []
            for j in range(tiles):
                band = band_of(lax.rem(base[1] + j, tiles), query_tile)
                parts.append(scores[:, j * T : (j + 1) * T] + bias[h, band])
            if is_cont:
                own = nt(masked, k[cont_keys, :]) + bias[h, 2]
                parts.append(jnp.where(place < live[0, cont], own, NEGATIVE))
            top = jnp.max(functools.reduce(jnp.maximum, parts), axis=1, keepdims=True)
            weights = [jnp.exp(part - top) for part in parts]
            total = jnp.sum(functools.reduce(jnp.add, weights), axis=1, keepdims=True)
            inverse = 1.0 / total
            probs = [(weight * inverse).astype(BF) for weight in weights]
            result = nn(jnp.concatenate(probs[:tiles], axis=1), v[0 : tiles * T, :])
            if is_cont:
                result = result + nn(probs[tiles], v[cont_keys, :])
            mixed.append(result)
            norm[h, rows, :] = top + jnp.log(total)
        out[rows, :] = jnp.where(first_half, mixed[0], mixed[1]).astype(BF)

    def prompt_tile(i, carry):
        tile(i, False)
        return carry

    def cont_tile(i, carry):
        tile(i, True)
        return carry

    lax.fori_loop(0, local_tiles, prompt_tile, 0)
    lax.fori_loop(local_tiles, local_tiles + conts, cont_tile, 0)


def attend(q, k, v, bias, live, base, tiles, local_tiles, conts):
    rows, width = q.shape
    keys = k.shape[0]
    pairs = width // (2 * HEAD)
    block = lambda n: pl.BlockSpec((n, 2 * HEAD), lambda h, *_: (0, h))
    return pl.pallas_call(
        functools.partial(attend_kernel, tiles, local_tiles, conts),
        grid_spec=pltpu.PrefetchScalarGridSpec(
            num_scalar_prefetch=2,
            grid=(pairs,),
            in_specs=[
                block(rows),
                block(keys),
                block(keys),
                pl.BlockSpec((2, BANDS, T, T), lambda h, *_: (h, 0, 0, 0)),
            ],
            out_specs=[block(rows), pl.BlockSpec((2, rows, 1), lambda h, *_: (h, 0, 0))],
        ),
        out_shape=[
            jax.ShapeDtypeStruct((rows, width), BF),
            jax.ShapeDtypeStruct((2 * pairs, rows, 1), F32),
        ],
        compiler_params=pltpu.CompilerParams(vmem_limit_bytes=VMEM_LIMIT),
    )(live, base, q, k, v, bias)


def attend_back_kernel(
    tiles,
    local_tiles,
    conts,
    live,
    base,
    q,
    k,
    v,
    bias,
    grad,
    out,
    norm,
    d_q,
    d_k,
    d_v,
    d_bias,
    k_sum,
    v_sum,
):
    first_half = lax.broadcasted_iota(jnp.int32, (T, 2 * HEAD), 1) < HEAD
    place = lax.broadcasted_iota(jnp.int32, (T, T), 1)
    k_sum[...] = jnp.zeros_like(k_sum)
    v_sum[...] = jnp.zeros_like(v_sum)
    d_bias[...] = jnp.zeros_like(d_bias)

    def tile(i, is_cont):
        rows = pl.ds(pl.multiple_of(i * T, T), T)
        queries = q[rows, :]
        grads = grad[rows, :]
        query_tile = tiles if is_cont else base[0] + i
        overlap = grads.astype(F32) * out[rows, :].astype(F32)
        mixed = []
        for h in range(2):
            mine = first_half if h == 0 else ~first_half
            masked = jnp.where(mine, queries, jnp.zeros_like(queries))
            masked_grad = jnp.where(mine, grads, jnp.zeros_like(grads))
            inner = jnp.sum(jnp.where(mine, overlap, 0.0), axis=1, keepdims=True)
            log_norm = norm[h, rows, :]

            def piece(keys, bands, allowed):
                scores = nt(masked, k[keys, :])
                d_probs = nt(masked_grad, v[keys, :])
                probs_low, scores_low = [], []
                for j, band in enumerate(bands):
                    cols = slice(j * T, (j + 1) * T)
                    logits = scores[:, cols] + bias[h, band]
                    if allowed is not None:
                        logits = jnp.where(allowed, logits, NEGATIVE)
                    probs = jnp.exp(logits - log_norm)
                    d_scores = probs * (d_probs[:, cols] - inner)
                    d_bias[h, band] += d_scores
                    probs_low.append(probs.astype(BF))
                    scores_low.append(d_scores.astype(BF))
                probs_low = jnp.concatenate(probs_low, axis=1)
                scores_low = jnp.concatenate(scores_low, axis=1)
                v_sum[keys, :] += tn(probs_low, masked_grad)
                k_sum[keys, :] += tn(scores_low, masked)
                return nn(scores_low, k[keys, :])

            bands = [band_of(lax.rem(base[1] + j, tiles), query_tile) for j in range(tiles)]
            result = piece(pl.ds(0, tiles * T), bands, None)
            if is_cont:
                cont = i - local_tiles
                cont_keys = pl.ds(pl.multiple_of((tiles + cont) * T, T), T)
                result = result + piece(cont_keys, [2], place < live[0, cont])
            mixed.append(result)
        d_q[rows, :] = jnp.where(first_half, mixed[0], mixed[1]).astype(BF)

    def prompt_tile(i, carry):
        tile(i, False)
        return carry

    def cont_tile(i, carry):
        tile(i, True)
        return carry

    lax.fori_loop(0, local_tiles, prompt_tile, 0)
    lax.fori_loop(local_tiles, local_tiles + conts, cont_tile, 0)
    d_k[...] = k_sum[...].astype(BF)
    d_v[...] = v_sum[...].astype(BF)


def attend_back(q, k, v, bias, grad, out, norm, live, base, tiles, local_tiles, conts):
    rows, width = q.shape
    keys = k.shape[0]
    pairs = width // (2 * HEAD)
    block = lambda n: pl.BlockSpec((n, 2 * HEAD), lambda h, *_: (0, h))
    bands = pl.BlockSpec((2, BANDS, T, T), lambda h, *_: (h, 0, 0, 0))
    return pl.pallas_call(
        functools.partial(attend_back_kernel, tiles, local_tiles, conts),
        grid_spec=pltpu.PrefetchScalarGridSpec(
            num_scalar_prefetch=2,
            grid=(pairs,),
            in_specs=[
                block(rows),
                block(keys),
                block(keys),
                bands,
                block(rows),
                block(rows),
                pl.BlockSpec((2, rows, 1), lambda h, *_: (h, 0, 0)),
            ],
            out_specs=[block(rows), block(keys), block(keys), bands],
            scratch_shapes=[pltpu.VMEM((keys, 2 * HEAD), F32), pltpu.VMEM((keys, 2 * HEAD), F32)],
        ),
        out_shape=[
            jax.ShapeDtypeStruct((rows, width), BF),
            jax.ShapeDtypeStruct((keys, width), BF),
            jax.ShapeDtypeStruct((keys, width), BF),
            jax.ShapeDtypeStruct((2 * pairs, BANDS, T, T), F32),
        ],
        compiler_params=pltpu.CompilerParams(vmem_limit_bytes=VMEM_LIMIT),
    )(live, base, q, k, v, bias, grad, out, norm)


GELU_SCALE = 0.7978845608028654
GELU_CUBIC = 0.044715


def gelu_and_slope(a):
    square = a * a
    tanh = jnp.tanh(GELU_SCALE * a * (1.0 + GELU_CUBIC * square))
    half = 0.5 * (1.0 + tanh)
    slope = half + 0.5 * a * (1.0 - tanh * tanh) * (
        GELU_SCALE * (1.0 + 3.0 * GELU_CUBIC * square)
    )
    return a * half, slope


def feed_load(x_hbm, dy_hbm, x, x_t, dy, dy_t, sem):
    load_x = pltpu.make_async_copy(x_hbm, x, sem.at[0])
    load_dy = pltpu.make_async_copy(dy_hbm, dy, sem.at[1])
    load_x.start()
    load_dy.start()
    load_x.wait()
    load_dy.wait()

    def turn(i, carry):
        part = pl.ds(pl.multiple_of(i * T, T), T)
        x_t[:, part] = x[part, :].T
        dy_t[:, part] = dy[part, :].T
        return carry

    lax.fori_loop(0, x.shape[0] // T, turn, 0)


def feed_chunk(read, write, blocks, out, d_x, x, x_t, dy, dy_t, hidden, d_gate, d_up):
    rows, width = x.shape
    row_block = min(rows, 256)
    width_block = width // blocks
    w_gate, w_up, w_down = [jnp.concatenate([read(0, i), read(1, i)], axis=1) for i in range(3)]

    def by_rows(i, carry):
        part = pl.ds(pl.multiple_of(i * row_block, row_block), row_block)
        gate = nn(x[part, :], w_gate)
        up = nn(x[part, :], w_up)
        d_hidden = nn(dy[part, :], w_down)
        active, slope = gelu_and_slope(gate)
        hidden_low = (active * up).astype(BF)
        d_gate_low = (d_hidden * up * slope).astype(BF)
        d_up_low = (d_hidden * active).astype(BF)
        hidden[part, :] = hidden_low
        d_gate[part, :] = d_gate_low
        d_up[part, :] = d_up_low
        out[part, :] += nt(hidden_low, w_down)
        d_x[part, :] += nt(d_gate_low, w_gate) + nt(d_up_low, w_up)
        return carry

    lax.fori_loop(0, rows // row_block, by_rows, 0)

    def by_width(i, carry):
        part = pl.ds(pl.multiple_of(i * width_block, width_block), width_block)
        pairs = ((x_t, d_gate), (x_t, d_up), (dy_t, hidden))
        for index, (left, right) in enumerate(pairs):
            total = nn(left[part, :], right[...]).astype(BF)
            write(0, index, i, total[:, :T])
            write(1, index, i, total[:, T:])
        return carry

    lax.fori_loop(0, blocks, by_width, 0)


def feed_kernel(x_hbm, dy_hbm, weights, out, d_x, grads, x, x_t, dy, dy_t, *rest):
    *work, sem = rest
    width_block = 512

    @pl.when(pl.program_id(0) == 0)
    def _():
        feed_load(x_hbm, dy_hbm, x, x_t, dy, dy_t, sem)
        out[...] = jnp.zeros_like(out)
        d_x[...] = jnp.zeros_like(d_x)

    def write(half, index, block, value):
        part = pl.ds(pl.multiple_of(block * width_block, width_block), width_block)
        grads[0, half, index, part, :] = value

    read = lambda half, index: weights[0, half, index]
    blocks = x.shape[1] // width_block
    feed_chunk(read, write, blocks, out, d_x, x, x_t, dy, dy_t, *work)


def feed_scratch(rows, width):
    return [
        pltpu.VMEM((rows, width), BF),
        pltpu.VMEM((width, rows), BF),
        pltpu.VMEM((rows, width), BF),
        pltpu.VMEM((width, rows), BF),
        pltpu.VMEM((rows, 2 * T), BF),
        pltpu.VMEM((rows, 2 * T), BF),
        pltpu.VMEM((rows, 2 * T), BF),
        pltpu.SemaphoreType.DMA((2,)),
    ]


def feed(x, dy, weights):
    rows, width = x.shape
    chunks = weights.shape[0]
    chunk = pl.BlockSpec((1, 2, 3, width, T), lambda j: (j, 0, 0, 0, 0))
    whole = pl.BlockSpec((rows, width), lambda j: (0, 0), pipeline_mode=pl.Buffered(1))
    return pl.pallas_call(
        feed_kernel,
        grid=(chunks,),
        in_specs=[pl.BlockSpec(memory_space=pl.ANY)] * 2 + [chunk],
        out_specs=[whole, whole, chunk],
        out_shape=[
            jax.ShapeDtypeStruct((rows, width), F32),
            jax.ShapeDtypeStruct((rows, width), F32),
            jax.ShapeDtypeStruct((chunks, 2, 3, width, T), BF),
        ],
        scratch_shapes=feed_scratch(rows, width),
        compiler_params=pltpu.CompilerParams(vmem_limit_bytes=VMEM_LIMIT),
    )(x, dy, weights)


def feed_moving_kernel(zs, xs, early, kept, *refs):
    x_hbm, dy_hbm, own, ready, out, d_x, whole, parts, sums = refs[:9]
    x, x_t, dy, dy_t, hidden, d_gate, d_up, sem = refs[9:17]
    held, w_buf, g_buf, local = refs[17:21]
    gather_sems, bufs, scatter_sems = refs[21:23], refs[23:30], refs[30:32]
    chunks = own.shape[0]
    place = Place(zs, xs)
    step = pl.program_id(0)
    lag = max(0, 5 - early)
    first_kept, end_kept = kept
    width = x.shape[1]

    @pl.when(step == 0)
    def _():
        place.barrier()

    fetch = Gather(place, own, whole, *gather_sems)
    fetch.tick(step, early, chunks)

    @pl.when(step == 0)
    def _():
        load = pltpu.make_async_copy(own, held, local.at[0])
        load.start()
        load.wait()
        mine = whole.at[:, :, :, place.z, place.y, place.c * place.xs + place.x]
        store = pltpu.make_async_copy(held, mine, local.at[1])
        store.start()
        store.wait()
        feed_load(x_hbm, dy_hbm, x, x_t, dy, dy_t, sem)
        out[...] = jnp.zeros_like(out)
        d_x[...] = jnp.zeros_like(d_x)

    def weight_load(j, source):
        return pltpu.make_async_copy(source.at[j], w_buf.at[j % 2], local.at[2 + j % 2])

    def start_load(j):
        if early > 0:

            @pl.when(j < early)
            def _():
                weight_load(j, ready).start()

        @pl.when(j >= early)
        def _():
            weight_load(j, whole).start()

    def part_store(j):
        return pltpu.make_async_copy(g_buf.at[j % 2], parts.at[j], local.at[4 + j % 2])

    def is_kept(j):
        return (j >= first_kept) & (j < end_kept)

    engine = Scatter(place, bufs, *scatter_sems, sums)
    due = lag + first_kept
    number = end_kept - first_kept
    grads_of = lambda k: g_buf.at[(k + first_kept) % 2]
    staged(step, due + 5, number, engine.finish)
    staged(step, due + 4, number, engine.start_fourth)
    staged(step, due + 3, number, engine.start_third)
    staged(step, due + 2, number, lambda k: engine.start_second(k, grads_of(k)))
    staged(step, due + 1, number, lambda k: engine.start_first(k, grads_of(k)))

    chunk = step - lag
    if lag == 0:

        @pl.when(step == 0)
        def _():
            start_load(0)

    @pl.when((chunk >= (0 if lag == 0 else -1)) & (chunk + 1 < chunks))
    def _():
        start_load(chunk + 1)

    @pl.when((chunk >= 2) & (chunk < chunks + 2) & ~is_kept(chunk - 2))
    def _():
        part_store(chunk - 2).wait()

    @pl.when((chunk >= 0) & (chunk < chunks))
    def _():
        weight_load(chunk, whole).wait()
        slot = chunk % 2

        def read(half, index):
            return w_buf[slot, half, index].reshape(width, T)

        def write(half, index, block, value):
            shape = g_buf.shape[4:]
            g_buf[slot, half, index, block] = value.reshape(shape)

        work = (hidden, d_gate, d_up)
        feed_chunk(read, write, zs, out, d_x, x, x_t, dy, dy_t, *work)

        @pl.when(~is_kept(chunk))
        def _():
            part_store(chunk).start()


def feed_moving(x, dy, own, ready, sizes, early, kept, collective_id):
    grp, seq = sizes
    rows, width = x.shape
    chunks, _, n, shard, lanes = own.shape
    zs = grp // (Y * C)
    tile = (2, n, zs, Y, C * seq, shard, lanes)
    whole = pl.BlockSpec((rows, width), lambda j: (0, 0), pipeline_mode=pl.Buffered(1))
    number = kept[1] - kept[0]
    sums = pl.BlockSpec(
        (number, 2, n, shard, lanes), lambda j: (0,) * 5, pipeline_mode=pl.Buffered(1)
    )
    lag = max(0, 5 - early)
    steps = lag + max(chunks + 2, kept[1] + 5)
    anywhere = pl.BlockSpec(memory_space=pl.ANY)
    sems = lambda *shape: pltpu.SemaphoreType.DMA(shape)
    return pl.pallas_call(
        functools.partial(feed_moving_kernel, zs, seq, early, kept),
        grid=(steps,),
        in_specs=[anywhere] * 4,
        out_specs=[whole, whole, anywhere, anywhere, sums],
        out_shape=[
            jax.ShapeDtypeStruct((rows, width), F32),
            jax.ShapeDtypeStruct((rows, width), F32),
            jax.ShapeDtypeStruct((chunks, *tile), BF),
            jax.ShapeDtypeStruct((chunks, *tile), BF),
            jax.ShapeDtypeStruct((number, 2, n, shard, lanes), F32),
        ],
        scratch_shapes=feed_scratch(rows, width)
        + [
            pltpu.VMEM(own.shape, BF),
            pltpu.VMEM((2, *tile), BF),
            pltpu.VMEM((2, *tile), BF),
            sems(6),
            sems(chunks, 2, zs + 2),
            sems(chunks, 2, zs + 2),
        ]
        + scatter_buffers(n, zs, seq, shard, lanes)
        + [sems(2, 2, zs + 2), sems(2, 2, zs + 2)],
        compiler_params=pltpu.CompilerParams(
            collective_id=collective_id, has_side_effects=True, vmem_limit_bytes=VMEM_LIMIT
        ),
    )(x, dy, own, ready)


def rms_scale(values):
    return lax.rsqrt(jnp.mean(values * values, axis=-1, keepdims=True) + EPS)


def norm_back(d_normed, unit, scale, gain):
    d_unit = d_normed * gain
    return scale * (d_unit - unit * jnp.mean(d_unit * unit, axis=-1, keepdims=True))


def pieces_of(matrix):
    rows, columns = matrix.shape
    return jnp.swapaxes(matrix.reshape(rows, columns // T, T), 0, 1)


def joined(pieces):
    count, rows, _ = pieces.shape
    return jnp.swapaxes(pieces, 0, 1).reshape(rows, count * T)


def attention_chunks(matrices):
    flat = jnp.concatenate([pieces_of(m) for m in matrices], axis=0)
    pad = -flat.shape[0] % 6
    flat = jnp.pad(flat, ((0, pad), (0, 0), (0, 0)))
    return flat.reshape(-1, 2, 3, *flat.shape[1:])


def feed_chunks(matrices):
    stacked = jnp.stack([pieces_of(m) for m in matrices], axis=1)
    pad = -stacked.shape[0] % 2
    stacked = jnp.pad(stacked, ((0, pad), (0, 0), (0, 0), (0, 0)))
    return stacked.reshape(-1, 2, *stacked.shape[1:])


def body(sizes, *args):
    (
        prompt_x,
        cont_x,
        cont_len,
        prompt_cot,
        cont_cot,
        norm1_gain,
        q_weight,
        k_weight,
        v_weight,
        o_weight,
        bucket_table,
        norm2_gain,
        gate_weight,
        up_weight,
        down_weight,
    ) = args
    _, local_prompt, width = prompt_x.shape
    conts, cont_rows = cont_x.shape[1], cont_x.shape[2]
    assert prompt_x.shape[0] == 1 and cont_rows == T and local_prompt % T == 0
    seq = sizes[1]
    num_buckets, heads = bucket_table.shape
    inner = q_weight.shape[1]
    assert inner == heads * HEAD
    shard = q_weight.shape[0]
    hidden_width = gate_weight.shape[1]
    local_tiles = local_prompt // T
    tiles = local_tiles * seq
    seq_index = lax.axis_index("seq")

    x_low = jnp.concatenate([prompt_x[0], cont_x[0].reshape(-1, width)], axis=0)
    dy_low = jnp.concatenate([prompt_cot[0], cont_cot[0].reshape(-1, width)], axis=0)
    x = x_low.astype(F32)
    dy = dy_low.astype(F32)

    lanes = jnp.zeros((shard, T - 2), F32)
    gains = jnp.concatenate([norm1_gain[:, None], norm2_gain[:, None], lanes], axis=1)
    own_attention = attention_chunks([q_weight, k_weight, v_weight, o_weight, gains]).astype(BF)
    own_feed = feed_chunks([gate_weight, up_weight, down_weight]).astype(BF)
    attention_whole = gather(own_attention, sizes, 0)
    count = inner // T
    flat = attention_whole.reshape(-1, width, T)
    q_full, k_full, v_full, o_full = [
        joined(flat[i * count : (i + 1) * count]) for i in range(4)
    ]
    gain_one = flat[4 * count, :, 0].astype(F32)
    gain_two = flat[4 * count, :, 1].astype(F32)

    scale_one = rms_scale(x)
    unit_one = x * scale_one
    normed_one = (unit_one * gain_one).astype(BF)
    kv = nn(normed_one, jnp.concatenate([k_full, v_full], axis=1)).astype(BF)
    queries = nn(normed_one, q_full).astype(BF)
    prompt_kv = kv[:local_prompt]
    if seq == 2:
        other = lax.ppermute(prompt_kv, "seq", [(0, 1), (1, 0)])
        every = jnp.concatenate([kv[:local_prompt], other, kv[local_prompt:]], axis=0)
        first_tile = seq_index * local_tiles
    else:
        gathered = lax.all_gather(prompt_kv, "seq", axis=0, tiled=True)
        every = jnp.concatenate([gathered, kv[local_prompt:]], axis=0)
        first_tile = jnp.zeros((), jnp.int32)
    keys, values = every[:, :inner], every[:, inner:]
    base = jnp.stack([seq_index * local_tiles, first_tile]).astype(jnp.int32)

    one_hot = band_one_hot(num_buckets)
    bias = jnp.einsum("cqkb,bh->hcqk", one_hot, bucket_table, precision=lax.Precision.HIGHEST)
    attended, log_norm = attend(
        queries, keys, values, bias, cont_len, base, tiles, local_tiles, conts
    )
    middle = x + nt(attended, o_full)
    scale_two = rms_scale(middle)
    unit_two = middle * scale_two
    normed_two = (unit_two * gain_two).astype(BF)

    moving = can_move(sizes, shard)
    if moving:
        kept = (0, own_feed.shape[0])
        out_sum, d_normed_two, _, _, feed_sums = feed_moving(
            normed_two, dy_low, own_feed, own_feed, sizes, 0, kept, 1
        )
    else:
        feed_whole = gather(own_feed, sizes, 1)
        out_sum, d_normed_two, feed_grads = feed(normed_two, dy_low, feed_whole)
        feed_sums = scatter(feed_grads, sizes, shard, 3)
    final = (middle + out_sum).astype(BF)

    d_gain_two = jnp.sum(d_normed_two * unit_two, axis=0)
    d_middle = dy + norm_back(d_normed_two, unit_two, scale_two, gain_two)
    d_branch = d_middle.astype(BF)
    d_attended = nn(d_branch, o_full).astype(BF)
    d_o = tn(d_branch, attended)

    d_queries, d_keys, d_values, d_bias = attend_back(
        queries,
        keys,
        values,
        bias,
        d_attended,
        attended,
        log_norm,
        cont_len,
        base,
        tiles,
        local_tiles,
        conts,
    )
    d_table = jnp.einsum("hcqk,cqkb->bh", d_bias, one_hot, precision=lax.Precision.HIGHEST)
    d_kv = jnp.concatenate([d_keys, d_values], axis=1)
    prompt_rows = local_prompt * seq
    if seq == 2:
        back = lax.ppermute(d_kv[local_prompt:prompt_rows], "seq", [(0, 1), (1, 0)])
        d_prompt = (d_kv[:local_prompt].astype(F32) + back.astype(F32)).astype(BF)
    else:
        d_prompt = lax.psum_scatter(
            d_kv[:prompt_rows], "seq", scatter_dimension=0, tiled=True
        )
    d_kv = jnp.concatenate([d_prompt, d_kv[prompt_rows:]], axis=0)
    d_normed_one = nt(d_queries, q_full) + nt(d_kv, jnp.concatenate([k_full, v_full], axis=1))
    d_q = tn(normed_one, d_queries)
    d_kv_weight = tn(normed_one, d_kv)
    d_gain_one = jnp.sum(d_normed_one * unit_one, axis=0)
    d_x = d_middle + norm_back(d_normed_one, unit_one, scale_one, gain_one)
    d_x = d_x.astype(BF)

    attention_parts = attention_chunks([d_q, d_kv_weight, d_o]).astype(BF)
    attention_sums = scatter(attention_parts, sizes, shard, 2).reshape(-1, shard, T)
    feed_sums = feed_sums.reshape(-1, 3, shard, T)
    feed_sums = feed_sums[: hidden_width // T]
    gate_grad, up_grad, down_grad = [joined(feed_sums[:, i]) for i in range(3)]
    q_grad, k_grad, v_grad, o_grad = [
        joined(attention_sums[i * count : (i + 1) * count]) for i in range(4)
    ]
    norm1_grad = lax.psum_scatter(d_gain_one, ("grp", "seq"), scatter_dimension=0, tiled=True)
    norm2_grad = lax.psum_scatter(d_gain_two, ("grp", "seq"), scatter_dimension=0, tiled=True)
    table_grad = lax.psum(d_table, ("grp", "seq"))
    split = lambda rows: (
        rows[:local_prompt][None],
        rows[local_prompt:].reshape(1, conts, cont_rows, width),
    )
    return (
        *split(final),
        *split(d_x),
        norm1_grad,
        q_grad,
        k_grad,
        v_grad,
        o_grad,
        table_grad,
        norm2_grad,
        gate_grad,
        up_grad,
        down_grad,
    )


def solution(mesh):
    sizes = (mesh.shape["grp"], mesh.shape["seq"])
    rows = P("grp", "seq", None)
    conts = P("grp", "seq", None, None)
    shard = P(("grp", "seq"), None)
    gain = P(("grp", "seq"))
    in_specs = (rows, conts, P("grp", "seq"), rows, conts, gain, shard, shard, shard, shard)
    in_specs += (P(), gain, shard, shard, shard)
    out_specs = (rows, conts, rows, conts, gain, shard, shard, shard, shard, P(), gain)
    out_specs += (shard, shard, shard)
    return jax.shard_map(
        functools.partial(body, sizes),
        mesh=mesh,
        in_specs=in_specs,
        out_specs=out_specs,
        check_vma=False,
    )
```

```python
import functools

import jax
import jax.numpy as jnp
from jax import lax
from jax.experimental import pallas as pl
from jax.experimental.pallas import tpu as pltpu
from jax.sharding import PartitionSpec as P

EPS = 1e-06
LIMITS = (8, 12, 16, 23, 32, 46, 64, 91)
NEGATIVE = -1e30
MESH = pl.DeviceIdType.MESH
T = 128
HEAD = 64
BANDS = 5
BF = jnp.bfloat16
F32 = jnp.float32
VMEM_LIMIT = 63 * 2**20
Y = 2
C = 2


def nn(left, right):
    return jnp.dot(left, right, preferred_element_type=F32)


def nt(left, right):
    return lax.dot_general(left, right, (((1,), (1,)), ((), ())), preferred_element_type=F32)


def tn(left, right):
    return lax.dot_general(left, right, (((0,), (0,)), ((), ())), preferred_element_type=F32)


def bucket_ids(relative):
    distance = jnp.abs(relative)
    coarse = 7 + sum(((distance >= boundary).astype(jnp.int32) for boundary in LIMITS))
    return jnp.where(distance < 8, distance, coarse) + 16 * (relative > 0).astype(jnp.int32)


def band_one_hot(num_buckets):
    band = jnp.arange(BANDS)[:, None, None] - 2
    query = jnp.arange(T)[None, :, None]
    key = jnp.arange(T)[None, None, :]
    ids = bucket_ids(band * T + key - query)
    return (ids[..., None] == jnp.arange(num_buckets)).astype(F32)


def can_move(sizes, rows):
    zs = sizes[0] // (Y * C)
    return rows % 16 == 0 and sizes[1] == 2 and sizes[0] % (Y * C) == 0 and zs in (2, 4, 8, 16)


class Place:
    def __init__(self, zs, xs):
        grp = lax.axis_index("grp")
        self.zs, self.xs = zs, xs
        self.x = lax.axis_index("seq")
        self.z = grp // (Y * C)
        self.y = (grp // C) % Y
        self.c = grp % C

    def device(self, z=None, y=None, c=None, x=None):
        z = self.z if z is None else z
        y = self.y if y is None else y
        c = self.c if c is None else c
        x = self.x if x is None else x
        return (z * (Y * C) + y * C + c, x)

    def peers(self):
        around = [self.device(z=(self.z + d) % self.zs) for d in range(1, self.zs)]
        return around + [
            self.device(y=1 - self.y),
            self.device(x=1 - self.x),
            self.device(c=1 - self.c),
        ]

    def barrier(self):
        sem = pltpu.get_barrier_semaphore()
        peers = self.peers()
        for peer in peers:
            pl.semaphore_signal(sem, inc=1, device_id=peer, device_id_type=MESH)
        pl.semaphore_wait(sem, len(peers))


def remote(src, dst, send_sem, recv_sem, device):
    return pltpu.make_async_remote_copy(
        src_ref=src,
        dst_ref=dst,
        send_sem=send_sem,
        recv_sem=recv_sem,
        device_id=device,
        device_id_type=MESH,
    )


def staged(step, offset, count, action):
    @pl.when((step >= offset) & (step < count + offset))
    def _():
        action(step - offset)


class Gather:
    def __init__(self, place, own, whole, send, recv):
        self.p, self.own, self.whole, self.send, self.recv = place, own, whole, send, recv

    def copy(self, k, half, index, src, dst, device):
        return remote(src, dst, self.send.at[k, half, index], self.recv.at[k, half, index], device)

    def along_z(self, k, half, d):
        p = self.p
        dst = self.whole.at[k, half, :, p.z, p.y, p.c * p.xs + p.x]
        return self.copy(k, half, d - 1, self.own.at[k, half], dst, p.device(z=(p.z + d) % p.zs))

    def second(self, k, half):
        p = self.p
        view = self.whole.at[k, half, :, :, p.y, p.c * p.xs + p.x]
        peer = p.device(x=1 - p.x) if half == 0 else p.device(y=1 - p.y)
        return self.copy(k, half, p.zs - 1, view, view, peer)

    def third(self, k, half):
        p = self.p
        if half == 0:
            view = self.whole.at[k, half, :, :, p.y, pl.ds(p.c * p.xs, p.xs)]
            peer = p.device(y=1 - p.y)
        else:
            view = self.whole.at[k, half, :, :, :, p.c * p.xs + p.x]
            peer = p.device(x=1 - p.x)
        return self.copy(k, half, p.zs, view, view, peer)

    def fourth(self, k, half):
        p = self.p
        view = self.whole.at[k, half, :, :, :, pl.ds(p.c * p.xs, p.xs)]
        return self.copy(k, half, p.zs + 1, view, view, p.device(c=1 - p.c))

    def tick(self, step, first, end):
        def start_z(k):
            for half in (0, 1):
                for d in range(1, self.p.zs):
                    self.along_z(k, half, d).start()

        def start_second(k):
            for half in (0, 1):
                for d in range(1, self.p.zs):
                    self.along_z(k, half, d).wait_recv()
                self.second(k, half).start()

        def start_third(k):
            for half in (0, 1):
                self.second(k, half).wait_recv()
                self.third(k, half).start()

        def start_fourth(k):
            for half in (0, 1):
                self.third(k, half).wait_recv()
                self.fourth(k, half).start()

        def finish(k):
            for half in (0, 1):
                self.fourth(k, half).wait_recv()
                for d in range(1, self.p.zs):
                    self.along_z(k, half, d).wait_send()
                self.second(k, half).wait_send()
                self.third(k, half).wait_send()
                self.fourth(k, half).wait_send()

        for offset, action in enumerate((start_z, start_second, start_third, start_fourth, finish)):
            staged(step, offset, end - first, lambda k, action=action: action(first + k))


def gather_kernel(zs, xs, own, whole, held, local, send, recv):
    place = Place(zs, xs)
    step = pl.program_id(0)

    @pl.when(step == 0)
    def _():
        place.barrier()
        load = pltpu.make_async_copy(own, held, local.at[0])
        load.start()
        load.wait()
        mine = whole.at[:, :, :, place.z, place.y, place.c * place.xs + place.x]
        store = pltpu.make_async_copy(held, mine, local.at[1])
        store.start()
        store.wait()

    Gather(place, held, whole, send, recv).tick(step, 0, own.shape[0])


def gather(own, sizes, collective_id):
    grp, seq = sizes
    chunks, halves, n, rows, lanes = own.shape
    if not can_move(sizes, rows):
        whole = lax.all_gather(own, ("grp", "seq"), axis=3, tiled=True)
        return whole
    zs = grp // (Y * C)
    slots = (chunks, 2, zs + 2)
    whole = pl.pallas_call(
        functools.partial(gather_kernel, zs, seq),
        grid=(chunks + 4,),
        out_shape=jax.ShapeDtypeStruct((chunks, 2, n, zs, Y, C * seq, rows, lanes), own.dtype),
        in_specs=[pl.BlockSpec(memory_space=pl.ANY)],
        out_specs=pl.BlockSpec(memory_space=pl.ANY),
        scratch_shapes=[
            pltpu.VMEM(own.shape, own.dtype),
            pltpu.SemaphoreType.DMA((2,)),
            pltpu.SemaphoreType.DMA(slots),
            pltpu.SemaphoreType.DMA(slots),
        ],
        compiler_params=pltpu.CompilerParams(collective_id=collective_id, has_side_effects=True),
    )(own)
    return whole.reshape(chunks, 2, n, grp * seq * rows, lanes)


class Scatter:
    def __init__(self, place, bufs, send, recv, out):
        self.p, self.send, self.recv, self.out = place, send, recv, out
        (self.in1, self.in2, self.in3, self.in4, self.sum1, self.sum2, self.sum3) = bufs

    def copy(self, k, half, index, src, dst, device):
        slot = k % 2
        return remote(
            src, dst, self.send.at[slot, half, index], self.recv.at[slot, half, index], device
        )

    def first(self, k, half, part):
        p = self.p
        src = part.at[half, :, :, :, pl.ds((1 - p.c) * p.xs, p.xs)]
        return self.copy(k, half, 0, src, self.in1.at[k % 2, half], p.device(c=1 - p.c))

    def second(self, k, half):
        p = self.p
        if half == 0:
            src, peer = self.sum1.at[k % 2, half, :, :, 1 - p.y], p.device(y=1 - p.y)
        else:
            src, peer = self.sum1.at[k % 2, half, :, :, :, 1 - p.x], p.device(x=1 - p.x)
        return self.copy(k, half, 1, src, self.in2.at[k % 2, half], peer)

    def third(self, k, half):
        p = self.p
        other = 1 - p.x if half == 0 else 1 - p.y
        peer = p.device(x=1 - p.x) if half == 0 else p.device(y=1 - p.y)
        src = self.sum2.at[k % 2, half, :, :, other]
        return self.copy(k, half, 2, src, self.in3.at[k % 2, half], peer)

    def fourth(self, k, half, d):
        p = self.p
        target = (p.z + d) % p.zs
        src = self.sum3.at[k % 2, half, :, target]
        dst = self.in4.at[k % 2, half, d - 1]
        return self.copy(k, half, 2 + d, src, dst, p.device(z=target))

    def finish(self, k):
        p = self.p
        slot = k % 2
        for half in (0, 1):
            total = self.sum3[slot, half, :, p.z].astype(F32)
            for d in range(1, p.zs):
                copy = self.fourth(k, half, d)
                copy.wait_recv()
                copy.wait_send()
                total = total + self.in4[slot, half, d - 1].astype(F32)
            self.out[k, half] = total

    def start_fourth(self, k):
        p = self.p
        slot = k % 2
        for half in (0, 1):
            copy = self.third(k, half)
            copy.wait_recv()
            copy.wait_send()
            keep = p.x if half == 0 else p.y
            for i in range(self.sum3.shape[2]):
                total = self.sum2[slot, half, i, :, keep].astype(F32)
                total = total + self.in3[slot, half, i].astype(F32)
                self.sum3[slot, half, i] = total.astype(BF)
            for d in range(1, p.zs):
                self.fourth(k, half, d).start()

    def start_third(self, k):
        p = self.p
        slot = k % 2
        for half in (0, 1):
            copy = self.second(k, half)
            copy.wait_recv()
            copy.wait_send()
            for i in range(self.sum2.shape[2]):
                if half == 0:
                    mine = self.sum1[slot, half, i, :, p.y]
                else:
                    mine = self.sum1[slot, half, i, :, :, p.x]
                total = mine.astype(F32) + self.in2[slot, half, i].astype(F32)
                self.sum2[slot, half, i] = total.astype(BF)
            self.third(k, half).start()

    def start_second(self, k, part):
        p = self.p
        slot = k % 2
        for half in (0, 1):
            copy = self.first(k, half, part)
            copy.wait_recv()
            copy.wait_send()

            def add(z, _, half=half):
                for i in range(self.sum1.shape[2]):
                    mine = part[half, i, z, :, pl.ds(p.c * p.xs, p.xs)]
                    total = mine.astype(F32) + self.in1[slot, half, i, z].astype(F32)
                    self.sum1[slot, half, i, z] = total.astype(BF)
                return 0

            lax.fori_loop(0, p.zs, add, 0)
            self.second(k, half).start()

    def start_first(self, k, part):
        for half in (0, 1):
            self.first(k, half, part).start()


def scatter_buffers(n, zs, xs, rows, lanes):
    shapes = [
        (2, 2, n, zs, Y, xs, rows, lanes),
        (2, 2, n, zs, 2, rows, lanes),
        (2, 2, n, zs, rows, lanes),
        (2, 2, zs - 1, n, rows, lanes),
        (2, 2, n, zs, Y, xs, rows, lanes),
        (2, 2, n, zs, 2, rows, lanes),
        (2, 2, n, zs, rows, lanes),
    ]
    return [pltpu.VMEM(shape, BF) for shape in shapes]


def scatter_kernel(zs, xs, chunks, parts, out, held, local, *rest):
    bufs, (send, recv) = rest[:7], rest[7:]
    place = Place(zs, xs)
    step = pl.program_id(0)
    engine = Scatter(place, bufs, send, recv, out)

    @pl.when(step == 0)
    def _():
        place.barrier()

    def load(k):
        return pltpu.make_async_copy(parts.at[k], held.at[k % 3], local.at[k % 3])

    def first(k):
        load(k).wait()
        engine.start_first(k, held.at[k % 3])

    staged(step, 5, chunks, engine.finish)
    staged(step, 4, chunks, engine.start_fourth)
    staged(step, 3, chunks, engine.start_third)
    staged(step, 2, chunks, lambda k: engine.start_second(k, held.at[k % 3]))
    staged(step, 1, chunks, first)
    staged(step, 0, chunks, lambda k: load(k).start())


def scatter(parts, sizes, rows, collective_id):
    grp, seq = sizes
    chunks, halves, n, _, lanes = parts.shape
    if not can_move(sizes, rows):
        return lax.psum_scatter(parts, ("grp", "seq"), scatter_dimension=3, tiled=True).astype(F32)
    zs = grp // (Y * C)
    view = parts.reshape(chunks, 2, n, zs, Y, C * seq, rows, lanes)
    sems = (2, 2, zs + 2)
    return pl.pallas_call(
        functools.partial(scatter_kernel, zs, seq, chunks),
        grid=(chunks + 5,),
        out_shape=jax.ShapeDtypeStruct((chunks, 2, n, rows, lanes), F32),
        in_specs=[pl.BlockSpec(memory_space=pl.ANY)],
        out_specs=pl.BlockSpec((chunks, 2, n, rows, lanes), lambda step: (0, 0, 0, 0, 0)),
        scratch_shapes=[
            pltpu.VMEM((3, 2, n, zs, Y, C * seq, rows, lanes), BF),
            pltpu.SemaphoreType.DMA((3,)),
        ]
        + scatter_buffers(n, zs, seq, rows, lanes)
        + [pltpu.SemaphoreType.DMA(sems), pltpu.SemaphoreType.DMA(sems)],
        compiler_params=pltpu.CompilerParams(
            collective_id=collective_id, has_side_effects=True, vmem_limit_bytes=VMEM_LIMIT
        ),
    )(view)


class Shape:
    def __init__(self, tiles, local_tiles, conts):
        self.tiles, self.local_tiles, self.conts = tiles, local_tiles, conts
        self.rows = (local_tiles + conts) * T
        self.keys = self.rows + (tiles - local_tiles) * T
        self.parts = [(0, range(local_tiles)), (self.rows, range(local_tiles, tiles))]
        self.parts = [(start, js) for start, js in self.parts if len(js)]


def band_of(key_tile, query_tile):
    return jnp.clip(key_tile - query_tile, -2, 2) + 2


def tile_lanes():
    first_half = lax.broadcasted_iota(jnp.int32, (T, 2 * HEAD), 1) < HEAD
    place = lax.broadcasted_iota(jnp.int32, (T, T), 1)
    return first_half, place


def tile_rows(i):
    return pl.ds(pl.multiple_of(i * T, T), T)


def attend_tile(shape, i, is_cont, live, base, q, k, v, bias, out, norm):
    first_half, place = tile_lanes()
    rows = tile_rows(i)
    queries = q[rows, :]
    query_tile = shape.tiles if is_cont else base + i
    mixed = []
    for h in range(2):
        mine = first_half if h == 0 else ~first_half
        masked = jnp.where(mine, queries, jnp.zeros_like(queries))
        logits = []
        for start, js in shape.parts:
            scores = nt(masked, k[start : start + len(js) * T, :])
            for at, j in enumerate(js):
                band = band_of(lax.rem(base + j, shape.tiles), query_tile)
                logits.append(scores[:, at * T : (at + 1) * T] + bias[h, band])
        if is_cont:
            own = nt(masked, k[rows, :]) + bias[h, 2]
            logits.append(jnp.where(place < live[0, i - shape.local_tiles], own, NEGATIVE))
        top = jnp.max(functools.reduce(jnp.maximum, logits), axis=1, keepdims=True)
        weights = [jnp.exp(part - top) for part in logits]
        total = jnp.sum(functools.reduce(jnp.add, weights), axis=1, keepdims=True)
        inverse = 1.0 / total
        probs = [(weight * inverse).astype(BF) for weight in weights]
        result = None
        for start, js in shape.parts:
            left = jnp.concatenate([probs[j] for j in js], axis=1)
            term = nn(left, v[start : start + len(js) * T, :])
            result = term if result is None else result + term
        if is_cont:
            result = result + nn(probs[shape.tiles], v[rows, :])
        mixed.append(result)
        norm[h, rows, :] = top + jnp.log(total)
    out[rows, :] = jnp.where(first_half, mixed[0], mixed[1]).astype(BF)


def for_tiles(shape, conts, action):
    first, last = (shape.local_tiles, shape.local_tiles + shape.conts) if conts else (0, shape.local_tiles)

    def one(i, carry):
        action(i, conts)
        return carry

    lax.fori_loop(first, last, one, 0)


def attend_kernel(shape, live, base, q, k, v, bias, out, norm):
    for conts in (False, True):
        for_tiles(
            shape,
            conts,
            lambda i, c: attend_tile(shape, i, c, live, base[0], q, k, v, bias, out, norm),
        )


def pair_block(n):
    return pl.BlockSpec((n, 2 * HEAD), lambda h, *_: (0, h))


def attend(q, k, v, bias, live, base, shape):
    rows, width = q.shape
    pairs = width // (2 * HEAD)
    return pl.pallas_call(
        functools.partial(attend_kernel, shape),
        grid_spec=pltpu.PrefetchScalarGridSpec(
            num_scalar_prefetch=2,
            grid=(pairs,),
            in_specs=[
                pair_block(rows),
                pair_block(shape.keys),
                pair_block(shape.keys),
                pl.BlockSpec((2, BANDS, T, T), lambda h, *_: (h, 0, 0, 0)),
            ],
            out_specs=[pair_block(rows), pl.BlockSpec((2, rows, 1), lambda h, *_: (h, 0, 0))],
        ),
        out_shape=[
            jax.ShapeDtypeStruct((rows, width), BF),
            jax.ShapeDtypeStruct((2 * pairs, rows, 1), F32),
        ],
        compiler_params=pltpu.CompilerParams(vmem_limit_bytes=VMEM_LIMIT),
    )(live, base, q, k, v, bias)


def attend_back_tile(
    shape, i, is_cont, live, base, q, k, v, bias, grad, out, norm, d_q, d_bias, k_sum, v_sum
):
    first_half, place = tile_lanes()
    rows = tile_rows(i)
    queries = q[rows, :]
    grads = grad[rows, :]
    query_tile = shape.tiles if is_cont else base + i
    overlap = grads.astype(F32) * out[rows, :].astype(F32)
    mixed = []
    for h in range(2):
        mine = first_half if h == 0 else ~first_half
        masked = jnp.where(mine, queries, jnp.zeros_like(queries))
        masked_grad = jnp.where(mine, grads, jnp.zeros_like(grads))
        inner = jnp.sum(jnp.where(mine, overlap, 0.0), axis=1, keepdims=True)
        log_norm = norm[h, rows, :]

        def piece(keys, bands, allowed):
            scores = nt(masked, k[keys, :])
            d_probs = nt(masked_grad, v[keys, :])
            probs_low, scores_low = [], []
            for at, band in enumerate(bands):
                cols = slice(at * T, (at + 1) * T)
                logits = scores[:, cols] + bias[h, band]
                if allowed is not None:
                    logits = jnp.where(allowed, logits, NEGATIVE)
                probs = jnp.exp(logits - log_norm)
                d_scores = probs * (d_probs[:, cols] - inner)
                d_bias[h, band] += d_scores
                probs_low.append(probs.astype(BF))
                scores_low.append(d_scores.astype(BF))
            probs_low = jnp.concatenate(probs_low, axis=1)
            scores_low = jnp.concatenate(scores_low, axis=1)
            v_sum[keys, :] += tn(probs_low, masked_grad)
            k_sum[keys, :] += tn(scores_low, masked)
            return nn(scores_low, k[keys, :])

        result = None
        for start, js in shape.parts:
            bands = [band_of(lax.rem(base + j, shape.tiles), query_tile) for j in js]
            term = piece(pl.ds(start, len(js) * T), bands, None)
            result = term if result is None else result + term
        if is_cont:
            result = result + piece(rows, [2], place < live[0, i - shape.local_tiles])
        mixed.append(result)
    d_q[rows, :] = jnp.where(first_half, mixed[0], mixed[1]).astype(BF)


def attend_back_kernel(
    shape, live, base, q, k, v, bias, grad, out, norm, d_q, d_k, d_v, d_bias, k_sum, v_sum
):
    k_sum[...] = jnp.zeros_like(k_sum)
    v_sum[...] = jnp.zeros_like(v_sum)
    d_bias[...] = jnp.zeros_like(d_bias)
    refs = (q, k, v, bias, grad, out, norm, d_q, d_bias, k_sum, v_sum)
    for conts in (False, True):
        for_tiles(shape, conts, lambda i, c: attend_back_tile(shape, i, c, live, base[0], *refs))
    d_k[...] = k_sum[...].astype(BF)
    d_v[...] = v_sum[...].astype(BF)


def attend_back(q, k, v, bias, grad, out, norm, live, base, shape):
    rows, width = q.shape
    pairs = width // (2 * HEAD)
    keys = shape.keys
    bands = pl.BlockSpec((2, BANDS, T, T), lambda h, *_: (h, 0, 0, 0))
    return pl.pallas_call(
        functools.partial(attend_back_kernel, shape),
        grid_spec=pltpu.PrefetchScalarGridSpec(
            num_scalar_prefetch=2,
            grid=(pairs,),
            in_specs=[
                pair_block(rows),
                pair_block(keys),
                pair_block(keys),
                bands,
                pair_block(rows),
                pair_block(rows),
                pl.BlockSpec((2, rows, 1), lambda h, *_: (h, 0, 0)),
            ],
            out_specs=[pair_block(rows), pair_block(keys), pair_block(keys), bands],
            scratch_shapes=[pltpu.VMEM((keys, 2 * HEAD), F32), pltpu.VMEM((keys, 2 * HEAD), F32)],
        ),
        out_shape=[
            jax.ShapeDtypeStruct((rows, width), BF),
            jax.ShapeDtypeStruct((keys, width), BF),
            jax.ShapeDtypeStruct((keys, width), BF),
            jax.ShapeDtypeStruct((2 * pairs, BANDS, T, T), F32),
        ],
        compiler_params=pltpu.CompilerParams(vmem_limit_bytes=VMEM_LIMIT),
    )(live, base, q, k, v, bias, grad, out, norm)


SPAN = 4 * T
VECTOR_ROWS = 8


def turned(tile):
    row = lax.broadcasted_iota(jnp.int32, tile.shape, 0)
    for bit in range(7):
        moved = pltpu.roll(tile, SPAN - (1 << bit), 1)
        tile = jnp.where((row >> bit) & 1 == 1, moved, tile)
    return tile


def band_sums(d_bias, h):
    near = jnp.concatenate([d_bias[h, 1], d_bias[h, 2], d_bias[h, 3]], axis=1)
    near = jnp.concatenate([near, jnp.zeros((T, T), F32)], axis=1)
    diagonal = jnp.sum(turned(near), axis=0, keepdims=True)
    rows = [diagonal[:, i * T : (i + 1) * T] for i in range(4)]
    rows += [jnp.sum(d_bias[h, band], axis=0, keepdims=True) for band in (0, 4)]
    return jnp.concatenate(rows + [jnp.zeros((2, T), F32)], axis=0)


def rows_of(vector):
    return [vector[:, i * T : (i + 1) * T] for i in range(vector.shape[1] // T)]


class Combine:
    def __init__(self, place, total, arrived, send, recv):
        self.p, self.total, self.arrived, self.send, self.recv = place, total, arrived, send, recv

    def partners(self):
        p = self.p
        found = [p.device(c=1 - p.c), p.device(x=1 - p.x), p.device(y=1 - p.y)]
        bit = 1
        while bit < p.zs:
            found.append(p.device(z=p.z + bit - 2 * bit * ((p.z // bit) % 2)))
            bit *= 2
        return found

    def copy(self, i):
        return remote(
            self.total.at[i],
            self.arrived.at[i],
            self.send.at[i],
            self.recv.at[i],
            self.partners()[i],
        )

    def start(self, i):
        self.copy(i).start()

    def finish(self, i):
        self.copy(i).wait_recv()
        self.copy(i).wait_send()
        self.total[i + 1] = self.total[i] + self.arrived[i]


def back_kernel(zs, xs, shape, width, kept, live, *refs):
    q, k, v, bias, grad, out, norm, attended, branch_hbm, normed_hbm, parts, weights_hbm = refs[:12]
    d_middle, x_low, gain, d_gain_two = refs[12:16]
    d_x, sums, vector_out = refs[16:19]
    (stage, turn_buf, d_q, d_kv, back_kv, k_sum, v_sum, d_bias) = refs[19:27]
    (w_buf, held, vector, total, arrived, gain_sum) = refs[27:33]
    (local, loads, kv_sems, both_sems) = refs[33:37]
    bufs, scatter_sems = refs[37:44], refs[44:46]
    place = Place(zs, xs)
    step = pl.program_id(0)
    rows, keys = shape.rows, shape.keys
    prompt = shape.local_tiles * T
    pairs = d_q.shape[0]
    last = 2 * pairs
    turns = rows // T
    first_kept, end_kept = kept
    fed = parts.shape[0] - (end_kept - first_kept)
    group_two = last - 1
    count = fed + 4
    blocks = rows // d_x.shape[0]

    def stage_load(source):
        return pltpu.make_async_copy(source, stage, local.at[0])

    def weights_load(i):
        return pltpu.make_async_copy(weights_hbm.at[i], w_buf.at[i], local.at[1 + i])

    def turn():
        def one(i, carry):
            part = tile_rows(i)
            turn_buf[:, part] = stage[part, :].T
            return carry

        lax.fori_loop(0, turns, one, 0)

    @pl.when(step == 0)
    def _():
        stage_load(branch_hbm).start()
        place.barrier()
        for i in range(3):
            weights_load(i).start()
        stage_load(branch_hbm).wait()
        turn()
        stage_load(normed_hbm).start()

    engine = Scatter(place, bufs, *scatter_sems, sums)

    def due(offset, action):
        at = step - offset
        chunk = jnp.where(at < group_two, at, at - group_two + fed)
        early = (at >= 0) & (at < fed)
        late = (at >= group_two) & (at < group_two + 4)

        @pl.when(early | late)
        def _():
            action(chunk)

    def part_load(c):
        j = jnp.where(c < first_kept, c, c + end_kept - first_kept)
        return pltpu.make_async_copy(parts.at[j], held.at[c % 3], loads.at[c % 3])

    def first(c):
        @pl.when(c < fed)
        def _():
            part_load(c).wait()

        engine.start_first(c, held.at[c % 3])

    due(5, engine.finish)
    due(4, engine.start_fourth)
    due(3, engine.start_third)
    due(2, lambda c: engine.start_second(c, held.at[c % 3]))
    due(1, first)

    @pl.when(step < fed)
    def _():
        part_load(step).start()

    def kv_send(p):
        src = d_kv.at[p, :, pl.ds(rows, keys - rows)]
        peer = place.device(x=1 - place.x)
        return remote(src, back_kv.at[p], kv_sems.at[0, p], kv_sems.at[1, p], peer)

    @pl.when((step >= 2) & (step <= last) & (step % 2 == 0))
    def _():
        kv_send(step // 2 - 1).start()

    @pl.when(step < last)
    def _():
        p = step // 2
        half = step % 2

        @pl.when(half == 0)
        def _():
            k_sum[...] = jnp.zeros_like(k_sum)
            v_sum[...] = jnp.zeros_like(v_sum)
            d_bias[...] = jnp.zeros_like(d_bias)

        inputs = (q, k, v, bias, grad, out, norm, d_q.at[p], d_bias, k_sum, v_sum)
        base = place.x * shape.local_tiles
        action = lambda i, c: attend_back_tile(shape, i, c, live, base, *inputs)

        @pl.when(half == 0)
        def _():
            for_tiles(shape, False, action)

        @pl.when(half == 1)
        def _():
            for_tiles(shape, True, action)
            d_kv[p, 0] = k_sum[...].astype(BF)
            d_kv[p, 1] = v_sum[...].astype(BF)
            for h in range(2):
                vector[2 * p + h] = band_sums(d_bias, h)

    def produce(c, right):
        slot = c % 3
        for m in range(3):
            operand = right(m)

            def one(z, carry, m=m, operand=operand):
                block = turn_buf.shape[0] // zs
                part = pl.ds(pl.multiple_of(z * block, block), block)
                result = nn(turn_buf[part, :], operand).astype(BF)
                for side in range(2):
                    index = 2 * m + side
                    value = result[:, side * T : (side + 1) * T]
                    held[slot, index // 3, index % 3, z] = value.reshape(held.shape[4:])
                return carry

            lax.fori_loop(0, zs, one, 0)

    @pl.when(step == last - 1)
    def _():
        produce(fed, lambda m: attended[:, 2 * m * T : 2 * (m + 1) * T])

    @pl.when(step == last)
    def _():
        stage_load(normed_hbm).wait()
        turn()
        produce(fed + 1, lambda m: jnp.concatenate([d_q[2 * m], d_q[2 * m + 1]], axis=1))

        def join(p, carry):
            kv_send(p).wait_recv()
            kv_send(p).wait_send()
            for side in range(2):
                own = d_kv[p, side, 0:prompt, :].astype(F32)
                d_kv[p, side, 0:prompt, :] = (own + back_kv[p, side].astype(F32)).astype(BF)
            return carry

        lax.fori_loop(0, pairs, join, 0)
        for i in range(3):
            weights_load(i).wait()
        gain_sum[...] = jnp.zeros_like(gain_sum)

    for side in range(2):

        @pl.when(step == last + 1 + side)
        def _(side=side):
            pick = lambda p: d_kv[p, side, 0:rows, :]
            produce(fed + 2 + side, lambda m: jnp.concatenate([pick(2 * m), pick(2 * m + 1)], axis=1))

    @pl.when((step >= last) & (step < last + blocks))
    def _():
        size = d_x.shape[0]
        part = pl.ds(pl.multiple_of((step - last) * size, size), size)
        d_normed = None
        for i in range(3):
            for m in range(pairs // 2):
                if i == 0:
                    left = [d_q[2 * m + e, part, :] for e in range(2)]
                else:
                    left = [d_kv[2 * m + e, i - 1, part, :] for e in range(2)]
                pieces = [2 * m, 2 * m + 1]
                right = [w_buf[i, j // 3, j % 3].reshape(width, T) for j in pieces]
                term = nt(jnp.concatenate(left, axis=1), jnp.concatenate(right, axis=1))
                d_normed = term if d_normed is None else d_normed + term
        x = x_low[...].astype(F32)
        scale = lax.rsqrt(jnp.mean(x * x, axis=-1, keepdims=True) + EPS)
        unit = x * scale
        gain_sum[...] += jnp.sum(d_normed * unit, axis=0, keepdims=True)
        d_unit = d_normed * gain[...]
        inner = jnp.mean(d_unit * unit, axis=-1, keepdims=True)
        d_x[...] = (d_middle[...] + scale * (d_unit - unit * inner)).astype(BF)

    mix = Combine(place, total, arrived, both_sems.at[0], both_sems.at[1])
    start = last + blocks
    stages = total.shape[0] - 1
    tiles = 2 * pairs

    @pl.when(step == start)
    def _():
        total[0, 0:tiles] = vector[...]
        both = rows_of(gain_sum[...]) + rows_of(d_gain_two[...])
        for i in range(len(both) // VECTOR_ROWS):
            group = both[i * VECTOR_ROWS : (i + 1) * VECTOR_ROWS]
            total[0, tiles + i] = jnp.concatenate(group, axis=0)

    for i in range(stages + 1):

        @pl.when(step == start + 1 + i)
        def _(i=i):
            if i > 0:
                mix.finish(i - 1)
            if i < stages:
                mix.start(i)
            else:
                vector_out[...] = total[stages]


def back(q, k, v, bias, grad, out, norm, branch, normed, parts, weights, d_middle, x_low, gain,
         d_gain_two, live, shape, sizes, kept, collective_id):
    grp, seq = sizes
    rows, width = x_low.shape
    inner = q.shape[1]
    pairs = inner // (2 * HEAD)
    zs = grp // (Y * C)
    keys = shape.keys
    chunks, _, n, _, _, _, shard, lanes = parts.shape
    count = chunks - (kept[1] - kept[0]) + 4
    assert chunks - (kept[1] - kept[0]) <= 2 * pairs - 1
    assert (pairs, n) == (6, 3) and 2 * width // T % VECTOR_ROWS == 0
    last = 2 * pairs
    size = min(rows, 256)
    blocks = rows // size
    tile = (2, n, zs, Y, C * seq, shard, lanes)
    stages = 3 + (zs - 1).bit_length()
    steps = last + blocks + stages + 2
    vector = (2 * pairs + 2 * width // T // VECTOR_ROWS, VECTOR_ROWS, T)
    pair = lambda s: jnp.minimum(s // 2, pairs - 1)
    by_pair = lambda rows_: pl.BlockSpec((rows_, 2 * HEAD), lambda s, *_: (0, pair(s)))
    row_block = lambda s: jnp.clip(s - last, 0, blocks - 1)
    by_rows = pl.BlockSpec((size, width), lambda s, *_: (row_block(s), 0))
    full = lambda *dims: pl.BlockSpec(
        dims, lambda s, *_: (0,) * len(dims), pipeline_mode=pl.Buffered(1)
    )
    anywhere = pl.BlockSpec(memory_space=pl.ANY)
    sems = lambda *dims: pltpu.SemaphoreType.DMA(dims)
    return pl.pallas_call(
        functools.partial(back_kernel, zs, seq, shape, width, kept),
        grid_spec=pltpu.PrefetchScalarGridSpec(
            num_scalar_prefetch=1,
            grid=(steps,),
            in_specs=[
                by_pair(rows),
                by_pair(keys),
                by_pair(keys),
                pl.BlockSpec((2, BANDS, T, T), lambda s, *_: (pair(s), 0, 0, 0)),
                by_pair(rows),
                by_pair(rows),
                pl.BlockSpec((2, rows, 1), lambda s, *_: (pair(s), 0, 0)),
                full(rows, inner),
                anywhere,
                anywhere,
                anywhere,
                anywhere,
                by_rows,
                by_rows,
                full(1, width),
                full(1, width),
            ],
            out_specs=[by_rows, full(count, 2, n, shard, lanes), full(*vector)],
            scratch_shapes=[
                pltpu.VMEM((rows, width), BF),
                pltpu.VMEM((width, rows), BF),
                pltpu.VMEM((pairs, rows, 2 * HEAD), BF),
                pltpu.VMEM((pairs, 2, keys, 2 * HEAD), BF),
                pltpu.VMEM((pairs, 2, keys - rows, 2 * HEAD), BF),
                pltpu.VMEM((keys, 2 * HEAD), F32),
                pltpu.VMEM((keys, 2 * HEAD), F32),
                pltpu.VMEM((2, BANDS, T, T), F32),
                pltpu.VMEM((3, *tile), BF),
                pltpu.VMEM((3, *tile), BF),
                pltpu.VMEM((2 * pairs, VECTOR_ROWS, T), F32),
                pltpu.VMEM((stages + 1, *vector), F32),
                pltpu.VMEM((stages, *vector), F32),
                pltpu.VMEM((1, width), F32),
                sems(4),
                sems(3),
                sems(2, pairs),
                sems(2, stages),
            ]
            + scatter_buffers(n, zs, seq, shard, lanes)
            + [sems(2, 2, zs + 2), sems(2, 2, zs + 2)],
        ),
        out_shape=[
            jax.ShapeDtypeStruct((rows, width), BF),
            jax.ShapeDtypeStruct((count, 2, n, shard, lanes), F32),
            jax.ShapeDtypeStruct(vector, F32),
        ],
        compiler_params=pltpu.CompilerParams(
            collective_id=collective_id, has_side_effects=True, vmem_limit_bytes=VMEM_LIMIT
        ),
    )(live, q, k, v, bias, grad, out, norm, out, branch, normed, parts, weights, d_middle,
      x_low, gain, d_gain_two)


GELU_SCALE = 0.7978845608028654
GELU_CUBIC = 0.044715


def gelu_and_slope(a):
    square = a * a
    tanh = jnp.tanh(GELU_SCALE * a * (1.0 + GELU_CUBIC * square))
    half = 0.5 * (1.0 + tanh)
    slope = half + 0.5 * a * (1.0 - tanh * tanh) * (
        GELU_SCALE * (1.0 + 3.0 * GELU_CUBIC * square)
    )
    return a * half, slope


def feed_load(x_hbm, dy_hbm, x, x_t, dy, dy_t, sem):
    load_x = pltpu.make_async_copy(x_hbm, x, sem.at[0])
    load_dy = pltpu.make_async_copy(dy_hbm, dy, sem.at[1])
    load_x.start()
    load_dy.start()
    load_x.wait()
    load_dy.wait()

    def turn(i, carry):
        part = pl.ds(pl.multiple_of(i * T, T), T)
        x_t[:, part] = x[part, :].T
        dy_t[:, part] = dy[part, :].T
        return carry

    lax.fori_loop(0, x.shape[0] // T, turn, 0)


def feed_chunk(read, write, blocks, out, d_x, x, x_t, dy, dy_t, hidden, d_gate, d_up):
    rows, width = x.shape
    row_block = min(rows, 256)
    width_block = width // blocks
    w_gate, w_up, w_down = [jnp.concatenate([read(0, i), read(1, i)], axis=1) for i in range(3)]

    def by_rows(i, carry):
        part = pl.ds(pl.multiple_of(i * row_block, row_block), row_block)
        gate = nn(x[part, :], w_gate)
        up = nn(x[part, :], w_up)
        d_hidden = nn(dy[part, :], w_down)
        active, slope = gelu_and_slope(gate)
        hidden_low = (active * up).astype(BF)
        d_gate_low = (d_hidden * up * slope).astype(BF)
        d_up_low = (d_hidden * active).astype(BF)
        hidden[part, :] = hidden_low
        d_gate[part, :] = d_gate_low
        d_up[part, :] = d_up_low
        out[part, :] += nt(hidden_low, w_down)
        d_x[part, :] += nt(d_gate_low, w_gate) + nt(d_up_low, w_up)
        return carry

    lax.fori_loop(0, rows // row_block, by_rows, 0)

    def by_width(i, carry):
        part = pl.ds(pl.multiple_of(i * width_block, width_block), width_block)
        pairs = ((x_t, d_gate), (x_t, d_up), (dy_t, hidden))
        for index, (left, right) in enumerate(pairs):
            total = nn(left[part, :], right[...]).astype(BF)
            write(0, index, i, total[:, :T])
            write(1, index, i, total[:, T:])
        return carry

    lax.fori_loop(0, blocks, by_width, 0)


def feed_kernel(x_hbm, dy_hbm, weights, out, d_x, grads, x, x_t, dy, dy_t, *rest):
    *work, sem = rest
    width_block = 512

    @pl.when(pl.program_id(0) == 0)
    def _():
        feed_load(x_hbm, dy_hbm, x, x_t, dy, dy_t, sem)
        out[...] = jnp.zeros_like(out)
        d_x[...] = jnp.zeros_like(d_x)

    def write(half, index, block, value):
        part = pl.ds(pl.multiple_of(block * width_block, width_block), width_block)
        grads[0, half, index, part, :] = value

    read = lambda half, index: weights[0, half, index]
    blocks = x.shape[1] // width_block
    feed_chunk(read, write, blocks, out, d_x, x, x_t, dy, dy_t, *work)


def feed_scratch(rows, width):
    return [
        pltpu.VMEM((rows, width), BF),
        pltpu.VMEM((width, rows), BF),
        pltpu.VMEM((rows, width), BF),
        pltpu.VMEM((width, rows), BF),
        pltpu.VMEM((rows, 2 * T), BF),
        pltpu.VMEM((rows, 2 * T), BF),
        pltpu.VMEM((rows, 2 * T), BF),
        pltpu.SemaphoreType.DMA((2,)),
    ]


def feed(x, dy, weights):
    rows, width = x.shape
    chunks = weights.shape[0]
    chunk = pl.BlockSpec((1, 2, 3, width, T), lambda j: (j, 0, 0, 0, 0))
    whole = pl.BlockSpec((rows, width), lambda j: (0, 0), pipeline_mode=pl.Buffered(1))
    return pl.pallas_call(
        feed_kernel,
        grid=(chunks,),
        in_specs=[pl.BlockSpec(memory_space=pl.ANY)] * 2 + [chunk],
        out_specs=[whole, whole, chunk],
        out_shape=[
            jax.ShapeDtypeStruct((rows, width), F32),
            jax.ShapeDtypeStruct((rows, width), F32),
            jax.ShapeDtypeStruct((chunks, 2, 3, width, T), BF),
        ],
        scratch_shapes=feed_scratch(rows, width),
        compiler_params=pltpu.CompilerParams(vmem_limit_bytes=VMEM_LIMIT),
    )(x, dy, weights)


def feed_moving_kernel(zs, xs, early, kept, *refs):
    x_hbm, dy_hbm, own, ready, out, d_x, whole, parts, sums = refs[:9]
    x, x_t, dy, dy_t, hidden, d_gate, d_up, sem = refs[9:17]
    held, w_buf, g_buf, local = refs[17:21]
    gather_sems, bufs, scatter_sems = refs[21:23], refs[23:30], refs[30:32]
    chunks = own.shape[0]
    place = Place(zs, xs)
    step = pl.program_id(0)
    lag = max(0, 5 - early)
    first_kept, end_kept = kept
    width = x.shape[1]

    @pl.when(step == 0)
    def _():
        place.barrier()

    fetch = Gather(place, own, whole, *gather_sems)
    fetch.tick(step, early, chunks)

    @pl.when(step == 0)
    def _():
        load = pltpu.make_async_copy(own, held, local.at[0])
        load.start()
        load.wait()
        mine = whole.at[:, :, :, place.z, place.y, place.c * place.xs + place.x]
        store = pltpu.make_async_copy(held, mine, local.at[1])
        store.start()
        store.wait()
        feed_load(x_hbm, dy_hbm, x, x_t, dy, dy_t, sem)
        out[...] = jnp.zeros_like(out)
        d_x[...] = jnp.zeros_like(d_x)

    def weight_load(j, source):
        return pltpu.make_async_copy(source.at[j], w_buf.at[j % 2], local.at[2 + j % 2])

    def start_load(j):
        if early > 0:

            @pl.when(j < early)
            def _():
                weight_load(j, ready).start()

        @pl.when(j >= early)
        def _():
            weight_load(j, whole).start()

    def part_store(j):
        return pltpu.make_async_copy(g_buf.at[j % 2], parts.at[j], local.at[4 + j % 2])

    def is_kept(j):
        return (j >= first_kept) & (j < end_kept)

    engine = Scatter(place, bufs, *scatter_sems, sums)
    due = lag + first_kept
    number = end_kept - first_kept
    grads_of = lambda k: g_buf.at[(k + first_kept) % 2]
    staged(step, due + 5, number, engine.finish)
    staged(step, due + 4, number, engine.start_fourth)
    staged(step, due + 3, number, engine.start_third)
    staged(step, due + 2, number, lambda k: engine.start_second(k, grads_of(k)))
    staged(step, due + 1, number, lambda k: engine.start_first(k, grads_of(k)))

    chunk = step - lag
    if lag == 0:

        @pl.when(step == 0)
        def _():
            start_load(0)

    @pl.when((chunk >= (0 if lag == 0 else -1)) & (chunk + 1 < chunks))
    def _():
        start_load(chunk + 1)

    @pl.when((chunk >= 2) & (chunk < chunks + 2) & ~is_kept(chunk - 2))
    def _():
        part_store(chunk - 2).wait()

    @pl.when((chunk >= 0) & (chunk < chunks))
    def _():
        weight_load(chunk, whole).wait()
        slot = chunk % 2

        def read(half, index):
            return w_buf[slot, half, index].reshape(width, T)

        def write(half, index, block, value):
            shape = g_buf.shape[4:]
            g_buf[slot, half, index, block] = value.reshape(shape)

        work = (hidden, d_gate, d_up)
        feed_chunk(read, write, zs, out, d_x, x, x_t, dy, dy_t, *work)

        @pl.when(~is_kept(chunk))
        def _():
            part_store(chunk).start()


def feed_moving(x, dy, own, ready, sizes, early, kept, collective_id):
    grp, seq = sizes
    rows, width = x.shape
    chunks, _, n, shard, lanes = own.shape
    zs = grp // (Y * C)
    tile = (2, n, zs, Y, C * seq, shard, lanes)
    whole = pl.BlockSpec((rows, width), lambda j: (0, 0), pipeline_mode=pl.Buffered(1))
    number = kept[1] - kept[0]
    sums = pl.BlockSpec(
        (number, 2, n, shard, lanes), lambda j: (0,) * 5, pipeline_mode=pl.Buffered(1)
    )
    lag = max(0, 5 - early)
    steps = lag + max(chunks + 2, kept[1] + 5)
    anywhere = pl.BlockSpec(memory_space=pl.ANY)
    sems = lambda *shape: pltpu.SemaphoreType.DMA(shape)
    return pl.pallas_call(
        functools.partial(feed_moving_kernel, zs, seq, early, kept),
        grid=(steps,),
        in_specs=[anywhere] * 4,
        out_specs=[whole, whole, anywhere, anywhere, sums],
        out_shape=[
            jax.ShapeDtypeStruct((rows, width), F32),
            jax.ShapeDtypeStruct((rows, width), F32),
            jax.ShapeDtypeStruct((chunks, *tile), BF),
            jax.ShapeDtypeStruct((chunks, *tile), BF),
            jax.ShapeDtypeStruct((number, 2, n, shard, lanes), F32),
        ],
        scratch_shapes=feed_scratch(rows, width)
        + [
            pltpu.VMEM(own.shape, BF),
            pltpu.VMEM((2, *tile), BF),
            pltpu.VMEM((2, *tile), BF),
            sems(6),
            sems(chunks, 2, zs + 2),
            sems(chunks, 2, zs + 2),
        ]
        + scatter_buffers(n, zs, seq, shard, lanes)
        + [sems(2, 2, zs + 2), sems(2, 2, zs + 2)],
        compiler_params=pltpu.CompilerParams(
            collective_id=collective_id, has_side_effects=True, vmem_limit_bytes=VMEM_LIMIT
        ),
    )(x, dy, own, ready)


def rms_scale(values):
    return lax.rsqrt(jnp.mean(values * values, axis=-1, keepdims=True) + EPS)


def norm_back(d_normed, unit, scale, gain):
    d_unit = d_normed * gain
    return scale * (d_unit - unit * jnp.mean(d_unit * unit, axis=-1, keepdims=True))


def pieces_of(matrix):
    rows, columns = matrix.shape
    return jnp.swapaxes(matrix.reshape(rows, columns // T, T), 0, 1)


def joined(pieces):
    count, rows, _ = pieces.shape
    return jnp.swapaxes(pieces, 0, 1).reshape(rows, count * T)


def attention_chunks(matrices):
    flat = jnp.concatenate([pieces_of(m) for m in matrices], axis=0)
    pad = -flat.shape[0] % 6
    flat = jnp.pad(flat, ((0, pad), (0, 0), (0, 0)))
    return flat.reshape(-1, 2, 3, *flat.shape[1:])


def feed_chunks(matrices):
    stacked = jnp.stack([pieces_of(m) for m in matrices], axis=1)
    pad = -stacked.shape[0] % 2
    stacked = jnp.pad(stacked, ((0, pad), (0, 0), (0, 0), (0, 0)))
    return stacked.reshape(-1, 2, *stacked.shape[1:])


def body(sizes, *args):
    (
        prompt_x,
        cont_x,
        cont_len,
        prompt_cot,
        cont_cot,
        norm1_gain,
        q_weight,
        k_weight,
        v_weight,
        o_weight,
        bucket_table,
        norm2_gain,
        gate_weight,
        up_weight,
        down_weight,
    ) = args
    _, local_prompt, width = prompt_x.shape
    conts, cont_rows = cont_x.shape[1], cont_x.shape[2]
    assert prompt_x.shape[0] == 1 and cont_rows == T and local_prompt % T == 0
    seq = sizes[1]
    num_buckets, heads = bucket_table.shape
    inner = q_weight.shape[1]
    assert inner == heads * HEAD
    shard = q_weight.shape[0]
    hidden_width = gate_weight.shape[1]
    local_tiles = local_prompt // T
    tiles = local_tiles * seq
    seq_index = lax.axis_index("seq")

    x_low = jnp.concatenate([prompt_x[0], cont_x[0].reshape(-1, width)], axis=0)
    dy_low = jnp.concatenate([prompt_cot[0], cont_cot[0].reshape(-1, width)], axis=0)
    x = x_low.astype(F32)
    dy = dy_low.astype(F32)

    lanes = jnp.zeros((shard, T - 2), F32)
    gains = jnp.concatenate([norm1_gain[:, None], norm2_gain[:, None], lanes], axis=1)
    own_attention = attention_chunks([q_weight, k_weight, v_weight, o_weight, gains]).astype(BF)
    own_feed = feed_chunks([gate_weight, up_weight, down_weight]).astype(BF)
    attention_whole = gather(own_attention, sizes, 0)
    count = inner // T
    flat = attention_whole.reshape(-1, width, T)
    q_full, k_full, v_full, o_full = [
        joined(flat[i * count : (i + 1) * count]) for i in range(4)
    ]
    gain_one = flat[4 * count, :, 0].astype(F32)
    gain_two = flat[4 * count, :, 1].astype(F32)

    scale_one = rms_scale(x)
    unit_one = x * scale_one
    normed_one = (unit_one * gain_one).astype(BF)
    kv = nn(normed_one, jnp.concatenate([k_full, v_full], axis=1)).astype(BF)
    queries = nn(normed_one, q_full).astype(BF)
    prompt_kv = kv[:local_prompt]
    if seq == 2:
        others = lax.ppermute(prompt_kv, "seq", [(0, 1), (1, 0)])
    else:
        gathered = lax.all_gather(prompt_kv, "seq", axis=0, tiled=True)
        others = jnp.roll(gathered, -seq_index * local_prompt, axis=0)[local_prompt:]
    every = jnp.concatenate([kv, others], axis=0)
    keys, values = every[:, :inner], every[:, inner:]
    base = (seq_index * local_tiles).reshape(1).astype(jnp.int32)

    one_hot = band_one_hot(num_buckets)
    bias = jnp.einsum("cqkb,bh->hcqk", one_hot, bucket_table, precision=lax.Precision.HIGHEST)
    shape = Shape(tiles, local_tiles, conts)
    attended, log_norm = attend(queries, keys, values, bias, cont_len, base, shape)
    middle = x + nt(attended, o_full)
    scale_two = rms_scale(middle)
    unit_two = middle * scale_two
    normed_two = (unit_two * gain_two).astype(BF)

    moving = can_move(sizes, shard)
    if moving:
        kept = (6, 13)
        out_sum, d_normed_two, _, feed_parts, kept_sums = feed_moving(
            normed_two, dy_low, own_feed, own_feed, sizes, 0, kept, 1
        )
    else:
        feed_whole = gather(own_feed, sizes, 1)
        out_sum, d_normed_two, feed_grads = feed(normed_two, dy_low, feed_whole)
        feed_sums = scatter(feed_grads, sizes, shard, 3)
    final = (middle + out_sum).astype(BF)

    d_gain_two = jnp.sum(d_normed_two * unit_two, axis=0)
    d_middle = dy + norm_back(d_normed_two, unit_two, scale_two, gain_two)
    d_branch = d_middle.astype(BF)
    d_attended = nn(d_branch, o_full).astype(BF)
    if moving:
        d_x, sums, vector = back(
            queries, keys, values, bias, d_attended, attended, log_norm, d_branch, normed_one,
            feed_parts, attention_whole.reshape(-1, *feed_parts.shape[1:]), d_middle, x_low,
            gain_one[None], d_gain_two[None], cont_len, shape, sizes, kept, 2,
        )
        fed = sums.shape[0] - 4
        feed_sums = jnp.concatenate([sums[: kept[0]], kept_sums, sums[kept[0] : fed]], axis=0)
        attention_sums = jnp.concatenate([sums[fed + 1 :], sums[fed : fed + 1]], axis=0)
        attention_sums = attention_sums.reshape(-1, shard, T)
        near = vector[:heads, :4].reshape(heads, SPAN)
        far = jnp.sum(vector[:heads, 4:6], axis=-1)
        relative = (jnp.arange(SPAN) + T) % SPAN - 2 * T
        ids = jnp.concatenate([bucket_ids(relative), bucket_ids(jnp.array([-T, T]))])
        hot = (ids[:, None] == jnp.arange(num_buckets)).astype(F32)
        both = jnp.concatenate([near, far], axis=1)
        table_grad = jnp.einsum("hr,rb->bh", both, hot, precision=lax.Precision.HIGHEST)
        gain_grads = vector[heads:].reshape(2, sizes[0] * seq, shard)
        me = lax.axis_index("grp") * seq + seq_index
        norm1_grad, norm2_grad = lax.dynamic_index_in_dim(gain_grads, me, 1, keepdims=False)
    else:
        d_o = tn(d_branch, attended)
        d_queries, d_keys, d_values, d_bias = attend_back(
            queries, keys, values, bias, d_attended, attended, log_norm, cont_len, base, shape
        )
        d_table = jnp.einsum("hcqk,cqkb->bh", d_bias, one_hot, precision=lax.Precision.HIGHEST)
        d_kv = jnp.concatenate([d_keys, d_values], axis=1)
        prompt_parts = jnp.concatenate([d_kv[:local_prompt], d_kv[shape.rows :]], axis=0)
        prompt_parts = jnp.roll(prompt_parts, seq_index * local_prompt, axis=0)
        d_prompt = lax.psum_scatter(prompt_parts, "seq", scatter_dimension=0, tiled=True)
        d_kv = jnp.concatenate([d_prompt, d_kv[local_prompt : shape.rows]], axis=0)
        d_normed_one = nt(d_queries, q_full) + nt(d_kv, jnp.concatenate([k_full, v_full], axis=1))
        d_q = tn(normed_one, d_queries)
        d_kv_weight = tn(normed_one, d_kv)
        d_gain_one = jnp.sum(d_normed_one * unit_one, axis=0)
        d_x = d_middle + norm_back(d_normed_one, unit_one, scale_one, gain_one)
        d_x = d_x.astype(BF)
        attention_parts = attention_chunks([d_q, d_kv_weight, d_o]).astype(BF)
        attention_sums = scatter(attention_parts, sizes, shard, 2).reshape(-1, shard, T)
        norm1_grad = lax.psum_scatter(d_gain_one, ("grp", "seq"), scatter_dimension=0, tiled=True)
        norm2_grad = lax.psum_scatter(d_gain_two, ("grp", "seq"), scatter_dimension=0, tiled=True)
        table_grad = lax.psum(d_table, ("grp", "seq"))
    feed_sums = feed_sums.reshape(-1, 3, shard, T)[: hidden_width // T]
    gate_grad, up_grad, down_grad = [joined(feed_sums[:, i]) for i in range(3)]
    q_grad, k_grad, v_grad, o_grad = [
        joined(attention_sums[i * count : (i + 1) * count]) for i in range(4)
    ]
    split = lambda rows: (
        rows[:local_prompt][None],
        rows[local_prompt:].reshape(1, conts, cont_rows, width),
    )
    return (
        *split(final),
        *split(d_x),
        norm1_grad,
        q_grad,
        k_grad,
        v_grad,
        o_grad,
        table_grad,
        norm2_grad,
        gate_grad,
        up_grad,
        down_grad,
    )


def solution(mesh):
    sizes = (mesh.shape["grp"], mesh.shape["seq"])
    rows = P("grp", "seq", None)
    conts = P("grp", "seq", None, None)
    shard = P(("grp", "seq"), None)
    gain = P(("grp", "seq"))
    in_specs = (rows, conts, P("grp", "seq"), rows, conts, gain, shard, shard, shard, shard)
    in_specs += (P(), gain, shard, shard, shard)
    out_specs = (rows, conts, rows, conts, gain, shard, shard, shard, shard, P(), gain)
    out_specs += (shard, shard, shard)
    return jax.shard_map(
        functools.partial(body, sizes),
        mesh=mesh,
        in_specs=in_specs,
        out_specs=out_specs,
        check_vma=False,
    )
```

```python
import functools

import jax
import jax.numpy as jnp
from jax import lax
from jax.experimental import pallas as pl
from jax.experimental.pallas import tpu as pltpu
from jax.sharding import PartitionSpec as P

EPS = 1e-06
LIMITS = (8, 12, 16, 23, 32, 46, 64, 91)
NEGATIVE = -1e30
MESH = pl.DeviceIdType.MESH
T = 128
HEAD = 64
BANDS = 5
BF = jnp.bfloat16
F32 = jnp.float32
VMEM_LIMIT = 63 * 2**20
Y = 2
C = 2


def nn(left, right):
    return jnp.dot(left, right, preferred_element_type=F32)


def nt(left, right):
    return lax.dot_general(left, right, (((1,), (1,)), ((), ())), preferred_element_type=F32)


def tn(left, right):
    return lax.dot_general(left, right, (((0,), (0,)), ((), ())), preferred_element_type=F32)


def bucket_ids(relative):
    distance = jnp.abs(relative)
    coarse = 7 + sum(((distance >= boundary).astype(jnp.int32) for boundary in LIMITS))
    return jnp.where(distance < 8, distance, coarse) + 16 * (relative > 0).astype(jnp.int32)


def band_one_hot(num_buckets):
    band = jnp.arange(BANDS)[:, None, None] - 2
    query = jnp.arange(T)[None, :, None]
    key = jnp.arange(T)[None, None, :]
    ids = bucket_ids(band * T + key - query)
    return (ids[..., None] == jnp.arange(num_buckets)).astype(F32)


def can_move(sizes, rows):
    zs = sizes[0] // (Y * C)
    return rows % 16 == 0 and sizes[1] == 2 and sizes[0] % (Y * C) == 0 and zs in (2, 4, 8, 16)


class Place:
    def __init__(self, zs, xs):
        grp = lax.axis_index("grp")
        self.zs, self.xs = zs, xs
        self.x = lax.axis_index("seq")
        self.z = grp // (Y * C)
        self.y = (grp // C) % Y
        self.c = grp % C

    def device(self, z=None, y=None, c=None, x=None):
        z = self.z if z is None else z
        y = self.y if y is None else y
        c = self.c if c is None else c
        x = self.x if x is None else x
        return (z * (Y * C) + y * C + c, x)

    def peers(self):
        around = [self.device(z=(self.z + d) % self.zs) for d in range(1, self.zs)]
        return around + [
            self.device(y=1 - self.y),
            self.device(x=1 - self.x),
            self.device(c=1 - self.c),
        ]

    def barrier(self):
        sem = pltpu.get_barrier_semaphore()
        peers = self.peers()
        for peer in peers:
            pl.semaphore_signal(sem, inc=1, device_id=peer, device_id_type=MESH)
        pl.semaphore_wait(sem, len(peers))


def remote(src, dst, send_sem, recv_sem, device):
    return pltpu.make_async_remote_copy(
        src_ref=src,
        dst_ref=dst,
        send_sem=send_sem,
        recv_sem=recv_sem,
        device_id=device,
        device_id_type=MESH,
    )


def staged(step, offset, count, action):
    @pl.when((step >= offset) & (step < count + offset))
    def _():
        action(step - offset)


class Gather:
    def __init__(self, place, own, whole, send, recv):
        self.p, self.own, self.whole, self.send, self.recv = place, own, whole, send, recv

    def copy(self, k, half, index, src, dst, device):
        return remote(src, dst, self.send.at[k, half, index], self.recv.at[k, half, index], device)

    def along_z(self, k, half, d):
        p = self.p
        dst = self.whole.at[k, half, :, p.z, p.y, p.c * p.xs + p.x]
        return self.copy(k, half, d - 1, self.own.at[k, half], dst, p.device(z=(p.z + d) % p.zs))

    def second(self, k, half):
        p = self.p
        view = self.whole.at[k, half, :, :, p.y, p.c * p.xs + p.x]
        peer = p.device(x=1 - p.x) if half == 0 else p.device(y=1 - p.y)
        return self.copy(k, half, p.zs - 1, view, view, peer)

    def third(self, k, half):
        p = self.p
        if half == 0:
            view = self.whole.at[k, half, :, :, p.y, pl.ds(p.c * p.xs, p.xs)]
            peer = p.device(y=1 - p.y)
        else:
            view = self.whole.at[k, half, :, :, :, p.c * p.xs + p.x]
            peer = p.device(x=1 - p.x)
        return self.copy(k, half, p.zs, view, view, peer)

    def fourth(self, k, half):
        p = self.p
        view = self.whole.at[k, half, :, :, :, pl.ds(p.c * p.xs, p.xs)]
        return self.copy(k, half, p.zs + 1, view, view, p.device(c=1 - p.c))

    def tick(self, step, first, end):
        def start_z(k):
            for half in (0, 1):
                for d in range(1, self.p.zs):
                    self.along_z(k, half, d).start()

        def start_second(k):
            for half in (0, 1):
                for d in range(1, self.p.zs):
                    self.along_z(k, half, d).wait_recv()
                self.second(k, half).start()

        def start_third(k):
            for half in (0, 1):
                self.second(k, half).wait_recv()
                self.third(k, half).start()

        def start_fourth(k):
            for half in (0, 1):
                self.third(k, half).wait_recv()
                self.fourth(k, half).start()

        def finish(k):
            for half in (0, 1):
                self.fourth(k, half).wait_recv()
                for d in range(1, self.p.zs):
                    self.along_z(k, half, d).wait_send()
                self.second(k, half).wait_send()
                self.third(k, half).wait_send()
                self.fourth(k, half).wait_send()

        for offset, action in enumerate((start_z, start_second, start_third, start_fourth, finish)):
            staged(step, offset, end - first, lambda k, action=action: action(first + k))


def gather_kernel(zs, xs, own, whole, held, local, send, recv):
    place = Place(zs, xs)
    step = pl.program_id(0)

    @pl.when(step == 0)
    def _():
        place.barrier()
        load = pltpu.make_async_copy(own, held, local.at[0])
        load.start()
        load.wait()
        mine = whole.at[:, :, :, place.z, place.y, place.c * place.xs + place.x]
        store = pltpu.make_async_copy(held, mine, local.at[1])
        store.start()
        store.wait()

    Gather(place, held, whole, send, recv).tick(step, 0, own.shape[0])


def gather(own, sizes, collective_id):
    grp, seq = sizes
    chunks, halves, n, rows, lanes = own.shape
    if not can_move(sizes, rows):
        whole = lax.all_gather(own, ("grp", "seq"), axis=3, tiled=True)
        return whole
    zs = grp // (Y * C)
    slots = (chunks, 2, zs + 2)
    whole = pl.pallas_call(
        functools.partial(gather_kernel, zs, seq),
        grid=(chunks + 4,),
        out_shape=jax.ShapeDtypeStruct((chunks, 2, n, zs, Y, C * seq, rows, lanes), own.dtype),
        in_specs=[pl.BlockSpec(memory_space=pl.ANY)],
        out_specs=pl.BlockSpec(memory_space=pl.ANY),
        scratch_shapes=[
            pltpu.VMEM(own.shape, own.dtype),
            pltpu.SemaphoreType.DMA((2,)),
            pltpu.SemaphoreType.DMA(slots),
            pltpu.SemaphoreType.DMA(slots),
        ],
        compiler_params=pltpu.CompilerParams(collective_id=collective_id, has_side_effects=True),
    )(own)
    return whole.reshape(chunks, 2, n, grp * seq * rows, lanes)


class Scatter:
    def __init__(self, place, bufs, send, recv, out):
        self.p, self.send, self.recv, self.out = place, send, recv, out
        (self.in1, self.in2, self.in3, self.in4, self.sum1, self.sum2, self.sum3) = bufs

    def copy(self, k, half, index, src, dst, device):
        slot = k % 2
        return remote(
            src, dst, self.send.at[slot, half, index], self.recv.at[slot, half, index], device
        )

    def first(self, k, half, part):
        p = self.p
        src = part.at[half, :, :, :, pl.ds((1 - p.c) * p.xs, p.xs)]
        return self.copy(k, half, 0, src, self.in1.at[k % 2, half], p.device(c=1 - p.c))

    def second(self, k, half):
        p = self.p
        if half == 0:
            src, peer = self.sum1.at[k % 2, half, :, :, 1 - p.y], p.device(y=1 - p.y)
        else:
            src, peer = self.sum1.at[k % 2, half, :, :, :, 1 - p.x], p.device(x=1 - p.x)
        return self.copy(k, half, 1, src, self.in2.at[k % 2, half], peer)

    def third(self, k, half):
        p = self.p
        other = 1 - p.x if half == 0 else 1 - p.y
        peer = p.device(x=1 - p.x) if half == 0 else p.device(y=1 - p.y)
        src = self.sum2.at[k % 2, half, :, :, other]
        return self.copy(k, half, 2, src, self.in3.at[k % 2, half], peer)

    def fourth(self, k, half, d):
        p = self.p
        target = (p.z + d) % p.zs
        src = self.sum3.at[k % 2, half, :, target]
        dst = self.in4.at[k % 2, half, d - 1]
        return self.copy(k, half, 2 + d, src, dst, p.device(z=target))

    def finish(self, k):
        p = self.p
        slot = k % 2
        for half in (0, 1):
            total = self.sum3[slot, half, :, p.z].astype(F32)
            for d in range(1, p.zs):
                copy = self.fourth(k, half, d)
                copy.wait_recv()
                copy.wait_send()
                total = total + self.in4[slot, half, d - 1].astype(F32)
            self.out[k, half] = total

    def start_fourth(self, k):
        p = self.p
        slot = k % 2
        for half in (0, 1):
            copy = self.third(k, half)
            copy.wait_recv()
            copy.wait_send()
            keep = p.x if half == 0 else p.y
            for i in range(self.sum3.shape[2]):
                total = self.sum2[slot, half, i, :, keep].astype(F32)
                total = total + self.in3[slot, half, i].astype(F32)
                self.sum3[slot, half, i] = total.astype(BF)
            for d in range(1, p.zs):
                self.fourth(k, half, d).start()

    def start_third(self, k):
        p = self.p
        slot = k % 2
        for half in (0, 1):
            copy = self.second(k, half)
            copy.wait_recv()
            copy.wait_send()
            for i in range(self.sum2.shape[2]):
                if half == 0:
                    mine = self.sum1[slot, half, i, :, p.y]
                else:
                    mine = self.sum1[slot, half, i, :, :, p.x]
                total = mine.astype(F32) + self.in2[slot, half, i].astype(F32)
                self.sum2[slot, half, i] = total.astype(BF)
            self.third(k, half).start()

    def start_second(self, k, part):
        p = self.p
        slot = k % 2
        for half in (0, 1):
            copy = self.first(k, half, part)
            copy.wait_recv()
            copy.wait_send()

            def add(z, _, half=half):
                for i in range(self.sum1.shape[2]):
                    mine = part[half, i, z, :, pl.ds(p.c * p.xs, p.xs)]
                    total = mine.astype(F32) + self.in1[slot, half, i, z].astype(F32)
                    self.sum1[slot, half, i, z] = total.astype(BF)
                return 0

            lax.fori_loop(0, p.zs, add, 0)
            self.second(k, half).start()

    def start_first(self, k, part):
        for half in (0, 1):
            self.first(k, half, part).start()


def scatter_buffers(n, zs, xs, rows, lanes):
    shapes = [
        (2, 2, n, zs, Y, xs, rows, lanes),
        (2, 2, n, zs, 2, rows, lanes),
        (2, 2, n, zs, rows, lanes),
        (2, 2, zs - 1, n, rows, lanes),
        (2, 2, n, zs, Y, xs, rows, lanes),
        (2, 2, n, zs, 2, rows, lanes),
        (2, 2, n, zs, rows, lanes),
    ]
    return [pltpu.VMEM(shape, BF) for shape in shapes]


def scatter_kernel(zs, xs, chunks, parts, out, held, local, *rest):
    bufs, (send, recv) = rest[:7], rest[7:]
    place = Place(zs, xs)
    step = pl.program_id(0)
    engine = Scatter(place, bufs, send, recv, out)

    @pl.when(step == 0)
    def _():
        place.barrier()

    def load(k):
        return pltpu.make_async_copy(parts.at[k], held.at[k % 3], local.at[k % 3])

    def first(k):
        load(k).wait()
        engine.start_first(k, held.at[k % 3])

    staged(step, 5, chunks, engine.finish)
    staged(step, 4, chunks, engine.start_fourth)
    staged(step, 3, chunks, engine.start_third)
    staged(step, 2, chunks, lambda k: engine.start_second(k, held.at[k % 3]))
    staged(step, 1, chunks, first)
    staged(step, 0, chunks, lambda k: load(k).start())


def scatter(parts, sizes, rows, collective_id):
    grp, seq = sizes
    chunks, halves, n, _, lanes = parts.shape
    if not can_move(sizes, rows):
        return lax.psum_scatter(parts, ("grp", "seq"), scatter_dimension=3, tiled=True).astype(F32)
    zs = grp // (Y * C)
    view = parts.reshape(chunks, 2, n, zs, Y, C * seq, rows, lanes)
    sems = (2, 2, zs + 2)
    return pl.pallas_call(
        functools.partial(scatter_kernel, zs, seq, chunks),
        grid=(chunks + 5,),
        out_shape=jax.ShapeDtypeStruct((chunks, 2, n, rows, lanes), F32),
        in_specs=[pl.BlockSpec(memory_space=pl.ANY)],
        out_specs=pl.BlockSpec((chunks, 2, n, rows, lanes), lambda step: (0, 0, 0, 0, 0)),
        scratch_shapes=[
            pltpu.VMEM((3, 2, n, zs, Y, C * seq, rows, lanes), BF),
            pltpu.SemaphoreType.DMA((3,)),
        ]
        + scatter_buffers(n, zs, seq, rows, lanes)
        + [pltpu.SemaphoreType.DMA(sems), pltpu.SemaphoreType.DMA(sems)],
        compiler_params=pltpu.CompilerParams(
            collective_id=collective_id, has_side_effects=True, vmem_limit_bytes=VMEM_LIMIT
        ),
    )(view)


class Shape:
    def __init__(self, tiles, local_tiles, conts):
        self.tiles, self.local_tiles, self.conts = tiles, local_tiles, conts
        self.rows = (local_tiles + conts) * T
        self.keys = self.rows + (tiles - local_tiles) * T
        self.parts = [(0, range(local_tiles)), (self.rows, range(local_tiles, tiles))]
        self.parts = [(start, js) for start, js in self.parts if len(js)]


def band_of(key_tile, query_tile):
    return jnp.clip(key_tile - query_tile, -2, 2) + 2


def tile_lanes():
    first_half = lax.broadcasted_iota(jnp.int32, (T, 2 * HEAD), 1) < HEAD
    place = lax.broadcasted_iota(jnp.int32, (T, T), 1)
    return first_half, place


def tile_rows(i):
    return pl.ds(pl.multiple_of(i * T, T), T)


def attend_tile(shape, i, is_cont, live, base, q, k, v, bias, out, norm):
    first_half, place = tile_lanes()
    rows = tile_rows(i)
    queries = q[rows, :]
    query_tile = shape.tiles if is_cont else base + i
    mixed = []
    for h in range(2):
        mine = first_half if h == 0 else ~first_half
        masked = jnp.where(mine, queries, jnp.zeros_like(queries))
        logits = []
        for start, js in shape.parts:
            scores = nt(masked, k[start : start + len(js) * T, :])
            for at, j in enumerate(js):
                band = band_of(lax.rem(base + j, shape.tiles), query_tile)
                logits.append(scores[:, at * T : (at + 1) * T] + bias[h, band])
        if is_cont:
            own = nt(masked, k[rows, :]) + bias[h, 2]
            logits.append(jnp.where(place < live[0, i - shape.local_tiles], own, NEGATIVE))
        top = jnp.max(functools.reduce(jnp.maximum, logits), axis=1, keepdims=True)
        weights = [jnp.exp(part - top) for part in logits]
        total = jnp.sum(functools.reduce(jnp.add, weights), axis=1, keepdims=True)
        inverse = 1.0 / total
        probs = [(weight * inverse).astype(BF) for weight in weights]
        result = None
        for start, js in shape.parts:
            left = jnp.concatenate([probs[j] for j in js], axis=1)
            term = nn(left, v[start : start + len(js) * T, :])
            result = term if result is None else result + term
        if is_cont:
            result = result + nn(probs[shape.tiles], v[rows, :])
        mixed.append(result)
        norm[h, rows, :] = top + jnp.log(total)
    out[rows, :] = jnp.where(first_half, mixed[0], mixed[1]).astype(BF)


def for_tiles(shape, conts, action):
    first, last = (shape.local_tiles, shape.local_tiles + shape.conts) if conts else (0, shape.local_tiles)

    def one(i, carry):
        action(i, conts)
        return carry

    lax.fori_loop(first, last, one, 0)


def attend_kernel(shape, live, base, q, k, v, bias, out, norm):
    for conts in (False, True):
        for_tiles(
            shape,
            conts,
            lambda i, c: attend_tile(shape, i, c, live, base[0], q, k, v, bias, out, norm),
        )


def pair_block(n):
    return pl.BlockSpec((n, 2 * HEAD), lambda h, *_: (0, h))


def attend_moving_kernel(zs, xs, shape, early, live, q, k, v, bias, own, out, norm, ready, *scratch):
    held, local, send, recv = scratch
    place = Place(zs, xs)
    step = pl.program_id(0)

    @pl.when(step == 0)
    def _():
        place.barrier()

    Gather(place, own, ready, send, recv).tick(step, 0, early)

    @pl.when(step == 0)
    def _():
        load = pltpu.make_async_copy(own.at[0:early], held, local.at[0])
        load.start()
        load.wait()
        mine = ready.at[:, :, :, place.z, place.y, place.c * place.xs + place.x]
        store = pltpu.make_async_copy(held, mine, local.at[1])
        store.start()
        store.wait()

    base = place.x * shape.local_tiles
    for part in range(2):

        @pl.when(step % 2 == part)
        def _(part=part):
            for_tiles(
                shape,
                part == 1,
                lambda i, c: attend_tile(shape, i, c, live, base, q, k, v, bias, out, norm),
            )


def attend_moving(q, k, v, bias, live, own, shape, sizes, early, collective_id):
    grp, seq = sizes
    rows, width = q.shape
    pairs = width // (2 * HEAD)
    _, _, n, shard, lanes = own.shape
    zs = grp // (Y * C)
    tile = (2, n, zs, Y, C * seq, shard, lanes)
    block = lambda count: pl.BlockSpec((count, 2 * HEAD), lambda s, *_: (0, s // 2))
    anywhere = pl.BlockSpec(memory_space=pl.ANY)
    sems = lambda *dims: pltpu.SemaphoreType.DMA(dims)
    assert early + 4 <= 2 * pairs
    return pl.pallas_call(
        functools.partial(attend_moving_kernel, zs, seq, shape, early),
        grid_spec=pltpu.PrefetchScalarGridSpec(
            num_scalar_prefetch=1,
            grid=(2 * pairs,),
            in_specs=[
                block(rows),
                block(shape.keys),
                block(shape.keys),
                pl.BlockSpec((2, BANDS, T, T), lambda s, *_: (s // 2, 0, 0, 0)),
                anywhere,
            ],
            out_specs=[
                block(rows),
                pl.BlockSpec((2, rows, 1), lambda s, *_: (s // 2, 0, 0)),
                anywhere,
            ],
            scratch_shapes=[
                pltpu.VMEM((early, *own.shape[1:]), BF),
                sems(2),
                sems(early, 2, zs + 2),
                sems(early, 2, zs + 2),
            ],
        ),
        out_shape=[
            jax.ShapeDtypeStruct((rows, width), BF),
            jax.ShapeDtypeStruct((2 * pairs, rows, 1), F32),
            jax.ShapeDtypeStruct((early, *tile), BF),
        ],
        compiler_params=pltpu.CompilerParams(
            collective_id=collective_id, has_side_effects=True, vmem_limit_bytes=VMEM_LIMIT
        ),
    )(live, q, k, v, bias, own)


def attend(q, k, v, bias, live, base, shape):
    rows, width = q.shape
    pairs = width // (2 * HEAD)
    return pl.pallas_call(
        functools.partial(attend_kernel, shape),
        grid_spec=pltpu.PrefetchScalarGridSpec(
            num_scalar_prefetch=2,
            grid=(pairs,),
            in_specs=[
                pair_block(rows),
                pair_block(shape.keys),
                pair_block(shape.keys),
                pl.BlockSpec((2, BANDS, T, T), lambda h, *_: (h, 0, 0, 0)),
            ],
            out_specs=[pair_block(rows), pl.BlockSpec((2, rows, 1), lambda h, *_: (h, 0, 0))],
        ),
        out_shape=[
            jax.ShapeDtypeStruct((rows, width), BF),
            jax.ShapeDtypeStruct((2 * pairs, rows, 1), F32),
        ],
        compiler_params=pltpu.CompilerParams(vmem_limit_bytes=VMEM_LIMIT),
    )(live, base, q, k, v, bias)


def attend_back_tile(
    shape, i, is_cont, live, base, q, k, v, bias, grad, out, norm, d_q, d_bias, k_sum, v_sum
):
    first_half, place = tile_lanes()
    rows = tile_rows(i)
    queries = q[rows, :]
    grads = grad[rows, :]
    query_tile = shape.tiles if is_cont else base + i
    overlap = grads.astype(F32) * out[rows, :].astype(F32)
    mixed = []
    for h in range(2):
        mine = first_half if h == 0 else ~first_half
        masked = jnp.where(mine, queries, jnp.zeros_like(queries))
        masked_grad = jnp.where(mine, grads, jnp.zeros_like(grads))
        inner = jnp.sum(jnp.where(mine, overlap, 0.0), axis=1, keepdims=True)
        log_norm = norm[h, rows, :]

        def piece(keys, bands, allowed):
            scores = nt(masked, k[keys, :])
            d_probs = nt(masked_grad, v[keys, :])
            probs_low, scores_low = [], []
            for at, band in enumerate(bands):
                cols = slice(at * T, (at + 1) * T)
                logits = scores[:, cols] + bias[h, band]
                if allowed is not None:
                    logits = jnp.where(allowed, logits, NEGATIVE)
                probs = jnp.exp(logits - log_norm)
                d_scores = probs * (d_probs[:, cols] - inner)
                d_bias[h, band] += d_scores
                probs_low.append(probs.astype(BF))
                scores_low.append(d_scores.astype(BF))
            probs_low = jnp.concatenate(probs_low, axis=1)
            scores_low = jnp.concatenate(scores_low, axis=1)
            v_sum[keys, :] += tn(probs_low, masked_grad)
            k_sum[keys, :] += tn(scores_low, masked)
            return nn(scores_low, k[keys, :])

        result = None
        for start, js in shape.parts:
            bands = [band_of(lax.rem(base + j, shape.tiles), query_tile) for j in js]
            term = piece(pl.ds(start, len(js) * T), bands, None)
            result = term if result is None else result + term
        if is_cont:
            result = result + piece(rows, [2], place < live[0, i - shape.local_tiles])
        mixed.append(result)
    d_q[rows, :] = jnp.where(first_half, mixed[0], mixed[1]).astype(BF)


def attend_back_kernel(
    shape, live, base, q, k, v, bias, grad, out, norm, d_q, d_k, d_v, d_bias, k_sum, v_sum
):
    k_sum[...] = jnp.zeros_like(k_sum)
    v_sum[...] = jnp.zeros_like(v_sum)
    d_bias[...] = jnp.zeros_like(d_bias)
    refs = (q, k, v, bias, grad, out, norm, d_q, d_bias, k_sum, v_sum)
    for conts in (False, True):
        for_tiles(shape, conts, lambda i, c: attend_back_tile(shape, i, c, live, base[0], *refs))
    d_k[...] = k_sum[...].astype(BF)
    d_v[...] = v_sum[...].astype(BF)


def attend_back(q, k, v, bias, grad, out, norm, live, base, shape):
    rows, width = q.shape
    pairs = width // (2 * HEAD)
    keys = shape.keys
    bands = pl.BlockSpec((2, BANDS, T, T), lambda h, *_: (h, 0, 0, 0))
    return pl.pallas_call(
        functools.partial(attend_back_kernel, shape),
        grid_spec=pltpu.PrefetchScalarGridSpec(
            num_scalar_prefetch=2,
            grid=(pairs,),
            in_specs=[
                pair_block(rows),
                pair_block(keys),
                pair_block(keys),
                bands,
                pair_block(rows),
                pair_block(rows),
                pl.BlockSpec((2, rows, 1), lambda h, *_: (h, 0, 0)),
            ],
            out_specs=[pair_block(rows), pair_block(keys), pair_block(keys), bands],
            scratch_shapes=[pltpu.VMEM((keys, 2 * HEAD), F32), pltpu.VMEM((keys, 2 * HEAD), F32)],
        ),
        out_shape=[
            jax.ShapeDtypeStruct((rows, width), BF),
            jax.ShapeDtypeStruct((keys, width), BF),
            jax.ShapeDtypeStruct((keys, width), BF),
            jax.ShapeDtypeStruct((2 * pairs, BANDS, T, T), F32),
        ],
        compiler_params=pltpu.CompilerParams(vmem_limit_bytes=VMEM_LIMIT),
    )(live, base, q, k, v, bias, grad, out, norm)


SPAN = 4 * T
VECTOR_ROWS = 8


def turned(tile):
    row = lax.broadcasted_iota(jnp.int32, tile.shape, 0)
    for bit in range(7):
        moved = pltpu.roll(tile, SPAN - (1 << bit), 1)
        tile = jnp.where((row >> bit) & 1 == 1, moved, tile)
    return tile


def band_sums(d_bias, h):
    near = jnp.concatenate([d_bias[h, 1], d_bias[h, 2], d_bias[h, 3]], axis=1)
    near = jnp.concatenate([near, jnp.zeros((T, T), F32)], axis=1)
    diagonal = jnp.sum(turned(near), axis=0, keepdims=True)
    rows = [diagonal[:, i * T : (i + 1) * T] for i in range(4)]
    rows += [jnp.sum(d_bias[h, band], axis=0, keepdims=True) for band in (0, 4)]
    return jnp.concatenate(rows + [jnp.zeros((2, T), F32)], axis=0)


def rows_of(vector):
    return [vector[:, i * T : (i + 1) * T] for i in range(vector.shape[1] // T)]


class Combine:
    def __init__(self, place, total, arrived, send, recv):
        self.p, self.total, self.arrived, self.send, self.recv = place, total, arrived, send, recv

    def partners(self):
        p = self.p
        found = [p.device(c=1 - p.c), p.device(x=1 - p.x), p.device(y=1 - p.y)]
        bit = 1
        while bit < p.zs:
            found.append(p.device(z=p.z + bit - 2 * bit * ((p.z // bit) % 2)))
            bit *= 2
        return found

    def copy(self, i):
        return remote(
            self.total.at[i],
            self.arrived.at[i],
            self.send.at[i],
            self.recv.at[i],
            self.partners()[i],
        )

    def start(self, i):
        self.copy(i).start()

    def finish(self, i):
        self.copy(i).wait_recv()
        self.copy(i).wait_send()
        self.total[i + 1] = self.total[i] + self.arrived[i]


def back_kernel(zs, xs, shape, width, kept, live, *refs):
    q, k, v, bias, grad, out, norm, attended, branch_hbm, normed_hbm, parts, weights_hbm = refs[:12]
    d_middle, x_low, gain, d_gain_two = refs[12:16]
    d_x, sums, vector_out = refs[16:19]
    (stage, turn_buf, d_q, d_kv, back_kv, k_sum, v_sum, d_bias) = refs[19:27]
    (w_buf, held, vector, total, arrived, gain_sum) = refs[27:33]
    (local, loads, kv_sems, both_sems) = refs[33:37]
    bufs, scatter_sems = refs[37:44], refs[44:46]
    place = Place(zs, xs)
    step = pl.program_id(0)
    rows, keys = shape.rows, shape.keys
    prompt = shape.local_tiles * T
    pairs = d_q.shape[0]
    last = 2 * pairs
    turns = rows // T
    first_kept, end_kept = kept
    fed = parts.shape[0] - (end_kept - first_kept)
    group_two = last - 1
    count = fed + 4
    blocks = rows // d_x.shape[0]

    def stage_load(source):
        return pltpu.make_async_copy(source, stage, local.at[0])

    def weights_load(i):
        return pltpu.make_async_copy(weights_hbm.at[i], w_buf.at[i], local.at[1 + i])

    def turn():
        def one(i, carry):
            part = tile_rows(i)
            turn_buf[:, part] = stage[part, :].T
            return carry

        lax.fori_loop(0, turns, one, 0)

    @pl.when(step == 0)
    def _():
        stage_load(branch_hbm).start()
        place.barrier()
        for i in range(3):
            weights_load(i).start()
        stage_load(branch_hbm).wait()
        turn()
        stage_load(normed_hbm).start()

    engine = Scatter(place, bufs, *scatter_sems, sums)

    def due(offset, action):
        at = step - offset
        chunk = jnp.where(at < group_two, at, at - group_two + fed)
        early = (at >= 0) & (at < fed)
        late = (at >= group_two) & (at < group_two + 4)

        @pl.when(early | late)
        def _():
            action(chunk)

    def part_load(c):
        j = jnp.where(c < first_kept, c, c + end_kept - first_kept)
        return pltpu.make_async_copy(parts.at[j], held.at[c % 3], loads.at[c % 3])

    def first(c):
        @pl.when(c < fed)
        def _():
            part_load(c).wait()

        engine.start_first(c, held.at[c % 3])

    due(5, engine.finish)
    due(4, engine.start_fourth)
    due(3, engine.start_third)
    due(2, lambda c: engine.start_second(c, held.at[c % 3]))
    due(1, first)

    @pl.when(step < fed)
    def _():
        part_load(step).start()

    def kv_send(p):
        src = d_kv.at[p, :, pl.ds(rows, keys - rows)]
        peer = place.device(x=1 - place.x)
        return remote(src, back_kv.at[p], kv_sems.at[0, p], kv_sems.at[1, p], peer)

    @pl.when((step >= 2) & (step <= last) & (step % 2 == 0))
    def _():
        kv_send(step // 2 - 1).start()

    @pl.when(step < last)
    def _():
        p = step // 2
        half = step % 2

        @pl.when(half == 0)
        def _():
            k_sum[...] = jnp.zeros_like(k_sum)
            v_sum[...] = jnp.zeros_like(v_sum)
            d_bias[...] = jnp.zeros_like(d_bias)

        inputs = (q, k, v, bias, grad, out, norm, d_q.at[p], d_bias, k_sum, v_sum)
        base = place.x * shape.local_tiles
        action = lambda i, c: attend_back_tile(shape, i, c, live, base, *inputs)

        @pl.when(half == 0)
        def _():
            for_tiles(shape, False, action)

        @pl.when(half == 1)
        def _():
            for_tiles(shape, True, action)
            d_kv[p, 0] = k_sum[...].astype(BF)
            d_kv[p, 1] = v_sum[...].astype(BF)
            for h in range(2):
                vector[2 * p + h] = band_sums(d_bias, h)

    def produce(c, right):
        slot = c % 3
        for m in range(3):
            operand = right(m)

            def one(z, carry, m=m, operand=operand):
                block = turn_buf.shape[0] // zs
                part = pl.ds(pl.multiple_of(z * block, block), block)
                result = nn(turn_buf[part, :], operand).astype(BF)
                for side in range(2):
                    index = 2 * m + side
                    value = result[:, side * T : (side + 1) * T]
                    held[slot, index // 3, index % 3, z] = value.reshape(held.shape[4:])
                return carry

            lax.fori_loop(0, zs, one, 0)

    @pl.when(step == last - 1)
    def _():
        produce(fed, lambda m: attended[:, 2 * m * T : 2 * (m + 1) * T])

    @pl.when(step == last)
    def _():
        stage_load(normed_hbm).wait()
        turn()
        produce(fed + 1, lambda m: jnp.concatenate([d_q[2 * m], d_q[2 * m + 1]], axis=1))

        def join(p, carry):
            kv_send(p).wait_recv()
            kv_send(p).wait_send()
            for side in range(2):
                own = d_kv[p, side, 0:prompt, :].astype(F32)
                d_kv[p, side, 0:prompt, :] = (own + back_kv[p, side].astype(F32)).astype(BF)
            return carry

        lax.fori_loop(0, pairs, join, 0)
        for i in range(3):
            weights_load(i).wait()
        gain_sum[...] = jnp.zeros_like(gain_sum)

    for side in range(2):

        @pl.when(step == last + 1 + side)
        def _(side=side):
            pick = lambda p: d_kv[p, side, 0:rows, :]
            produce(fed + 2 + side, lambda m: jnp.concatenate([pick(2 * m), pick(2 * m + 1)], axis=1))

    @pl.when((step >= last) & (step < last + blocks))
    def _():
        size = d_x.shape[0]
        part = pl.ds(pl.multiple_of((step - last) * size, size), size)
        d_normed = None
        for i in range(3):
            for m in range(pairs // 2):
                if i == 0:
                    left = [d_q[2 * m + e, part, :] for e in range(2)]
                else:
                    left = [d_kv[2 * m + e, i - 1, part, :] for e in range(2)]
                pieces = [2 * m, 2 * m + 1]
                right = [w_buf[i, j // 3, j % 3].reshape(width, T) for j in pieces]
                term = nt(jnp.concatenate(left, axis=1), jnp.concatenate(right, axis=1))
                d_normed = term if d_normed is None else d_normed + term
        x = x_low[...].astype(F32)
        scale = lax.rsqrt(jnp.mean(x * x, axis=-1, keepdims=True) + EPS)
        unit = x * scale
        gain_sum[...] += jnp.sum(d_normed * unit, axis=0, keepdims=True)
        d_unit = d_normed * gain[...]
        inner = jnp.mean(d_unit * unit, axis=-1, keepdims=True)
        d_x[...] = (d_middle[...] + scale * (d_unit - unit * inner)).astype(BF)

    mix = Combine(place, total, arrived, both_sems.at[0], both_sems.at[1])
    start = last + blocks
    stages = total.shape[0] - 1
    tiles = 2 * pairs

    @pl.when(step == start)
    def _():
        total[0, 0:tiles] = vector[...]
        both = rows_of(gain_sum[...]) + rows_of(d_gain_two[...])
        for i in range(len(both) // VECTOR_ROWS):
            group = both[i * VECTOR_ROWS : (i + 1) * VECTOR_ROWS]
            total[0, tiles + i] = jnp.concatenate(group, axis=0)

    for i in range(stages + 1):

        @pl.when(step == start + 1 + i)
        def _(i=i):
            if i > 0:
                mix.finish(i - 1)
            if i < stages:
                mix.start(i)
            else:
                vector_out[...] = total[stages]


def back(q, k, v, bias, grad, out, norm, branch, normed, parts, weights, d_middle, x_low, gain,
         d_gain_two, live, shape, sizes, kept, collective_id):
    grp, seq = sizes
    rows, width = x_low.shape
    inner = q.shape[1]
    pairs = inner // (2 * HEAD)
    zs = grp // (Y * C)
    keys = shape.keys
    chunks, _, n, _, _, _, shard, lanes = parts.shape
    count = chunks - (kept[1] - kept[0]) + 4
    assert chunks - (kept[1] - kept[0]) <= 2 * pairs - 1
    assert (pairs, n) == (6, 3) and 2 * width // T % VECTOR_ROWS == 0
    last = 2 * pairs
    size = min(rows, 256)
    blocks = rows // size
    tile = (2, n, zs, Y, C * seq, shard, lanes)
    stages = 3 + (zs - 1).bit_length()
    steps = last + blocks + stages + 2
    vector = (2 * pairs + 2 * width // T // VECTOR_ROWS, VECTOR_ROWS, T)
    pair = lambda s: jnp.minimum(s // 2, pairs - 1)
    by_pair = lambda rows_: pl.BlockSpec((rows_, 2 * HEAD), lambda s, *_: (0, pair(s)))
    row_block = lambda s: jnp.clip(s - last, 0, blocks - 1)
    by_rows = pl.BlockSpec((size, width), lambda s, *_: (row_block(s), 0))
    full = lambda *dims: pl.BlockSpec(
        dims, lambda s, *_: (0,) * len(dims), pipeline_mode=pl.Buffered(1)
    )
    anywhere = pl.BlockSpec(memory_space=pl.ANY)
    sems = lambda *dims: pltpu.SemaphoreType.DMA(dims)
    return pl.pallas_call(
        functools.partial(back_kernel, zs, seq, shape, width, kept),
        grid_spec=pltpu.PrefetchScalarGridSpec(
            num_scalar_prefetch=1,
            grid=(steps,),
            in_specs=[
                by_pair(rows),
                by_pair(keys),
                by_pair(keys),
                pl.BlockSpec((2, BANDS, T, T), lambda s, *_: (pair(s), 0, 0, 0)),
                by_pair(rows),
                by_pair(rows),
                pl.BlockSpec((2, rows, 1), lambda s, *_: (pair(s), 0, 0)),
                full(rows, inner),
                anywhere,
                anywhere,
                anywhere,
                anywhere,
                by_rows,
                by_rows,
                full(1, width),
                full(1, width),
            ],
            out_specs=[by_rows, full(count, 2, n, shard, lanes), full(*vector)],
            scratch_shapes=[
                pltpu.VMEM((rows, width), BF),
                pltpu.VMEM((width, rows), BF),
                pltpu.VMEM((pairs, rows, 2 * HEAD), BF),
                pltpu.VMEM((pairs, 2, keys, 2 * HEAD), BF),
                pltpu.VMEM((pairs, 2, keys - rows, 2 * HEAD), BF),
                pltpu.VMEM((keys, 2 * HEAD), F32),
                pltpu.VMEM((keys, 2 * HEAD), F32),
                pltpu.VMEM((2, BANDS, T, T), F32),
                pltpu.VMEM((3, *tile), BF),
                pltpu.VMEM((3, *tile), BF),
                pltpu.VMEM((2 * pairs, VECTOR_ROWS, T), F32),
                pltpu.VMEM((stages + 1, *vector), F32),
                pltpu.VMEM((stages, *vector), F32),
                pltpu.VMEM((1, width), F32),
                sems(4),
                sems(3),
                sems(2, pairs),
                sems(2, stages),
            ]
            + scatter_buffers(n, zs, seq, shard, lanes)
            + [sems(2, 2, zs + 2), sems(2, 2, zs + 2)],
        ),
        out_shape=[
            jax.ShapeDtypeStruct((rows, width), BF),
            jax.ShapeDtypeStruct((count, 2, n, shard, lanes), F32),
            jax.ShapeDtypeStruct(vector, F32),
        ],
        compiler_params=pltpu.CompilerParams(
            collective_id=collective_id, has_side_effects=True, vmem_limit_bytes=VMEM_LIMIT
        ),
    )(live, q, k, v, bias, grad, out, norm, out, branch, normed, parts, weights, d_middle,
      x_low, gain, d_gain_two)


GELU_SCALE = 0.7978845608028654
GELU_CUBIC = 0.044715


def gelu_and_slope(a):
    square = a * a
    tanh = jnp.tanh(GELU_SCALE * a * (1.0 + GELU_CUBIC * square))
    half = 0.5 * (1.0 + tanh)
    slope = half + 0.5 * a * (1.0 - tanh * tanh) * (
        GELU_SCALE * (1.0 + 3.0 * GELU_CUBIC * square)
    )
    return a * half, slope


def feed_load(x_hbm, dy_hbm, x, x_t, dy, dy_t, sem):
    load_x = pltpu.make_async_copy(x_hbm, x, sem.at[0])
    load_dy = pltpu.make_async_copy(dy_hbm, dy, sem.at[1])
    load_x.start()
    load_dy.start()
    load_x.wait()
    load_dy.wait()

    def turn(i, carry):
        part = pl.ds(pl.multiple_of(i * T, T), T)
        x_t[:, part] = x[part, :].T
        dy_t[:, part] = dy[part, :].T
        return carry

    lax.fori_loop(0, x.shape[0] // T, turn, 0)


def feed_chunk(read, write, blocks, out, d_x, x, x_t, dy, dy_t, hidden, d_gate, d_up):
    rows, width = x.shape
    row_block = min(rows, 256)
    width_block = width // blocks
    w_gate, w_up, w_down = [jnp.concatenate([read(0, i), read(1, i)], axis=1) for i in range(3)]

    def by_rows(i, carry):
        part = pl.ds(pl.multiple_of(i * row_block, row_block), row_block)
        gate = nn(x[part, :], w_gate)
        up = nn(x[part, :], w_up)
        d_hidden = nn(dy[part, :], w_down)
        active, slope = gelu_and_slope(gate)
        hidden_low = (active * up).astype(BF)
        d_gate_low = (d_hidden * up * slope).astype(BF)
        d_up_low = (d_hidden * active).astype(BF)
        hidden[part, :] = hidden_low
        d_gate[part, :] = d_gate_low
        d_up[part, :] = d_up_low
        out[part, :] += nt(hidden_low, w_down)
        d_x[part, :] += nt(d_gate_low, w_gate) + nt(d_up_low, w_up)
        return carry

    lax.fori_loop(0, rows // row_block, by_rows, 0)

    def by_width(i, carry):
        part = pl.ds(pl.multiple_of(i * width_block, width_block), width_block)
        pairs = ((x_t, d_gate), (x_t, d_up), (dy_t, hidden))
        for index, (left, right) in enumerate(pairs):
            total = nn(left[part, :], right[...]).astype(BF)
            write(0, index, i, total[:, :T])
            write(1, index, i, total[:, T:])
        return carry

    lax.fori_loop(0, blocks, by_width, 0)


def feed_kernel(x_hbm, dy_hbm, weights, out, d_x, grads, x, x_t, dy, dy_t, *rest):
    *work, sem = rest
    width_block = 512

    @pl.when(pl.program_id(0) == 0)
    def _():
        feed_load(x_hbm, dy_hbm, x, x_t, dy, dy_t, sem)
        out[...] = jnp.zeros_like(out)
        d_x[...] = jnp.zeros_like(d_x)

    def write(half, index, block, value):
        part = pl.ds(pl.multiple_of(block * width_block, width_block), width_block)
        grads[0, half, index, part, :] = value

    read = lambda half, index: weights[0, half, index]
    blocks = x.shape[1] // width_block
    feed_chunk(read, write, blocks, out, d_x, x, x_t, dy, dy_t, *work)


def feed_scratch(rows, width):
    return [
        pltpu.VMEM((rows, width), BF),
        pltpu.VMEM((width, rows), BF),
        pltpu.VMEM((rows, width), BF),
        pltpu.VMEM((width, rows), BF),
        pltpu.VMEM((rows, 2 * T), BF),
        pltpu.VMEM((rows, 2 * T), BF),
        pltpu.VMEM((rows, 2 * T), BF),
        pltpu.SemaphoreType.DMA((2,)),
    ]


def feed(x, dy, weights):
    rows, width = x.shape
    chunks = weights.shape[0]
    chunk = pl.BlockSpec((1, 2, 3, width, T), lambda j: (j, 0, 0, 0, 0))
    whole = pl.BlockSpec((rows, width), lambda j: (0, 0), pipeline_mode=pl.Buffered(1))
    return pl.pallas_call(
        feed_kernel,
        grid=(chunks,),
        in_specs=[pl.BlockSpec(memory_space=pl.ANY)] * 2 + [chunk],
        out_specs=[whole, whole, chunk],
        out_shape=[
            jax.ShapeDtypeStruct((rows, width), F32),
            jax.ShapeDtypeStruct((rows, width), F32),
            jax.ShapeDtypeStruct((chunks, 2, 3, width, T), BF),
        ],
        scratch_shapes=feed_scratch(rows, width),
        compiler_params=pltpu.CompilerParams(vmem_limit_bytes=VMEM_LIMIT),
    )(x, dy, weights)


def feed_moving_kernel(zs, xs, early, kept, *refs):
    x_hbm, dy_hbm, own, ready, out, d_x, whole, parts, sums = refs[:9]
    x, x_t, dy, dy_t, hidden, d_gate, d_up, sem = refs[9:17]
    held, w_buf, g_buf, local = refs[17:21]
    gather_sems, bufs, scatter_sems = refs[21:23], refs[23:30], refs[30:32]
    chunks = own.shape[0]
    place = Place(zs, xs)
    step = pl.program_id(0)
    lag = max(0, 5 - early)
    first_kept, end_kept = kept
    width = x.shape[1]

    @pl.when(step == 0)
    def _():
        place.barrier()

    fetch = Gather(place, own, whole, *gather_sems)
    fetch.tick(step, early, chunks)

    @pl.when(step == 0)
    def _():
        load = pltpu.make_async_copy(own, held, local.at[0])
        load.start()
        load.wait()
        mine = whole.at[:, :, :, place.z, place.y, place.c * place.xs + place.x]
        store = pltpu.make_async_copy(held, mine, local.at[1])
        store.start()
        store.wait()
        feed_load(x_hbm, dy_hbm, x, x_t, dy, dy_t, sem)
        out[...] = jnp.zeros_like(out)
        d_x[...] = jnp.zeros_like(d_x)

    def weight_load(j, source):
        return pltpu.make_async_copy(source.at[j], w_buf.at[j % 2], local.at[2 + j % 2])

    def start_load(j):
        if early > 0:

            @pl.when(j < early)
            def _():
                weight_load(j, ready).start()

        @pl.when(j >= early)
        def _():
            weight_load(j, whole).start()

    def part_store(j):
        return pltpu.make_async_copy(g_buf.at[j % 2], parts.at[j], local.at[4 + j % 2])

    def is_kept(j):
        return (j >= first_kept) & (j < end_kept)

    engine = Scatter(place, bufs, *scatter_sems, sums)
    due = lag + first_kept
    number = end_kept - first_kept
    grads_of = lambda k: g_buf.at[(k + first_kept) % 2]
    staged(step, due + 5, number, engine.finish)
    staged(step, due + 4, number, engine.start_fourth)
    staged(step, due + 3, number, engine.start_third)
    staged(step, due + 2, number, lambda k: engine.start_second(k, grads_of(k)))
    staged(step, due + 1, number, lambda k: engine.start_first(k, grads_of(k)))

    chunk = step - lag
    if lag == 0:

        @pl.when(step == 0)
        def _():
            start_load(0)

    @pl.when((chunk >= (0 if lag == 0 else -1)) & (chunk + 1 < chunks))
    def _():
        start_load(chunk + 1)

    @pl.when((chunk >= 2) & (chunk < chunks + 2) & ~is_kept(chunk - 2))
    def _():
        part_store(chunk - 2).wait()

    @pl.when((chunk >= 0) & (chunk < chunks))
    def _():
        weight_load(chunk, whole).wait()
        slot = chunk % 2

        def read(half, index):
            return w_buf[slot, half, index].reshape(width, T)

        def write(half, index, block, value):
            shape = g_buf.shape[4:]
            g_buf[slot, half, index, block] = value.reshape(shape)

        work = (hidden, d_gate, d_up)
        feed_chunk(read, write, zs, out, d_x, x, x_t, dy, dy_t, *work)

        @pl.when(~is_kept(chunk))
        def _():
            part_store(chunk).start()


def feed_moving(x, dy, own, ready, sizes, early, kept, collective_id):
    grp, seq = sizes
    rows, width = x.shape
    chunks, _, n, shard, lanes = own.shape
    zs = grp // (Y * C)
    tile = (2, n, zs, Y, C * seq, shard, lanes)
    whole = pl.BlockSpec((rows, width), lambda j: (0, 0), pipeline_mode=pl.Buffered(1))
    number = kept[1] - kept[0]
    sums = pl.BlockSpec(
        (number, 2, n, shard, lanes), lambda j: (0,) * 5, pipeline_mode=pl.Buffered(1)
    )
    lag = max(0, 5 - early)
    steps = lag + max(chunks + 2, kept[1] + 5)
    anywhere = pl.BlockSpec(memory_space=pl.ANY)
    sems = lambda *shape: pltpu.SemaphoreType.DMA(shape)
    return pl.pallas_call(
        functools.partial(feed_moving_kernel, zs, seq, early, kept),
        grid=(steps,),
        in_specs=[anywhere] * 4,
        out_specs=[whole, whole, anywhere, anywhere, sums],
        out_shape=[
            jax.ShapeDtypeStruct((rows, width), F32),
            jax.ShapeDtypeStruct((rows, width), F32),
            jax.ShapeDtypeStruct((chunks, *tile), BF),
            jax.ShapeDtypeStruct((chunks, *tile), BF),
            jax.ShapeDtypeStruct((number, 2, n, shard, lanes), F32),
        ],
        scratch_shapes=feed_scratch(rows, width)
        + [
            pltpu.VMEM(own.shape, BF),
            pltpu.VMEM((2, *tile), BF),
            pltpu.VMEM((2, *tile), BF),
            sems(6),
            sems(chunks, 2, zs + 2),
            sems(chunks, 2, zs + 2),
        ]
        + scatter_buffers(n, zs, seq, shard, lanes)
        + [sems(2, 2, zs + 2), sems(2, 2, zs + 2)],
        compiler_params=pltpu.CompilerParams(
            collective_id=collective_id, has_side_effects=True, vmem_limit_bytes=VMEM_LIMIT
        ),
    )(x, dy, own, ready)


def rms_scale(values):
    return lax.rsqrt(jnp.mean(values * values, axis=-1, keepdims=True) + EPS)


def norm_back(d_normed, unit, scale, gain):
    d_unit = d_normed * gain
    return scale * (d_unit - unit * jnp.mean(d_unit * unit, axis=-1, keepdims=True))


def pieces_of(matrix):
    rows, columns = matrix.shape
    return jnp.swapaxes(matrix.reshape(rows, columns // T, T), 0, 1)


def joined(pieces):
    count, rows, _ = pieces.shape
    return jnp.swapaxes(pieces, 0, 1).reshape(rows, count * T)


def attention_chunks(matrices):
    flat = jnp.concatenate([pieces_of(m) for m in matrices], axis=0)
    pad = -flat.shape[0] % 6
    flat = jnp.pad(flat, ((0, pad), (0, 0), (0, 0)))
    return flat.reshape(-1, 2, 3, *flat.shape[1:])


def feed_chunks(matrices):
    stacked = jnp.stack([pieces_of(m) for m in matrices], axis=1)
    pad = -stacked.shape[0] % 2
    stacked = jnp.pad(stacked, ((0, pad), (0, 0), (0, 0), (0, 0)))
    return stacked.reshape(-1, 2, *stacked.shape[1:])


def body(sizes, *args):
    (
        prompt_x,
        cont_x,
        cont_len,
        prompt_cot,
        cont_cot,
        norm1_gain,
        q_weight,
        k_weight,
        v_weight,
        o_weight,
        bucket_table,
        norm2_gain,
        gate_weight,
        up_weight,
        down_weight,
    ) = args
    _, local_prompt, width = prompt_x.shape
    conts, cont_rows = cont_x.shape[1], cont_x.shape[2]
    assert prompt_x.shape[0] == 1 and cont_rows == T and local_prompt % T == 0
    seq = sizes[1]
    num_buckets, heads = bucket_table.shape
    inner = q_weight.shape[1]
    assert inner == heads * HEAD
    shard = q_weight.shape[0]
    hidden_width = gate_weight.shape[1]
    local_tiles = local_prompt // T
    tiles = local_tiles * seq
    seq_index = lax.axis_index("seq")

    x_low = jnp.concatenate([prompt_x[0], cont_x[0].reshape(-1, width)], axis=0)
    dy_low = jnp.concatenate([prompt_cot[0], cont_cot[0].reshape(-1, width)], axis=0)
    x = x_low.astype(F32)
    dy = dy_low.astype(F32)

    lanes = jnp.zeros((shard, T - 2), F32)
    gains = jnp.concatenate([norm1_gain[:, None], norm2_gain[:, None], lanes], axis=1)
    own_attention = attention_chunks([q_weight, k_weight, v_weight, o_weight, gains]).astype(BF)
    own_feed = feed_chunks([gate_weight, up_weight, down_weight]).astype(BF)
    attention_whole = gather(own_attention, sizes, 0)
    count = inner // T
    flat = attention_whole.reshape(-1, width, T)
    q_full, k_full, v_full, o_full = [
        joined(flat[i * count : (i + 1) * count]) for i in range(4)
    ]
    gain_one = flat[4 * count, :, 0].astype(F32)
    gain_two = flat[4 * count, :, 1].astype(F32)

    scale_one = rms_scale(x)
    unit_one = x * scale_one
    normed_one = (unit_one * gain_one).astype(BF)
    kv = nn(normed_one, jnp.concatenate([k_full, v_full], axis=1)).astype(BF)
    queries = nn(normed_one, q_full).astype(BF)
    prompt_kv = kv[:local_prompt]
    if seq == 2:
        others = lax.ppermute(prompt_kv, "seq", [(0, 1), (1, 0)])
    else:
        gathered = lax.all_gather(prompt_kv, "seq", axis=0, tiled=True)
        others = jnp.roll(gathered, -seq_index * local_prompt, axis=0)[local_prompt:]
    every = jnp.concatenate([kv, others], axis=0)
    keys, values = every[:, :inner], every[:, inner:]
    base = (seq_index * local_tiles).reshape(1).astype(jnp.int32)

    one_hot = band_one_hot(num_buckets)
    bias = jnp.einsum("cqkb,bh->hcqk", one_hot, bucket_table, precision=lax.Precision.HIGHEST)
    shape = Shape(tiles, local_tiles, conts)
    moving = can_move(sizes, shard)
    early, kept = 5, (8, 14)
    if moving:
        attended, log_norm, ready = attend_moving(
            queries, keys, values, bias, cont_len, own_feed, shape, sizes, early, 3
        )
    else:
        attended, log_norm = attend(queries, keys, values, bias, cont_len, base, shape)
    middle = x + nt(attended, o_full)
    scale_two = rms_scale(middle)
    unit_two = middle * scale_two
    normed_two = (unit_two * gain_two).astype(BF)

    if moving:
        out_sum, d_normed_two, _, feed_parts, kept_sums = feed_moving(
            normed_two, dy_low, own_feed, ready, sizes, early, kept, 1
        )
    else:
        feed_whole = gather(own_feed, sizes, 1)
        out_sum, d_normed_two, feed_grads = feed(normed_two, dy_low, feed_whole)
        feed_sums = scatter(feed_grads, sizes, shard, 4)
    final = (middle + out_sum).astype(BF)

    d_gain_two = jnp.sum(d_normed_two * unit_two, axis=0)
    d_middle = dy + norm_back(d_normed_two, unit_two, scale_two, gain_two)
    d_branch = d_middle.astype(BF)
    d_attended = nn(d_branch, o_full).astype(BF)
    if moving:
        d_x, sums, vector = back(
            queries, keys, values, bias, d_attended, attended, log_norm, d_branch, normed_one,
            feed_parts, attention_whole.reshape(-1, *feed_parts.shape[1:]), d_middle, x_low,
            gain_one[None], d_gain_two[None], cont_len, shape, sizes, kept, 2,
        )
        fed = sums.shape[0] - 4
        feed_sums = jnp.concatenate([sums[: kept[0]], kept_sums, sums[kept[0] : fed]], axis=0)
        attention_sums = jnp.concatenate([sums[fed + 1 :], sums[fed : fed + 1]], axis=0)
        attention_sums = attention_sums.reshape(-1, shard, T)
        near = vector[:heads, :4].reshape(heads, SPAN)
        far = jnp.sum(vector[:heads, 4:6], axis=-1)
        relative = (jnp.arange(SPAN) + T) % SPAN - 2 * T
        ids = jnp.concatenate([bucket_ids(relative), bucket_ids(jnp.array([-T, T]))])
        hot = (ids[:, None] == jnp.arange(num_buckets)).astype(F32)
        both = jnp.concatenate([near, far], axis=1)
        table_grad = jnp.einsum("hr,rb->bh", both, hot, precision=lax.Precision.HIGHEST)
        gain_grads = vector[heads:].reshape(2, sizes[0] * seq, shard)
        me = lax.axis_index("grp") * seq + seq_index
        norm1_grad, norm2_grad = lax.dynamic_index_in_dim(gain_grads, me, 1, keepdims=False)
    else:
        d_o = tn(d_branch, attended)
        d_queries, d_keys, d_values, d_bias = attend_back(
            queries, keys, values, bias, d_attended, attended, log_norm, cont_len, base, shape
        )
        d_table = jnp.einsum("hcqk,cqkb->bh", d_bias, one_hot, precision=lax.Precision.HIGHEST)
        d_kv = jnp.concatenate([d_keys, d_values], axis=1)
        prompt_parts = jnp.concatenate([d_kv[:local_prompt], d_kv[shape.rows :]], axis=0)
        prompt_parts = jnp.roll(prompt_parts, seq_index * local_prompt, axis=0)
        d_prompt = lax.psum_scatter(prompt_parts, "seq", scatter_dimension=0, tiled=True)
        d_kv = jnp.concatenate([d_prompt, d_kv[local_prompt : shape.rows]], axis=0)
        d_normed_one = nt(d_queries, q_full) + nt(d_kv, jnp.concatenate([k_full, v_full], axis=1))
        d_q = tn(normed_one, d_queries)
        d_kv_weight = tn(normed_one, d_kv)
        d_gain_one = jnp.sum(d_normed_one * unit_one, axis=0)
        d_x = d_middle + norm_back(d_normed_one, unit_one, scale_one, gain_one)
        d_x = d_x.astype(BF)
        attention_parts = attention_chunks([d_q, d_kv_weight, d_o]).astype(BF)
        attention_sums = scatter(attention_parts, sizes, shard, 2).reshape(-1, shard, T)
        norm1_grad = lax.psum_scatter(d_gain_one, ("grp", "seq"), scatter_dimension=0, tiled=True)
        norm2_grad = lax.psum_scatter(d_gain_two, ("grp", "seq"), scatter_dimension=0, tiled=True)
        table_grad = lax.psum(d_table, ("grp", "seq"))
    feed_sums = feed_sums.reshape(-1, 3, shard, T)[: hidden_width // T]
    gate_grad, up_grad, down_grad = [joined(feed_sums[:, i]) for i in range(3)]
    q_grad, k_grad, v_grad, o_grad = [
        joined(attention_sums[i * count : (i + 1) * count]) for i in range(4)
    ]
    split = lambda rows: (
        rows[:local_prompt][None],
        rows[local_prompt:].reshape(1, conts, cont_rows, width),
    )
    return (
        *split(final),
        *split(d_x),
        norm1_grad,
        q_grad,
        k_grad,
        v_grad,
        o_grad,
        table_grad,
        norm2_grad,
        gate_grad,
        up_grad,
        down_grad,
    )


def solution(mesh):
    sizes = (mesh.shape["grp"], mesh.shape["seq"])
    rows = P("grp", "seq", None)
    conts = P("grp", "seq", None, None)
    shard = P(("grp", "seq"), None)
    gain = P(("grp", "seq"))
    in_specs = (rows, conts, P("grp", "seq"), rows, conts, gain, shard, shard, shard, shard)
    in_specs += (P(), gain, shard, shard, shard)
    out_specs = (rows, conts, rows, conts, gain, shard, shard, shard, shard, P(), gain)
    out_specs += (shard, shard, shard)
    return jax.shard_map(
        functools.partial(body, sizes),
        mesh=mesh,
        in_specs=in_specs,
        out_specs=out_specs,
        check_vma=False,
    )
```

```python
import functools

import jax
import jax.numpy as jnp
from jax import lax
from jax.experimental import pallas as pl
from jax.experimental.pallas import tpu as pltpu
from jax.sharding import PartitionSpec as P

EPS = 1e-06
LIMITS = (8, 12, 16, 23, 32, 46, 64, 91)
NEGATIVE = -1e30
MESH = pl.DeviceIdType.MESH
T = 128
HEAD = 64
BANDS = 5
BF = jnp.bfloat16
F32 = jnp.float32
VMEM_LIMIT = 63 * 2**20
Y = 2
C = 2


def nn(left, right):
    return jnp.dot(left, right, preferred_element_type=F32)


def nt(left, right):
    return lax.dot_general(left, right, (((1,), (1,)), ((), ())), preferred_element_type=F32)


def tn(left, right):
    return lax.dot_general(left, right, (((0,), (0,)), ((), ())), preferred_element_type=F32)


def bucket_ids(relative):
    distance = jnp.abs(relative)
    coarse = 7 + sum(((distance >= boundary).astype(jnp.int32) for boundary in LIMITS))
    return jnp.where(distance < 8, distance, coarse) + 16 * (relative > 0).astype(jnp.int32)


def band_one_hot(num_buckets):
    band = jnp.arange(BANDS)[:, None, None] - 2
    query = jnp.arange(T)[None, :, None]
    key = jnp.arange(T)[None, None, :]
    ids = bucket_ids(band * T + key - query)
    return (ids[..., None] == jnp.arange(num_buckets)).astype(F32)


def can_move(sizes, rows):
    zs = sizes[0] // (Y * C)
    return rows % 16 == 0 and sizes[1] == 2 and sizes[0] % (Y * C) == 0 and zs in (2, 4, 8, 16)


class Place:
    def __init__(self, zs, xs):
        grp = lax.axis_index("grp")
        self.zs, self.xs = zs, xs
        self.x = lax.axis_index("seq")
        self.z = grp // (Y * C)
        self.y = (grp // C) % Y
        self.c = grp % C

    def device(self, z=None, y=None, c=None, x=None):
        z = self.z if z is None else z
        y = self.y if y is None else y
        c = self.c if c is None else c
        x = self.x if x is None else x
        return (z * (Y * C) + y * C + c, x)

    def peers(self):
        around = [self.device(z=(self.z + d) % self.zs) for d in range(1, self.zs)]
        return around + [
            self.device(y=1 - self.y),
            self.device(x=1 - self.x),
            self.device(c=1 - self.c),
        ]

    def barrier(self):
        sem = pltpu.get_barrier_semaphore()
        peers = self.peers()
        for peer in peers:
            pl.semaphore_signal(sem, inc=1, device_id=peer, device_id_type=MESH)
        pl.semaphore_wait(sem, len(peers))


def remote(src, dst, send_sem, recv_sem, device):
    return pltpu.make_async_remote_copy(
        src_ref=src,
        dst_ref=dst,
        send_sem=send_sem,
        recv_sem=recv_sem,
        device_id=device,
        device_id_type=MESH,
    )


def staged(step, offset, count, action):
    @pl.when((step >= offset) & (step < count + offset))
    def _():
        action(step - offset)


class Gather:
    def __init__(self, place, own, whole, send, recv):
        self.p, self.own, self.whole, self.send, self.recv = place, own, whole, send, recv

    def copy(self, k, half, index, src, dst, device):
        return remote(src, dst, self.send.at[k, half, index], self.recv.at[k, half, index], device)

    def along_z(self, k, half, d):
        p = self.p
        dst = self.whole.at[k, half, :, p.z, p.y, p.c * p.xs + p.x]
        return self.copy(k, half, d - 1, self.own.at[k, half], dst, p.device(z=(p.z + d) % p.zs))

    def second(self, k, half):
        p = self.p
        view = self.whole.at[k, half, :, :, p.y, p.c * p.xs + p.x]
        peer = p.device(x=1 - p.x) if half == 0 else p.device(y=1 - p.y)
        return self.copy(k, half, p.zs - 1, view, view, peer)

    def third(self, k, half):
        p = self.p
        if half == 0:
            view = self.whole.at[k, half, :, :, p.y, pl.ds(p.c * p.xs, p.xs)]
            peer = p.device(y=1 - p.y)
        else:
            view = self.whole.at[k, half, :, :, :, p.c * p.xs + p.x]
            peer = p.device(x=1 - p.x)
        return self.copy(k, half, p.zs, view, view, peer)

    def fourth(self, k, half):
        p = self.p
        view = self.whole.at[k, half, :, :, :, pl.ds(p.c * p.xs, p.xs)]
        return self.copy(k, half, p.zs + 1, view, view, p.device(c=1 - p.c))

    def tick(self, step, first, end):
        def start_z(k):
            for half in (0, 1):
                for d in range(1, self.p.zs):
                    self.along_z(k, half, d).start()

        def start_second(k):
            for half in (0, 1):
                for d in range(1, self.p.zs):
                    self.along_z(k, half, d).wait_recv()
                self.second(k, half).start()

        def start_third(k):
            for half in (0, 1):
                self.second(k, half).wait_recv()
                self.third(k, half).start()

        def start_fourth(k):
            for half in (0, 1):
                self.third(k, half).wait_recv()
                self.fourth(k, half).start()

        def finish(k):
            for half in (0, 1):
                self.fourth(k, half).wait_recv()
                for d in range(1, self.p.zs):
                    self.along_z(k, half, d).wait_send()
                self.second(k, half).wait_send()
                self.third(k, half).wait_send()
                self.fourth(k, half).wait_send()

        for offset, action in enumerate((start_z, start_second, start_third, start_fourth, finish)):
            staged(step, offset, end - first, lambda k, action=action: action(first + k))


def gather(own, sizes):
    return lax.all_gather(own, ("grp", "seq"), axis=3, tiled=True)


class Scatter:
    def __init__(self, place, bufs, send, recv, out):
        self.p, self.send, self.recv, self.out = place, send, recv, out
        (self.in1, self.in2, self.in3, self.in4, self.sum1, self.sum2, self.sum3) = bufs

    def copy(self, k, half, index, src, dst, device):
        slot = k % 2
        return remote(
            src, dst, self.send.at[slot, half, index], self.recv.at[slot, half, index], device
        )

    def first(self, k, half, part):
        p = self.p
        src = part.at[half, :, :, :, pl.ds((1 - p.c) * p.xs, p.xs)]
        return self.copy(k, half, 0, src, self.in1.at[k % 2, half], p.device(c=1 - p.c))

    def second(self, k, half):
        p = self.p
        if half == 0:
            src, peer = self.sum1.at[k % 2, half, :, :, 1 - p.y], p.device(y=1 - p.y)
        else:
            src, peer = self.sum1.at[k % 2, half, :, :, :, 1 - p.x], p.device(x=1 - p.x)
        return self.copy(k, half, 1, src, self.in2.at[k % 2, half], peer)

    def third(self, k, half):
        p = self.p
        other = 1 - p.x if half == 0 else 1 - p.y
        peer = p.device(x=1 - p.x) if half == 0 else p.device(y=1 - p.y)
        src = self.sum2.at[k % 2, half, :, :, other]
        return self.copy(k, half, 2, src, self.in3.at[k % 2, half], peer)

    def fourth(self, k, half, d):
        p = self.p
        target = (p.z + d) % p.zs
        src = self.sum3.at[k % 2, half, :, target]
        dst = self.in4.at[k % 2, half, d - 1]
        return self.copy(k, half, 2 + d, src, dst, p.device(z=target))

    def finish(self, k):
        p = self.p
        slot = k % 2
        for half in (0, 1):
            total = self.sum3[slot, half, :, p.z].astype(F32)
            for d in range(1, p.zs):
                copy = self.fourth(k, half, d)
                copy.wait_recv()
                copy.wait_send()
                total = total + self.in4[slot, half, d - 1].astype(F32)
            self.out[k, half] = total

    def start_fourth(self, k):
        p = self.p
        slot = k % 2
        for half in (0, 1):
            copy = self.third(k, half)
            copy.wait_recv()
            copy.wait_send()
            keep = p.x if half == 0 else p.y
            for i in range(self.sum3.shape[2]):
                total = self.sum2[slot, half, i, :, keep].astype(F32)
                total = total + self.in3[slot, half, i].astype(F32)
                self.sum3[slot, half, i] = total.astype(BF)
            for d in range(1, p.zs):
                self.fourth(k, half, d).start()

    def start_third(self, k):
        p = self.p
        slot = k % 2
        for half in (0, 1):
            copy = self.second(k, half)
            copy.wait_recv()
            copy.wait_send()
            for i in range(self.sum2.shape[2]):
                if half == 0:
                    mine = self.sum1[slot, half, i, :, p.y]
                else:
                    mine = self.sum1[slot, half, i, :, :, p.x]
                total = mine.astype(F32) + self.in2[slot, half, i].astype(F32)
                self.sum2[slot, half, i] = total.astype(BF)
            self.third(k, half).start()

    def start_second(self, k, part):
        p = self.p
        slot = k % 2
        for half in (0, 1):
            copy = self.first(k, half, part)
            copy.wait_recv()
            copy.wait_send()

            def add(z, _, half=half):
                for i in range(self.sum1.shape[2]):
                    mine = part[half, i, z, :, pl.ds(p.c * p.xs, p.xs)]
                    total = mine.astype(F32) + self.in1[slot, half, i, z].astype(F32)
                    self.sum1[slot, half, i, z] = total.astype(BF)
                return 0

            lax.fori_loop(0, p.zs, add, 0)
            self.second(k, half).start()

    def start_first(self, k, part):
        for half in (0, 1):
            self.first(k, half, part).start()


def scatter_buffers(n, zs, xs, rows, lanes):
    shapes = [
        (2, 2, n, zs, Y, xs, rows, lanes),
        (2, 2, n, zs, 2, rows, lanes),
        (2, 2, n, zs, rows, lanes),
        (2, 2, zs - 1, n, rows, lanes),
        (2, 2, n, zs, Y, xs, rows, lanes),
        (2, 2, n, zs, 2, rows, lanes),
        (2, 2, n, zs, rows, lanes),
    ]
    return [pltpu.VMEM(shape, BF) for shape in shapes]


def scatter(parts):
    return lax.psum_scatter(parts, ("grp", "seq"), scatter_dimension=3, tiled=True).astype(F32)


class Shape:
    def __init__(self, tiles, local_tiles, conts):
        self.tiles, self.local_tiles, self.conts = tiles, local_tiles, conts
        self.rows = (local_tiles + conts) * T
        self.keys = self.rows + (tiles - local_tiles) * T
        self.parts = [(0, range(local_tiles)), (self.rows, range(local_tiles, tiles))]
        self.parts = [(start, js) for start, js in self.parts if len(js)]


def band_of(key_tile, query_tile):
    return jnp.clip(key_tile - query_tile, -2, 2) + 2


def tile_lanes():
    first_half = lax.broadcasted_iota(jnp.int32, (T, 2 * HEAD), 1) < HEAD
    place = lax.broadcasted_iota(jnp.int32, (T, T), 1)
    return first_half, place


def tile_rows(i):
    return pl.ds(pl.multiple_of(i * T, T), T)


def attend_tile(shape, i, is_cont, live, base, q, k, v, bias, out, norm):
    first_half, place = tile_lanes()
    rows = tile_rows(i)
    queries = q[rows, :]
    query_tile = shape.tiles if is_cont else base + i
    mixed = []
    for h in range(2):
        mine = first_half if h == 0 else ~first_half
        masked = jnp.where(mine, queries, jnp.zeros_like(queries))
        logits = []
        for start, js in shape.parts:
            scores = nt(masked, k[start : start + len(js) * T, :])
            for at, j in enumerate(js):
                band = band_of(lax.rem(base + j, shape.tiles), query_tile)
                logits.append(scores[:, at * T : (at + 1) * T] + bias[h, band])
        if is_cont:
            own = nt(masked, k[rows, :]) + bias[h, 2]
            logits.append(jnp.where(place < live[0, i - shape.local_tiles], own, NEGATIVE))
        top = jnp.max(functools.reduce(jnp.maximum, logits), axis=1, keepdims=True)
        weights = [jnp.exp(part - top) for part in logits]
        total = jnp.sum(functools.reduce(jnp.add, weights), axis=1, keepdims=True)
        inverse = 1.0 / total
        probs = [(weight * inverse).astype(BF) for weight in weights]
        result = None
        for start, js in shape.parts:
            left = jnp.concatenate([probs[j] for j in js], axis=1)
            term = nn(left, v[start : start + len(js) * T, :])
            result = term if result is None else result + term
        if is_cont:
            result = result + nn(probs[shape.tiles], v[rows, :])
        mixed.append(result)
        norm[h, rows, :] = top + jnp.log(total)
    out[rows, :] = jnp.where(first_half, mixed[0], mixed[1]).astype(BF)


def for_tiles(shape, conts, action):
    first, last = (shape.local_tiles, shape.local_tiles + shape.conts) if conts else (0, shape.local_tiles)

    def one(i, carry):
        action(i, conts)
        return carry

    lax.fori_loop(first, last, one, 0)


def attend_kernel(shape, live, base, q, k, v, bias, out, norm):
    for conts in (False, True):
        for_tiles(
            shape,
            conts,
            lambda i, c: attend_tile(shape, i, c, live, base[0], q, k, v, bias, out, norm),
        )


def pair_block(n):
    return pl.BlockSpec((n, 2 * HEAD), lambda h, *_: (0, h))


def attend(q, k, v, bias, live, base, shape):
    rows, width = q.shape
    pairs = width // (2 * HEAD)
    return pl.pallas_call(
        functools.partial(attend_kernel, shape),
        grid_spec=pltpu.PrefetchScalarGridSpec(
            num_scalar_prefetch=2,
            grid=(pairs,),
            in_specs=[
                pair_block(rows),
                pair_block(shape.keys),
                pair_block(shape.keys),
                pl.BlockSpec((2, BANDS, T, T), lambda h, *_: (h, 0, 0, 0)),
            ],
            out_specs=[pair_block(rows), pl.BlockSpec((2, rows, 1), lambda h, *_: (h, 0, 0))],
        ),
        out_shape=[
            jax.ShapeDtypeStruct((rows, width), BF),
            jax.ShapeDtypeStruct((2 * pairs, rows, 1), F32),
        ],
        compiler_params=pltpu.CompilerParams(vmem_limit_bytes=VMEM_LIMIT),
    )(live, base, q, k, v, bias)


def attend_back_tile(
    shape, i, is_cont, live, base, q, k, v, bias, grad, out, norm, d_q, d_bias, k_sum, v_sum
):
    first_half, place = tile_lanes()
    rows = tile_rows(i)
    queries = q[rows, :]
    grads = grad[rows, :]
    query_tile = shape.tiles if is_cont else base + i
    overlap = grads.astype(F32) * out[rows, :].astype(F32)
    mixed = []
    for h in range(2):
        mine = first_half if h == 0 else ~first_half
        masked = jnp.where(mine, queries, jnp.zeros_like(queries))
        masked_grad = jnp.where(mine, grads, jnp.zeros_like(grads))
        inner = jnp.sum(jnp.where(mine, overlap, 0.0), axis=1, keepdims=True)
        log_norm = norm[h, rows, :]

        def piece(keys, bands, allowed):
            scores = nt(masked, k[keys, :])
            d_probs = nt(masked_grad, v[keys, :])
            probs_low, scores_low = [], []
            for at, band in enumerate(bands):
                cols = slice(at * T, (at + 1) * T)
                logits = scores[:, cols] + bias[h, band]
                if allowed is not None:
                    logits = jnp.where(allowed, logits, NEGATIVE)
                probs = jnp.exp(logits - log_norm)
                d_scores = probs * (d_probs[:, cols] - inner)
                d_bias[h, band] += d_scores
                probs_low.append(probs.astype(BF))
                scores_low.append(d_scores.astype(BF))
            probs_low = jnp.concatenate(probs_low, axis=1)
            scores_low = jnp.concatenate(scores_low, axis=1)
            v_sum[keys, :] += tn(probs_low, masked_grad)
            k_sum[keys, :] += tn(scores_low, masked)
            return nn(scores_low, k[keys, :])

        result = None
        for start, js in shape.parts:
            bands = [band_of(lax.rem(base + j, shape.tiles), query_tile) for j in js]
            term = piece(pl.ds(start, len(js) * T), bands, None)
            result = term if result is None else result + term
        if is_cont:
            result = result + piece(rows, [2], place < live[0, i - shape.local_tiles])
        mixed.append(result)
    d_q[rows, :] = jnp.where(first_half, mixed[0], mixed[1]).astype(BF)


def attend_back_kernel(
    shape, live, base, q, k, v, bias, grad, out, norm, d_q, d_k, d_v, d_bias, k_sum, v_sum
):
    k_sum[...] = jnp.zeros_like(k_sum)
    v_sum[...] = jnp.zeros_like(v_sum)
    d_bias[...] = jnp.zeros_like(d_bias)
    refs = (q, k, v, bias, grad, out, norm, d_q, d_bias, k_sum, v_sum)
    for conts in (False, True):
        for_tiles(shape, conts, lambda i, c: attend_back_tile(shape, i, c, live, base[0], *refs))
    d_k[...] = k_sum[...].astype(BF)
    d_v[...] = v_sum[...].astype(BF)


def attend_back(q, k, v, bias, grad, out, norm, live, base, shape):
    rows, width = q.shape
    pairs = width // (2 * HEAD)
    keys = shape.keys
    bands = pl.BlockSpec((2, BANDS, T, T), lambda h, *_: (h, 0, 0, 0))
    return pl.pallas_call(
        functools.partial(attend_back_kernel, shape),
        grid_spec=pltpu.PrefetchScalarGridSpec(
            num_scalar_prefetch=2,
            grid=(pairs,),
            in_specs=[
                pair_block(rows),
                pair_block(keys),
                pair_block(keys),
                bands,
                pair_block(rows),
                pair_block(rows),
                pl.BlockSpec((2, rows, 1), lambda h, *_: (h, 0, 0)),
            ],
            out_specs=[pair_block(rows), pair_block(keys), pair_block(keys), bands],
            scratch_shapes=[pltpu.VMEM((keys, 2 * HEAD), F32), pltpu.VMEM((keys, 2 * HEAD), F32)],
        ),
        out_shape=[
            jax.ShapeDtypeStruct((rows, width), BF),
            jax.ShapeDtypeStruct((keys, width), BF),
            jax.ShapeDtypeStruct((keys, width), BF),
            jax.ShapeDtypeStruct((2 * pairs, BANDS, T, T), F32),
        ],
        compiler_params=pltpu.CompilerParams(vmem_limit_bytes=VMEM_LIMIT),
    )(live, base, q, k, v, bias, grad, out, norm)


ORDER = (1, 2, 0, 3)
FIRST_PAIR = 8


def joined_pieces(w_buf, slot, m):
    pieces = [w_buf[slot, j // 3, j % 3] for j in (2 * m, 2 * m + 1)]
    return jnp.concatenate([piece.reshape(-1, T) for piece in pieces], axis=1)


def front_kernel(zs, xs, shape, early, live, *refs):
    (prompt_x, cont_x, own_gain, *weights) = refs[:10]
    table = refs[10]
    (whole, own_out, x_out, normed_out, kv_out, bias_out) = refs[11:17]
    (q, attended, norm, middle, normed_two, gains) = refs[17:23]
    (x, normed, kv, bias, held, w_buf, gain_whole) = refs[23:30]
    (local, kv_sems, send, recv, gain_send, gain_recv) = refs[30:36]
    place = Place(zs, xs)
    step = pl.program_id(0)
    rows, width = x.shape
    prompt = shape.local_tiles * T
    pairs = q.shape[0]
    size = middle.shape[0]
    blocks = rows // size
    last = FIRST_PAIR + pairs
    count = 4 + early
    feed_weights = weights[4:]
    columns = feed_weights[0].shape[1] // T

    def x_load(i):
        source, part = ((prompt_x, pl.ds(0, prompt)), (cont_x, pl.ds(prompt, rows - prompt)))[i]
        return pltpu.make_async_copy(source, x.at[part], local.at[i])

    def mine_store():
        mine = whole.at[:, :, :, place.z, place.y, place.c * place.xs + place.x]
        return pltpu.make_async_copy(held.at[pl.ds(0, count)], mine, local.at[2])

    feed_own = held.at[pl.ds(4, held.shape[0] - 4)]
    kept = ((feed_own, own_out), (x, x_out), (normed, normed_out), (bias, bias_out), (kv, kv_out))

    def result(i):
        return pltpu.make_async_copy(*kept[i], local.at[3 + i])

    def weight_load(k):
        return pltpu.make_async_copy(whole.at[k], w_buf.at[k % 2], local.at[8 + k])

    @pl.when(step == 0)
    def _():
        place.barrier()
        x_load(0).start()
        x_load(1).start()
        for c, matrix in enumerate(ORDER):
            for j in range(6):
                held[c, j // 3, j % 3] = weights[matrix][:, j * T : (j + 1) * T].astype(BF)
        gain_whole[0, :, :, place.z, place.y, place.c * place.xs + place.x] = own_gain[0]

    Gather(place, own_gain, gain_whole, gain_send, gain_recv).tick(step, 0, 1)
    Gather(place, held, whole, send, recv).tick(step, 0, count)

    @pl.when(step == 0)
    def _():
        def convert(j, carry):
            part = pl.ds(pl.multiple_of(j * T, T), T)
            for i in range(3):
                held[4 + j // 2, j % 2, i] = feed_weights[i][:, part].astype(BF)
            return carry

        lax.fori_loop(0, columns, convert, 0)
        if columns % 2:
            held[4 + columns // 2, 1] = jnp.zeros(held.shape[2:], BF)
        mine_store().start()
        mine_store().wait()
        result(0).start()
        x_load(0).wait()
        x_load(1).wait()
        result(1).start()

    @pl.when(step == 1)
    def _():
        query = lax.broadcasted_iota(jnp.int32, (T, T), 0)
        key = lax.broadcasted_iota(jnp.int32, (T, T), 1)
        half = table.shape[0] // 2
        ids = [bucket_ids(band * T + key - query) for band in (-1, 0, 1)]
        found = (range(1, half), [*range(half), *range(half + 1, 2 * half)], range(half + 1, 2 * half))

        def one(h, carry):
            bias[h, 0] = jnp.full((T, T), table[half - 1, h])
            bias[h, 4] = jnp.full((T, T), table[2 * half - 1, h])
            for band in range(3):
                value = jnp.zeros((T, T), F32)
                for bucket in found[band]:
                    value = jnp.where(ids[band] == bucket, table[bucket, h], value)
                bias[h, 1 + band] = value
            return carry

        lax.fori_loop(0, bias.shape[0], one, 0)

    for k in range(4):

        @pl.when(step == 4 + k)
        def _(k=k):
            weight_load(k).start()

    def by_rows(action):
        def one(i, carry):
            action(pl.ds(pl.multiple_of(i * size, size), size))
            return carry

        lax.fori_loop(0, blocks, one, 0)

    @pl.when(step == 4)
    def _():
        result(3).start()
        eye = lax.broadcasted_iota(jnp.int32, (T, T), 0) == lax.broadcasted_iota(jnp.int32, (T, T), 1)
        for g in range(2):
            column = gain_whole[0, g, 0].reshape(width, T).astype(F32)
            for i in range(width // T):
                cols = slice(i * T, (i + 1) * T)
                gains[g, :, cols] = jnp.sum(jnp.where(eye, column[cols], 0.0), axis=0, keepdims=True)

        def norm_rows(part):
            values = x[part, :].astype(F32)
            scale = lax.rsqrt(jnp.mean(values * values, axis=-1, keepdims=True) + EPS)
            normed[part, :] = (values * scale * gains[0]).astype(BF)

        by_rows(norm_rows)
        result(2).start()

    def project(slot, target):
        for m in range(pairs // 2):
            right = joined_pieces(w_buf, slot, m)

            def rows_of_product(part, m=m, right=right):
                product = nn(normed[part, :], right).astype(BF)
                target[2 * m, part, :] = product[:, :T]
                target[2 * m + 1, part, :] = product[:, T:]

            by_rows(rows_of_product)

    def kv_send(side, p):
        src = kv.at[side, p, pl.ds(0, prompt)]
        dst = kv.at[side, p, pl.ds(rows, prompt)]
        peer = place.device(x=1 - place.x)
        return remote(src, dst, kv_sems.at[0, side, p], kv_sems.at[1, side, p], peer)

    for k in range(3):

        @pl.when(step == 5 + k)
        def _(k=k):
            weight_load(k).wait()
            project(k % 2, kv.at[k] if k < 2 else q)
            if k < 2:
                for p in range(pairs):
                    kv_send(k, p).start()

    @pl.when(step == FIRST_PAIR)
    def _():
        weight_load(3).wait()

    @pl.when((step >= FIRST_PAIR) & (step < last))
    def _():
        p = step - FIRST_PAIR
        for side in range(2):
            kv_send(side, p).wait_recv()
            kv_send(side, p).wait_send()
        base = place.x * shape.local_tiles
        inputs = (q.at[p], kv.at[0, p], kv.at[1, p], bias.at[pl.ds(2 * p, 2)], attended.at[p], norm)
        for conts in (False, True):
            for_tiles(shape, conts, lambda i, c: attend_tile(shape, i, c, live, base, *inputs))

    @pl.when(step == last)
    def _():
        result(4).start()

    @pl.when(step >= last)
    def _():
        part = pl.ds(pl.multiple_of((step - last) * size, size), size)
        branch = None
        for m in range(pairs // 2):
            left = jnp.concatenate([attended[2 * m + e, part, :] for e in range(2)], axis=1)
            term = nt(left, joined_pieces(w_buf, 1, m))
            branch = term if branch is None else branch + term
        total = x[part, :].astype(F32) + branch
        middle[...] = total
        scale = lax.rsqrt(jnp.mean(total * total, axis=-1, keepdims=True) + EPS)
        normed_two[...] = (total * scale * gains[1]).astype(BF)

    @pl.when(step == last + blocks - 1)
    def _():
        for i in range(len(kept)):
            result(i).wait()


def front(prompt_x, cont_x, own_gain, weights, table, live, shape, sizes, early, collective_id):
    grp, seq = sizes
    rows, width = shape.rows, prompt_x.shape[1]
    shard, inner = weights[0].shape
    feed_columns = weights[4].shape[1] // T
    pairs, keys, heads = inner // (2 * HEAD), shape.keys, table.shape[1]
    assert pairs == 6 and table.shape[0] == 32 and keys - rows == prompt_x.shape[0]
    zs = grp // (Y * C)
    chunks = 4 + (feed_columns + 1) // 2
    count = 4 + early
    own = (2, 3, shard, T)
    tile = (2, 3, zs, Y, C * seq, shard, T)
    size = min(rows, 256)
    blocks = rows // size
    last = FIRST_PAIR + pairs
    steps = last + blocks
    assert count + 4 <= steps and count <= chunks
    full = lambda *dims: pl.BlockSpec(
        dims, lambda s, *_: (0,) * len(dims), pipeline_mode=pl.Buffered(1)
    )
    by_rows = pl.BlockSpec((size, width), lambda s, *_: (jnp.clip(s - last, 0, blocks - 1), 0))
    anywhere = pl.BlockSpec(memory_space=pl.ANY)
    sems = lambda *dims: pltpu.SemaphoreType.DMA(dims)
    out = jax.ShapeDtypeStruct
    return pl.pallas_call(
        functools.partial(front_kernel, zs, seq, shape, early),
        grid_spec=pltpu.PrefetchScalarGridSpec(
            num_scalar_prefetch=1,
            grid=(steps,),
            in_specs=[anywhere, anywhere, full(*own_gain.shape)]
            + [full(*w.shape) for w in weights]
            + [pl.BlockSpec(memory_space=pltpu.SMEM)],
            out_specs=[anywhere] * 6
            + [
                full(pairs, rows, 2 * HEAD),
                full(pairs, rows, 2 * HEAD),
                pl.BlockSpec(
                    (2, rows, 1), lambda s, *_: (jnp.clip(s - FIRST_PAIR, 0, pairs - 1), 0, 0)
                ),
                by_rows,
                by_rows,
                full(2, 1, width),
            ],
            scratch_shapes=[
                pltpu.VMEM((rows, width), BF),
                pltpu.VMEM((rows, width), BF),
                pltpu.VMEM((2, pairs, keys, 2 * HEAD), BF),
                pltpu.VMEM((heads, BANDS, T, T), F32),
                pltpu.VMEM((chunks, *own), BF),
                pltpu.VMEM((2, *tile), BF),
                pltpu.VMEM((1, 2, 1, zs, Y, C * seq, shard, T), BF),
                sems(12),
                sems(2, 2, pairs),
                sems(count, 2, zs + 2),
                sems(count, 2, zs + 2),
                sems(1, 2, zs + 2),
                sems(1, 2, zs + 2),
            ],
        ),
        out_shape=[
            out((count, *tile), BF),
            out((chunks - 4, *own), BF),
            out((rows, width), BF),
            out((rows, width), BF),
            out((2, pairs, keys, 2 * HEAD), BF),
            out((heads, BANDS, T, T), F32),
            out((pairs, rows, 2 * HEAD), BF),
            out((pairs, rows, 2 * HEAD), BF),
            out((2 * pairs, rows, 1), F32),
            out((rows, width), F32),
            out((rows, width), BF),
            out((2, 1, width), F32),
        ],
        compiler_params=pltpu.CompilerParams(
            collective_id=collective_id, has_side_effects=True, vmem_limit_bytes=VMEM_LIMIT
        ),
    )(live, prompt_x, cont_x, own_gain, *weights, table)


SPAN = 4 * T
VECTOR_ROWS = 8


def turned(tile):
    row = lax.broadcasted_iota(jnp.int32, tile.shape, 0)
    for bit in range(7):
        moved = pltpu.roll(tile, SPAN - (1 << bit), 1)
        tile = jnp.where((row >> bit) & 1 == 1, moved, tile)
    return tile


def band_sums(d_bias, h):
    near = jnp.concatenate([d_bias[h, 1], d_bias[h, 2], d_bias[h, 3]], axis=1)
    near = jnp.concatenate([near, jnp.zeros((T, T), F32)], axis=1)
    diagonal = jnp.sum(turned(near), axis=0, keepdims=True)
    rows = [diagonal[:, i * T : (i + 1) * T] for i in range(4)]
    rows += [jnp.sum(d_bias[h, band], axis=0, keepdims=True) for band in (0, 4)]
    return jnp.concatenate(rows + [jnp.zeros((2, T), F32)], axis=0)


def rows_of(vector):
    return [vector[:, i * T : (i + 1) * T] for i in range(vector.shape[1] // T)]


class Combine:
    def __init__(self, place, total, arrived, send, recv):
        self.p, self.total, self.arrived, self.send, self.recv = place, total, arrived, send, recv

    def partners(self):
        p = self.p
        found = [p.device(c=1 - p.c), p.device(x=1 - p.x), p.device(y=1 - p.y)]
        bit = 1
        while bit < p.zs:
            found.append(p.device(z=p.z + bit - 2 * bit * ((p.z // bit) % 2)))
            bit *= 2
        return found

    def copy(self, i):
        return remote(
            self.total.at[i],
            self.arrived.at[i],
            self.send.at[i],
            self.recv.at[i],
            self.partners()[i],
        )

    def start(self, i):
        self.copy(i).start()

    def finish(self, i):
        self.copy(i).wait_recv()
        self.copy(i).wait_send()
        self.total[i + 1] = self.total[i] + self.arrived[i]


def back_kernel(zs, xs, shape, width, kept, live, *refs):
    q, k, v, bias, grad, out, norm, attended, branch_hbm, normed_hbm, parts, weights_hbm = refs[:12]
    d_middle, x_low, gain, d_gain_two = refs[12:16]
    d_x, sums, vector_out = refs[16:19]
    (stage, turn_buf, d_q, d_kv, back_kv, k_sum, v_sum, d_bias) = refs[19:27]
    (w_buf, held, vector, total, arrived, gain_sum) = refs[27:33]
    (local, loads, kv_sems, both_sems) = refs[33:37]
    bufs, scatter_sems = refs[37:44], refs[44:46]
    place = Place(zs, xs)
    step = pl.program_id(0)
    rows, keys = shape.rows, shape.keys
    prompt = shape.local_tiles * T
    pairs = d_q.shape[0]
    last = 2 * pairs
    turns = rows // T
    first_kept, end_kept = kept
    fed = parts.shape[0] - (end_kept - first_kept)
    group_two = last - 1
    count = fed + 4
    blocks = rows // d_x.shape[0]

    def stage_load(source):
        return pltpu.make_async_copy(source, stage, local.at[0])

    def weights_load(i):
        return pltpu.make_async_copy(weights_hbm.at[(2, 0, 1)[i]], w_buf.at[i], local.at[1 + i])

    def turn():
        def one(i, carry):
            part = tile_rows(i)
            turn_buf[:, part] = stage[part, :].T
            return carry

        lax.fori_loop(0, turns, one, 0)

    @pl.when(step == 0)
    def _():
        stage_load(branch_hbm).start()
        place.barrier()
        for i in range(3):
            weights_load(i).start()
        stage_load(branch_hbm).wait()
        turn()
        stage_load(normed_hbm).start()

    engine = Scatter(place, bufs, *scatter_sems, sums)

    def due(offset, action):
        at = step - offset
        chunk = jnp.where(at < group_two, at, at - group_two + fed)
        early = (at >= 0) & (at < fed)
        late = (at >= group_two) & (at < group_two + 4)

        @pl.when(early | late)
        def _():
            action(chunk)

    def part_load(c):
        j = jnp.where(c < first_kept, c, c + end_kept - first_kept)
        return pltpu.make_async_copy(parts.at[j], held.at[c % 3], loads.at[c % 3])

    def first(c):
        @pl.when(c < fed)
        def _():
            part_load(c).wait()

        engine.start_first(c, held.at[c % 3])

    due(5, engine.finish)
    due(4, engine.start_fourth)
    due(3, engine.start_third)
    due(2, lambda c: engine.start_second(c, held.at[c % 3]))
    due(1, first)

    @pl.when(step < fed)
    def _():
        part_load(step).start()

    def kv_send(p):
        src = d_kv.at[p, :, pl.ds(rows, keys - rows)]
        peer = place.device(x=1 - place.x)
        return remote(src, back_kv.at[p], kv_sems.at[0, p], kv_sems.at[1, p], peer)

    @pl.when((step >= 2) & (step <= last) & (step % 2 == 0))
    def _():
        kv_send(step // 2 - 1).start()

    @pl.when(step < last)
    def _():
        p = step // 2
        half = step % 2

        @pl.when(half == 0)
        def _():
            k_sum[...] = jnp.zeros_like(k_sum)
            v_sum[...] = jnp.zeros_like(v_sum)
            d_bias[...] = jnp.zeros_like(d_bias)

        inputs = (q, k, v, bias, grad, out, norm, d_q.at[p], d_bias, k_sum, v_sum)
        base = place.x * shape.local_tiles
        action = lambda i, c: attend_back_tile(shape, i, c, live, base, *inputs)

        @pl.when(half == 0)
        def _():
            for_tiles(shape, False, action)

        @pl.when(half == 1)
        def _():
            for_tiles(shape, True, action)
            d_kv[p, 0] = k_sum[...].astype(BF)
            d_kv[p, 1] = v_sum[...].astype(BF)
            for h in range(2):
                vector[2 * p + h] = band_sums(d_bias, h)

    def produce(c, right):
        slot = c % 3
        for m in range(3):
            operand = right(m)

            def one(z, carry, m=m, operand=operand):
                block = turn_buf.shape[0] // zs
                part = pl.ds(pl.multiple_of(z * block, block), block)
                result = nn(turn_buf[part, :], operand).astype(BF)
                for side in range(2):
                    index = 2 * m + side
                    value = result[:, side * T : (side + 1) * T]
                    held[slot, index // 3, index % 3, z] = value.reshape(held.shape[4:])
                return carry

            lax.fori_loop(0, zs, one, 0)

    @pl.when(step == last - 1)
    def _():
        produce(fed, lambda m: jnp.concatenate([attended[2 * m], attended[2 * m + 1]], axis=1))

    @pl.when(step == last)
    def _():
        stage_load(normed_hbm).wait()
        turn()
        produce(fed + 1, lambda m: jnp.concatenate([d_q[2 * m], d_q[2 * m + 1]], axis=1))

        def join(p, carry):
            kv_send(p).wait_recv()
            kv_send(p).wait_send()
            for side in range(2):
                own = d_kv[p, side, 0:prompt, :].astype(F32)
                d_kv[p, side, 0:prompt, :] = (own + back_kv[p, side].astype(F32)).astype(BF)
            return carry

        lax.fori_loop(0, pairs, join, 0)
        for i in range(3):
            weights_load(i).wait()
        gain_sum[...] = jnp.zeros_like(gain_sum)

    for side in range(2):

        @pl.when(step == last + 1 + side)
        def _(side=side):
            pick = lambda p: d_kv[p, side, 0:rows, :]
            produce(fed + 2 + side, lambda m: jnp.concatenate([pick(2 * m), pick(2 * m + 1)], axis=1))

    @pl.when((step >= last) & (step < last + blocks))
    def _():
        size = d_x.shape[0]
        part = pl.ds(pl.multiple_of((step - last) * size, size), size)
        d_normed = None
        for i in range(3):
            for m in range(pairs // 2):
                if i == 0:
                    left = [d_q[2 * m + e, part, :] for e in range(2)]
                else:
                    left = [d_kv[2 * m + e, i - 1, part, :] for e in range(2)]
                pieces = [2 * m, 2 * m + 1]
                right = [w_buf[i, j // 3, j % 3].reshape(width, T) for j in pieces]
                term = nt(jnp.concatenate(left, axis=1), jnp.concatenate(right, axis=1))
                d_normed = term if d_normed is None else d_normed + term
        x = x_low[...].astype(F32)
        scale = lax.rsqrt(jnp.mean(x * x, axis=-1, keepdims=True) + EPS)
        unit = x * scale
        gain_sum[...] += jnp.sum(d_normed * unit, axis=0, keepdims=True)
        d_unit = d_normed * gain[...]
        inner = jnp.mean(d_unit * unit, axis=-1, keepdims=True)
        d_x[...] = (d_middle[...] + scale * (d_unit - unit * inner)).astype(BF)

    mix = Combine(place, total, arrived, both_sems.at[0], both_sems.at[1])
    start = last + blocks
    stages = total.shape[0] - 1
    tiles = 2 * pairs

    @pl.when(step == start)
    def _():
        total[0, 0:tiles] = vector[...]
        both = rows_of(gain_sum[...]) + rows_of(d_gain_two[...])
        for i in range(len(both) // VECTOR_ROWS):
            group = both[i * VECTOR_ROWS : (i + 1) * VECTOR_ROWS]
            total[0, tiles + i] = jnp.concatenate(group, axis=0)

    for i in range(stages + 1):

        @pl.when(step == start + 1 + i)
        def _(i=i):
            if i > 0:
                mix.finish(i - 1)
            if i < stages:
                mix.start(i)
            else:
                vector_out[...] = total[stages]


def back(q, kv, bias, grad, out, norm, branch, normed, parts, weights, d_middle, x_low, gain,
         d_gain_two, live, shape, sizes, kept, collective_id):
    grp, seq = sizes
    rows, width = x_low.shape
    pairs = q.shape[0]
    zs = grp // (Y * C)
    keys = shape.keys
    chunks, _, n, _, _, _, shard, lanes = parts.shape
    count = chunks - (kept[1] - kept[0]) + 4
    assert chunks - (kept[1] - kept[0]) <= 2 * pairs - 1
    assert (pairs, n) == (6, 3) and 2 * width // T % VECTOR_ROWS == 0
    last = 2 * pairs
    size = min(rows, 256)
    blocks = rows // size
    tile = (2, n, zs, Y, C * seq, shard, lanes)
    stages = 3 + (zs - 1).bit_length()
    steps = last + blocks + stages + 2
    vector = (2 * pairs + 2 * width // T // VECTOR_ROWS, VECTOR_ROWS, T)
    pair = lambda s: jnp.minimum(s // 2, pairs - 1)
    by_pair = lambda rows_: pl.BlockSpec((rows_, 2 * HEAD), lambda s, *_: (0, pair(s)))
    in_pair = pl.BlockSpec((None, rows, 2 * HEAD), lambda s, *_: (pair(s), 0, 0))
    of_keys = lambda side: pl.BlockSpec(
        (None, None, keys, 2 * HEAD), lambda s, *_: (side, pair(s), 0, 0)
    )
    row_block = lambda s: jnp.clip(s - last, 0, blocks - 1)
    by_rows = pl.BlockSpec((size, width), lambda s, *_: (row_block(s), 0))
    full = lambda *dims: pl.BlockSpec(
        dims, lambda s, *_: (0,) * len(dims), pipeline_mode=pl.Buffered(1)
    )
    anywhere = pl.BlockSpec(memory_space=pl.ANY)
    sems = lambda *dims: pltpu.SemaphoreType.DMA(dims)
    return pl.pallas_call(
        functools.partial(back_kernel, zs, seq, shape, width, kept),
        grid_spec=pltpu.PrefetchScalarGridSpec(
            num_scalar_prefetch=1,
            grid=(steps,),
            in_specs=[
                in_pair,
                of_keys(0),
                of_keys(1),
                pl.BlockSpec((2, BANDS, T, T), lambda s, *_: (pair(s), 0, 0, 0)),
                by_pair(rows),
                in_pair,
                pl.BlockSpec((2, rows, 1), lambda s, *_: (pair(s), 0, 0)),
                full(pairs, rows, 2 * HEAD),
                anywhere,
                anywhere,
                anywhere,
                anywhere,
                by_rows,
                by_rows,
                full(1, width),
                full(1, width),
            ],
            out_specs=[by_rows, full(count, 2, n, shard, lanes), full(*vector)],
            scratch_shapes=[
                pltpu.VMEM((rows, width), BF),
                pltpu.VMEM((width, rows), BF),
                pltpu.VMEM((pairs, rows, 2 * HEAD), BF),
                pltpu.VMEM((pairs, 2, keys, 2 * HEAD), BF),
                pltpu.VMEM((pairs, 2, keys - rows, 2 * HEAD), BF),
                pltpu.VMEM((keys, 2 * HEAD), F32),
                pltpu.VMEM((keys, 2 * HEAD), F32),
                pltpu.VMEM((2, BANDS, T, T), F32),
                pltpu.VMEM((3, *tile), BF),
                pltpu.VMEM((3, *tile), BF),
                pltpu.VMEM((2 * pairs, VECTOR_ROWS, T), F32),
                pltpu.VMEM((stages + 1, *vector), F32),
                pltpu.VMEM((stages, *vector), F32),
                pltpu.VMEM((1, width), F32),
                sems(4),
                sems(3),
                sems(2, pairs),
                sems(2, stages),
            ]
            + scatter_buffers(n, zs, seq, shard, lanes)
            + [sems(2, 2, zs + 2), sems(2, 2, zs + 2)],
        ),
        out_shape=[
            jax.ShapeDtypeStruct((rows, width), BF),
            jax.ShapeDtypeStruct((count, 2, n, shard, lanes), F32),
            jax.ShapeDtypeStruct(vector, F32),
        ],
        compiler_params=pltpu.CompilerParams(
            collective_id=collective_id, has_side_effects=True, vmem_limit_bytes=VMEM_LIMIT
        ),
    )(live, q, kv, kv, bias, grad, out, norm, out, branch, normed, parts, weights, d_middle,
      x_low, gain, d_gain_two)


GELU_SCALE = 0.7978845608028654
GELU_CUBIC = 0.044715


def gelu_and_slope(a):
    square = a * a
    tanh = jnp.tanh(GELU_SCALE * a * (1.0 + GELU_CUBIC * square))
    half = 0.5 * (1.0 + tanh)
    slope = half + 0.5 * a * (1.0 - tanh * tanh) * (
        GELU_SCALE * (1.0 + 3.0 * GELU_CUBIC * square)
    )
    return a * half, slope


def feed_load(x_hbm, dy_parts, x, x_t, dy, dy_t, sem):
    loads = [pltpu.make_async_copy(x_hbm, x, sem.at[0])]
    start = 0
    for i, part in enumerate(dy_parts):
        target = dy.at[pl.ds(start, part.shape[0])]
        loads.append(pltpu.make_async_copy(part, target, sem.at[1 + i]))
        start += part.shape[0]
    for load in loads:
        load.start()
    for load in loads:
        load.wait()

    def turn(i, carry):
        part = pl.ds(pl.multiple_of(i * T, T), T)
        x_t[:, part] = x[part, :].T
        dy_t[:, part] = dy[part, :].T
        return carry

    lax.fori_loop(0, x.shape[0] // T, turn, 0)


def feed_chunk(read, write, blocks, out, d_x, x, x_t, dy, dy_t, hidden, d_gate, d_up):
    rows, width = x.shape
    row_block = min(rows, 256)
    width_block = width // blocks
    w_gate, w_up, w_down = [jnp.concatenate([read(0, i), read(1, i)], axis=1) for i in range(3)]

    def by_rows(i, carry):
        part = pl.ds(pl.multiple_of(i * row_block, row_block), row_block)
        gate = nn(x[part, :], w_gate)
        up = nn(x[part, :], w_up)
        d_hidden = nn(dy[part, :], w_down)
        active, slope = gelu_and_slope(gate)
        hidden_low = (active * up).astype(BF)
        d_gate_low = (d_hidden * up * slope).astype(BF)
        d_up_low = (d_hidden * active).astype(BF)
        hidden[part, :] = hidden_low
        d_gate[part, :] = d_gate_low
        d_up[part, :] = d_up_low
        out[part, :] += nt(hidden_low, w_down)
        d_x[part, :] += nt(d_gate_low, w_gate) + nt(d_up_low, w_up)
        return carry

    lax.fori_loop(0, rows // row_block, by_rows, 0)

    def by_width(i, carry):
        part = pl.ds(pl.multiple_of(i * width_block, width_block), width_block)
        pairs = ((x_t, d_gate), (x_t, d_up), (dy_t, hidden))
        for index, (left, right) in enumerate(pairs):
            total = nn(left[part, :], right[...]).astype(BF)
            write(0, index, i, total[:, :T])
            write(1, index, i, total[:, T:])
        return carry

    lax.fori_loop(0, blocks, by_width, 0)


def feed_kernel(x_hbm, dy_hbm, weights, out, d_x, grads, x, x_t, dy, dy_t, *rest):
    *work, sem = rest
    width_block = 512

    @pl.when(pl.program_id(0) == 0)
    def _():
        feed_load(x_hbm, [dy_hbm], x, x_t, dy, dy_t, sem)
        out[...] = jnp.zeros_like(out)
        d_x[...] = jnp.zeros_like(d_x)

    def write(half, index, block, value):
        part = pl.ds(pl.multiple_of(block * width_block, width_block), width_block)
        grads[0, half, index, part, :] = value

    read = lambda half, index: weights[0, half, index]
    blocks = x.shape[1] // width_block
    feed_chunk(read, write, blocks, out, d_x, x, x_t, dy, dy_t, *work)


def feed_scratch(rows, width):
    return [
        pltpu.VMEM((rows, width), BF),
        pltpu.VMEM((width, rows), BF),
        pltpu.VMEM((rows, width), BF),
        pltpu.VMEM((width, rows), BF),
        pltpu.VMEM((rows, 2 * T), BF),
        pltpu.VMEM((rows, 2 * T), BF),
        pltpu.VMEM((rows, 2 * T), BF),
        pltpu.SemaphoreType.DMA((3,)),
    ]


def feed(x, dy, weights):
    rows, width = x.shape
    chunks = weights.shape[0]
    chunk = pl.BlockSpec((1, 2, 3, width, T), lambda j: (j, 0, 0, 0, 0))
    whole = pl.BlockSpec((rows, width), lambda j: (0, 0), pipeline_mode=pl.Buffered(1))
    return pl.pallas_call(
        feed_kernel,
        grid=(chunks,),
        in_specs=[pl.BlockSpec(memory_space=pl.ANY)] * 2 + [chunk],
        out_specs=[whole, whole, chunk],
        out_shape=[
            jax.ShapeDtypeStruct((rows, width), F32),
            jax.ShapeDtypeStruct((rows, width), F32),
            jax.ShapeDtypeStruct((chunks, 2, 3, width, T), BF),
        ],
        scratch_shapes=feed_scratch(rows, width),
        compiler_params=pltpu.CompilerParams(vmem_limit_bytes=VMEM_LIMIT),
    )(x, dy, weights)


def feed_moving_kernel(zs, xs, early, kept, *refs):
    x_hbm, dy_one, dy_two, own, ready, out, d_x, whole, parts, sums = refs[:10]
    x, x_t, dy, dy_t, hidden, d_gate, d_up, sem = refs[10:18]
    held, w_buf, g_buf, local = refs[18:22]
    gather_sems, bufs, scatter_sems = refs[22:24], refs[24:31], refs[31:33]
    chunks = own.shape[0]
    place = Place(zs, xs)
    step = pl.program_id(0)
    lag = max(0, 5 - early)
    first_kept, end_kept = kept
    width = x.shape[1]

    @pl.when(step == 0)
    def _():
        place.barrier()

    fetch = Gather(place, own, whole, *gather_sems)
    fetch.tick(step, early, chunks)

    @pl.when(step == 0)
    def _():
        load = pltpu.make_async_copy(own, held, local.at[0])
        load.start()
        load.wait()
        mine = whole.at[:, :, :, place.z, place.y, place.c * place.xs + place.x]
        store = pltpu.make_async_copy(held, mine, local.at[1])
        store.start()
        store.wait()
        feed_load(x_hbm, [dy_one, dy_two], x, x_t, dy, dy_t, sem)
        out[...] = jnp.zeros_like(out)
        d_x[...] = jnp.zeros_like(d_x)

    skipped = ready.shape[0] - early

    def weight_load(j, source, first=0):
        return pltpu.make_async_copy(source.at[first + j], w_buf.at[j % 2], local.at[2 + j % 2])

    def start_load(j):
        if early > 0:

            @pl.when(j < early)
            def _():
                weight_load(j, ready, skipped).start()

        @pl.when(j >= early)
        def _():
            weight_load(j, whole).start()

    def part_store(j):
        return pltpu.make_async_copy(g_buf.at[j % 2], parts.at[j], local.at[4 + j % 2])

    def is_kept(j):
        return (j >= first_kept) & (j < end_kept)

    engine = Scatter(place, bufs, *scatter_sems, sums)
    due = lag + first_kept
    number = end_kept - first_kept
    grads_of = lambda k: g_buf.at[(k + first_kept) % 2]
    staged(step, due + 5, number, engine.finish)
    staged(step, due + 4, number, engine.start_fourth)
    staged(step, due + 3, number, engine.start_third)
    staged(step, due + 2, number, lambda k: engine.start_second(k, grads_of(k)))
    staged(step, due + 1, number, lambda k: engine.start_first(k, grads_of(k)))

    chunk = step - lag
    if lag == 0:

        @pl.when(step == 0)
        def _():
            start_load(0)

    @pl.when((chunk >= (0 if lag == 0 else -1)) & (chunk + 1 < chunks))
    def _():
        start_load(chunk + 1)

    @pl.when((chunk >= 2) & (chunk < chunks + 2) & ~is_kept(chunk - 2))
    def _():
        part_store(chunk - 2).wait()

    @pl.when((chunk >= 0) & (chunk < chunks))
    def _():
        weight_load(chunk, whole).wait()
        slot = chunk % 2

        def read(half, index):
            return w_buf[slot, half, index].reshape(width, T)

        def write(half, index, block, value):
            shape = g_buf.shape[4:]
            g_buf[slot, half, index, block] = value.reshape(shape)

        work = (hidden, d_gate, d_up)
        feed_chunk(read, write, zs, out, d_x, x, x_t, dy, dy_t, *work)

        @pl.when(~is_kept(chunk))
        def _():
            part_store(chunk).start()


def feed_moving(x, dy_one, dy_two, own, ready, sizes, early, kept, collective_id):
    grp, seq = sizes
    rows, width = x.shape
    chunks, _, n, shard, lanes = own.shape
    zs = grp // (Y * C)
    tile = (2, n, zs, Y, C * seq, shard, lanes)
    whole = pl.BlockSpec((rows, width), lambda j: (0, 0), pipeline_mode=pl.Buffered(1))
    number = kept[1] - kept[0]
    sums = pl.BlockSpec(
        (number, 2, n, shard, lanes), lambda j: (0,) * 5, pipeline_mode=pl.Buffered(1)
    )
    lag = max(0, 5 - early)
    steps = lag + max(chunks + 2, kept[1] + 5)
    anywhere = pl.BlockSpec(memory_space=pl.ANY)
    sems = lambda *shape: pltpu.SemaphoreType.DMA(shape)
    return pl.pallas_call(
        functools.partial(feed_moving_kernel, zs, seq, early, kept),
        grid=(steps,),
        in_specs=[anywhere] * 5,
        out_specs=[whole, whole, anywhere, anywhere, sums],
        out_shape=[
            jax.ShapeDtypeStruct((rows, width), F32),
            jax.ShapeDtypeStruct((rows, width), F32),
            jax.ShapeDtypeStruct((chunks, *tile), BF),
            jax.ShapeDtypeStruct((chunks, *tile), BF),
            jax.ShapeDtypeStruct((number, 2, n, shard, lanes), F32),
        ],
        scratch_shapes=feed_scratch(rows, width)
        + [
            pltpu.VMEM(own.shape, BF),
            pltpu.VMEM((2, *tile), BF),
            pltpu.VMEM((2, *tile), BF),
            sems(6),
            sems(chunks, 2, zs + 2),
            sems(chunks, 2, zs + 2),
        ]
        + scatter_buffers(n, zs, seq, shard, lanes)
        + [sems(2, 2, zs + 2), sems(2, 2, zs + 2)],
        compiler_params=pltpu.CompilerParams(
            collective_id=collective_id, has_side_effects=True, vmem_limit_bytes=VMEM_LIMIT
        ),
    )(x, dy_one, dy_two, own, ready)


def rms_scale(values):
    return lax.rsqrt(jnp.mean(values * values, axis=-1, keepdims=True) + EPS)


def norm_back(d_normed, unit, scale, gain):
    d_unit = d_normed * gain
    return scale * (d_unit - unit * jnp.mean(d_unit * unit, axis=-1, keepdims=True))


def pieces_of(matrix):
    rows, columns = matrix.shape
    return jnp.swapaxes(matrix.reshape(rows, columns // T, T), 0, 1)


def joined(pieces):
    count, rows, _ = pieces.shape
    return jnp.swapaxes(pieces, 0, 1).reshape(rows, count * T)


def attention_chunks(matrices):
    flat = jnp.concatenate([pieces_of(m) for m in matrices], axis=0)
    pad = -flat.shape[0] % 6
    flat = jnp.pad(flat, ((0, pad), (0, 0), (0, 0)))
    return flat.reshape(-1, 2, 3, *flat.shape[1:])


def feed_chunks(matrices):
    stacked = jnp.stack([pieces_of(m) for m in matrices], axis=1)
    pad = -stacked.shape[0] % 2
    stacked = jnp.pad(stacked, ((0, pad), (0, 0), (0, 0), (0, 0)))
    return stacked.reshape(-1, 2, *stacked.shape[1:])


def body(sizes, *args):
    (
        prompt_x,
        cont_x,
        cont_len,
        prompt_cot,
        cont_cot,
        norm1_gain,
        q_weight,
        k_weight,
        v_weight,
        o_weight,
        bucket_table,
        norm2_gain,
        gate_weight,
        up_weight,
        down_weight,
    ) = args
    _, local_prompt, width = prompt_x.shape
    conts, cont_rows = cont_x.shape[1], cont_x.shape[2]
    assert prompt_x.shape[0] == 1 and cont_rows == T and local_prompt % T == 0
    seq = sizes[1]
    num_buckets, heads = bucket_table.shape
    inner = q_weight.shape[1]
    assert inner == heads * HEAD
    shard = q_weight.shape[0]
    hidden_width = gate_weight.shape[1]
    local_tiles = local_prompt // T
    tiles = local_tiles * seq
    seq_index = lax.axis_index("seq")

    split = lambda rows: (
        rows[:local_prompt][None],
        rows[local_prompt:].reshape(1, conts, cont_rows, width),
    )
    shape = Shape(tiles, local_tiles, conts)
    count = inner // T
    if can_move(sizes, shard):
        early, kept = 7, (9, 15)
        own_gain = jnp.stack([norm1_gain, norm2_gain])[None, :, None, :, None]
        own_gain = jnp.broadcast_to(own_gain, (1, 2, 1, shard, T)).astype(BF)
        cont_dy = cont_cot[0].reshape(-1, width)
        matrices = (q_weight, k_weight, v_weight, o_weight, gate_weight, up_weight, down_weight)
        (whole, own_feed, x_low, normed_one, kv, bias, queries, attended, log_norm, middle,
         normed_two, gains) = front(
            prompt_x[0], cont_x[0].reshape(-1, width), own_gain, matrices, bucket_table, cont_len,
            shape, sizes, early, 0,
        )
        gain_one, gain_two = gains[0], gains[1]
        scale_two = rms_scale(middle)
        unit_two = middle * scale_two
        out_sum, d_normed_two, _, feed_parts, kept_sums = feed_moving(
            normed_two, prompt_cot[0], cont_dy, own_feed, whole, sizes, early, kept, 1
        )
        final = (middle + out_sum).astype(BF)
        dy = jnp.concatenate([prompt_cot[0], cont_dy], axis=0).astype(F32)
        d_gain_two = jnp.sum(d_normed_two * unit_two, axis=0)
        d_middle = dy + norm_back(d_normed_two, unit_two, scale_two, gain_two)
        d_branch = d_middle.astype(BF)
        o_full = joined(whole[3].reshape(-1, width, T))
        d_attended = nn(d_branch, o_full).astype(BF)
        d_x, sums, vector = back(
            queries, kv, bias, d_attended, attended, log_norm, d_branch, normed_one, feed_parts,
            whole, d_middle, x_low, gain_one, d_gain_two[None], cont_len, shape, sizes, kept, 2,
        )
        fed = sums.shape[0] - 4
        feed_sums = jnp.concatenate([sums[: kept[0]], kept_sums, sums[kept[0] : fed]], axis=0)
        attention_sums = jnp.concatenate([sums[fed + 1 :], sums[fed : fed + 1]], axis=0)
        attention_sums = attention_sums.reshape(-1, shard, T)
        near = vector[:heads, :4].reshape(heads, SPAN)
        far = jnp.sum(vector[:heads, 4:6], axis=-1)
        relative = (jnp.arange(SPAN) + T) % SPAN - 2 * T
        ids = jnp.concatenate([bucket_ids(relative), bucket_ids(jnp.array([-T, T]))])
        hot = (ids[:, None] == jnp.arange(num_buckets)).astype(F32)
        both = jnp.concatenate([near, far], axis=1)
        table_grad = jnp.einsum("hr,rb->bh", both, hot, precision=lax.Precision.HIGHEST)
        gain_grads = vector[heads:].reshape(2, sizes[0] * seq, shard)
        me = lax.axis_index("grp") * seq + seq_index
        norm1_grad, norm2_grad = lax.dynamic_index_in_dim(gain_grads, me, 1, keepdims=False)
    else:
        x_low = jnp.concatenate([prompt_x[0], cont_x[0].reshape(-1, width)], axis=0)
        dy_low = jnp.concatenate([prompt_cot[0], cont_cot[0].reshape(-1, width)], axis=0)
        x = x_low.astype(F32)
        dy = dy_low.astype(F32)
        lanes = jnp.zeros((shard, T - 2), F32)
        gains = jnp.concatenate([norm1_gain[:, None], norm2_gain[:, None], lanes], axis=1)
        own_attention = attention_chunks([q_weight, k_weight, v_weight, o_weight, gains]).astype(BF)
        own_feed = feed_chunks([gate_weight, up_weight, down_weight]).astype(BF)
        attention_whole = gather(own_attention, sizes)
        flat = attention_whole.reshape(-1, width, T)
        q_full, k_full, v_full, o_full = [
            joined(flat[i * count : (i + 1) * count]) for i in range(4)
        ]
        gain_one = flat[4 * count, :, 0].astype(F32)
        gain_two = flat[4 * count, :, 1].astype(F32)
        scale_one = rms_scale(x)
        unit_one = x * scale_one
        normed_one = (unit_one * gain_one).astype(BF)
        kv = nn(normed_one, jnp.concatenate([k_full, v_full], axis=1)).astype(BF)
        queries = nn(normed_one, q_full).astype(BF)
        gathered = lax.all_gather(kv[:local_prompt], "seq", axis=0, tiled=True)
        others = jnp.roll(gathered, -seq_index * local_prompt, axis=0)[local_prompt:]
        every = jnp.concatenate([kv, others], axis=0)
        keys, values = every[:, :inner], every[:, inner:]
        base = (seq_index * local_tiles).reshape(1).astype(jnp.int32)
        one_hot = band_one_hot(num_buckets)
        bias = jnp.einsum("cqkb,bh->hcqk", one_hot, bucket_table, precision=lax.Precision.HIGHEST)
        attended, log_norm = attend(queries, keys, values, bias, cont_len, base, shape)
        middle = x + nt(attended, o_full)
        scale_two = rms_scale(middle)
        unit_two = middle * scale_two
        normed_two = (unit_two * gain_two).astype(BF)
        out_sum, d_normed_two, feed_grads = feed(normed_two, dy_low, gather(own_feed, sizes))
        feed_sums = scatter(feed_grads)
        final = (middle + out_sum).astype(BF)
        d_gain_two = jnp.sum(d_normed_two * unit_two, axis=0)
        d_middle = dy + norm_back(d_normed_two, unit_two, scale_two, gain_two)
        d_branch = d_middle.astype(BF)
        d_attended = nn(d_branch, o_full).astype(BF)
        d_o = tn(d_branch, attended)
        d_queries, d_keys, d_values, d_bias = attend_back(
            queries, keys, values, bias, d_attended, attended, log_norm, cont_len, base, shape
        )
        d_table = jnp.einsum("hcqk,cqkb->bh", d_bias, one_hot, precision=lax.Precision.HIGHEST)
        d_kv = jnp.concatenate([d_keys, d_values], axis=1)
        prompt_parts = jnp.concatenate([d_kv[:local_prompt], d_kv[shape.rows :]], axis=0)
        prompt_parts = jnp.roll(prompt_parts, seq_index * local_prompt, axis=0)
        d_prompt = lax.psum_scatter(prompt_parts, "seq", scatter_dimension=0, tiled=True)
        d_kv = jnp.concatenate([d_prompt, d_kv[local_prompt : shape.rows]], axis=0)
        d_normed_one = nt(d_queries, q_full) + nt(d_kv, jnp.concatenate([k_full, v_full], axis=1))
        d_q = tn(normed_one, d_queries)
        d_kv_weight = tn(normed_one, d_kv)
        d_gain_one = jnp.sum(d_normed_one * unit_one, axis=0)
        d_x = d_middle + norm_back(d_normed_one, unit_one, scale_one, gain_one)
        d_x = d_x.astype(BF)
        attention_parts = attention_chunks([d_q, d_kv_weight, d_o]).astype(BF)
        attention_sums = scatter(attention_parts).reshape(-1, shard, T)
        norm1_grad = lax.psum_scatter(d_gain_one, ("grp", "seq"), scatter_dimension=0, tiled=True)
        norm2_grad = lax.psum_scatter(d_gain_two, ("grp", "seq"), scatter_dimension=0, tiled=True)
        table_grad = lax.psum(d_table, ("grp", "seq"))
    feed_sums = feed_sums.reshape(-1, 3, shard, T)[: hidden_width // T]
    gate_grad, up_grad, down_grad = [joined(feed_sums[:, i]) for i in range(3)]
    q_grad, k_grad, v_grad, o_grad = [
        joined(attention_sums[i * count : (i + 1) * count]) for i in range(4)
    ]
    return (
        *split(final),
        *split(d_x),
        norm1_grad,
        q_grad,
        k_grad,
        v_grad,
        o_grad,
        table_grad,
        norm2_grad,
        gate_grad,
        up_grad,
        down_grad,
    )


def solution(mesh):
    sizes = (mesh.shape["grp"], mesh.shape["seq"])
    rows = P("grp", "seq", None)
    conts = P("grp", "seq", None, None)
    shard = P(("grp", "seq"), None)
    gain = P(("grp", "seq"))
    in_specs = (rows, conts, P("grp", "seq"), rows, conts, gain, shard, shard, shard, shard)
    in_specs += (P(), gain, shard, shard, shard)
    out_specs = (rows, conts, rows, conts, gain, shard, shard, shard, shard, P(), gain)
    out_specs += (shard, shard, shard)
    return jax.shard_map(
        functools.partial(body, sizes),
        mesh=mesh,
        in_specs=in_specs,
        out_specs=out_specs,
        check_vma=False,
    )
```

```python
import functools

import jax
import jax.numpy as jnp
from jax import lax
from jax.experimental import pallas as pl
from jax.experimental.pallas import tpu as pltpu
from jax.sharding import PartitionSpec as P

EPS = 1e-06
LIMITS = (8, 12, 16, 23, 32, 46, 64, 91)
NEGATIVE = -1e30
MESH = pl.DeviceIdType.MESH
T = 128
HEAD = 64
BANDS = 5
BF = jnp.bfloat16
F32 = jnp.float32
VMEM_LIMIT = 63 * 2**20
Y = 2
C = 2


def nn(left, right):
    return jnp.dot(left, right, preferred_element_type=F32)


def nt(left, right):
    return lax.dot_general(left, right, (((1,), (1,)), ((), ())), preferred_element_type=F32)


def tn(left, right):
    return lax.dot_general(left, right, (((0,), (0,)), ((), ())), preferred_element_type=F32)


def bucket_ids(relative):
    distance = jnp.abs(relative)
    coarse = 7 + sum(((distance >= boundary).astype(jnp.int32) for boundary in LIMITS))
    return jnp.where(distance < 8, distance, coarse) + 16 * (relative > 0).astype(jnp.int32)


def band_one_hot(num_buckets):
    band = jnp.arange(BANDS)[:, None, None] - 2
    query = jnp.arange(T)[None, :, None]
    key = jnp.arange(T)[None, None, :]
    ids = bucket_ids(band * T + key - query)
    return (ids[..., None] == jnp.arange(num_buckets)).astype(F32)


def can_move(sizes, rows):
    zs = sizes[0] // (Y * C)
    return rows % 16 == 0 and sizes[1] == 2 and sizes[0] % (Y * C) == 0 and zs in (2, 4, 8, 16)


class Place:
    def __init__(self, zs, xs):
        grp = lax.axis_index("grp")
        self.zs, self.xs = zs, xs
        self.x = lax.axis_index("seq")
        self.z = grp // (Y * C)
        self.y = (grp // C) % Y
        self.c = grp % C

    def device(self, z=None, y=None, c=None, x=None):
        z = self.z if z is None else z
        y = self.y if y is None else y
        c = self.c if c is None else c
        x = self.x if x is None else x
        return (z * (Y * C) + y * C + c, x)

    def peers(self):
        around = [self.device(z=(self.z + d) % self.zs) for d in range(1, self.zs)]
        return around + [
            self.device(y=1 - self.y),
            self.device(x=1 - self.x),
            self.device(c=1 - self.c),
        ]

    def barrier(self):
        sem = pltpu.get_barrier_semaphore()
        peers = self.peers()
        for peer in peers:
            pl.semaphore_signal(sem, inc=1, device_id=peer, device_id_type=MESH)
        pl.semaphore_wait(sem, len(peers))


def remote(src, dst, send_sem, recv_sem, device):
    return pltpu.make_async_remote_copy(
        src_ref=src,
        dst_ref=dst,
        send_sem=send_sem,
        recv_sem=recv_sem,
        device_id=device,
        device_id_type=MESH,
    )


def staged(step, offset, count, action):
    @pl.when((step >= offset) & (step < count + offset))
    def _():
        action(step - offset)


class Gather:
    def __init__(self, place, own, whole, send, recv):
        self.p, self.own, self.whole, self.send, self.recv = place, own, whole, send, recv

    def copy(self, k, half, index, src, dst, device):
        return remote(src, dst, self.send.at[k, half, index], self.recv.at[k, half, index], device)

    def alone(self, k, half):
        p = self.p
        dst = self.whole.at[k, half, :, p.z, p.y, p.c * p.xs + p.x]
        src = self.own.at[k, half]
        if half == 0:
            return [self.copy(k, half, 0, src, dst, p.device(x=1 - p.x))]
        peers = [p.device(z=(p.z + d) % p.zs) for d in range(1, p.zs)]
        return [self.copy(k, half, i, src, dst, peer) for i, peer in enumerate(peers)]

    def second(self, k, half):
        p = self.p
        if half == 0:
            view = self.whole.at[k, half, :, p.z, p.y, pl.ds(p.c * p.xs, p.xs)]
            peers = [p.device(z=(p.z + d) % p.zs) for d in range(1, p.zs)]
            return [self.copy(k, half, 1 + i, view, view, peer) for i, peer in enumerate(peers)]
        view = self.whole.at[k, half, :, :, p.y, p.c * p.xs + p.x]
        return [self.copy(k, half, p.zs - 1, view, view, p.device(y=1 - p.y))]

    def third(self, k, half):
        p = self.p
        if half == 0:
            view = self.whole.at[k, half, :, :, p.y, pl.ds(p.c * p.xs, p.xs)]
            peer = p.device(y=1 - p.y)
        else:
            view = self.whole.at[k, half, :, :, :, p.c * p.xs + p.x]
            peer = p.device(x=1 - p.x)
        return [self.copy(k, half, p.zs, view, view, peer)]

    def fourth(self, k, half):
        p = self.p
        view = self.whole.at[k, half, :, :, :, pl.ds(p.c * p.xs, p.xs)]
        return [self.copy(k, half, p.zs + 1, view, view, p.device(c=1 - p.c))]

    def tick(self, step, first, end):
        stages = (self.alone, self.second, self.third, self.fourth)

        def advance(offset, k):
            for half in (0, 1):
                if offset > 0:
                    for copy in stages[offset - 1](k, half):
                        copy.wait_recv()
                if offset < 4:
                    for copy in stages[offset](k, half):
                        copy.start()
                else:
                    for stage in stages:
                        for copy in stage(k, half):
                            copy.wait_send()

        for offset in range(5):
            staged(step, offset, end - first, lambda k, offset=offset: advance(offset, first + k))


def gather(own, sizes):
    return lax.all_gather(own, ("grp", "seq"), axis=3, tiled=True)


class Scatter:
    def __init__(self, place, bufs, send, recv, out):
        self.p, self.send, self.recv, self.out = place, send, recv, out
        (self.in1, self.in2, self.sum1, self.sum2) = bufs[:4]
        self.in3, self.in4, self.sum3 = bufs[4:6], bufs[6:8], bufs[8:10]

    def copy(self, k, half, index, src, dst, device):
        slot = k % 2
        return remote(
            src, dst, self.send.at[slot, half, index], self.recv.at[slot, half, index], device
        )

    def first(self, k, half, part):
        p = self.p
        src = part.at[half, :, :, :, pl.ds((1 - p.c) * p.xs, p.xs)]
        return self.copy(k, half, 0, src, self.in1.at[k % 2, half], p.device(c=1 - p.c))

    def second(self, k, half):
        p = self.p
        if half == 0:
            src, peer = self.sum1.at[k % 2, half, :, :, 1 - p.y], p.device(y=1 - p.y)
        else:
            src, peer = self.sum1.at[k % 2, half, :, :, :, 1 - p.x], p.device(x=1 - p.x)
        return self.copy(k, half, 1, src, self.in2.at[k % 2, half], peer)

    def third(self, k, half):
        p, slot = self.p, k % 2
        if half == 1:
            src = self.sum2.at[slot, half, :, :, 1 - p.y]
            return [self.copy(k, half, 2, src, self.in3[1].at[slot], p.device(y=1 - p.y))]
        copies = []
        for d in range(1, p.zs):
            target = (p.z + d) % p.zs
            src = self.sum2.at[slot, half, :, target]
            dst = self.in3[0].at[slot, d - 1]
            copies.append(self.copy(k, half, 1 + d, src, dst, p.device(z=target)))
        return copies

    def fourth(self, k, half):
        p, slot = self.p, k % 2
        if half == 0:
            src = self.sum3[0].at[slot, :, 1 - p.x]
            return [self.copy(k, half, p.zs + 1, src, self.in4[0].at[slot, 0], p.device(x=1 - p.x))]
        copies = []
        for d in range(1, p.zs):
            target = (p.z + d) % p.zs
            src = self.sum3[1].at[slot, :, target]
            dst = self.in4[1].at[slot, d - 1]
            copies.append(self.copy(k, half, 2 + d, src, dst, p.device(z=target)))
        return copies

    def finish(self, k):
        p, slot = self.p, k % 2
        for half in (0, 1):
            total = self.sum3[half][slot, :, p.x if half == 0 else p.z].astype(F32)
            for i, copy in enumerate(self.fourth(k, half)):
                copy.wait_recv()
                copy.wait_send()
                total = total + self.in4[half][slot, i].astype(F32)
            self.out[k, half] = total

    def start_fourth(self, k):
        p, slot = self.p, k % 2
        for half in (0, 1):
            for copy in self.third(k, half):
                copy.wait_recv()
                copy.wait_send()
            for i in range(self.sum2.shape[2]):
                if half == 0:
                    total = self.sum2[slot, half, i, p.z].astype(F32)
                    for d in range(1, p.zs):
                        total = total + self.in3[0][slot, d - 1, i].astype(F32)
                else:
                    total = self.sum2[slot, half, i, :, p.y].astype(F32)
                    total = total + self.in3[1][slot, i].astype(F32)
                self.sum3[half][slot, i] = total.astype(BF)
            for copy in self.fourth(k, half):
                copy.start()

    def start_third(self, k):
        p, slot = self.p, k % 2
        for half in (0, 1):
            copy = self.second(k, half)
            copy.wait_recv()
            copy.wait_send()
            for i in range(self.sum2.shape[2]):
                if half == 0:
                    mine = self.sum1[slot, half, i, :, p.y]
                else:
                    mine = self.sum1[slot, half, i, :, :, p.x]
                total = mine.astype(F32) + self.in2[slot, half, i].astype(F32)
                self.sum2[slot, half, i] = total.astype(BF)
            for copy in self.third(k, half):
                copy.start()

    def start_second(self, k, part):
        p, slot = self.p, k % 2
        for half in (0, 1):
            copy = self.first(k, half, part)
            copy.wait_recv()
            copy.wait_send()

            def add(z, _, half=half):
                for i in range(self.sum1.shape[2]):
                    mine = part[half, i, z, :, pl.ds(p.c * p.xs, p.xs)]
                    total = mine.astype(F32) + self.in1[slot, half, i, z].astype(F32)
                    self.sum1[slot, half, i, z] = total.astype(BF)
                return 0

            lax.fori_loop(0, p.zs, add, 0)
            self.second(k, half).start()

    def start_first(self, k, part):
        for half in (0, 1):
            self.first(k, half, part).start()


BUFFERS = 10


def scatter_buffers(n, zs, xs, rows, lanes):
    block = (rows, lanes)
    shapes = [
        (2, 2, n, zs, Y, xs, *block),
        (2, 2, n, zs, 2, *block),
        (2, 2, n, zs, Y, xs, *block),
        (2, 2, n, zs, 2, *block),
        (2, zs - 1, n, 2, *block),
        (2, n, zs, *block),
        (2, 1, n, *block),
        (2, zs - 1, n, *block),
        (2, n, 2, *block),
        (2, n, zs, *block),
    ]
    return [pltpu.VMEM(shape, BF) for shape in shapes]


def scatter(parts):
    return lax.psum_scatter(parts, ("grp", "seq"), scatter_dimension=3, tiled=True).astype(F32)


class Shape:
    def __init__(self, tiles, local_tiles, conts):
        self.tiles, self.local_tiles, self.conts = tiles, local_tiles, conts
        self.rows = (local_tiles + conts) * T
        self.keys = self.rows + (tiles - local_tiles) * T
        self.parts = [(0, range(local_tiles)), (self.rows, range(local_tiles, tiles))]
        self.parts = [(start, js) for start, js in self.parts if len(js)]


def band_of(key_tile, query_tile):
    return jnp.clip(key_tile - query_tile, -2, 2) + 2


def tile_lanes():
    first_half = lax.broadcasted_iota(jnp.int32, (T, 2 * HEAD), 1) < HEAD
    place = lax.broadcasted_iota(jnp.int32, (T, T), 1)
    return first_half, place


def tile_rows(i):
    return pl.ds(pl.multiple_of(i * T, T), T)


def attend_tile(shape, i, is_cont, live, base, q, k, v, bias, out, norm):
    first_half, place = tile_lanes()
    rows = tile_rows(i)
    queries = q[rows, :]
    query_tile = shape.tiles if is_cont else base + i
    mixed = []
    for h in range(2):
        mine = first_half if h == 0 else ~first_half
        masked = jnp.where(mine, queries, jnp.zeros_like(queries))
        logits = []
        for start, js in shape.parts:
            scores = nt(masked, k[start : start + len(js) * T, :])
            for at, j in enumerate(js):
                band = band_of(lax.rem(base + j, shape.tiles), query_tile)
                logits.append(scores[:, at * T : (at + 1) * T] + bias[h, band])
        if is_cont:
            own = nt(masked, k[rows, :]) + bias[h, 2]
            logits.append(jnp.where(place < live[0, i - shape.local_tiles], own, NEGATIVE))
        top = jnp.max(functools.reduce(jnp.maximum, logits), axis=1, keepdims=True)
        weights = [jnp.exp(part - top) for part in logits]
        total = jnp.sum(functools.reduce(jnp.add, weights), axis=1, keepdims=True)
        inverse = 1.0 / total
        probs = [(weight * inverse).astype(BF) for weight in weights]
        result = None
        for start, js in shape.parts:
            left = jnp.concatenate([probs[j] for j in js], axis=1)
            term = nn(left, v[start : start + len(js) * T, :])
            result = term if result is None else result + term
        if is_cont:
            result = result + nn(probs[shape.tiles], v[rows, :])
        mixed.append(result)
        norm[h, rows, :] = top + jnp.log(total)
    out[rows, :] = jnp.where(first_half, mixed[0], mixed[1]).astype(BF)


def for_tiles(shape, conts, action):
    first, last = (shape.local_tiles, shape.local_tiles + shape.conts) if conts else (0, shape.local_tiles)

    def one(i, carry):
        action(i, conts)
        return carry

    lax.fori_loop(first, last, one, 0)


def attend_kernel(shape, live, base, q, k, v, bias, out, norm):
    for conts in (False, True):
        for_tiles(
            shape,
            conts,
            lambda i, c: attend_tile(shape, i, c, live, base[0], q, k, v, bias, out, norm),
        )


def pair_block(n):
    return pl.BlockSpec((n, 2 * HEAD), lambda h, *_: (0, h))


def attend(q, k, v, bias, live, base, shape):
    rows, width = q.shape
    pairs = width // (2 * HEAD)
    return pl.pallas_call(
        functools.partial(attend_kernel, shape),
        grid_spec=pltpu.PrefetchScalarGridSpec(
            num_scalar_prefetch=2,
            grid=(pairs,),
            in_specs=[
                pair_block(rows),
                pair_block(shape.keys),
                pair_block(shape.keys),
                pl.BlockSpec((2, BANDS, T, T), lambda h, *_: (h, 0, 0, 0)),
            ],
            out_specs=[pair_block(rows), pl.BlockSpec((2, rows, 1), lambda h, *_: (h, 0, 0))],
        ),
        out_shape=[
            jax.ShapeDtypeStruct((rows, width), BF),
            jax.ShapeDtypeStruct((2 * pairs, rows, 1), F32),
        ],
        compiler_params=pltpu.CompilerParams(vmem_limit_bytes=VMEM_LIMIT),
    )(live, base, q, k, v, bias)


def attend_back_tile(
    shape, i, is_cont, live, base, q, k, v, bias, grad, out, norm, d_q, d_bias, k_sum, v_sum
):
    first_half, place = tile_lanes()
    rows = tile_rows(i)
    queries = q[rows, :]
    grads = grad[rows, :]
    query_tile = shape.tiles if is_cont else base + i
    overlap = grads.astype(F32) * out[rows, :].astype(F32)
    mixed = []
    for h in range(2):
        mine = first_half if h == 0 else ~first_half
        masked = jnp.where(mine, queries, jnp.zeros_like(queries))
        masked_grad = jnp.where(mine, grads, jnp.zeros_like(grads))
        inner = jnp.sum(jnp.where(mine, overlap, 0.0), axis=1, keepdims=True)
        log_norm = norm[h, rows, :]

        def piece(keys, bands, allowed):
            scores = nt(masked, k[keys, :])
            d_probs = nt(masked_grad, v[keys, :])
            probs_low, scores_low = [], []
            for at, band in enumerate(bands):
                cols = slice(at * T, (at + 1) * T)
                logits = scores[:, cols] + bias[h, band]
                if allowed is not None:
                    logits = jnp.where(allowed, logits, NEGATIVE)
                probs = jnp.exp(logits - log_norm)
                d_scores = probs * (d_probs[:, cols] - inner)
                d_bias[h, band] += d_scores
                probs_low.append(probs.astype(BF))
                scores_low.append(d_scores.astype(BF))
            probs_low = jnp.concatenate(probs_low, axis=1)
            scores_low = jnp.concatenate(scores_low, axis=1)
            v_sum[keys, :] += tn(probs_low, masked_grad)
            k_sum[keys, :] += tn(scores_low, masked)
            return nn(scores_low, k[keys, :])

        result = None
        for start, js in shape.parts:
            bands = [band_of(lax.rem(base + j, shape.tiles), query_tile) for j in js]
            term = piece(pl.ds(start, len(js) * T), bands, None)
            result = term if result is None else result + term
        if is_cont:
            result = result + piece(rows, [2], place < live[0, i - shape.local_tiles])
        mixed.append(result)
    d_q[rows, :] = jnp.where(first_half, mixed[0], mixed[1]).astype(BF)


def attend_back_kernel(
    shape, live, base, q, k, v, bias, grad, out, norm, d_q, d_k, d_v, d_bias, k_sum, v_sum
):
    k_sum[...] = jnp.zeros_like(k_sum)
    v_sum[...] = jnp.zeros_like(v_sum)
    d_bias[...] = jnp.zeros_like(d_bias)
    refs = (q, k, v, bias, grad, out, norm, d_q, d_bias, k_sum, v_sum)
    for conts in (False, True):
        for_tiles(shape, conts, lambda i, c: attend_back_tile(shape, i, c, live, base[0], *refs))
    d_k[...] = k_sum[...].astype(BF)
    d_v[...] = v_sum[...].astype(BF)


def attend_back(q, k, v, bias, grad, out, norm, live, base, shape):
    rows, width = q.shape
    pairs = width // (2 * HEAD)
    keys = shape.keys
    bands = pl.BlockSpec((2, BANDS, T, T), lambda h, *_: (h, 0, 0, 0))
    return pl.pallas_call(
        functools.partial(attend_back_kernel, shape),
        grid_spec=pltpu.PrefetchScalarGridSpec(
            num_scalar_prefetch=2,
            grid=(pairs,),
            in_specs=[
                pair_block(rows),
                pair_block(keys),
                pair_block(keys),
                bands,
                pair_block(rows),
                pair_block(rows),
                pl.BlockSpec((2, rows, 1), lambda h, *_: (h, 0, 0)),
            ],
            out_specs=[pair_block(rows), pair_block(keys), pair_block(keys), bands],
            scratch_shapes=[pltpu.VMEM((keys, 2 * HEAD), F32), pltpu.VMEM((keys, 2 * HEAD), F32)],
        ),
        out_shape=[
            jax.ShapeDtypeStruct((rows, width), BF),
            jax.ShapeDtypeStruct((keys, width), BF),
            jax.ShapeDtypeStruct((keys, width), BF),
            jax.ShapeDtypeStruct((2 * pairs, BANDS, T, T), F32),
        ],
        compiler_params=pltpu.CompilerParams(vmem_limit_bytes=VMEM_LIMIT),
    )(live, base, q, k, v, bias, grad, out, norm)


ORDER = (1, 2, 0, 3)
FIRST_PAIR = 8


def joined_pieces(w_buf, slot, m):
    pieces = [w_buf[slot, j // 3, j % 3] for j in (2 * m, 2 * m + 1)]
    return jnp.concatenate([piece.reshape(-1, T) for piece in pieces], axis=1)


def front_kernel(zs, xs, shape, early, live, *refs):
    (prompt_x, cont_x, own_gain, *weights) = refs[:10]
    table = refs[10]
    (whole, own_out, x_out, normed_out, kv_out, bias_out) = refs[11:17]
    (q, attended, norm, middle, normed_two, gains) = refs[17:23]
    (x, normed, kv, bias, held, w_buf, gain_whole) = refs[23:30]
    (local, kv_sems, send, recv, gain_send, gain_recv) = refs[30:36]
    place = Place(zs, xs)
    step = pl.program_id(0)
    rows, width = x.shape
    prompt = shape.local_tiles * T
    pairs = q.shape[0]
    size = middle.shape[0]
    blocks = rows // size
    last = FIRST_PAIR + pairs
    count = 4 + early
    feed_weights = weights[4:]
    columns = feed_weights[0].shape[1] // T

    def x_load(i):
        source, part = ((prompt_x, pl.ds(0, prompt)), (cont_x, pl.ds(prompt, rows - prompt)))[i]
        return pltpu.make_async_copy(source, x.at[part], local.at[i])

    def mine_store():
        mine = whole.at[:, :, :, place.z, place.y, place.c * place.xs + place.x]
        return pltpu.make_async_copy(held.at[pl.ds(0, count)], mine, local.at[2])

    feed_own = held.at[pl.ds(4, held.shape[0] - 4)]
    kept = ((feed_own, own_out), (x, x_out), (normed, normed_out), (bias, bias_out), (kv, kv_out))

    def result(i):
        return pltpu.make_async_copy(*kept[i], local.at[3 + i])

    def weight_load(k):
        return pltpu.make_async_copy(whole.at[k], w_buf.at[k % 2], local.at[8 + k])

    @pl.when(step == 0)
    def _():
        place.barrier()
        x_load(0).start()
        x_load(1).start()
        for c, matrix in enumerate(ORDER):
            for j in range(6):
                held[c, j // 3, j % 3] = weights[matrix][:, j * T : (j + 1) * T].astype(BF)
        gain_whole[0, :, :, place.z, place.y, place.c * place.xs + place.x] = own_gain[0]

    Gather(place, own_gain, gain_whole, gain_send, gain_recv).tick(step, 0, 1)
    Gather(place, held, whole, send, recv).tick(step, 0, count)

    @pl.when(step == 0)
    def _():
        def convert(j, carry):
            part = pl.ds(pl.multiple_of(j * T, T), T)
            for i in range(3):
                held[4 + j // 2, j % 2, i] = feed_weights[i][:, part].astype(BF)
            return carry

        lax.fori_loop(0, columns, convert, 0)
        if columns % 2:
            held[4 + columns // 2, 1] = jnp.zeros(held.shape[2:], BF)
        mine_store().start()
        mine_store().wait()
        result(0).start()
        x_load(0).wait()
        x_load(1).wait()
        result(1).start()

    @pl.when(step == 1)
    def _():
        query = lax.broadcasted_iota(jnp.int32, (T, T), 0)
        key = lax.broadcasted_iota(jnp.int32, (T, T), 1)
        half = table.shape[0] // 2
        ids = [bucket_ids(band * T + key - query) for band in (-1, 0, 1)]
        found = (range(1, half), [*range(half), *range(half + 1, 2 * half)], range(half + 1, 2 * half))

        def one(h, carry):
            bias[h, 0] = jnp.full((T, T), table[half - 1, h])
            bias[h, 4] = jnp.full((T, T), table[2 * half - 1, h])
            for band in range(3):
                value = jnp.zeros((T, T), F32)
                for bucket in found[band]:
                    value = jnp.where(ids[band] == bucket, table[bucket, h], value)
                bias[h, 1 + band] = value
            return carry

        lax.fori_loop(0, bias.shape[0], one, 0)

    for k in range(4):

        @pl.when(step == 4 + k)
        def _(k=k):
            weight_load(k).start()

    def by_rows(action):
        def one(i, carry):
            action(pl.ds(pl.multiple_of(i * size, size), size))
            return carry

        lax.fori_loop(0, blocks, one, 0)

    @pl.when(step == 4)
    def _():
        result(3).start()
        eye = lax.broadcasted_iota(jnp.int32, (T, T), 0) == lax.broadcasted_iota(jnp.int32, (T, T), 1)
        for g in range(2):
            column = gain_whole[0, g, 0].reshape(width, T).astype(F32)
            for i in range(width // T):
                cols = slice(i * T, (i + 1) * T)
                gains[g, :, cols] = jnp.sum(jnp.where(eye, column[cols], 0.0), axis=0, keepdims=True)

        def norm_rows(part):
            values = x[part, :].astype(F32)
            scale = lax.rsqrt(jnp.mean(values * values, axis=-1, keepdims=True) + EPS)
            normed[part, :] = (values * scale * gains[0]).astype(BF)

        by_rows(norm_rows)
        result(2).start()

    def project(slot, target):
        for m in range(pairs // 2):
            right = joined_pieces(w_buf, slot, m)

            def rows_of_product(part, m=m, right=right):
                product = nn(normed[part, :], right).astype(BF)
                target[2 * m, part, :] = product[:, :T]
                target[2 * m + 1, part, :] = product[:, T:]

            by_rows(rows_of_product)

    def kv_send(side, p):
        src = kv.at[side, p, pl.ds(0, prompt)]
        dst = kv.at[side, p, pl.ds(rows, prompt)]
        peer = place.device(x=1 - place.x)
        return remote(src, dst, kv_sems.at[0, side, p], kv_sems.at[1, side, p], peer)

    for k in range(3):

        @pl.when(step == 5 + k)
        def _(k=k):
            weight_load(k).wait()
            project(k % 2, kv.at[k] if k < 2 else q)
            if k < 2:
                for p in range(pairs):
                    kv_send(k, p).start()

    @pl.when(step == FIRST_PAIR)
    def _():
        weight_load(3).wait()

    @pl.when((step >= FIRST_PAIR) & (step < last))
    def _():
        p = step - FIRST_PAIR
        for side in range(2):
            kv_send(side, p).wait_recv()
            kv_send(side, p).wait_send()
        base = place.x * shape.local_tiles
        inputs = (q.at[p], kv.at[0, p], kv.at[1, p], bias.at[pl.ds(2 * p, 2)], attended.at[p], norm)
        for conts in (False, True):
            for_tiles(shape, conts, lambda i, c: attend_tile(shape, i, c, live, base, *inputs))

    @pl.when(step == last)
    def _():
        result(4).start()

    @pl.when(step >= last)
    def _():
        part = pl.ds(pl.multiple_of((step - last) * size, size), size)
        branch = None
        for m in range(pairs // 2):
            left = jnp.concatenate([attended[2 * m + e, part, :] for e in range(2)], axis=1)
            term = nt(left, joined_pieces(w_buf, 1, m))
            branch = term if branch is None else branch + term
        total = x[part, :].astype(F32) + branch
        middle[...] = total
        scale = lax.rsqrt(jnp.mean(total * total, axis=-1, keepdims=True) + EPS)
        normed_two[...] = (total * scale * gains[1]).astype(BF)

    @pl.when(step == last + blocks - 1)
    def _():
        for i in range(len(kept)):
            result(i).wait()


def front(prompt_x, cont_x, own_gain, weights, table, live, shape, sizes, early, collective_id):
    grp, seq = sizes
    rows, width = shape.rows, prompt_x.shape[1]
    shard, inner = weights[0].shape
    feed_columns = weights[4].shape[1] // T
    pairs, keys, heads = inner // (2 * HEAD), shape.keys, table.shape[1]
    assert pairs == 6 and table.shape[0] == 32 and keys - rows == prompt_x.shape[0]
    zs = grp // (Y * C)
    chunks = 4 + (feed_columns + 1) // 2
    count = 4 + early
    own = (2, 3, shard, T)
    tile = (2, 3, zs, Y, C * seq, shard, T)
    size = min(rows, 256)
    blocks = rows // size
    last = FIRST_PAIR + pairs
    steps = last + blocks
    assert count + 4 <= steps and count <= chunks
    full = lambda *dims: pl.BlockSpec(
        dims, lambda s, *_: (0,) * len(dims), pipeline_mode=pl.Buffered(1)
    )
    by_rows = pl.BlockSpec((size, width), lambda s, *_: (jnp.clip(s - last, 0, blocks - 1), 0))
    anywhere = pl.BlockSpec(memory_space=pl.ANY)
    sems = lambda *dims: pltpu.SemaphoreType.DMA(dims)
    out = jax.ShapeDtypeStruct
    return pl.pallas_call(
        functools.partial(front_kernel, zs, seq, shape, early),
        grid_spec=pltpu.PrefetchScalarGridSpec(
            num_scalar_prefetch=1,
            grid=(steps,),
            in_specs=[anywhere, anywhere, full(*own_gain.shape)]
            + [full(*w.shape) for w in weights]
            + [pl.BlockSpec(memory_space=pltpu.SMEM)],
            out_specs=[anywhere] * 6
            + [
                full(pairs, rows, 2 * HEAD),
                full(pairs, rows, 2 * HEAD),
                pl.BlockSpec(
                    (2, rows, 1), lambda s, *_: (jnp.clip(s - FIRST_PAIR, 0, pairs - 1), 0, 0)
                ),
                by_rows,
                by_rows,
                full(2, 1, width),
            ],
            scratch_shapes=[
                pltpu.VMEM((rows, width), BF),
                pltpu.VMEM((rows, width), BF),
                pltpu.VMEM((2, pairs, keys, 2 * HEAD), BF),
                pltpu.VMEM((heads, BANDS, T, T), F32),
                pltpu.VMEM((chunks, *own), BF),
                pltpu.VMEM((2, *tile), BF),
                pltpu.VMEM((1, 2, 1, zs, Y, C * seq, shard, T), BF),
                sems(12),
                sems(2, 2, pairs),
                sems(count, 2, zs + 2),
                sems(count, 2, zs + 2),
                sems(1, 2, zs + 2),
                sems(1, 2, zs + 2),
            ],
        ),
        out_shape=[
            out((count, *tile), BF),
            out((chunks - 4, *own), BF),
            out((rows, width), BF),
            out((rows, width), BF),
            out((2, pairs, keys, 2 * HEAD), BF),
            out((heads, BANDS, T, T), F32),
            out((pairs, rows, 2 * HEAD), BF),
            out((pairs, rows, 2 * HEAD), BF),
            out((2 * pairs, rows, 1), F32),
            out((rows, width), F32),
            out((rows, width), BF),
            out((2, 1, width), F32),
        ],
        compiler_params=pltpu.CompilerParams(
            collective_id=collective_id, has_side_effects=True, vmem_limit_bytes=VMEM_LIMIT
        ),
    )(live, prompt_x, cont_x, own_gain, *weights, table)


SPAN = 4 * T
VECTOR_ROWS = 8


def turned(tile):
    row = lax.broadcasted_iota(jnp.int32, tile.shape, 0)
    for bit in range(7):
        moved = pltpu.roll(tile, SPAN - (1 << bit), 1)
        tile = jnp.where((row >> bit) & 1 == 1, moved, tile)
    return tile


def band_sums(d_bias, h):
    near = jnp.concatenate([d_bias[h, 1], d_bias[h, 2], d_bias[h, 3]], axis=1)
    near = jnp.concatenate([near, jnp.zeros((T, T), F32)], axis=1)
    diagonal = jnp.sum(turned(near), axis=0, keepdims=True)
    rows = [diagonal[:, i * T : (i + 1) * T] for i in range(4)]
    rows += [jnp.sum(d_bias[h, band], axis=0, keepdims=True) for band in (0, 4)]
    return jnp.concatenate(rows + [jnp.zeros((2, T), F32)], axis=0)


def put(i, first_blocks, targets, value):
    @pl.when(i < first_blocks)
    def _():
        targets[0][...] = value

    @pl.when(i >= first_blocks)
    def _():
        targets[1][...] = value


def two_parts(size, width, first_blocks, blocks, first_step):
    one = lambda s, *_: (jnp.clip(s - first_step, 0, first_blocks - 1), 0)
    two = lambda s, *_: (jnp.clip(s - first_step - first_blocks, 0, blocks - first_blocks - 1), 0)
    return [pl.BlockSpec((size, width), one), pl.BlockSpec((size, width), two)]


def rows_of(vector):
    return [vector[:, i * T : (i + 1) * T] for i in range(vector.shape[1] // T)]


class Combine:
    def __init__(self, place, total, arrived, send, recv):
        self.p, self.total, self.arrived, self.send, self.recv = place, total, arrived, send, recv

    def partners(self):
        p = self.p
        found = [p.device(c=1 - p.c), p.device(x=1 - p.x), p.device(y=1 - p.y)]
        bit = 1
        while bit < p.zs:
            found.append(p.device(z=p.z + bit - 2 * bit * ((p.z // bit) % 2)))
            bit *= 2
        return found

    def copy(self, i):
        return remote(
            self.total.at[i],
            self.arrived.at[i],
            self.send.at[i],
            self.recv.at[i],
            self.partners()[i],
        )

    def start(self, i):
        self.copy(i).start()

    def finish(self, i):
        self.copy(i).wait_recv()
        self.copy(i).wait_send()
        self.total[i + 1] = self.total[i] + self.arrived[i]


def back_kernel(zs, xs, shape, width, kept, live, *refs):
    q, k, v, bias, grad, out, norm, attended, branch_hbm, normed_hbm, parts, weights_hbm = refs[:12]
    d_middle, x_low, gain, d_gain_two = refs[12:16]
    d_x, (sums, vector_out) = refs[16:18], refs[18:20]
    (stage, turn_buf, d_q, d_kv, back_kv, k_sum, v_sum, d_bias) = refs[20:28]
    (w_buf, held, vector, total, arrived, gain_sum) = refs[28:34]
    (local, loads, kv_sems, both_sems) = refs[34:38]
    bufs, scatter_sems = refs[38 : 38 + BUFFERS], refs[38 + BUFFERS :]
    place = Place(zs, xs)
    step = pl.program_id(0)
    rows, keys = shape.rows, shape.keys
    prompt = shape.local_tiles * T
    pairs = d_q.shape[0]
    last = 2 * pairs
    turns = rows // T
    first_kept, end_kept = kept
    fed = parts.shape[0] - (end_kept - first_kept)
    size = d_x[0].shape[0]
    blocks = rows // size

    def stage_load(source):
        return pltpu.make_async_copy(source, stage, local.at[0])

    def weights_load(i):
        return pltpu.make_async_copy(weights_hbm.at[(2, 0, 1)[i]], w_buf.at[i], local.at[1 + i])

    def turn():
        def one(i, carry):
            part = tile_rows(i)
            turn_buf[:, part] = stage[part, :].T
            return carry

        lax.fori_loop(0, turns, one, 0)

    def part_load(c):
        j = jnp.where(c < first_kept, c, c + end_kept - first_kept)
        return pltpu.make_async_copy(parts.at[j], held.at[c % 3], loads.at[c % 3])

    @pl.when(step == 0)
    def _():
        part_load(step).start()
        stage_load(branch_hbm).start()
        place.barrier()
        for i in range(3):
            weights_load(i).start()

    engine = Scatter(place, bufs, *scatter_sems, sums)

    def due(offset, action):
        at = step - offset
        chunk = jnp.where(at < last, at, at - last + fed)
        early = (at >= 0) & (at < fed)
        late = (at >= last) & (at < last + 4)

        @pl.when(early | late)
        def _():
            action(chunk)

    def first(c):
        @pl.when(c < fed)
        def _():
            part_load(c).wait()

        engine.start_first(c, held.at[c % 3])

    due(4, engine.finish)
    due(3, engine.start_fourth)
    due(2, engine.start_third)
    due(1, lambda c: engine.start_second(c, held.at[c % 3]))
    due(0, first)

    @pl.when(step + 1 < fed)
    def _():
        part_load(step + 1).start()

    @pl.when(step == 0)
    def _():
        stage_load(branch_hbm).wait()
        turn()
        stage_load(normed_hbm).start()

    def kv_send(p):
        src = d_kv.at[p, :, pl.ds(rows, keys - rows)]
        peer = place.device(x=1 - place.x)
        return remote(src, back_kv.at[p], kv_sems.at[0, p], kv_sems.at[1, p], peer)

    @pl.when((step >= 2) & (step <= last) & (step % 2 == 0))
    def _():
        kv_send(step // 2 - 1).start()

    @pl.when(step < last)
    def _():
        p = step // 2
        half = step % 2

        @pl.when(half == 0)
        def _():
            k_sum[...] = jnp.zeros_like(k_sum)
            v_sum[...] = jnp.zeros_like(v_sum)
            d_bias[...] = jnp.zeros_like(d_bias)

        inputs = (q, k, v, bias, grad, out, norm, d_q.at[p], d_bias, k_sum, v_sum)
        base = place.x * shape.local_tiles
        action = lambda i, c: attend_back_tile(shape, i, c, live, base, *inputs)

        @pl.when(half == 0)
        def _():
            for_tiles(shape, False, action)

        @pl.when(half == 1)
        def _():
            for_tiles(shape, True, action)
            d_kv[p, 0] = k_sum[...].astype(BF)
            d_kv[p, 1] = v_sum[...].astype(BF)
            for h in range(2):
                vector[2 * p + h] = band_sums(d_bias, h)

    def produce(c, right):
        slot = c % 3
        for m in range(3):
            operand = right(m)

            def one(z, carry, m=m, operand=operand):
                block = turn_buf.shape[0] // zs
                part = pl.ds(pl.multiple_of(z * block, block), block)
                result = nn(turn_buf[part, :], operand).astype(BF)
                for side in range(2):
                    index = 2 * m + side
                    value = result[:, side * T : (side + 1) * T]
                    held[slot, index // 3, index % 3, z] = value.reshape(held.shape[4:])
                return carry

            lax.fori_loop(0, zs, one, 0)

    @pl.when(step == last - 1)
    def _():
        produce(fed, lambda m: jnp.concatenate([attended[2 * m], attended[2 * m + 1]], axis=1))

    @pl.when(step == last)
    def _():
        stage_load(normed_hbm).wait()
        turn()
        produce(fed + 1, lambda m: jnp.concatenate([d_q[2 * m], d_q[2 * m + 1]], axis=1))

        def join(p, carry):
            kv_send(p).wait_recv()
            kv_send(p).wait_send()
            for side in range(2):
                own = d_kv[p, side, 0:prompt, :].astype(F32)
                d_kv[p, side, 0:prompt, :] = (own + back_kv[p, side].astype(F32)).astype(BF)
            return carry

        lax.fori_loop(0, pairs, join, 0)
        for i in range(3):
            weights_load(i).wait()
        gain_sum[...] = jnp.zeros_like(gain_sum)

    for side in range(2):

        @pl.when(step == last + 1 + side)
        def _(side=side):
            pick = lambda p: d_kv[p, side, 0:rows, :]
            produce(fed + 2 + side, lambda m: jnp.concatenate([pick(2 * m), pick(2 * m + 1)], axis=1))

    @pl.when((step >= last) & (step < last + blocks))
    def _():
        part = pl.ds(pl.multiple_of((step - last) * size, size), size)
        d_normed = None
        for i in range(3):
            for m in range(pairs // 2):
                if i == 0:
                    left = [d_q[2 * m + e, part, :] for e in range(2)]
                else:
                    left = [d_kv[2 * m + e, i - 1, part, :] for e in range(2)]
                pieces = [2 * m, 2 * m + 1]
                right = [w_buf[i, j // 3, j % 3].reshape(width, T) for j in pieces]
                term = nt(jnp.concatenate(left, axis=1), jnp.concatenate(right, axis=1))
                d_normed = term if d_normed is None else d_normed + term
        x = x_low[...].astype(F32)
        scale = lax.rsqrt(jnp.mean(x * x, axis=-1, keepdims=True) + EPS)
        unit = x * scale
        gain_sum[...] += jnp.sum(d_normed * unit, axis=0, keepdims=True)
        d_unit = d_normed * gain[...]
        inner = jnp.mean(d_unit * unit, axis=-1, keepdims=True)
        value = (d_middle[...] + scale * (d_unit - unit * inner)).astype(BF)
        put(step - last, prompt // size, d_x, value)

    mix = Combine(place, total, arrived, both_sems.at[0], both_sems.at[1])
    start = last + blocks
    stages = total.shape[0] - 1
    tiles = 2 * pairs

    @pl.when(step == start)
    def _():
        total[0, 0:tiles] = vector[...]
        both = rows_of(gain_sum[...]) + rows_of(d_gain_two[...])
        for i in range(len(both) // VECTOR_ROWS):
            group = both[i * VECTOR_ROWS : (i + 1) * VECTOR_ROWS]
            total[0, tiles + i] = jnp.concatenate(group, axis=0)

    for i in range(stages + 1):

        @pl.when(step == start + 1 + i)
        def _(i=i):
            if i > 0:
                mix.finish(i - 1)
            if i < stages:
                mix.start(i)
            else:
                vector_out[...] = total[stages]


def back(q, kv, bias, grad, out, norm, branch, normed, parts, weights, d_middle, x_low, gain,
         d_gain_two, live, shape, sizes, kept, collective_id):
    grp, seq = sizes
    rows, width = x_low.shape
    pairs = q.shape[0]
    zs = grp // (Y * C)
    keys = shape.keys
    chunks, _, n, _, _, _, shard, lanes = parts.shape
    count = chunks - (kept[1] - kept[0]) + 4
    assert chunks - (kept[1] - kept[0]) <= 2 * pairs
    assert (pairs, n) == (6, 3) and 2 * width // T % VECTOR_ROWS == 0
    last = 2 * pairs
    size = min(rows, 256)
    blocks = rows // size
    prompt = shape.local_tiles * T
    assert prompt % size == 0
    tile = (2, n, zs, Y, C * seq, shard, lanes)
    stages = 3 + (zs - 1).bit_length()
    steps = last + blocks + stages + 2
    vector = (2 * pairs + 2 * width // T // VECTOR_ROWS, VECTOR_ROWS, T)
    pair = lambda s: jnp.minimum(s // 2, pairs - 1)
    by_pair = lambda rows_: pl.BlockSpec((rows_, 2 * HEAD), lambda s, *_: (0, pair(s)))
    in_pair = pl.BlockSpec((None, rows, 2 * HEAD), lambda s, *_: (pair(s), 0, 0))
    of_keys = lambda side: pl.BlockSpec(
        (None, None, keys, 2 * HEAD), lambda s, *_: (side, pair(s), 0, 0)
    )
    row_block = lambda s: jnp.clip(s - last, 0, blocks - 1)
    by_rows = pl.BlockSpec((size, width), lambda s, *_: (row_block(s), 0))
    full = lambda *dims: pl.BlockSpec(
        dims, lambda s, *_: (0,) * len(dims), pipeline_mode=pl.Buffered(1)
    )
    anywhere = pl.BlockSpec(memory_space=pl.ANY)
    sems = lambda *dims: pltpu.SemaphoreType.DMA(dims)
    return pl.pallas_call(
        functools.partial(back_kernel, zs, seq, shape, width, kept),
        grid_spec=pltpu.PrefetchScalarGridSpec(
            num_scalar_prefetch=1,
            grid=(steps,),
            in_specs=[
                in_pair,
                of_keys(0),
                of_keys(1),
                pl.BlockSpec((2, BANDS, T, T), lambda s, *_: (pair(s), 0, 0, 0)),
                by_pair(rows),
                in_pair,
                pl.BlockSpec((2, rows, 1), lambda s, *_: (pair(s), 0, 0)),
                full(pairs, rows, 2 * HEAD),
                anywhere,
                anywhere,
                anywhere,
                anywhere,
                by_rows,
                by_rows,
                full(1, width),
                full(1, width),
            ],
            out_specs=two_parts(size, width, prompt // size, blocks, last)
            + [full(count, 2, n, shard, lanes), full(*vector)],
            scratch_shapes=[
                pltpu.VMEM((rows, width), BF),
                pltpu.VMEM((width, rows), BF),
                pltpu.VMEM((pairs, rows, 2 * HEAD), BF),
                pltpu.VMEM((pairs, 2, keys, 2 * HEAD), BF),
                pltpu.VMEM((pairs, 2, keys - rows, 2 * HEAD), BF),
                pltpu.VMEM((keys, 2 * HEAD), F32),
                pltpu.VMEM((keys, 2 * HEAD), F32),
                pltpu.VMEM((2, BANDS, T, T), F32),
                pltpu.VMEM((3, *tile), BF),
                pltpu.VMEM((3, *tile), BF),
                pltpu.VMEM((2 * pairs, VECTOR_ROWS, T), F32),
                pltpu.VMEM((stages + 1, *vector), F32),
                pltpu.VMEM((stages, *vector), F32),
                pltpu.VMEM((1, width), F32),
                sems(4),
                sems(3),
                sems(2, pairs),
                sems(2, stages),
            ]
            + scatter_buffers(n, zs, seq, shard, lanes)
            + [sems(2, 2, zs + 2), sems(2, 2, zs + 2)],
        ),
        out_shape=[
            jax.ShapeDtypeStruct((prompt, width), BF),
            jax.ShapeDtypeStruct((rows - prompt, width), BF),
            jax.ShapeDtypeStruct((count, 2, n, shard, lanes), F32),
            jax.ShapeDtypeStruct(vector, F32),
        ],
        compiler_params=pltpu.CompilerParams(
            collective_id=collective_id, has_side_effects=True, vmem_limit_bytes=VMEM_LIMIT
        ),
    )(live, q, kv, kv, bias, grad, out, norm, out, branch, normed, parts, weights, d_middle,
      x_low, gain, d_gain_two)


GELU_SCALE = 0.7978845608028654
GELU_CUBIC = 0.044715


def gelu_and_slope(a):
    square = a * a
    tanh = jnp.tanh(GELU_SCALE * a * (1.0 + GELU_CUBIC * square))
    half = 0.5 * (1.0 + tanh)
    slope = half + 0.5 * a * (1.0 - tanh * tanh) * (
        GELU_SCALE * (1.0 + 3.0 * GELU_CUBIC * square)
    )
    return a * half, slope


def feed_load(x_hbm, dy_parts, x, x_t, dy, dy_t, sem):
    loads = [pltpu.make_async_copy(x_hbm, x, sem.at[0])]
    start = 0
    for i, part in enumerate(dy_parts):
        target = dy.at[pl.ds(start, part.shape[0])]
        loads.append(pltpu.make_async_copy(part, target, sem.at[1 + i]))
        start += part.shape[0]
    for load in loads:
        load.start()
    for load in loads:
        load.wait()

    def turn(i, carry):
        part = pl.ds(pl.multiple_of(i * T, T), T)
        x_t[:, part] = x[part, :].T
        dy_t[:, part] = dy[part, :].T
        return carry

    lax.fori_loop(0, x.shape[0] // T, turn, 0)


def feed_chunk(read, write, blocks, out, d_x, x, x_t, dy, dy_t, hidden, d_gate, d_up):
    rows, width = x.shape
    row_block = min(rows, 256)
    width_block = width // blocks
    w_gate, w_up, w_down = [jnp.concatenate([read(0, i), read(1, i)], axis=1) for i in range(3)]

    def by_rows(i, carry):
        part = pl.ds(pl.multiple_of(i * row_block, row_block), row_block)
        gate = nn(x[part, :], w_gate)
        up = nn(x[part, :], w_up)
        d_hidden = nn(dy[part, :], w_down)
        active, slope = gelu_and_slope(gate)
        hidden_low = (active * up).astype(BF)
        d_gate_low = (d_hidden * up * slope).astype(BF)
        d_up_low = (d_hidden * active).astype(BF)
        hidden[part, :] = hidden_low
        d_gate[part, :] = d_gate_low
        d_up[part, :] = d_up_low
        out[part, :] += nt(hidden_low, w_down)
        d_x[part, :] += nt(d_gate_low, w_gate) + nt(d_up_low, w_up)
        return carry

    lax.fori_loop(0, rows // row_block, by_rows, 0)

    def by_width(i, carry):
        part = pl.ds(pl.multiple_of(i * width_block, width_block), width_block)
        pairs = ((x_t, d_gate), (x_t, d_up), (dy_t, hidden))
        for index, (left, right) in enumerate(pairs):
            total = nn(left[part, :], right[...]).astype(BF)
            write(0, index, i, total[:, :T])
            write(1, index, i, total[:, T:])
        return carry

    lax.fori_loop(0, blocks, by_width, 0)


def feed_kernel(x_hbm, dy_hbm, weights, out, d_x, grads, x, x_t, dy, dy_t, *rest):
    *work, sem = rest
    width_block = 512

    @pl.when(pl.program_id(0) == 0)
    def _():
        feed_load(x_hbm, [dy_hbm], x, x_t, dy, dy_t, sem)
        out[...] = jnp.zeros_like(out)
        d_x[...] = jnp.zeros_like(d_x)

    def write(half, index, block, value):
        part = pl.ds(pl.multiple_of(block * width_block, width_block), width_block)
        grads[0, half, index, part, :] = value

    read = lambda half, index: weights[0, half, index]
    blocks = x.shape[1] // width_block
    feed_chunk(read, write, blocks, out, d_x, x, x_t, dy, dy_t, *work)


def feed_scratch(rows, width):
    return [
        pltpu.VMEM((rows, width), BF),
        pltpu.VMEM((width, rows), BF),
        pltpu.VMEM((rows, width), BF),
        pltpu.VMEM((width, rows), BF),
        pltpu.VMEM((rows, 2 * T), BF),
        pltpu.VMEM((rows, 2 * T), BF),
        pltpu.VMEM((rows, 2 * T), BF),
        pltpu.SemaphoreType.DMA((3,)),
    ]


def feed(x, dy, weights):
    rows, width = x.shape
    chunks = weights.shape[0]
    chunk = pl.BlockSpec((1, 2, 3, width, T), lambda j: (j, 0, 0, 0, 0))
    whole = pl.BlockSpec((rows, width), lambda j: (0, 0), pipeline_mode=pl.Buffered(1))
    return pl.pallas_call(
        feed_kernel,
        grid=(chunks,),
        in_specs=[pl.BlockSpec(memory_space=pl.ANY)] * 2 + [chunk],
        out_specs=[whole, whole, chunk],
        out_shape=[
            jax.ShapeDtypeStruct((rows, width), F32),
            jax.ShapeDtypeStruct((rows, width), F32),
            jax.ShapeDtypeStruct((chunks, 2, 3, width, T), BF),
        ],
        scratch_shapes=feed_scratch(rows, width),
        compiler_params=pltpu.CompilerParams(vmem_limit_bytes=VMEM_LIMIT),
    )(x, dy, weights)


def feed_moving_kernel(zs, xs, early, kept, *refs):
    x_hbm, dy_one, dy_two, own, ready, middle, gain, whole, parts, sums = refs[:10]
    final, (d_middle, d_branch, d_attended, d_gain) = refs[10:12], refs[12:16]
    x, x_t, dy, dy_t, hidden, d_gate, d_up, sem = refs[16:24]
    out, d_x, held, w_buf, g_buf, local = refs[24:30]
    gather_sems, bufs = refs[30:32], refs[32 : 32 + BUFFERS]
    scatter_sems = refs[32 + BUFFERS :]
    chunks = own.shape[0]
    place = Place(zs, xs)
    step = pl.program_id(0)
    lag = max(0, 5 - early)
    first_kept, end_kept = kept
    width = x.shape[1]

    @pl.when(step == 0)
    def _():
        place.barrier()

    fetch = Gather(place, own, whole, *gather_sems)
    fetch.tick(step, early, chunks)

    @pl.when(step == 0)
    def _():
        load = pltpu.make_async_copy(own, held, local.at[0])
        load.start()
        load.wait()
        mine = whole.at[:, :, :, place.z, place.y, place.c * place.xs + place.x]
        store = pltpu.make_async_copy(held, mine, local.at[1])
        store.start()
        store.wait()
        feed_load(x_hbm, [dy_one, dy_two], x, x_t, dy, dy_t, sem)
        out[...] = jnp.zeros_like(out)
        d_x[...] = jnp.zeros_like(d_x)

    skipped = ready.shape[0] - early

    def weight_load(j, source, first=0):
        return pltpu.make_async_copy(source.at[first + j], w_buf.at[j % 2], local.at[2 + j % 2])

    def start_load(j):
        if early > 0:

            @pl.when(j < early)
            def _():
                weight_load(j, ready, skipped).start()

        @pl.when(j >= early)
        def _():
            weight_load(j, whole).start()

    def part_store(j):
        return pltpu.make_async_copy(g_buf.at[j % 2], parts.at[j], local.at[4 + j % 2])

    def is_kept(j):
        return (j >= first_kept) & (j < end_kept)

    engine = Scatter(place, bufs, *scatter_sems, sums)
    due = lag + first_kept
    number = end_kept - first_kept
    grads_of = lambda k: g_buf.at[(k + first_kept) % 2]
    staged(step, due + 5, number, engine.finish)
    staged(step, due + 4, number, engine.start_fourth)
    staged(step, due + 3, number, engine.start_third)
    staged(step, due + 2, number, lambda k: engine.start_second(k, grads_of(k)))
    staged(step, due + 1, number, lambda k: engine.start_first(k, grads_of(k)))

    chunk = step - lag
    if lag == 0:

        @pl.when(step == 0)
        def _():
            start_load(0)

    @pl.when((chunk >= (0 if lag == 0 else -1)) & (chunk + 1 < chunks))
    def _():
        start_load(chunk + 1)

    @pl.when((chunk >= 2) & (chunk < chunks + 2) & ~is_kept(chunk - 2))
    def _():
        part_store(chunk - 2).wait()

    @pl.when((chunk >= 0) & (chunk < chunks))
    def _():
        weight_load(chunk, whole).wait()
        slot = chunk % 2

        def read(half, index):
            return w_buf[slot, half, index].reshape(width, T)

        def write(half, index, block, value):
            shape = g_buf.shape[4:]
            g_buf[slot, half, index, block] = value.reshape(shape)

        work = (hidden, d_gate, d_up)
        feed_chunk(read, write, zs, out, d_x, x, x_t, dy, dy_t, *work)

        @pl.when(~is_kept(chunk))
        def _():
            part_store(chunk).start()

    spare = chunks % 2
    rows, size = x.shape[0], middle.shape[0]
    blocks = rows // size

    def o_load():
        return pltpu.make_async_copy(ready.at[skipped - 1], w_buf.at[spare], local.at[6])

    @pl.when(chunk == chunks - 1)
    def _():
        o_load().start()
        d_gain[...] = jnp.zeros_like(d_gain)

    @pl.when(chunk == chunks)
    def _():
        o_load().wait()

    @pl.when((chunk >= chunks) & (chunk < chunks + blocks))
    def _():
        i = chunk - chunks
        part = pl.ds(pl.multiple_of(i * size, size), size)
        values = middle[...]
        put(i, dy_one.shape[0] // size, final, (values + out[part, :]).astype(BF))
        scale = rms_scale(values)
        unit = values * scale
        d_normed = d_x[part, :]
        d_gain[...] += jnp.sum(d_normed * unit, axis=0, keepdims=True)
        total = dy[part, :].astype(F32) + norm_back(d_normed, unit, scale, gain[...])
        d_middle[...] = total
        low = total.astype(BF)
        d_branch[...] = low
        for m in range(d_attended.shape[1] // (2 * T)):
            right = joined_pieces(w_buf, spare, m)
            d_attended[:, 2 * m * T : 2 * (m + 1) * T] = nn(low, right).astype(BF)


def feed_moving(x, dy_one, dy_two, own, ready, middle, gain, inner, sizes, early, kept, collective_id):
    grp, seq = sizes
    rows, width = x.shape
    chunks, _, n, shard, lanes = own.shape
    zs = grp // (Y * C)
    tile = (2, n, zs, Y, C * seq, shard, lanes)
    one = pl.BlockSpec((1, width), lambda j: (0, 0), pipeline_mode=pl.Buffered(1))
    number = kept[1] - kept[0]
    sums = pl.BlockSpec(
        (number, 2, n, shard, lanes), lambda j: (0,) * 5, pipeline_mode=pl.Buffered(1)
    )
    lag = max(0, 5 - early)
    size = min(rows, 256)
    blocks = rows // size
    assert dy_one.shape[0] % size == 0
    steps = lag + max(chunks + max(2, blocks), kept[1] + 5)
    tail = lag + chunks
    by_rows = lambda columns: pl.BlockSpec(
        (size, columns), lambda j: (jnp.clip(j - tail, 0, blocks - 1), 0)
    )
    out = jax.ShapeDtypeStruct
    anywhere = pl.BlockSpec(memory_space=pl.ANY)
    sems = lambda *shape: pltpu.SemaphoreType.DMA(shape)
    return pl.pallas_call(
        functools.partial(feed_moving_kernel, zs, seq, early, kept),
        grid=(steps,),
        in_specs=[anywhere] * 5 + [by_rows(width), one],
        out_specs=[anywhere, anywhere, sums]
        + two_parts(size, width, dy_one.shape[0] // size, blocks, tail)
        + [by_rows(width), by_rows(width), by_rows(inner), one],
        out_shape=[
            out((chunks, *tile), BF),
            out((chunks, *tile), BF),
            out((number, 2, n, shard, lanes), F32),
            out(dy_one.shape, BF),
            out(dy_two.shape, BF),
            out((rows, width), F32),
            out((rows, width), BF),
            out((rows, inner), BF),
            out((1, width), F32),
        ],
        scratch_shapes=feed_scratch(rows, width)
        + [
            pltpu.VMEM((rows, width), F32),
            pltpu.VMEM((rows, width), F32),
            pltpu.VMEM(own.shape, BF),
            pltpu.VMEM((2, *tile), BF),
            pltpu.VMEM((2, *tile), BF),
            sems(7),
            sems(chunks, 2, zs + 2),
            sems(chunks, 2, zs + 2),
        ]
        + scatter_buffers(n, zs, seq, shard, lanes)
        + [sems(2, 2, zs + 2), sems(2, 2, zs + 2)],
        compiler_params=pltpu.CompilerParams(
            collective_id=collective_id, has_side_effects=True, vmem_limit_bytes=VMEM_LIMIT
        ),
    )(x, dy_one, dy_two, own, ready, middle, gain)


def rms_scale(values):
    return lax.rsqrt(jnp.mean(values * values, axis=-1, keepdims=True) + EPS)


def norm_back(d_normed, unit, scale, gain):
    d_unit = d_normed * gain
    return scale * (d_unit - unit * jnp.mean(d_unit * unit, axis=-1, keepdims=True))


def pieces_of(matrix):
    rows, columns = matrix.shape
    return jnp.swapaxes(matrix.reshape(rows, columns // T, T), 0, 1)


def joined(pieces):
    count, rows, _ = pieces.shape
    return jnp.swapaxes(pieces, 0, 1).reshape(rows, count * T)


def attention_chunks(matrices):
    flat = jnp.concatenate([pieces_of(m) for m in matrices], axis=0)
    pad = -flat.shape[0] % 6
    flat = jnp.pad(flat, ((0, pad), (0, 0), (0, 0)))
    return flat.reshape(-1, 2, 3, *flat.shape[1:])


def feed_chunks(matrices):
    stacked = jnp.stack([pieces_of(m) for m in matrices], axis=1)
    pad = -stacked.shape[0] % 2
    stacked = jnp.pad(stacked, ((0, pad), (0, 0), (0, 0), (0, 0)))
    return stacked.reshape(-1, 2, *stacked.shape[1:])


def body(sizes, *args):
    (
        prompt_x,
        cont_x,
        cont_len,
        prompt_cot,
        cont_cot,
        norm1_gain,
        q_weight,
        k_weight,
        v_weight,
        o_weight,
        bucket_table,
        norm2_gain,
        gate_weight,
        up_weight,
        down_weight,
    ) = args
    _, local_prompt, width = prompt_x.shape
    conts, cont_rows = cont_x.shape[1], cont_x.shape[2]
    assert prompt_x.shape[0] == 1 and cont_rows == T and local_prompt % T == 0
    seq = sizes[1]
    num_buckets, heads = bucket_table.shape
    inner = q_weight.shape[1]
    assert inner == heads * HEAD
    shard = q_weight.shape[0]
    hidden_width = gate_weight.shape[1]
    local_tiles = local_prompt // T
    tiles = local_tiles * seq
    seq_index = lax.axis_index("seq")

    split = lambda parts: (parts[0][None], parts[1].reshape(1, conts, cont_rows, width))
    cut = lambda values: (values[:local_prompt], values[local_prompt:])
    shape = Shape(tiles, local_tiles, conts)
    count = inner // T
    if can_move(sizes, shard):
        early, kept = 7, (9, 15)
        own_gain = jnp.stack([norm1_gain, norm2_gain])[None, :, None, :, None]
        own_gain = jnp.broadcast_to(own_gain, (1, 2, 1, shard, T)).astype(BF)
        cont_dy = cont_cot[0].reshape(-1, width)
        matrices = (q_weight, k_weight, v_weight, o_weight, gate_weight, up_weight, down_weight)
        (whole, own_feed, x_low, normed_one, kv, bias, queries, attended, log_norm, middle,
         normed_two, gains) = front(
            prompt_x[0], cont_x[0].reshape(-1, width), own_gain, matrices, bucket_table, cont_len,
            shape, sizes, early, 0,
        )
        _, feed_parts, kept_sums, *final, d_middle, d_branch, d_attended, d_gain_two = feed_moving(
            normed_two, prompt_cot[0], cont_dy, own_feed, whole, middle, gains[1], inner, sizes,
            early, kept, 1,
        )
        *d_x, sums, vector = back(
            queries, kv, bias, d_attended, attended, log_norm, d_branch, normed_one, feed_parts,
            whole, d_middle, x_low, gains[0], d_gain_two, cont_len, shape, sizes, kept, 2,
        )
        fed = sums.shape[0] - 4
        feed_sums = jnp.concatenate([sums[: kept[0]], kept_sums, sums[kept[0] : fed]], axis=0)
        attention_sums = jnp.concatenate([sums[fed + 1 :], sums[fed : fed + 1]], axis=0)
        attention_sums = attention_sums.reshape(-1, shard, T)
        near = vector[:heads, :4].reshape(heads, SPAN)
        far = jnp.sum(vector[:heads, 4:6], axis=-1)
        relative = (jnp.arange(SPAN) + T) % SPAN - 2 * T
        ids = jnp.concatenate([bucket_ids(relative), bucket_ids(jnp.array([-T, T]))])
        hot = (ids[:, None] == jnp.arange(num_buckets)).astype(F32)
        both = jnp.concatenate([near, far], axis=1)
        table_grad = jnp.einsum("hr,rb->bh", both, hot, precision=lax.Precision.HIGHEST)
        gain_grads = vector[heads:].reshape(2, sizes[0] * seq, shard)
        me = lax.axis_index("grp") * seq + seq_index
        norm1_grad, norm2_grad = lax.dynamic_index_in_dim(gain_grads, me, 1, keepdims=False)
    else:
        x_low = jnp.concatenate([prompt_x[0], cont_x[0].reshape(-1, width)], axis=0)
        dy_low = jnp.concatenate([prompt_cot[0], cont_cot[0].reshape(-1, width)], axis=0)
        x = x_low.astype(F32)
        dy = dy_low.astype(F32)
        lanes = jnp.zeros((shard, T - 2), F32)
        gains = jnp.concatenate([norm1_gain[:, None], norm2_gain[:, None], lanes], axis=1)
        own_attention = attention_chunks([q_weight, k_weight, v_weight, o_weight, gains]).astype(BF)
        own_feed = feed_chunks([gate_weight, up_weight, down_weight]).astype(BF)
        attention_whole = gather(own_attention, sizes)
        flat = attention_whole.reshape(-1, width, T)
        q_full, k_full, v_full, o_full = [
            joined(flat[i * count : (i + 1) * count]) for i in range(4)
        ]
        gain_one = flat[4 * count, :, 0].astype(F32)
        gain_two = flat[4 * count, :, 1].astype(F32)
        scale_one = rms_scale(x)
        unit_one = x * scale_one
        normed_one = (unit_one * gain_one).astype(BF)
        kv = nn(normed_one, jnp.concatenate([k_full, v_full], axis=1)).astype(BF)
        queries = nn(normed_one, q_full).astype(BF)
        gathered = lax.all_gather(kv[:local_prompt], "seq", axis=0, tiled=True)
        others = jnp.roll(gathered, -seq_index * local_prompt, axis=0)[local_prompt:]
        every = jnp.concatenate([kv, others], axis=0)
        keys, values = every[:, :inner], every[:, inner:]
        base = (seq_index * local_tiles).reshape(1).astype(jnp.int32)
        one_hot = band_one_hot(num_buckets)
        bias = jnp.einsum("cqkb,bh->hcqk", one_hot, bucket_table, precision=lax.Precision.HIGHEST)
        attended, log_norm = attend(queries, keys, values, bias, cont_len, base, shape)
        middle = x + nt(attended, o_full)
        scale_two = rms_scale(middle)
        unit_two = middle * scale_two
        normed_two = (unit_two * gain_two).astype(BF)
        out_sum, d_normed_two, feed_grads = feed(normed_two, dy_low, gather(own_feed, sizes))
        feed_sums = scatter(feed_grads)
        final = cut((middle + out_sum).astype(BF))
        d_gain_two = jnp.sum(d_normed_two * unit_two, axis=0)
        d_middle = dy + norm_back(d_normed_two, unit_two, scale_two, gain_two)
        d_branch = d_middle.astype(BF)
        d_attended = nn(d_branch, o_full).astype(BF)
        d_o = tn(d_branch, attended)
        d_queries, d_keys, d_values, d_bias = attend_back(
            queries, keys, values, bias, d_attended, attended, log_norm, cont_len, base, shape
        )
        d_table = jnp.einsum("hcqk,cqkb->bh", d_bias, one_hot, precision=lax.Precision.HIGHEST)
        d_kv = jnp.concatenate([d_keys, d_values], axis=1)
        prompt_parts = jnp.concatenate([d_kv[:local_prompt], d_kv[shape.rows :]], axis=0)
        prompt_parts = jnp.roll(prompt_parts, seq_index * local_prompt, axis=0)
        d_prompt = lax.psum_scatter(prompt_parts, "seq", scatter_dimension=0, tiled=True)
        d_kv = jnp.concatenate([d_prompt, d_kv[local_prompt : shape.rows]], axis=0)
        d_normed_one = nt(d_queries, q_full) + nt(d_kv, jnp.concatenate([k_full, v_full], axis=1))
        d_q = tn(normed_one, d_queries)
        d_kv_weight = tn(normed_one, d_kv)
        d_gain_one = jnp.sum(d_normed_one * unit_one, axis=0)
        d_x = d_middle + norm_back(d_normed_one, unit_one, scale_one, gain_one)
        d_x = cut(d_x.astype(BF))
        attention_parts = attention_chunks([d_q, d_kv_weight, d_o]).astype(BF)
        attention_sums = scatter(attention_parts).reshape(-1, shard, T)
        norm1_grad = lax.psum_scatter(d_gain_one, ("grp", "seq"), scatter_dimension=0, tiled=True)
        norm2_grad = lax.psum_scatter(d_gain_two, ("grp", "seq"), scatter_dimension=0, tiled=True)
        table_grad = lax.psum(d_table, ("grp", "seq"))
    feed_sums = feed_sums.reshape(-1, 3, shard, T)[: hidden_width // T]
    gate_grad, up_grad, down_grad = [joined(feed_sums[:, i]) for i in range(3)]
    q_grad, k_grad, v_grad, o_grad = [
        joined(attention_sums[i * count : (i + 1) * count]) for i in range(4)
    ]
    return (
        *split(final),
        *split(d_x),
        norm1_grad,
        q_grad,
        k_grad,
        v_grad,
        o_grad,
        table_grad,
        norm2_grad,
        gate_grad,
        up_grad,
        down_grad,
    )


def solution(mesh):
    sizes = (mesh.shape["grp"], mesh.shape["seq"])
    rows = P("grp", "seq", None)
    conts = P("grp", "seq", None, None)
    shard = P(("grp", "seq"), None)
    gain = P(("grp", "seq"))
    in_specs = (rows, conts, P("grp", "seq"), rows, conts, gain, shard, shard, shard, shard)
    in_specs += (P(), gain, shard, shard, shard)
    out_specs = (rows, conts, rows, conts, gain, shard, shard, shard, shard, P(), gain)
    out_specs += (shard, shard, shard)
    return jax.shard_map(
        functools.partial(body, sizes),
        mesh=mesh,
        in_specs=in_specs,
        out_specs=out_specs,
        check_vma=False,
    )
```

```python
import functools

import jax
import jax.numpy as jnp
from jax import lax
from jax.experimental import pallas as pl
from jax.experimental.pallas import tpu as pltpu
from jax.sharding import PartitionSpec as P

EPS = 1e-06
LIMITS = (8, 12, 16, 23, 32, 46, 64, 91)
NEGATIVE = -1e30
MESH = pl.DeviceIdType.MESH
T = 128
HEAD = 64
BANDS = 5
BF = jnp.bfloat16
F32 = jnp.float32
VMEM_LIMIT = 63 * 2**20
Y = 2
C = 2


def nn(left, right):
    return jnp.dot(left, right, preferred_element_type=F32)


def nt(left, right):
    return lax.dot_general(left, right, (((1,), (1,)), ((), ())), preferred_element_type=F32)


def tn(left, right):
    return lax.dot_general(left, right, (((0,), (0,)), ((), ())), preferred_element_type=F32)


def bucket_ids(relative):
    distance = jnp.abs(relative)
    coarse = 7 + sum(((distance >= boundary).astype(jnp.int32) for boundary in LIMITS))
    return jnp.where(distance < 8, distance, coarse) + 16 * (relative > 0).astype(jnp.int32)


def band_one_hot(num_buckets):
    band = jnp.arange(BANDS)[:, None, None] - 2
    query = jnp.arange(T)[None, :, None]
    key = jnp.arange(T)[None, None, :]
    ids = bucket_ids(band * T + key - query)
    return (ids[..., None] == jnp.arange(num_buckets)).astype(F32)


def can_move(sizes, rows):
    zs = sizes[0] // (Y * C)
    return rows % 16 == 0 and sizes[1] == 2 and sizes[0] % (Y * C) == 0 and zs in (2, 4, 8, 16)


class Place:
    def __init__(self, zs, xs):
        grp = lax.axis_index("grp")
        self.zs, self.xs = zs, xs
        self.x = lax.axis_index("seq")
        self.z = grp // (Y * C)
        self.y = (grp // C) % Y
        self.c = grp % C

    def device(self, z=None, y=None, c=None, x=None):
        z = self.z if z is None else z
        y = self.y if y is None else y
        c = self.c if c is None else c
        x = self.x if x is None else x
        return (z * (Y * C) + y * C + c, x)

    def peers(self):
        around = [self.device(z=(self.z + d) % self.zs) for d in range(1, self.zs)]
        return around + [
            self.device(y=1 - self.y),
            self.device(x=1 - self.x),
            self.device(c=1 - self.c),
        ]

    def barrier(self):
        sem = pltpu.get_barrier_semaphore()
        peers = self.peers()
        for peer in peers:
            pl.semaphore_signal(sem, inc=1, device_id=peer, device_id_type=MESH)
        pl.semaphore_wait(sem, len(peers))


def remote(src, dst, send_sem, recv_sem, device):
    return pltpu.make_async_remote_copy(
        src_ref=src,
        dst_ref=dst,
        send_sem=send_sem,
        recv_sem=recv_sem,
        device_id=device,
        device_id_type=MESH,
    )


def staged(step, offset, count, action):
    @pl.when((step >= offset) & (step < count + offset))
    def _():
        action(step - offset)


class Gather:
    def __init__(self, place, own, whole, send, recv):
        self.p, self.own, self.whole, self.send, self.recv = place, own, whole, send, recv

    def copy(self, k, half, index, src, dst, device):
        return remote(src, dst, self.send.at[k, half, index], self.recv.at[k, half, index], device)

    def alone(self, k, half):
        p = self.p
        dst = self.whole.at[k, half, :, p.z, p.y, p.c * p.xs + p.x]
        src = self.own.at[k, half]
        if half == 0:
            return [self.copy(k, half, 0, src, dst, p.device(x=1 - p.x))]
        peers = [p.device(z=(p.z + d) % p.zs) for d in range(1, p.zs)]
        return [self.copy(k, half, i, src, dst, peer) for i, peer in enumerate(peers)]

    def second(self, k, half):
        p = self.p
        if half == 0:
            view = self.whole.at[k, half, :, p.z, p.y, pl.ds(p.c * p.xs, p.xs)]
            peers = [p.device(z=(p.z + d) % p.zs) for d in range(1, p.zs)]
            return [self.copy(k, half, 1 + i, view, view, peer) for i, peer in enumerate(peers)]
        view = self.whole.at[k, half, :, :, p.y, p.c * p.xs + p.x]
        return [self.copy(k, half, p.zs - 1, view, view, p.device(y=1 - p.y))]

    def third(self, k, half):
        p = self.p
        if half == 0:
            view = self.whole.at[k, half, :, :, p.y, pl.ds(p.c * p.xs, p.xs)]
            peer = p.device(y=1 - p.y)
        else:
            view = self.whole.at[k, half, :, :, :, p.c * p.xs + p.x]
            peer = p.device(x=1 - p.x)
        return [self.copy(k, half, p.zs, view, view, peer)]

    def fourth(self, k, half):
        p = self.p
        view = self.whole.at[k, half, :, :, :, pl.ds(p.c * p.xs, p.xs)]
        return [self.copy(k, half, p.zs + 1, view, view, p.device(c=1 - p.c))]

    def tick(self, step, first, end):
        stages = (self.alone, self.second, self.third, self.fourth)

        def advance(offset, k):
            for half in (0, 1):
                if offset > 0:
                    for copy in stages[offset - 1](k, half):
                        copy.wait_recv()
                if offset < 4:
                    for copy in stages[offset](k, half):
                        copy.start()
                else:
                    for stage in stages:
                        for copy in stage(k, half):
                            copy.wait_send()

        for offset in range(5):
            staged(step, offset, end - first, lambda k, offset=offset: advance(offset, first + k))


def gather(own, sizes):
    return lax.all_gather(own, ("grp", "seq"), axis=3, tiled=True)


class Scatter:
    def __init__(self, place, bufs, send, recv, out):
        self.p, self.send, self.recv, self.out = place, send, recv, out
        (self.in1, self.in2, self.sum1, self.sum2) = bufs[:4]
        self.in3, self.in4, self.sum3 = bufs[4:6], bufs[6:8], bufs[8:10]

    def copy(self, k, half, index, src, dst, device):
        slot = k % 2
        return remote(
            src, dst, self.send.at[slot, half, index], self.recv.at[slot, half, index], device
        )

    def first(self, k, half, part):
        p = self.p
        src = part.at[half, :, :, :, pl.ds((1 - p.c) * p.xs, p.xs)]
        return self.copy(k, half, 0, src, self.in1.at[k % 2, half], p.device(c=1 - p.c))

    def second(self, k, half):
        p = self.p
        if half == 0:
            src, peer = self.sum1.at[k % 2, half, :, :, 1 - p.y], p.device(y=1 - p.y)
        else:
            src, peer = self.sum1.at[k % 2, half, :, :, :, 1 - p.x], p.device(x=1 - p.x)
        return self.copy(k, half, 1, src, self.in2.at[k % 2, half], peer)

    def third(self, k, half):
        p, slot = self.p, k % 2
        if half == 1:
            src = self.sum2.at[slot, half, :, :, 1 - p.y]
            return [self.copy(k, half, 2, src, self.in3[1].at[slot], p.device(y=1 - p.y))]
        copies = []
        for d in range(1, p.zs):
            target = (p.z + d) % p.zs
            src = self.sum2.at[slot, half, :, target]
            dst = self.in3[0].at[slot, d - 1]
            copies.append(self.copy(k, half, 1 + d, src, dst, p.device(z=target)))
        return copies

    def fourth(self, k, half):
        p, slot = self.p, k % 2
        if half == 0:
            src = self.sum3[0].at[slot, :, 1 - p.x]
            return [self.copy(k, half, p.zs + 1, src, self.in4[0].at[slot, 0], p.device(x=1 - p.x))]
        copies = []
        for d in range(1, p.zs):
            target = (p.z + d) % p.zs
            src = self.sum3[1].at[slot, :, target]
            dst = self.in4[1].at[slot, d - 1]
            copies.append(self.copy(k, half, 2 + d, src, dst, p.device(z=target)))
        return copies

    def finish(self, k):
        p, slot = self.p, k % 2
        for half in (0, 1):
            total = self.sum3[half][slot, :, p.x if half == 0 else p.z].astype(F32)
            for i, copy in enumerate(self.fourth(k, half)):
                copy.wait_recv()
                copy.wait_send()
                total = total + self.in4[half][slot, i].astype(F32)
            self.out(k, half, total)

    def start_fourth(self, k):
        p, slot = self.p, k % 2
        for half in (0, 1):
            for copy in self.third(k, half):
                copy.wait_recv()
                copy.wait_send()
            for i in range(self.sum2.shape[2]):
                if half == 0:
                    total = self.sum2[slot, half, i, p.z].astype(F32)
                    for d in range(1, p.zs):
                        total = total + self.in3[0][slot, d - 1, i].astype(F32)
                else:
                    total = self.sum2[slot, half, i, :, p.y].astype(F32)
                    total = total + self.in3[1][slot, i].astype(F32)
                self.sum3[half][slot, i] = total.astype(BF)
            for copy in self.fourth(k, half):
                copy.start()

    def start_third(self, k):
        p, slot = self.p, k % 2
        for half in (0, 1):
            copy = self.second(k, half)
            copy.wait_recv()
            copy.wait_send()
            for i in range(self.sum2.shape[2]):
                if half == 0:
                    mine = self.sum1[slot, half, i, :, p.y]
                else:
                    mine = self.sum1[slot, half, i, :, :, p.x]
                total = mine.astype(F32) + self.in2[slot, half, i].astype(F32)
                self.sum2[slot, half, i] = total.astype(BF)
            for copy in self.third(k, half):
                copy.start()

    def start_second(self, k, part):
        p, slot = self.p, k % 2
        for half in (0, 1):
            copy = self.first(k, half, part)
            copy.wait_recv()
            copy.wait_send()

            def add(z, _, half=half):
                for i in range(self.sum1.shape[2]):
                    mine = part[half, i, z, :, pl.ds(p.c * p.xs, p.xs)]
                    total = mine.astype(F32) + self.in1[slot, half, i, z].astype(F32)
                    self.sum1[slot, half, i, z] = total.astype(BF)
                return 0

            lax.fori_loop(0, p.zs, add, 0)
            self.second(k, half).start()

    def start_first(self, k, part):
        for half in (0, 1):
            self.first(k, half, part).start()


BUFFERS = 10


def scatter_buffers(n, zs, xs, rows, lanes):
    block = (rows, lanes)
    shapes = [
        (2, 2, n, zs, Y, xs, *block),
        (2, 2, n, zs, 2, *block),
        (2, 2, n, zs, Y, xs, *block),
        (2, 2, n, zs, 2, *block),
        (2, zs - 1, n, 2, *block),
        (2, n, zs, *block),
        (2, 1, n, *block),
        (2, zs - 1, n, *block),
        (2, n, 2, *block),
        (2, n, zs, *block),
    ]
    return [pltpu.VMEM(shape, BF) for shape in shapes]


def scatter(parts):
    return lax.psum_scatter(parts, ("grp", "seq"), scatter_dimension=3, tiled=True).astype(F32)


class Shape:
    def __init__(self, tiles, local_tiles, conts):
        self.tiles, self.local_tiles, self.conts = tiles, local_tiles, conts
        self.rows = (local_tiles + conts) * T
        self.keys = self.rows + (tiles - local_tiles) * T
        self.parts = [(0, range(local_tiles)), (self.rows, range(local_tiles, tiles))]
        self.parts = [(start, js) for start, js in self.parts if len(js)]


def band_of(key_tile, query_tile):
    return jnp.clip(key_tile - query_tile, -2, 2) + 2


def tile_lanes():
    first_half = lax.broadcasted_iota(jnp.int32, (T, 2 * HEAD), 1) < HEAD
    place = lax.broadcasted_iota(jnp.int32, (T, T), 1)
    return first_half, place


def tile_rows(i):
    return pl.ds(pl.multiple_of(i * T, T), T)


def attend_tile(shape, i, is_cont, live, base, q, k, v, bias, out, norm):
    first_half, place = tile_lanes()
    rows = tile_rows(i)
    queries = q[rows, :]
    query_tile = shape.tiles if is_cont else base + i
    mixed = []
    for h in range(2):
        mine = first_half if h == 0 else ~first_half
        masked = jnp.where(mine, queries, jnp.zeros_like(queries))
        logits = []
        for start, js in shape.parts:
            scores = nt(masked, k[start : start + len(js) * T, :])
            for at, j in enumerate(js):
                band = band_of(lax.rem(base + j, shape.tiles), query_tile)
                logits.append(scores[:, at * T : (at + 1) * T] + bias[h, band])
        if is_cont:
            own = nt(masked, k[rows, :]) + bias[h, 2]
            logits.append(jnp.where(place < live[0, i - shape.local_tiles], own, NEGATIVE))
        top = jnp.max(functools.reduce(jnp.maximum, logits), axis=1, keepdims=True)
        weights = [jnp.exp(part - top) for part in logits]
        total = jnp.sum(functools.reduce(jnp.add, weights), axis=1, keepdims=True)
        inverse = 1.0 / total
        probs = [(weight * inverse).astype(BF) for weight in weights]
        result = None
        for start, js in shape.parts:
            left = jnp.concatenate([probs[j] for j in js], axis=1)
            term = nn(left, v[start : start + len(js) * T, :])
            result = term if result is None else result + term
        if is_cont:
            result = result + nn(probs[shape.tiles], v[rows, :])
        mixed.append(result)
        norm[h, rows, :] = top + jnp.log(total)
    out[rows, :] = jnp.where(first_half, mixed[0], mixed[1]).astype(BF)


def for_tiles(shape, conts, action):
    first, last = (shape.local_tiles, shape.local_tiles + shape.conts) if conts else (0, shape.local_tiles)

    def one(i, carry):
        action(i, conts)
        return carry

    lax.fori_loop(first, last, one, 0)


def attend_kernel(shape, live, base, q, k, v, bias, out, norm):
    for conts in (False, True):
        for_tiles(
            shape,
            conts,
            lambda i, c: attend_tile(shape, i, c, live, base[0], q, k, v, bias, out, norm),
        )


def pair_block(n):
    return pl.BlockSpec((n, 2 * HEAD), lambda h, *_: (0, h))


def attend(q, k, v, bias, live, base, shape):
    rows, width = q.shape
    pairs = width // (2 * HEAD)
    return pl.pallas_call(
        functools.partial(attend_kernel, shape),
        grid_spec=pltpu.PrefetchScalarGridSpec(
            num_scalar_prefetch=2,
            grid=(pairs,),
            in_specs=[
                pair_block(rows),
                pair_block(shape.keys),
                pair_block(shape.keys),
                pl.BlockSpec((2, BANDS, T, T), lambda h, *_: (h, 0, 0, 0)),
            ],
            out_specs=[pair_block(rows), pl.BlockSpec((2, rows, 1), lambda h, *_: (h, 0, 0))],
        ),
        out_shape=[
            jax.ShapeDtypeStruct((rows, width), BF),
            jax.ShapeDtypeStruct((2 * pairs, rows, 1), F32),
        ],
        compiler_params=pltpu.CompilerParams(vmem_limit_bytes=VMEM_LIMIT),
    )(live, base, q, k, v, bias)


def attend_back_tile(
    shape, i, is_cont, live, base, q, k, v, bias, grad, out, norm, d_q, d_bias, k_sum, v_sum
):
    first_half, place = tile_lanes()
    rows = tile_rows(i)
    queries = q[rows, :]
    grads = grad[rows, :]
    query_tile = shape.tiles if is_cont else base + i
    overlap = grads.astype(F32) * out[rows, :].astype(F32)
    mixed = []
    for h in range(2):
        mine = first_half if h == 0 else ~first_half
        masked = jnp.where(mine, queries, jnp.zeros_like(queries))
        masked_grad = jnp.where(mine, grads, jnp.zeros_like(grads))
        inner = jnp.sum(jnp.where(mine, overlap, 0.0), axis=1, keepdims=True)
        log_norm = norm[h, rows, :]

        def piece(keys, bands, allowed):
            scores = nt(masked, k[keys, :])
            d_probs = nt(masked_grad, v[keys, :])
            probs_low, scores_low = [], []
            for at, band in enumerate(bands):
                cols = slice(at * T, (at + 1) * T)
                logits = scores[:, cols] + bias[h, band]
                if allowed is not None:
                    logits = jnp.where(allowed, logits, NEGATIVE)
                probs = jnp.exp(logits - log_norm)
                d_scores = probs * (d_probs[:, cols] - inner)
                d_bias[h, band] += d_scores
                probs_low.append(probs.astype(BF))
                scores_low.append(d_scores.astype(BF))
            probs_low = jnp.concatenate(probs_low, axis=1)
            scores_low = jnp.concatenate(scores_low, axis=1)
            v_sum[keys, :] += tn(probs_low, masked_grad)
            k_sum[keys, :] += tn(scores_low, masked)
            return nn(scores_low, k[keys, :])

        result = None
        for start, js in shape.parts:
            bands = [band_of(lax.rem(base + j, shape.tiles), query_tile) for j in js]
            term = piece(pl.ds(start, len(js) * T), bands, None)
            result = term if result is None else result + term
        if is_cont:
            result = result + piece(rows, [2], place < live[0, i - shape.local_tiles])
        mixed.append(result)
    d_q[rows, :] = jnp.where(first_half, mixed[0], mixed[1]).astype(BF)


def attend_back_kernel(
    shape, live, base, q, k, v, bias, grad, out, norm, d_q, d_k, d_v, d_bias, k_sum, v_sum
):
    k_sum[...] = jnp.zeros_like(k_sum)
    v_sum[...] = jnp.zeros_like(v_sum)
    d_bias[...] = jnp.zeros_like(d_bias)
    refs = (q, k, v, bias, grad, out, norm, d_q, d_bias, k_sum, v_sum)
    for conts in (False, True):
        for_tiles(shape, conts, lambda i, c: attend_back_tile(shape, i, c, live, base[0], *refs))
    d_k[...] = k_sum[...].astype(BF)
    d_v[...] = v_sum[...].astype(BF)


def attend_back(q, k, v, bias, grad, out, norm, live, base, shape):
    rows, width = q.shape
    pairs = width // (2 * HEAD)
    keys = shape.keys
    bands = pl.BlockSpec((2, BANDS, T, T), lambda h, *_: (h, 0, 0, 0))
    return pl.pallas_call(
        functools.partial(attend_back_kernel, shape),
        grid_spec=pltpu.PrefetchScalarGridSpec(
            num_scalar_prefetch=2,
            grid=(pairs,),
            in_specs=[
                pair_block(rows),
                pair_block(keys),
                pair_block(keys),
                bands,
                pair_block(rows),
                pair_block(rows),
                pl.BlockSpec((2, rows, 1), lambda h, *_: (h, 0, 0)),
            ],
            out_specs=[pair_block(rows), pair_block(keys), pair_block(keys), bands],
            scratch_shapes=[pltpu.VMEM((keys, 2 * HEAD), F32), pltpu.VMEM((keys, 2 * HEAD), F32)],
        ),
        out_shape=[
            jax.ShapeDtypeStruct((rows, width), BF),
            jax.ShapeDtypeStruct((keys, width), BF),
            jax.ShapeDtypeStruct((keys, width), BF),
            jax.ShapeDtypeStruct((2 * pairs, BANDS, T, T), F32),
        ],
        compiler_params=pltpu.CompilerParams(vmem_limit_bytes=VMEM_LIMIT),
    )(live, base, q, k, v, bias, grad, out, norm)


ORDER = (1, 2, 0, 3)
FIRST_PAIR = 8


def joined_pieces(w_buf, slot, m):
    pieces = [w_buf[slot, j // 3, j % 3] for j in (2 * m, 2 * m + 1)]
    return jnp.concatenate([piece.reshape(-1, T) for piece in pieces], axis=1)


def front_kernel(zs, xs, shape, early, live, *refs):
    (prompt_x, cont_x, own_gain, *weights) = refs[:10]
    table = refs[10]
    (whole, own_out, x_out, normed_out, kv_out, bias_out) = refs[11:17]
    (q, attended, norm, middle, normed_two, gains) = refs[17:23]
    (x, normed, kv, bias, held, w_buf, gain_whole) = refs[23:30]
    (local, kv_sems, send, recv, gain_send, gain_recv) = refs[30:36]
    place = Place(zs, xs)
    step = pl.program_id(0)
    rows, width = x.shape
    prompt = shape.local_tiles * T
    pairs = q.shape[0]
    size = middle.shape[0]
    blocks = rows // size
    last = FIRST_PAIR + pairs
    count = 4 + early
    feed_weights = weights[4:]
    columns = feed_weights[0].shape[1] // T

    def x_load(i):
        source, part = ((prompt_x, pl.ds(0, prompt)), (cont_x, pl.ds(prompt, rows - prompt)))[i]
        return pltpu.make_async_copy(source, x.at[part], local.at[i])

    def mine_store():
        mine = whole.at[:, :, :, place.z, place.y, place.c * place.xs + place.x]
        return pltpu.make_async_copy(held.at[pl.ds(0, count)], mine, local.at[2])

    feed_own = held.at[pl.ds(4, held.shape[0] - 4)]
    kept = ((feed_own, own_out), (x, x_out), (normed, normed_out), (bias, bias_out), (kv, kv_out))

    def result(i):
        return pltpu.make_async_copy(*kept[i], local.at[3 + i])

    def weight_load(k):
        return pltpu.make_async_copy(whole.at[k], w_buf.at[k % 2], local.at[8 + k])

    @pl.when(step == 0)
    def _():
        place.barrier()
        x_load(0).start()
        x_load(1).start()
        for c, matrix in enumerate(ORDER):
            for j in range(6):
                held[c, j // 3, j % 3] = weights[matrix][:, j * T : (j + 1) * T].astype(BF)
        gain_whole[0, :, :, place.z, place.y, place.c * place.xs + place.x] = own_gain[0]

    Gather(place, own_gain, gain_whole, gain_send, gain_recv).tick(step, 0, 1)
    Gather(place, held, whole, send, recv).tick(step, 0, count)

    @pl.when(step == 0)
    def _():
        def convert(j, carry):
            part = pl.ds(pl.multiple_of(j * T, T), T)
            for i in range(3):
                held[4 + j // 2, j % 2, i] = feed_weights[i][:, part].astype(BF)
            return carry

        lax.fori_loop(0, columns, convert, 0)
        if columns % 2:
            held[4 + columns // 2, 1] = jnp.zeros(held.shape[2:], BF)
        mine_store().start()
        mine_store().wait()
        result(0).start()
        x_load(0).wait()
        x_load(1).wait()
        result(1).start()

    @pl.when(step == 1)
    def _():
        query = lax.broadcasted_iota(jnp.int32, (T, T), 0)
        key = lax.broadcasted_iota(jnp.int32, (T, T), 1)
        half = table.shape[0] // 2
        ids = [bucket_ids(band * T + key - query) for band in (-1, 0, 1)]
        found = (range(1, half), [*range(half), *range(half + 1, 2 * half)], range(half + 1, 2 * half))

        def one(h, carry):
            bias[h, 0] = jnp.full((T, T), table[half - 1, h])
            bias[h, 4] = jnp.full((T, T), table[2 * half - 1, h])
            for band in range(3):
                value = jnp.zeros((T, T), F32)
                for bucket in found[band]:
                    value = jnp.where(ids[band] == bucket, table[bucket, h], value)
                bias[h, 1 + band] = value
            return carry

        lax.fori_loop(0, bias.shape[0], one, 0)

    for k in range(4):

        @pl.when(step == 4 + k)
        def _(k=k):
            weight_load(k).start()

    def by_rows(action):
        def one(i, carry):
            action(pl.ds(pl.multiple_of(i * size, size), size))
            return carry

        lax.fori_loop(0, blocks, one, 0)

    @pl.when(step == 4)
    def _():
        result(3).start()
        eye = lax.broadcasted_iota(jnp.int32, (T, T), 0) == lax.broadcasted_iota(jnp.int32, (T, T), 1)
        for g in range(2):
            column = gain_whole[0, g, 0].reshape(width, T).astype(F32)
            for i in range(width // T):
                cols = slice(i * T, (i + 1) * T)
                gains[g, :, cols] = jnp.sum(jnp.where(eye, column[cols], 0.0), axis=0, keepdims=True)

        def norm_rows(part):
            values = x[part, :].astype(F32)
            scale = lax.rsqrt(jnp.mean(values * values, axis=-1, keepdims=True) + EPS)
            normed[part, :] = (values * scale * gains[0]).astype(BF)

        by_rows(norm_rows)
        result(2).start()

    def project(slot, target):
        for m in range(pairs // 2):
            right = joined_pieces(w_buf, slot, m)

            def rows_of_product(part, m=m, right=right):
                product = nn(normed[part, :], right).astype(BF)
                target[2 * m, part, :] = product[:, :T]
                target[2 * m + 1, part, :] = product[:, T:]

            by_rows(rows_of_product)

    def kv_send(side, p):
        src = kv.at[side, p, pl.ds(0, prompt)]
        dst = kv.at[side, p, pl.ds(rows, prompt)]
        peer = place.device(x=1 - place.x)
        return remote(src, dst, kv_sems.at[0, side, p], kv_sems.at[1, side, p], peer)

    for k in range(3):

        @pl.when(step == 5 + k)
        def _(k=k):
            weight_load(k).wait()
            project(k % 2, kv.at[k] if k < 2 else q)
            if k < 2:
                for p in range(pairs):
                    kv_send(k, p).start()

    @pl.when(step == FIRST_PAIR)
    def _():
        weight_load(3).wait()

    @pl.when((step >= FIRST_PAIR) & (step < last))
    def _():
        p = step - FIRST_PAIR
        for side in range(2):
            kv_send(side, p).wait_recv()
            kv_send(side, p).wait_send()
        base = place.x * shape.local_tiles
        inputs = (q.at[p], kv.at[0, p], kv.at[1, p], bias.at[pl.ds(2 * p, 2)], attended.at[p], norm)
        for conts in (False, True):
            for_tiles(shape, conts, lambda i, c: attend_tile(shape, i, c, live, base, *inputs))

    @pl.when(step == last)
    def _():
        result(4).start()

    @pl.when(step >= last)
    def _():
        part = pl.ds(pl.multiple_of((step - last) * size, size), size)
        branch = None
        for m in range(pairs // 2):
            left = jnp.concatenate([attended[2 * m + e, part, :] for e in range(2)], axis=1)
            term = nt(left, joined_pieces(w_buf, 1, m))
            branch = term if branch is None else branch + term
        total = x[part, :].astype(F32) + branch
        middle[...] = total
        scale = lax.rsqrt(jnp.mean(total * total, axis=-1, keepdims=True) + EPS)
        normed_two[...] = (total * scale * gains[1]).astype(BF)

    @pl.when(step == last + blocks - 1)
    def _():
        for i in range(len(kept)):
            result(i).wait()


def front(prompt_x, cont_x, own_gain, weights, table, live, shape, sizes, early, collective_id):
    grp, seq = sizes
    rows, width = shape.rows, prompt_x.shape[1]
    shard, inner = weights[0].shape
    feed_columns = weights[4].shape[1] // T
    pairs, keys, heads = inner // (2 * HEAD), shape.keys, table.shape[1]
    assert pairs == 6 and table.shape[0] == 32 and keys - rows == prompt_x.shape[0]
    zs = grp // (Y * C)
    chunks = 4 + (feed_columns + 1) // 2
    count = 4 + early
    own = (2, 3, shard, T)
    tile = (2, 3, zs, Y, C * seq, shard, T)
    size = min(rows, 256)
    blocks = rows // size
    last = FIRST_PAIR + pairs
    steps = last + blocks
    assert count + 4 <= steps and count <= chunks
    full = lambda *dims: pl.BlockSpec(
        dims, lambda s, *_: (0,) * len(dims), pipeline_mode=pl.Buffered(1)
    )
    by_rows = pl.BlockSpec((size, width), lambda s, *_: (jnp.clip(s - last, 0, blocks - 1), 0))
    anywhere = pl.BlockSpec(memory_space=pl.ANY)
    sems = lambda *dims: pltpu.SemaphoreType.DMA(dims)
    out = jax.ShapeDtypeStruct
    return pl.pallas_call(
        functools.partial(front_kernel, zs, seq, shape, early),
        grid_spec=pltpu.PrefetchScalarGridSpec(
            num_scalar_prefetch=1,
            grid=(steps,),
            in_specs=[anywhere, anywhere, full(*own_gain.shape)]
            + [full(*w.shape) for w in weights]
            + [pl.BlockSpec(memory_space=pltpu.SMEM)],
            out_specs=[anywhere] * 6
            + [
                full(pairs, rows, 2 * HEAD),
                full(pairs, rows, 2 * HEAD),
                pl.BlockSpec(
                    (2, rows, 1), lambda s, *_: (jnp.clip(s - FIRST_PAIR, 0, pairs - 1), 0, 0)
                ),
                by_rows,
                by_rows,
                full(2, 1, width),
            ],
            scratch_shapes=[
                pltpu.VMEM((rows, width), BF),
                pltpu.VMEM((rows, width), BF),
                pltpu.VMEM((2, pairs, keys, 2 * HEAD), BF),
                pltpu.VMEM((heads, BANDS, T, T), F32),
                pltpu.VMEM((chunks, *own), BF),
                pltpu.VMEM((2, *tile), BF),
                pltpu.VMEM((1, 2, 1, zs, Y, C * seq, shard, T), BF),
                sems(12),
                sems(2, 2, pairs),
                sems(count, 2, zs + 2),
                sems(count, 2, zs + 2),
                sems(1, 2, zs + 2),
                sems(1, 2, zs + 2),
            ],
        ),
        out_shape=[
            out((count, *tile), BF),
            out((chunks - 4, *own), BF),
            out((rows, width), BF),
            out((rows, width), BF),
            out((2, pairs, keys, 2 * HEAD), BF),
            out((heads, BANDS, T, T), F32),
            out((pairs, rows, 2 * HEAD), BF),
            out((pairs, rows, 2 * HEAD), BF),
            out((2 * pairs, rows, 1), F32),
            out((rows, width), F32),
            out((rows, width), BF),
            out((2, 1, width), F32),
        ],
        compiler_params=pltpu.CompilerParams(
            collective_id=collective_id, has_side_effects=True, vmem_limit_bytes=VMEM_LIMIT
        ),
    )(live, prompt_x, cont_x, own_gain, *weights, table)


SPAN = 4 * T
VECTOR_ROWS = 8


def turned(tile):
    row = lax.broadcasted_iota(jnp.int32, tile.shape, 0)
    for bit in range(7):
        moved = pltpu.roll(tile, SPAN - (1 << bit), 1)
        tile = jnp.where((row >> bit) & 1 == 1, moved, tile)
    return tile


def band_sums(d_bias, h):
    near = jnp.concatenate([d_bias[h, 1], d_bias[h, 2], d_bias[h, 3]], axis=1)
    near = jnp.concatenate([near, jnp.zeros((T, T), F32)], axis=1)
    diagonal = jnp.sum(turned(near), axis=0, keepdims=True)
    rows = [diagonal[:, i * T : (i + 1) * T] for i in range(4)]
    rows += [jnp.sum(d_bias[h, band], axis=0, keepdims=True) for band in (0, 4)]
    return jnp.concatenate(rows + [jnp.zeros((2, T), F32)], axis=0)


def put(i, first_blocks, targets, value):
    @pl.when(i < first_blocks)
    def _():
        targets[0][...] = value

    @pl.when(i >= first_blocks)
    def _():
        targets[1][...] = value


def two_parts(size, width, first_blocks, blocks, first_step):
    one = lambda s, *_: (jnp.clip(s - first_step, 0, first_blocks - 1), 0)
    two = lambda s, *_: (jnp.clip(s - first_step - first_blocks, 0, blocks - first_blocks - 1), 0)
    return [pl.BlockSpec((size, width), one), pl.BlockSpec((size, width), two)]


def rows_of(vector):
    return [vector[:, i * T : (i + 1) * T] for i in range(vector.shape[1] // T)]


class Combine:
    STAGES = 4

    def __init__(self, place, total, arrived, send, recv):
        self.p, self.total, self.arrived, self.send, self.recv = place, total, arrived, send, recv

    def copies(self, i):
        p = self.p
        if i < 3:
            peers = [(i, (p.device(c=1 - p.c), p.device(x=1 - p.x), p.device(y=1 - p.y))[i])]
        else:
            peers = [(3 + d, p.device(z=(p.z + d) % p.zs)) for d in range(1, p.zs)]
        return [
            remote(self.total.at[i], self.arrived.at[at], self.send.at[at], self.recv.at[at], peer)
            for at, peer in peers
        ]

    def start(self, i):
        for copy in self.copies(i):
            copy.start()

    def finish(self, i):
        p = self.p
        for copy in self.copies(i):
            copy.wait_recv()
            copy.wait_send()
        if i < 3:
            self.total[i + 1] = self.total[i] + self.arrived[i]
        else:
            self.arrived[3] = self.total[i]
            terms = [self.arrived[3 + (p.z - z + p.zs) % p.zs] for z in range(p.zs)]
            self.total[i + 1] = functools.reduce(jnp.add, terms)


def back_kernel(zs, xs, shape, width, kept, live, *refs):
    q, k, v, bias, grad, out, norm, attended, branch_hbm, normed_hbm, parts, weights_hbm = refs[:12]
    d_middle, x_low, gain, d_gain_two, kept_sums = refs[12:17]
    d_x, feed_out, attention_out, vector_out = refs[17:19], refs[19:22], refs[22:26], refs[26]
    refs = refs[7:]
    (stage, turn_buf, d_q, d_kv, back_kv, k_sum, v_sum, d_bias) = refs[20:28]
    (w_buf, held, vector, total, arrived, gain_sum) = refs[28:34]
    (local, loads, kv_sems, both_sems) = refs[34:38]
    bufs, scatter_sems = refs[38 : 38 + BUFFERS], refs[38 + BUFFERS :]
    place = Place(zs, xs)
    step = pl.program_id(0)
    rows, keys = shape.rows, shape.keys
    prompt = shape.local_tiles * T
    pairs = d_q.shape[0]
    last = 2 * pairs
    turns = rows // T
    first_kept, end_kept = kept
    fed = parts.shape[0] - (end_kept - first_kept)
    size = d_x[0].shape[0]
    blocks = rows // size

    def stage_load(source):
        return pltpu.make_async_copy(source, stage, local.at[0])

    def weights_load(i):
        return pltpu.make_async_copy(weights_hbm.at[(2, 0, 1)[i]], w_buf.at[i], local.at[1 + i])

    def turn():
        def one(i, carry):
            part = tile_rows(i)
            turn_buf[:, part] = stage[part, :].T
            return carry

        lax.fori_loop(0, turns, one, 0)

    def part_load(c):
        j = jnp.where(c < first_kept, c, c + end_kept - first_kept)
        return pltpu.make_async_copy(parts.at[j], held.at[c % 3], loads.at[c % 3])

    @pl.when(step == 0)
    def _():
        part_load(step).start()
        stage_load(branch_hbm).start()
        place.barrier()
        for i in range(3):
            weights_load(i).start()

    def feed_store(j, half, total):
        piece = 2 * j + half

        @pl.when(piece < feed_out[0].shape[1] // T)
        def _():
            part = pl.ds(pl.multiple_of(piece * T, T), T)
            for i in range(3):
                feed_out[i][:, part] = total[i]

    def keep(c, half, total):
        @pl.when(c < fed)
        def _():
            feed_store(jnp.where(c < first_kept, c, c + end_kept - first_kept), half, total)

        for m, matrix in enumerate((3, 0, 1, 2)):

            @pl.when(c == fed + m)
            def _(matrix=matrix):
                for i in range(3):
                    piece = 3 * half + i
                    attention_out[matrix][:, piece * T : (piece + 1) * T] = total[i]

    @pl.when(step == 1)
    def _():
        def one(k, carry):
            for half in range(2):
                feed_store(k + first_kept, half, kept_sums[k, half])
            return carry

        lax.fori_loop(0, end_kept - first_kept, one, 0)

    engine = Scatter(place, bufs, *scatter_sems, keep)

    def due(offset, action):
        at = step - offset
        chunk = jnp.where(at < last, at, at - last + fed)
        early = (at >= 0) & (at < fed)
        late = (at >= last) & (at < last + 4)

        @pl.when(early | late)
        def _():
            action(chunk)

    def first(c):
        @pl.when(c < fed)
        def _():
            part_load(c).wait()

        engine.start_first(c, held.at[c % 3])

    due(4, engine.finish)
    due(3, engine.start_fourth)
    due(2, engine.start_third)
    due(1, lambda c: engine.start_second(c, held.at[c % 3]))
    due(0, first)

    @pl.when(step + 1 < fed)
    def _():
        part_load(step + 1).start()

    @pl.when(step == 0)
    def _():
        stage_load(branch_hbm).wait()
        turn()
        stage_load(normed_hbm).start()

    def kv_send(p):
        src = d_kv.at[p, :, pl.ds(rows, keys - rows)]
        peer = place.device(x=1 - place.x)
        return remote(src, back_kv.at[p], kv_sems.at[0, p], kv_sems.at[1, p], peer)

    @pl.when(step < last)
    def _():
        p = step // 2
        half = step % 2

        @pl.when(half == 0)
        def _():
            k_sum[...] = jnp.zeros_like(k_sum)
            v_sum[...] = jnp.zeros_like(v_sum)
            d_bias[...] = jnp.zeros_like(d_bias)

        inputs = (q, k, v, bias, grad, out, norm, d_q.at[p], d_bias, k_sum, v_sum)
        base = place.x * shape.local_tiles
        action = lambda i, c: attend_back_tile(shape, i, c, live, base, *inputs)

        @pl.when(half == 0)
        def _():
            for_tiles(shape, False, action)

        @pl.when(half == 1)
        def _():
            for_tiles(shape, True, action)
            d_kv[p, 0] = k_sum[...].astype(BF)
            d_kv[p, 1] = v_sum[...].astype(BF)
            kv_send(p).start()
            for h in range(2):
                vector[2 * p + h] = band_sums(d_bias, h)

    def produce(c, right):
        slot = c % 3
        for m in range(3):
            operand = right(m)

            def one(z, carry, m=m, operand=operand):
                block = turn_buf.shape[0] // zs
                part = pl.ds(pl.multiple_of(z * block, block), block)
                result = nn(turn_buf[part, :], operand).astype(BF)
                for side in range(2):
                    index = 2 * m + side
                    value = result[:, side * T : (side + 1) * T]
                    held[slot, index // 3, index % 3, z] = value.reshape(held.shape[4:])
                return carry

            lax.fori_loop(0, zs, one, 0)

    @pl.when(step == last - 1)
    def _():
        produce(fed, lambda m: jnp.concatenate([attended[2 * m], attended[2 * m + 1]], axis=1))

    @pl.when(step == last)
    def _():
        stage_load(normed_hbm).wait()
        turn()
        produce(fed + 1, lambda m: jnp.concatenate([d_q[2 * m], d_q[2 * m + 1]], axis=1))

        def join(p, carry):
            kv_send(p).wait_recv()
            kv_send(p).wait_send()
            for side in range(2):
                own = d_kv[p, side, 0:prompt, :].astype(F32)
                d_kv[p, side, 0:prompt, :] = (own + back_kv[p, side].astype(F32)).astype(BF)
            return carry

        lax.fori_loop(0, pairs, join, 0)
        for i in range(3):
            weights_load(i).wait()
        gain_sum[...] = jnp.zeros_like(gain_sum)

    for side in range(2):

        @pl.when(step == last + 1 + side)
        def _(side=side):
            pick = lambda p: d_kv[p, side, 0:rows, :]
            produce(fed + 2 + side, lambda m: jnp.concatenate([pick(2 * m), pick(2 * m + 1)], axis=1))

    @pl.when((step >= last) & (step < last + blocks))
    def _():
        part = pl.ds(pl.multiple_of((step - last) * size, size), size)
        d_normed = None
        for i in range(3):
            for m in range(pairs // 2):
                if i == 0:
                    left = [d_q[2 * m + e, part, :] for e in range(2)]
                else:
                    left = [d_kv[2 * m + e, i - 1, part, :] for e in range(2)]
                pieces = [2 * m, 2 * m + 1]
                right = [w_buf[i, j // 3, j % 3].reshape(width, T) for j in pieces]
                term = nt(jnp.concatenate(left, axis=1), jnp.concatenate(right, axis=1))
                d_normed = term if d_normed is None else d_normed + term
        x = x_low[...].astype(F32)
        scale = lax.rsqrt(jnp.mean(x * x, axis=-1, keepdims=True) + EPS)
        unit = x * scale
        gain_sum[...] += jnp.sum(d_normed * unit, axis=0, keepdims=True)
        d_unit = d_normed * gain[...]
        inner = jnp.mean(d_unit * unit, axis=-1, keepdims=True)
        value = (d_middle[...] + scale * (d_unit - unit * inner)).astype(BF)
        put(step - last, prompt // size, d_x, value)

    mix = Combine(place, total, arrived, both_sems.at[0], both_sems.at[1])
    start = last + blocks
    tiles = 2 * pairs

    @pl.when(step == start - 1)
    def _():
        total[0, 0:tiles] = vector[...]
        both = rows_of(gain_sum[...]) + rows_of(d_gain_two[...])
        for i in range(len(both) // VECTOR_ROWS):
            group = both[i * VECTOR_ROWS : (i + 1) * VECTOR_ROWS]
            total[0, tiles + i] = jnp.concatenate(group, axis=0)
        mix.start(0)

    for i in range(mix.STAGES):

        @pl.when(step == start + i)
        def _(i=i):
            mix.finish(i)
            if i + 1 < mix.STAGES:
                mix.start(i + 1)
            else:
                vector_out[...] = total[mix.STAGES]


def back(q, kv, bias, grad, out, norm, branch, normed, parts, weights, d_middle, x_low, gain,
         d_gain_two, kept_sums, hidden, live, shape, sizes, kept, collective_id):
    grp, seq = sizes
    rows, width = x_low.shape
    pairs = q.shape[0]
    zs = grp // (Y * C)
    keys = shape.keys
    chunks, _, n, _, _, _, shard, lanes = parts.shape
    assert chunks - (kept[1] - kept[0]) <= 2 * pairs
    assert (pairs, n) == (6, 3) and 2 * width // T % VECTOR_ROWS == 0
    last = 2 * pairs
    size = min(rows, 256)
    blocks = rows // size
    prompt = shape.local_tiles * T
    assert prompt % size == 0
    tile = (2, n, zs, Y, C * seq, shard, lanes)
    stages = Combine.STAGES
    steps = max(last + blocks + stages, last + 8)
    inner = pairs * 2 * HEAD
    vector = (2 * pairs + 2 * width // T // VECTOR_ROWS, VECTOR_ROWS, T)
    pair = lambda s: jnp.minimum(s // 2, pairs - 1)
    by_pair = lambda rows_: pl.BlockSpec((rows_, 2 * HEAD), lambda s, *_: (0, pair(s)))
    in_pair = pl.BlockSpec((None, rows, 2 * HEAD), lambda s, *_: (pair(s), 0, 0))
    of_keys = lambda side: pl.BlockSpec(
        (None, None, keys, 2 * HEAD), lambda s, *_: (side, pair(s), 0, 0)
    )
    row_block = lambda s: jnp.clip(s - last, 0, blocks - 1)
    by_rows = pl.BlockSpec((size, width), lambda s, *_: (row_block(s), 0))
    full = lambda *dims: pl.BlockSpec(
        dims, lambda s, *_: (0,) * len(dims), pipeline_mode=pl.Buffered(1)
    )
    anywhere = pl.BlockSpec(memory_space=pl.ANY)
    sems = lambda *dims: pltpu.SemaphoreType.DMA(dims)
    return pl.pallas_call(
        functools.partial(back_kernel, zs, seq, shape, width, kept),
        grid_spec=pltpu.PrefetchScalarGridSpec(
            num_scalar_prefetch=1,
            grid=(steps,),
            in_specs=[
                in_pair,
                of_keys(0),
                of_keys(1),
                pl.BlockSpec((2, BANDS, T, T), lambda s, *_: (pair(s), 0, 0, 0)),
                by_pair(rows),
                in_pair,
                pl.BlockSpec((2, rows, 1), lambda s, *_: (pair(s), 0, 0)),
                full(pairs, rows, 2 * HEAD),
                anywhere,
                anywhere,
                anywhere,
                anywhere,
                by_rows,
                by_rows,
                full(1, width),
                full(1, width),
                full(*kept_sums.shape),
            ],
            out_specs=two_parts(size, width, prompt // size, blocks, last)
            + [full(shard, hidden)] * 3
            + [full(shard, inner)] * 4
            + [full(*vector)],
            scratch_shapes=[
                pltpu.VMEM((rows, width), BF),
                pltpu.VMEM((width, rows), BF),
                pltpu.VMEM((pairs, rows, 2 * HEAD), BF),
                pltpu.VMEM((pairs, 2, keys, 2 * HEAD), BF),
                pltpu.VMEM((pairs, 2, keys - rows, 2 * HEAD), BF),
                pltpu.VMEM((keys, 2 * HEAD), F32),
                pltpu.VMEM((keys, 2 * HEAD), F32),
                pltpu.VMEM((2, BANDS, T, T), F32),
                pltpu.VMEM((3, *tile), BF),
                pltpu.VMEM((3, *tile), BF),
                pltpu.VMEM((2 * pairs, VECTOR_ROWS, T), F32),
                pltpu.VMEM((stages + 1, *vector), F32),
                pltpu.VMEM((3 + zs, *vector), F32),
                pltpu.VMEM((1, width), F32),
                sems(4),
                sems(3),
                sems(2, pairs),
                sems(2, 3 + zs),
            ]
            + scatter_buffers(n, zs, seq, shard, lanes)
            + [sems(2, 2, zs + 2), sems(2, 2, zs + 2)],
        ),
        out_shape=[
            jax.ShapeDtypeStruct((prompt, width), BF),
            jax.ShapeDtypeStruct((rows - prompt, width), BF),
        ]
        + [jax.ShapeDtypeStruct((shard, hidden), F32)] * 3
        + [jax.ShapeDtypeStruct((shard, inner), F32)] * 4
        + [
            jax.ShapeDtypeStruct(vector, F32),
        ],
        compiler_params=pltpu.CompilerParams(
            collective_id=collective_id, has_side_effects=True, vmem_limit_bytes=VMEM_LIMIT
        ),
    )(live, q, kv, kv, bias, grad, out, norm, out, branch, normed, parts, weights, d_middle,
      x_low, gain, d_gain_two, kept_sums)


GELU_SCALE = 0.7978845608028654
GELU_CUBIC = 0.044715


def gelu_and_slope(a):
    square = a * a
    tanh = jnp.tanh(GELU_SCALE * a * (1.0 + GELU_CUBIC * square))
    half = 0.5 * (1.0 + tanh)
    slope = half + 0.5 * a * (1.0 - tanh * tanh) * (
        GELU_SCALE * (1.0 + 3.0 * GELU_CUBIC * square)
    )
    return a * half, slope


def feed_load(x_hbm, dy_parts, x, x_t, dy, dy_t, sem):
    loads = [pltpu.make_async_copy(x_hbm, x, sem.at[0])]
    start = 0
    for i, part in enumerate(dy_parts):
        target = dy.at[pl.ds(start, part.shape[0])]
        loads.append(pltpu.make_async_copy(part, target, sem.at[1 + i]))
        start += part.shape[0]
    for load in loads:
        load.start()
    for load in loads:
        load.wait()

    def turn(i, carry):
        part = pl.ds(pl.multiple_of(i * T, T), T)
        x_t[:, part] = x[part, :].T
        dy_t[:, part] = dy[part, :].T
        return carry

    lax.fori_loop(0, x.shape[0] // T, turn, 0)


def feed_chunk(read, write, blocks, out, d_x, x, x_t, dy, dy_t, hidden, d_gate, d_up):
    rows, width = x.shape
    row_block = min(rows, 256)
    width_block = width // blocks
    w_gate, w_up, w_down = [jnp.concatenate([read(0, i), read(1, i)], axis=1) for i in range(3)]

    def by_rows(i, carry):
        part = pl.ds(pl.multiple_of(i * row_block, row_block), row_block)
        gate = nn(x[part, :], w_gate)
        up = nn(x[part, :], w_up)
        d_hidden = nn(dy[part, :], w_down)
        active, slope = gelu_and_slope(gate)
        hidden_low = (active * up).astype(BF)
        d_gate_low = (d_hidden * up * slope).astype(BF)
        d_up_low = (d_hidden * active).astype(BF)
        hidden[part, :] = hidden_low
        d_gate[part, :] = d_gate_low
        d_up[part, :] = d_up_low
        out[part, :] += nt(hidden_low, w_down)
        d_x[part, :] += nt(d_gate_low, w_gate) + nt(d_up_low, w_up)
        return carry

    lax.fori_loop(0, rows // row_block, by_rows, 0)

    def by_width(i, carry):
        part = pl.ds(pl.multiple_of(i * width_block, width_block), width_block)
        pairs = ((x_t, d_gate), (x_t, d_up), (dy_t, hidden))
        for index, (left, right) in enumerate(pairs):
            total = nn(left[part, :], right[...]).astype(BF)
            write(0, index, i, total[:, :T])
            write(1, index, i, total[:, T:])
        return carry

    lax.fori_loop(0, blocks, by_width, 0)


def feed_kernel(x_hbm, dy_hbm, weights, out, d_x, grads, x, x_t, dy, dy_t, *rest):
    *work, sem = rest
    width_block = 512

    @pl.when(pl.program_id(0) == 0)
    def _():
        feed_load(x_hbm, [dy_hbm], x, x_t, dy, dy_t, sem)
        out[...] = jnp.zeros_like(out)
        d_x[...] = jnp.zeros_like(d_x)

    def write(half, index, block, value):
        part = pl.ds(pl.multiple_of(block * width_block, width_block), width_block)
        grads[0, half, index, part, :] = value

    read = lambda half, index: weights[0, half, index]
    blocks = x.shape[1] // width_block
    feed_chunk(read, write, blocks, out, d_x, x, x_t, dy, dy_t, *work)


def feed_scratch(rows, width):
    return [
        pltpu.VMEM((rows, width), BF),
        pltpu.VMEM((width, rows), BF),
        pltpu.VMEM((rows, width), BF),
        pltpu.VMEM((width, rows), BF),
        pltpu.VMEM((rows, 2 * T), BF),
        pltpu.VMEM((rows, 2 * T), BF),
        pltpu.VMEM((rows, 2 * T), BF),
        pltpu.SemaphoreType.DMA((3,)),
    ]


def feed(x, dy, weights):
    rows, width = x.shape
    chunks = weights.shape[0]
    chunk = pl.BlockSpec((1, 2, 3, width, T), lambda j: (j, 0, 0, 0, 0))
    whole = pl.BlockSpec((rows, width), lambda j: (0, 0), pipeline_mode=pl.Buffered(1))
    return pl.pallas_call(
        feed_kernel,
        grid=(chunks,),
        in_specs=[pl.BlockSpec(memory_space=pl.ANY)] * 2 + [chunk],
        out_specs=[whole, whole, chunk],
        out_shape=[
            jax.ShapeDtypeStruct((rows, width), F32),
            jax.ShapeDtypeStruct((rows, width), F32),
            jax.ShapeDtypeStruct((chunks, 2, 3, width, T), BF),
        ],
        scratch_shapes=feed_scratch(rows, width),
        compiler_params=pltpu.CompilerParams(vmem_limit_bytes=VMEM_LIMIT),
    )(x, dy, weights)


def feed_moving_kernel(zs, xs, early, kept, *refs):
    x_hbm, dy_one, dy_two, own, ready, middle, gain, whole, parts, sums = refs[:10]
    final, (d_middle, d_branch, d_attended, d_gain) = refs[10:12], refs[12:16]
    x, x_t, dy, dy_t, hidden, d_gate, d_up, sem = refs[16:24]
    out, d_x, held, w_buf, g_buf, local = refs[24:30]
    gather_sems, bufs = refs[30:32], refs[32 : 32 + BUFFERS]
    scatter_sems = refs[32 + BUFFERS :]
    chunks = own.shape[0]
    place = Place(zs, xs)
    step = pl.program_id(0)
    lag = max(0, 5 - early)
    first_kept, end_kept = kept
    width = x.shape[1]

    @pl.when(step == 0)
    def _():
        place.barrier()

    fetch = Gather(place, own, whole, *gather_sems)
    fetch.tick(step, early, chunks)

    @pl.when(step == 0)
    def _():
        load = pltpu.make_async_copy(own, held, local.at[0])
        load.start()
        load.wait()
        mine = whole.at[:, :, :, place.z, place.y, place.c * place.xs + place.x]
        store = pltpu.make_async_copy(held, mine, local.at[1])
        store.start()
        store.wait()
        feed_load(x_hbm, [dy_one, dy_two], x, x_t, dy, dy_t, sem)
        out[...] = jnp.zeros_like(out)
        d_x[...] = jnp.zeros_like(d_x)

    skipped = ready.shape[0] - early

    def weight_load(j, source, first=0):
        return pltpu.make_async_copy(source.at[first + j], w_buf.at[j % 2], local.at[2 + j % 2])

    def start_load(j):
        if early > 0:

            @pl.when(j < early)
            def _():
                weight_load(j, ready, skipped).start()

        @pl.when(j >= early)
        def _():
            weight_load(j, whole).start()

    def part_store(j):
        return pltpu.make_async_copy(g_buf.at[j % 2], parts.at[j], local.at[4 + j % 2])

    def is_kept(j):
        return (j >= first_kept) & (j < end_kept)

    def keep(k, half, total):
        sums[k, half] = total

    engine = Scatter(place, bufs, *scatter_sems, keep)
    due = lag + first_kept
    number = end_kept - first_kept
    grads_of = lambda k: g_buf.at[(k + first_kept) % 2]
    staged(step, due + 5, number, engine.finish)
    staged(step, due + 4, number, engine.start_fourth)
    staged(step, due + 3, number, engine.start_third)
    staged(step, due + 2, number, lambda k: engine.start_second(k, grads_of(k)))
    staged(step, due + 1, number, lambda k: engine.start_first(k, grads_of(k)))

    chunk = step - lag
    if lag == 0:

        @pl.when(step == 0)
        def _():
            start_load(0)

    @pl.when((chunk >= (0 if lag == 0 else -1)) & (chunk + 1 < chunks))
    def _():
        start_load(chunk + 1)

    @pl.when((chunk >= 2) & (chunk < chunks + 2) & ~is_kept(chunk - 2))
    def _():
        part_store(chunk - 2).wait()

    @pl.when((chunk >= 0) & (chunk < chunks))
    def _():
        weight_load(chunk, whole).wait()
        slot = chunk % 2

        def read(half, index):
            return w_buf[slot, half, index].reshape(width, T)

        def write(half, index, block, value):
            shape = g_buf.shape[4:]
            g_buf[slot, half, index, block] = value.reshape(shape)

        work = (hidden, d_gate, d_up)
        feed_chunk(read, write, zs, out, d_x, x, x_t, dy, dy_t, *work)

        @pl.when(~is_kept(chunk))
        def _():
            part_store(chunk).start()

    spare = chunks % 2
    rows, size = x.shape[0], middle.shape[0]
    blocks = rows // size

    def o_load():
        return pltpu.make_async_copy(ready.at[skipped - 1], w_buf.at[spare], local.at[6])

    @pl.when(chunk == chunks - 1)
    def _():
        o_load().start()
        d_gain[...] = jnp.zeros_like(d_gain)

    @pl.when(chunk == chunks)
    def _():
        o_load().wait()

    @pl.when((chunk >= chunks) & (chunk < chunks + blocks))
    def _():
        i = chunk - chunks
        part = pl.ds(pl.multiple_of(i * size, size), size)
        values = middle[...]
        put(i, dy_one.shape[0] // size, final, (values + out[part, :]).astype(BF))
        scale = rms_scale(values)
        unit = values * scale
        d_normed = d_x[part, :]
        d_gain[...] += jnp.sum(d_normed * unit, axis=0, keepdims=True)
        total = dy[part, :].astype(F32) + norm_back(d_normed, unit, scale, gain[...])
        d_middle[...] = total
        low = total.astype(BF)
        d_branch[...] = low
        for m in range(d_attended.shape[1] // (2 * T)):
            right = joined_pieces(w_buf, spare, m)
            d_attended[:, 2 * m * T : 2 * (m + 1) * T] = nn(low, right).astype(BF)


def feed_moving(x, dy_one, dy_two, own, ready, middle, gain, inner, sizes, early, kept, collective_id):
    grp, seq = sizes
    rows, width = x.shape
    chunks, _, n, shard, lanes = own.shape
    zs = grp // (Y * C)
    tile = (2, n, zs, Y, C * seq, shard, lanes)
    one = pl.BlockSpec((1, width), lambda j: (0, 0), pipeline_mode=pl.Buffered(1))
    number = kept[1] - kept[0]
    sums = pl.BlockSpec(
        (number, 2, n, shard, lanes), lambda j: (0,) * 5, pipeline_mode=pl.Buffered(1)
    )
    lag = max(0, 5 - early)
    size = min(rows, 256)
    blocks = rows // size
    assert dy_one.shape[0] % size == 0
    steps = lag + max(chunks + max(2, blocks), kept[1] + 5)
    tail = lag + chunks
    by_rows = lambda columns: pl.BlockSpec(
        (size, columns), lambda j: (jnp.clip(j - tail, 0, blocks - 1), 0)
    )
    out = jax.ShapeDtypeStruct
    anywhere = pl.BlockSpec(memory_space=pl.ANY)
    sems = lambda *shape: pltpu.SemaphoreType.DMA(shape)
    return pl.pallas_call(
        functools.partial(feed_moving_kernel, zs, seq, early, kept),
        grid=(steps,),
        in_specs=[anywhere] * 5 + [by_rows(width), one],
        out_specs=[anywhere, anywhere, sums]
        + two_parts(size, width, dy_one.shape[0] // size, blocks, tail)
        + [by_rows(width), by_rows(width), by_rows(inner), one],
        out_shape=[
            out((chunks, *tile), BF),
            out((chunks, *tile), BF),
            out((number, 2, n, shard, lanes), F32),
            out(dy_one.shape, BF),
            out(dy_two.shape, BF),
            out((rows, width), F32),
            out((rows, width), BF),
            out((rows, inner), BF),
            out((1, width), F32),
        ],
        scratch_shapes=feed_scratch(rows, width)
        + [
            pltpu.VMEM((rows, width), F32),
            pltpu.VMEM((rows, width), F32),
            pltpu.VMEM(own.shape, BF),
            pltpu.VMEM((2, *tile), BF),
            pltpu.VMEM((2, *tile), BF),
            sems(7),
            sems(chunks, 2, zs + 2),
            sems(chunks, 2, zs + 2),
        ]
        + scatter_buffers(n, zs, seq, shard, lanes)
        + [sems(2, 2, zs + 2), sems(2, 2, zs + 2)],
        compiler_params=pltpu.CompilerParams(
            collective_id=collective_id, has_side_effects=True, vmem_limit_bytes=VMEM_LIMIT
        ),
    )(x, dy_one, dy_two, own, ready, middle, gain)


def settle_kernel(*refs):
    *refs, sem = refs
    count = len(refs) // 3
    sources, targets, held = refs[:count], refs[count : 2 * count], refs[2 * count :]
    loads = [pltpu.make_async_copy(sources[i], held[i], sem.at[i]) for i in range(count)]
    stores = [pltpu.make_async_copy(held[i], targets[i], sem.at[count + i]) for i in range(count)]
    for load in loads:
        load.start()
    for load, store in zip(loads, stores):
        load.wait()
        store.start()
    for store in stores:
        store.wait()


def settle(*arrays):
    anywhere = pl.BlockSpec(memory_space=pl.ANY)
    return pl.pallas_call(
        settle_kernel,
        in_specs=[anywhere] * len(arrays),
        out_specs=[anywhere] * len(arrays),
        out_shape=[jax.ShapeDtypeStruct(a.shape, a.dtype) for a in arrays],
        scratch_shapes=[pltpu.VMEM(a.shape, a.dtype) for a in arrays]
        + [pltpu.SemaphoreType.DMA((2 * len(arrays),))],
        compiler_params=pltpu.CompilerParams(vmem_limit_bytes=VMEM_LIMIT),
    )(*arrays)


def rms_scale(values):
    return lax.rsqrt(jnp.mean(values * values, axis=-1, keepdims=True) + EPS)


def norm_back(d_normed, unit, scale, gain):
    d_unit = d_normed * gain
    return scale * (d_unit - unit * jnp.mean(d_unit * unit, axis=-1, keepdims=True))


def pieces_of(matrix):
    rows, columns = matrix.shape
    return jnp.swapaxes(matrix.reshape(rows, columns // T, T), 0, 1)


def joined(pieces):
    count, rows, _ = pieces.shape
    return jnp.swapaxes(pieces, 0, 1).reshape(rows, count * T)


def attention_chunks(matrices):
    flat = jnp.concatenate([pieces_of(m) for m in matrices], axis=0)
    pad = -flat.shape[0] % 6
    flat = jnp.pad(flat, ((0, pad), (0, 0), (0, 0)))
    return flat.reshape(-1, 2, 3, *flat.shape[1:])


def feed_chunks(matrices):
    stacked = jnp.stack([pieces_of(m) for m in matrices], axis=1)
    pad = -stacked.shape[0] % 2
    stacked = jnp.pad(stacked, ((0, pad), (0, 0), (0, 0), (0, 0)))
    return stacked.reshape(-1, 2, *stacked.shape[1:])


def body(sizes, *args):
    (
        prompt_x,
        cont_x,
        cont_len,
        prompt_cot,
        cont_cot,
        norm1_gain,
        q_weight,
        k_weight,
        v_weight,
        o_weight,
        bucket_table,
        norm2_gain,
        gate_weight,
        up_weight,
        down_weight,
    ) = args
    _, local_prompt, width = prompt_x.shape
    conts, cont_rows = cont_x.shape[1], cont_x.shape[2]
    assert prompt_x.shape[0] == 1 and cont_rows == T and local_prompt % T == 0
    seq = sizes[1]
    num_buckets, heads = bucket_table.shape
    inner = q_weight.shape[1]
    assert inner == heads * HEAD
    shard = q_weight.shape[0]
    hidden_width = gate_weight.shape[1]
    local_tiles = local_prompt // T
    tiles = local_tiles * seq
    seq_index = lax.axis_index("seq")

    split = lambda parts: (parts[0][None], parts[1].reshape(1, conts, cont_rows, width))
    cut = lambda values: (values[:local_prompt], values[local_prompt:])
    shape = Shape(tiles, local_tiles, conts)
    count = inner // T
    if can_move(sizes, shard):
        early, kept = 7, (9, 15)
        own_gain = jnp.stack([norm1_gain, norm2_gain])[None, :, None, :, None]
        own_gain = jnp.broadcast_to(own_gain, (1, 2, 1, shard, T)).astype(BF)
        cont_dy = cont_cot[0].reshape(-1, width)
        matrices = (q_weight, k_weight, v_weight, o_weight, gate_weight, up_weight, down_weight)
        (whole, own_feed, x_low, normed_one, kv, bias, queries, attended, log_norm, middle,
         normed_two, gains) = front(
            prompt_x[0], cont_x[0].reshape(-1, width), own_gain, matrices, bucket_table, cont_len,
            shape, sizes, early, 0,
        )
        _, feed_parts, kept_sums, *final, d_middle, d_branch, d_attended, d_gain_two = feed_moving(
            normed_two, prompt_cot[0], cont_dy, own_feed, whole, middle, gains[1], inner, sizes,
            early, kept, 1,
        )
        (*d_x, gate_grad, up_grad, down_grad, q_grad, k_grad, v_grad, o_grad, vector) = back(
            queries, kv, bias, d_attended, attended, log_norm, d_branch, normed_one, feed_parts,
            whole, d_middle, x_low, gains[0], d_gain_two, kept_sums, hidden_width, cont_len, shape,
            sizes, kept, 2,
        )
        settled = settle(
            *final, *d_x, gate_grad, up_grad, down_grad, q_grad, k_grad, v_grad, o_grad
        )
        final, d_x = settled[:2], settled[2:4]
        gate_grad, up_grad, down_grad, q_grad, k_grad, v_grad, o_grad = settled[4:]
        near = vector[:heads, :4].reshape(heads, SPAN)
        far = jnp.sum(vector[:heads, 4:6], axis=-1)
        relative = (jnp.arange(SPAN) + T) % SPAN - 2 * T
        ids = jnp.concatenate([bucket_ids(relative), bucket_ids(jnp.array([-T, T]))])
        hot = (ids[:, None] == jnp.arange(num_buckets)).astype(F32)
        both = jnp.concatenate([near, far], axis=1)
        table_grad = jnp.einsum("hr,rb->bh", both, hot, precision=lax.Precision.HIGHEST)
        gain_grads = vector[heads:].reshape(2, sizes[0] * seq, shard)
        me = lax.axis_index("grp") * seq + seq_index
        norm1_grad, norm2_grad = lax.dynamic_index_in_dim(gain_grads, me, 1, keepdims=False)
    else:
        x_low = jnp.concatenate([prompt_x[0], cont_x[0].reshape(-1, width)], axis=0)
        dy_low = jnp.concatenate([prompt_cot[0], cont_cot[0].reshape(-1, width)], axis=0)
        x = x_low.astype(F32)
        dy = dy_low.astype(F32)
        lanes = jnp.zeros((shard, T - 2), F32)
        gains = jnp.concatenate([norm1_gain[:, None], norm2_gain[:, None], lanes], axis=1)
        own_attention = attention_chunks([q_weight, k_weight, v_weight, o_weight, gains]).astype(BF)
        own_feed = feed_chunks([gate_weight, up_weight, down_weight]).astype(BF)
        attention_whole = gather(own_attention, sizes)
        flat = attention_whole.reshape(-1, width, T)
        q_full, k_full, v_full, o_full = [
            joined(flat[i * count : (i + 1) * count]) for i in range(4)
        ]
        gain_one = flat[4 * count, :, 0].astype(F32)
        gain_two = flat[4 * count, :, 1].astype(F32)
        scale_one = rms_scale(x)
        unit_one = x * scale_one
        normed_one = (unit_one * gain_one).astype(BF)
        kv = nn(normed_one, jnp.concatenate([k_full, v_full], axis=1)).astype(BF)
        queries = nn(normed_one, q_full).astype(BF)
        gathered = lax.all_gather(kv[:local_prompt], "seq", axis=0, tiled=True)
        others = jnp.roll(gathered, -seq_index * local_prompt, axis=0)[local_prompt:]
        every = jnp.concatenate([kv, others], axis=0)
        keys, values = every[:, :inner], every[:, inner:]
        base = (seq_index * local_tiles).reshape(1).astype(jnp.int32)
        one_hot = band_one_hot(num_buckets)
        bias = jnp.einsum("cqkb,bh->hcqk", one_hot, bucket_table, precision=lax.Precision.HIGHEST)
        attended, log_norm = attend(queries, keys, values, bias, cont_len, base, shape)
        middle = x + nt(attended, o_full)
        scale_two = rms_scale(middle)
        unit_two = middle * scale_two
        normed_two = (unit_two * gain_two).astype(BF)
        out_sum, d_normed_two, feed_grads = feed(normed_two, dy_low, gather(own_feed, sizes))
        feed_sums = scatter(feed_grads)
        final = cut((middle + out_sum).astype(BF))
        d_gain_two = jnp.sum(d_normed_two * unit_two, axis=0)
        d_middle = dy + norm_back(d_normed_two, unit_two, scale_two, gain_two)
        d_branch = d_middle.astype(BF)
        d_attended = nn(d_branch, o_full).astype(BF)
        d_o = tn(d_branch, attended)
        d_queries, d_keys, d_values, d_bias = attend_back(
            queries, keys, values, bias, d_attended, attended, log_norm, cont_len, base, shape
        )
        d_table = jnp.einsum("hcqk,cqkb->bh", d_bias, one_hot, precision=lax.Precision.HIGHEST)
        d_kv = jnp.concatenate([d_keys, d_values], axis=1)
        prompt_parts = jnp.concatenate([d_kv[:local_prompt], d_kv[shape.rows :]], axis=0)
        prompt_parts = jnp.roll(prompt_parts, seq_index * local_prompt, axis=0)
        d_prompt = lax.psum_scatter(prompt_parts, "seq", scatter_dimension=0, tiled=True)
        d_kv = jnp.concatenate([d_prompt, d_kv[local_prompt : shape.rows]], axis=0)
        d_normed_one = nt(d_queries, q_full) + nt(d_kv, jnp.concatenate([k_full, v_full], axis=1))
        d_q = tn(normed_one, d_queries)
        d_kv_weight = tn(normed_one, d_kv)
        d_gain_one = jnp.sum(d_normed_one * unit_one, axis=0)
        d_x = d_middle + norm_back(d_normed_one, unit_one, scale_one, gain_one)
        d_x = cut(d_x.astype(BF))
        attention_parts = attention_chunks([d_q, d_kv_weight, d_o]).astype(BF)
        attention_sums = scatter(attention_parts).reshape(-1, shard, T)
        norm1_grad = lax.psum_scatter(d_gain_one, ("grp", "seq"), scatter_dimension=0, tiled=True)
        norm2_grad = lax.psum_scatter(d_gain_two, ("grp", "seq"), scatter_dimension=0, tiled=True)
        table_grad = lax.psum(d_table, ("grp", "seq"))
        feed_sums = feed_sums.reshape(-1, 3, shard, T)[: hidden_width // T]
        gate_grad, up_grad, down_grad = [joined(feed_sums[:, i]) for i in range(3)]
        q_grad, k_grad, v_grad, o_grad = [
            joined(attention_sums[i * count : (i + 1) * count]) for i in range(4)
        ]
    return (
        *split(final),
        *split(d_x),
        norm1_grad,
        q_grad,
        k_grad,
        v_grad,
        o_grad,
        table_grad,
        norm2_grad,
        gate_grad,
        up_grad,
        down_grad,
    )


def solution(mesh):
    sizes = (mesh.shape["grp"], mesh.shape["seq"])
    rows = P("grp", "seq", None)
    conts = P("grp", "seq", None, None)
    shard = P(("grp", "seq"), None)
    gain = P(("grp", "seq"))
    in_specs = (rows, conts, P("grp", "seq"), rows, conts, gain, shard, shard, shard, shard)
    in_specs += (P(), gain, shard, shard, shard)
    out_specs = (rows, conts, rows, conts, gain, shard, shard, shard, shard, P(), gain)
    out_specs += (shard, shard, shard)
    return jax.shard_map(
        functools.partial(body, sizes),
        mesh=mesh,
        in_specs=in_specs,
        out_specs=out_specs,
        check_vma=False,
    )
```

```python
import functools

import jax
import jax.numpy as jnp
from jax import lax
from jax.experimental import pallas as pl
from jax.experimental.pallas import tpu as pltpu
from jax.sharding import PartitionSpec as P

EPS = 1e-06
LIMITS = (8, 12, 16, 23, 32, 46, 64, 91)
NEGATIVE = -1e30
MESH = pl.DeviceIdType.MESH
T = 128
HEAD = 64
BANDS = 5
BF = jnp.bfloat16
F32 = jnp.float32
VMEM_LIMIT = 63 * 2**20
Y = 2
C = 2


def nn(left, right):
    return jnp.dot(left, right, preferred_element_type=F32)


def nt(left, right):
    return lax.dot_general(left, right, (((1,), (1,)), ((), ())), preferred_element_type=F32)


def tn(left, right):
    return lax.dot_general(left, right, (((0,), (0,)), ((), ())), preferred_element_type=F32)


def bucket_ids(relative):
    distance = jnp.abs(relative)
    coarse = 7 + sum(((distance >= boundary).astype(jnp.int32) for boundary in LIMITS))
    return jnp.where(distance < 8, distance, coarse) + 16 * (relative > 0).astype(jnp.int32)


def band_one_hot(num_buckets):
    band = jnp.arange(BANDS)[:, None, None] - 2
    query = jnp.arange(T)[None, :, None]
    key = jnp.arange(T)[None, None, :]
    ids = bucket_ids(band * T + key - query)
    return (ids[..., None] == jnp.arange(num_buckets)).astype(F32)


def can_move(sizes, rows):
    zs = sizes[0] // (Y * C)
    return rows % 16 == 0 and sizes[1] == 2 and sizes[0] % (Y * C) == 0 and zs in (2, 4, 8, 16)


class Place:
    def __init__(self, zs, xs):
        grp = lax.axis_index("grp")
        self.zs, self.xs = zs, xs
        self.x = lax.axis_index("seq")
        self.z = grp // (Y * C)
        self.y = (grp // C) % Y
        self.c = grp % C

    def device(self, z=None, y=None, c=None, x=None):
        z = self.z if z is None else z
        y = self.y if y is None else y
        c = self.c if c is None else c
        x = self.x if x is None else x
        return (z * (Y * C) + y * C + c, x)

    def peers(self):
        around = [self.device(z=(self.z + d) % self.zs) for d in range(1, self.zs)]
        return around + [
            self.device(y=1 - self.y),
            self.device(x=1 - self.x),
            self.device(c=1 - self.c),
        ]

    def barrier(self):
        sem = pltpu.get_barrier_semaphore()
        peers = self.peers()
        for peer in peers:
            pl.semaphore_signal(sem, inc=1, device_id=peer, device_id_type=MESH)
        pl.semaphore_wait(sem, len(peers))


def remote(src, dst, send_sem, recv_sem, device):
    return pltpu.make_async_remote_copy(
        src_ref=src,
        dst_ref=dst,
        send_sem=send_sem,
        recv_sem=recv_sem,
        device_id=device,
        device_id_type=MESH,
    )


def staged(step, offset, count, action):
    @pl.when((step >= offset) & (step < count + offset))
    def _():
        action(step - offset)


class Gather:
    def __init__(self, place, own, whole, send, recv):
        self.p, self.own, self.whole, self.send, self.recv = place, own, whole, send, recv

    def copy(self, k, half, index, src, dst, device):
        return remote(src, dst, self.send.at[k, half, index], self.recv.at[k, half, index], device)

    def alone(self, k, half):
        p = self.p
        dst = self.whole.at[k, half, :, p.z, p.y, p.c * p.xs + p.x]
        src = self.own.at[k, half]
        if half == 0:
            return [self.copy(k, half, 0, src, dst, p.device(x=1 - p.x))]
        peers = [p.device(z=(p.z + d) % p.zs) for d in range(1, p.zs)]
        return [self.copy(k, half, i, src, dst, peer) for i, peer in enumerate(peers)]

    def second(self, k, half):
        p = self.p
        if half == 0:
            view = self.whole.at[k, half, :, p.z, p.y, pl.ds(p.c * p.xs, p.xs)]
            peers = [p.device(z=(p.z + d) % p.zs) for d in range(1, p.zs)]
            return [self.copy(k, half, 1 + i, view, view, peer) for i, peer in enumerate(peers)]
        view = self.whole.at[k, half, :, :, p.y, p.c * p.xs + p.x]
        return [self.copy(k, half, p.zs - 1, view, view, p.device(y=1 - p.y))]

    def third(self, k, half):
        p = self.p
        if half == 0:
            view = self.whole.at[k, half, :, :, p.y, pl.ds(p.c * p.xs, p.xs)]
            peer = p.device(y=1 - p.y)
        else:
            view = self.whole.at[k, half, :, :, :, p.c * p.xs + p.x]
            peer = p.device(x=1 - p.x)
        return [self.copy(k, half, p.zs, view, view, peer)]

    def fourth(self, k, half):
        p = self.p
        view = self.whole.at[k, half, :, :, :, pl.ds(p.c * p.xs, p.xs)]
        return [self.copy(k, half, p.zs + 1, view, view, p.device(c=1 - p.c))]

    def tick(self, step, first, end):
        stages = (self.alone, self.second, self.third, self.fourth)

        def advance(offset, k):
            for half in (0, 1):
                if offset > 0:
                    for copy in stages[offset - 1](k, half):
                        copy.wait_recv()
                if offset < 4:
                    for copy in stages[offset](k, half):
                        copy.start()
                else:
                    for stage in stages:
                        for copy in stage(k, half):
                            copy.wait_send()

        for offset in range(5):
            staged(step, offset, end - first, lambda k, offset=offset: advance(offset, first + k))


def gather(own, sizes):
    return lax.all_gather(own, ("grp", "seq"), axis=3, tiled=True)


class Scatter:
    def __init__(self, place, bufs, send, recv, out):
        self.p, self.send, self.recv, self.out = place, send, recv, out
        (self.in1, self.in2, self.sum1, self.sum2) = bufs[:4]
        self.in3, self.in4, self.sum3 = bufs[4:6], bufs[6:8], bufs[8:10]

    def copy(self, k, half, index, src, dst, device):
        slot = k % 2
        return remote(
            src, dst, self.send.at[slot, half, index], self.recv.at[slot, half, index], device
        )

    def first(self, k, half, part):
        p = self.p
        src = part.at[half, :, :, :, pl.ds((1 - p.c) * p.xs, p.xs)]
        return self.copy(k, half, 0, src, self.in1.at[k % 2, half], p.device(c=1 - p.c))

    def second(self, k, half):
        p = self.p
        if half == 0:
            src, peer = self.sum1.at[k % 2, half, :, :, 1 - p.y], p.device(y=1 - p.y)
        else:
            src, peer = self.sum1.at[k % 2, half, :, :, :, 1 - p.x], p.device(x=1 - p.x)
        return self.copy(k, half, 1, src, self.in2.at[k % 2, half], peer)

    def third(self, k, half):
        p, slot = self.p, k % 2
        if half == 1:
            src = self.sum2.at[slot, half, :, :, 1 - p.y]
            return [self.copy(k, half, 2, src, self.in3[1].at[slot], p.device(y=1 - p.y))]
        copies = []
        for d in range(1, p.zs):
            target = (p.z + d) % p.zs
            src = self.sum2.at[slot, half, :, target]
            dst = self.in3[0].at[slot, d - 1]
            copies.append(self.copy(k, half, 1 + d, src, dst, p.device(z=target)))
        return copies

    def fourth(self, k, half):
        p, slot = self.p, k % 2
        if half == 0:
            src = self.sum3[0].at[slot, :, 1 - p.x]
            return [self.copy(k, half, p.zs + 1, src, self.in4[0].at[slot, 0], p.device(x=1 - p.x))]
        copies = []
        for d in range(1, p.zs):
            target = (p.z + d) % p.zs
            src = self.sum3[1].at[slot, :, target]
            dst = self.in4[1].at[slot, d - 1]
            copies.append(self.copy(k, half, 2 + d, src, dst, p.device(z=target)))
        return copies

    def finish(self, k):
        p, slot = self.p, k % 2
        for half in (0, 1):
            total = self.sum3[half][slot, :, p.x if half == 0 else p.z].astype(F32)
            for i, copy in enumerate(self.fourth(k, half)):
                copy.wait_recv()
                copy.wait_send()
                total = total + self.in4[half][slot, i].astype(F32)
            self.out(k, half, total)

    def start_fourth(self, k):
        p, slot = self.p, k % 2
        for half in (0, 1):
            for copy in self.third(k, half):
                copy.wait_recv()
                copy.wait_send()
            for i in range(self.sum2.shape[2]):
                if half == 0:
                    total = self.sum2[slot, half, i, p.z].astype(F32)
                    for d in range(1, p.zs):
                        total = total + self.in3[0][slot, d - 1, i].astype(F32)
                else:
                    total = self.sum2[slot, half, i, :, p.y].astype(F32)
                    total = total + self.in3[1][slot, i].astype(F32)
                self.sum3[half][slot, i] = total.astype(BF)
            for copy in self.fourth(k, half):
                copy.start()

    def start_third(self, k):
        p, slot = self.p, k % 2
        for half in (0, 1):
            copy = self.second(k, half)
            copy.wait_recv()
            copy.wait_send()
            for i in range(self.sum2.shape[2]):
                if half == 0:
                    mine = self.sum1[slot, half, i, :, p.y]
                else:
                    mine = self.sum1[slot, half, i, :, :, p.x]
                total = mine.astype(F32) + self.in2[slot, half, i].astype(F32)
                self.sum2[slot, half, i] = total.astype(BF)
            for copy in self.third(k, half):
                copy.start()

    def start_second(self, k, part):
        p, slot = self.p, k % 2
        for half in (0, 1):
            copy = self.first(k, half, part)
            copy.wait_recv()
            copy.wait_send()

            def add(z, _, half=half):
                for i in range(self.sum1.shape[2]):
                    mine = part[half, i, z, :, pl.ds(p.c * p.xs, p.xs)]
                    total = mine.astype(F32) + self.in1[slot, half, i, z].astype(F32)
                    self.sum1[slot, half, i, z] = total.astype(BF)
                return 0

            lax.fori_loop(0, p.zs, add, 0)
            self.second(k, half).start()

    def start_first(self, k, part):
        for half in (0, 1):
            self.first(k, half, part).start()


BUFFERS = 10


def scatter_buffers(n, zs, xs, rows, lanes):
    block = (rows, lanes)
    shapes = [
        (2, 2, n, zs, Y, xs, *block),
        (2, 2, n, zs, 2, *block),
        (2, 2, n, zs, Y, xs, *block),
        (2, 2, n, zs, 2, *block),
        (2, zs - 1, n, 2, *block),
        (2, n, zs, *block),
        (2, 1, n, *block),
        (2, zs - 1, n, *block),
        (2, n, 2, *block),
        (2, n, zs, *block),
    ]
    return [pltpu.VMEM(shape, BF) for shape in shapes]


def scatter(parts):
    return lax.psum_scatter(parts, ("grp", "seq"), scatter_dimension=3, tiled=True).astype(F32)


class Shape:
    def __init__(self, tiles, local_tiles, conts):
        self.tiles, self.local_tiles, self.conts = tiles, local_tiles, conts
        self.rows = (local_tiles + conts) * T
        self.keys = self.rows + (tiles - local_tiles) * T
        self.parts = [(0, range(local_tiles)), (self.rows, range(local_tiles, tiles))]
        self.parts = [(start, js) for start, js in self.parts if len(js)]


def band_of(key_tile, query_tile):
    return jnp.clip(key_tile - query_tile, -2, 2) + 2


def tile_lanes():
    first_half = lax.broadcasted_iota(jnp.int32, (T, 2 * HEAD), 1) < HEAD
    place = lax.broadcasted_iota(jnp.int32, (T, T), 1)
    return first_half, place


def tile_rows(i):
    return pl.ds(pl.multiple_of(i * T, T), T)


def attend_tile(shape, i, is_cont, live, base, q, k, v, bias, out, norm):
    first_half, place = tile_lanes()
    rows = tile_rows(i)
    queries = q[rows, :]
    query_tile = shape.tiles if is_cont else base + i
    mixed = []
    for h in range(2):
        mine = first_half if h == 0 else ~first_half
        masked = jnp.where(mine, queries, jnp.zeros_like(queries))
        logits = []
        for start, js in shape.parts:
            scores = nt(masked, k[start : start + len(js) * T, :])
            for at, j in enumerate(js):
                band = band_of(lax.rem(base + j, shape.tiles), query_tile)
                logits.append(scores[:, at * T : (at + 1) * T] + bias[h, band])
        if is_cont:
            own = nt(masked, k[rows, :]) + bias[h, 2]
            logits.append(jnp.where(place < live[0, i - shape.local_tiles], own, NEGATIVE))
        top = jnp.max(functools.reduce(jnp.maximum, logits), axis=1, keepdims=True)
        weights = [jnp.exp(part - top) for part in logits]
        total = jnp.sum(functools.reduce(jnp.add, weights), axis=1, keepdims=True)
        inverse = 1.0 / total
        probs = [(weight * inverse).astype(BF) for weight in weights]
        result = None
        for start, js in shape.parts:
            left = jnp.concatenate([probs[j] for j in js], axis=1)
            term = nn(left, v[start : start + len(js) * T, :])
            result = term if result is None else result + term
        if is_cont:
            result = result + nn(probs[shape.tiles], v[rows, :])
        mixed.append(result)
        norm[h, rows, :] = top + jnp.log(total)
    out[rows, :] = jnp.where(first_half, mixed[0], mixed[1]).astype(BF)


def for_tiles(shape, conts, action):
    first, last = (shape.local_tiles, shape.local_tiles + shape.conts) if conts else (0, shape.local_tiles)

    def one(i, carry):
        action(i, conts)
        return carry

    lax.fori_loop(first, last, one, 0)


def attend_kernel(shape, live, base, q, k, v, bias, out, norm):
    for conts in (False, True):
        for_tiles(
            shape,
            conts,
            lambda i, c: attend_tile(shape, i, c, live, base[0], q, k, v, bias, out, norm),
        )


def pair_block(n):
    return pl.BlockSpec((n, 2 * HEAD), lambda h, *_: (0, h))


def attend(q, k, v, bias, live, base, shape):
    rows, width = q.shape
    pairs = width // (2 * HEAD)
    return pl.pallas_call(
        functools.partial(attend_kernel, shape),
        grid_spec=pltpu.PrefetchScalarGridSpec(
            num_scalar_prefetch=2,
            grid=(pairs,),
            in_specs=[
                pair_block(rows),
                pair_block(shape.keys),
                pair_block(shape.keys),
                pl.BlockSpec((2, BANDS, T, T), lambda h, *_: (h, 0, 0, 0)),
            ],
            out_specs=[pair_block(rows), pl.BlockSpec((2, rows, 1), lambda h, *_: (h, 0, 0))],
        ),
        out_shape=[
            jax.ShapeDtypeStruct((rows, width), BF),
            jax.ShapeDtypeStruct((2 * pairs, rows, 1), F32),
        ],
        compiler_params=pltpu.CompilerParams(vmem_limit_bytes=VMEM_LIMIT),
    )(live, base, q, k, v, bias)


def attend_back_tile(
    shape, i, is_cont, live, base, q, k, v, bias, grad, out, norm, d_q, d_bias, k_sum, v_sum
):
    first_half, place = tile_lanes()
    rows = tile_rows(i)
    queries = q[rows, :]
    grads = grad[rows, :]
    query_tile = shape.tiles if is_cont else base + i
    overlap = grads.astype(F32) * out[rows, :].astype(F32)
    mixed = []
    for h in range(2):
        mine = first_half if h == 0 else ~first_half
        masked = jnp.where(mine, queries, jnp.zeros_like(queries))
        masked_grad = jnp.where(mine, grads, jnp.zeros_like(grads))
        inner = jnp.sum(jnp.where(mine, overlap, 0.0), axis=1, keepdims=True)
        log_norm = norm[h, rows, :]

        def piece(keys, bands, allowed):
            scores = nt(masked, k[keys, :])
            d_probs = nt(masked_grad, v[keys, :])
            probs_low, scores_low = [], []
            for at, band in enumerate(bands):
                cols = slice(at * T, (at + 1) * T)
                logits = scores[:, cols] + bias[h, band]
                if allowed is not None:
                    logits = jnp.where(allowed, logits, NEGATIVE)
                probs = jnp.exp(logits - log_norm)
                d_scores = probs * (d_probs[:, cols] - inner)
                d_bias[h, band] += d_scores
                probs_low.append(probs.astype(BF))
                scores_low.append(d_scores.astype(BF))
            probs_low = jnp.concatenate(probs_low, axis=1)
            scores_low = jnp.concatenate(scores_low, axis=1)
            v_sum[keys, :] += tn(probs_low, masked_grad)
            k_sum[keys, :] += tn(scores_low, masked)
            return nn(scores_low, k[keys, :])

        result = None
        for start, js in shape.parts:
            bands = [band_of(lax.rem(base + j, shape.tiles), query_tile) for j in js]
            term = piece(pl.ds(start, len(js) * T), bands, None)
            result = term if result is None else result + term
        if is_cont:
            result = result + piece(rows, [2], place < live[0, i - shape.local_tiles])
        mixed.append(result)
    d_q[rows, :] = jnp.where(first_half, mixed[0], mixed[1]).astype(BF)


def attend_back_kernel(
    shape, live, base, q, k, v, bias, grad, out, norm, d_q, d_k, d_v, d_bias, k_sum, v_sum
):
    k_sum[...] = jnp.zeros_like(k_sum)
    v_sum[...] = jnp.zeros_like(v_sum)
    d_bias[...] = jnp.zeros_like(d_bias)
    refs = (q, k, v, bias, grad, out, norm, d_q, d_bias, k_sum, v_sum)
    for conts in (False, True):
        for_tiles(shape, conts, lambda i, c: attend_back_tile(shape, i, c, live, base[0], *refs))
    d_k[...] = k_sum[...].astype(BF)
    d_v[...] = v_sum[...].astype(BF)


def attend_back(q, k, v, bias, grad, out, norm, live, base, shape):
    rows, width = q.shape
    pairs = width // (2 * HEAD)
    keys = shape.keys
    bands = pl.BlockSpec((2, BANDS, T, T), lambda h, *_: (h, 0, 0, 0))
    return pl.pallas_call(
        functools.partial(attend_back_kernel, shape),
        grid_spec=pltpu.PrefetchScalarGridSpec(
            num_scalar_prefetch=2,
            grid=(pairs,),
            in_specs=[
                pair_block(rows),
                pair_block(keys),
                pair_block(keys),
                bands,
                pair_block(rows),
                pair_block(rows),
                pl.BlockSpec((2, rows, 1), lambda h, *_: (h, 0, 0)),
            ],
            out_specs=[pair_block(rows), pair_block(keys), pair_block(keys), bands],
            scratch_shapes=[pltpu.VMEM((keys, 2 * HEAD), F32), pltpu.VMEM((keys, 2 * HEAD), F32)],
        ),
        out_shape=[
            jax.ShapeDtypeStruct((rows, width), BF),
            jax.ShapeDtypeStruct((keys, width), BF),
            jax.ShapeDtypeStruct((keys, width), BF),
            jax.ShapeDtypeStruct((2 * pairs, BANDS, T, T), F32),
        ],
        compiler_params=pltpu.CompilerParams(vmem_limit_bytes=VMEM_LIMIT),
    )(live, base, q, k, v, bias, grad, out, norm)


ORDER = (1, 2, 0, 3)
FIRST_PAIR = 8


def joined_pieces(w_buf, slot, m):
    pieces = [w_buf[slot, j // 3, j % 3] for j in (2 * m, 2 * m + 1)]
    return jnp.concatenate([piece.reshape(-1, T) for piece in pieces], axis=1)


def front_kernel(zs, xs, shape, early, live, *refs):
    (prompt_x, cont_x, own_gain, *weights) = refs[:10]
    table = refs[10]
    (whole, own_out, x_out, normed_out, kv_out, bias_out) = refs[11:17]
    (q, attended, norm, middle, normed_two, *gains) = refs[17:24]
    (x, normed, kv, bias, held, w_buf, gain_whole) = refs[24:31]
    (local, kv_sems, send, recv, gain_send, gain_recv) = refs[31:37]
    place = Place(zs, xs)
    step = pl.program_id(0)
    rows, width = x.shape
    prompt = shape.local_tiles * T
    pairs = q.shape[0]
    size = middle.shape[0]
    blocks = rows // size
    last = FIRST_PAIR + pairs
    count = 4 + early
    feed_weights = weights[4:]
    columns = feed_weights[0].shape[1] // T

    def x_load(i):
        source, part = ((prompt_x, pl.ds(0, prompt)), (cont_x, pl.ds(prompt, rows - prompt)))[i]
        return pltpu.make_async_copy(source, x.at[part], local.at[i])

    def mine_store():
        mine = whole.at[:, :, :, place.z, place.y, place.c * place.xs + place.x]
        return pltpu.make_async_copy(held.at[pl.ds(0, count)], mine, local.at[2])

    feed_own = held.at[pl.ds(4, held.shape[0] - 4)]
    kept = ((feed_own, own_out), (x, x_out), (normed, normed_out), (bias, bias_out), (kv, kv_out))

    def result(i):
        return pltpu.make_async_copy(*kept[i], local.at[3 + i])

    def weight_load(k):
        return pltpu.make_async_copy(whole.at[k], w_buf.at[k % 2], local.at[8 + k])

    @pl.when(step == 0)
    def _():
        place.barrier()
        x_load(0).start()
        x_load(1).start()
        for c, matrix in enumerate(ORDER):
            for j in range(6):
                held[c, j // 3, j % 3] = weights[matrix][:, j * T : (j + 1) * T].astype(BF)
        gain_whole[0, :, :, place.z, place.y, place.c * place.xs + place.x] = own_gain[0]

    Gather(place, own_gain, gain_whole, gain_send, gain_recv).tick(step, 0, 1)
    Gather(place, held, whole, send, recv).tick(step, 0, count)

    @pl.when(step == 0)
    def _():
        def convert(j, carry):
            part = pl.ds(pl.multiple_of(j * T, T), T)
            for i in range(3):
                held[4 + j // 2, j % 2, i] = feed_weights[i][:, part].astype(BF)
            return carry

        lax.fori_loop(0, columns, convert, 0)
        if columns % 2:
            held[4 + columns // 2, 1] = jnp.zeros(held.shape[2:], BF)
        mine_store().start()
        mine_store().wait()
        result(0).start()
        x_load(0).wait()
        x_load(1).wait()
        result(1).start()

    @pl.when(step == 1)
    def _():
        query = lax.broadcasted_iota(jnp.int32, (T, T), 0)
        key = lax.broadcasted_iota(jnp.int32, (T, T), 1)
        half = table.shape[1] // 2
        ids = [bucket_ids(band * T + key - query) for band in (-1, 0, 1)]
        found = (range(1, half), [*range(half), *range(half + 1, 2 * half)], range(half + 1, 2 * half))

        def one(h, carry):
            bias[h, 0] = jnp.full((T, T), table[h, half - 1])
            bias[h, 4] = jnp.full((T, T), table[h, 2 * half - 1])
            for band in range(3):
                value = jnp.zeros((T, T), F32)
                for bucket in found[band]:
                    value = jnp.where(ids[band] == bucket, table[h, bucket], value)
                bias[h, 1 + band] = value
            return carry

        lax.fori_loop(0, bias.shape[0], one, 0)

    for k in range(4):

        @pl.when(step == 4 + k)
        def _(k=k):
            weight_load(k).start()

    def by_rows(action):
        def one(i, carry):
            action(pl.ds(pl.multiple_of(i * size, size), size))
            return carry

        lax.fori_loop(0, blocks, one, 0)

    @pl.when(step == 4)
    def _():
        result(3).start()
        eye = lax.broadcasted_iota(jnp.int32, (T, T), 0) == lax.broadcasted_iota(jnp.int32, (T, T), 1)
        for g in range(2):
            column = gain_whole[0, g, 0].reshape(width, T).astype(F32)
            for i in range(width // T):
                cols = slice(i * T, (i + 1) * T)
                gains[g][:, cols] = jnp.sum(jnp.where(eye, column[cols], 0.0), axis=0, keepdims=True)

        def norm_rows(part):
            values = x[part, :].astype(F32)
            scale = lax.rsqrt(jnp.mean(values * values, axis=-1, keepdims=True) + EPS)
            normed[part, :] = (values * scale * gains[0][...]).astype(BF)

        by_rows(norm_rows)
        result(2).start()

    def project(slot, target):
        for m in range(pairs // 2):
            right = joined_pieces(w_buf, slot, m)

            def rows_of_product(part, m=m, right=right):
                product = nn(normed[part, :], right).astype(BF)
                target[2 * m, part, :] = product[:, :T]
                target[2 * m + 1, part, :] = product[:, T:]

            by_rows(rows_of_product)

    def kv_send(side, p):
        src = kv.at[side, p, pl.ds(0, prompt)]
        dst = kv.at[side, p, pl.ds(rows, prompt)]
        peer = place.device(x=1 - place.x)
        return remote(src, dst, kv_sems.at[0, side, p], kv_sems.at[1, side, p], peer)

    for k in range(3):

        @pl.when(step == 5 + k)
        def _(k=k):
            weight_load(k).wait()
            project(k % 2, kv.at[k] if k < 2 else q)
            if k < 2:
                for p in range(pairs):
                    kv_send(k, p).start()

    @pl.when(step == FIRST_PAIR)
    def _():
        weight_load(3).wait()

    @pl.when((step >= FIRST_PAIR) & (step < last))
    def _():
        p = step - FIRST_PAIR
        for side in range(2):
            kv_send(side, p).wait_recv()
            kv_send(side, p).wait_send()
        base = place.x * shape.local_tiles
        inputs = (q.at[p], kv.at[0, p], kv.at[1, p], bias.at[pl.ds(2 * p, 2)], attended.at[p], norm)
        for conts in (False, True):
            for_tiles(shape, conts, lambda i, c: attend_tile(shape, i, c, live, base, *inputs))

    @pl.when(step == last)
    def _():
        result(4).start()

    @pl.when(step >= last)
    def _():
        part = pl.ds(pl.multiple_of((step - last) * size, size), size)
        branch = None
        for m in range(pairs // 2):
            left = jnp.concatenate([attended[2 * m + e, part, :] for e in range(2)], axis=1)
            term = nt(left, joined_pieces(w_buf, 1, m))
            branch = term if branch is None else branch + term
        total = x[part, :].astype(F32) + branch
        middle[...] = total
        scale = lax.rsqrt(jnp.mean(total * total, axis=-1, keepdims=True) + EPS)
        normed_two[...] = (total * scale * gains[1][...]).astype(BF)

    @pl.when(step == last + blocks - 1)
    def _():
        for i in range(len(kept)):
            result(i).wait()


def front(prompt_x, cont_x, own_gain, weights, table, live, shape, sizes, early, collective_id):
    grp, seq = sizes
    rows, width = shape.rows, prompt_x.shape[1]
    shard, inner = weights[0].shape
    feed_columns = weights[4].shape[1] // T
    pairs, keys, heads = inner // (2 * HEAD), shape.keys, table.shape[0]
    assert pairs == 6 and table.shape[1] == 32 and keys - rows == prompt_x.shape[0]
    zs = grp // (Y * C)
    chunks = 4 + (feed_columns + 1) // 2
    count = 4 + early
    own = (2, 3, shard, T)
    tile = (2, 3, zs, Y, C * seq, shard, T)
    size = min(rows, 256)
    blocks = rows // size
    last = FIRST_PAIR + pairs
    steps = last + blocks
    assert count + 4 <= steps and count <= chunks
    full = lambda *dims: pl.BlockSpec(
        dims, lambda s, *_: (0,) * len(dims), pipeline_mode=pl.Buffered(1)
    )
    by_rows = pl.BlockSpec((size, width), lambda s, *_: (jnp.clip(s - last, 0, blocks - 1), 0))
    anywhere = pl.BlockSpec(memory_space=pl.ANY)
    sems = lambda *dims: pltpu.SemaphoreType.DMA(dims)
    out = jax.ShapeDtypeStruct
    return pl.pallas_call(
        functools.partial(front_kernel, zs, seq, shape, early),
        grid_spec=pltpu.PrefetchScalarGridSpec(
            num_scalar_prefetch=1,
            grid=(steps,),
            in_specs=[anywhere, anywhere, full(*own_gain.shape)]
            + [full(*w.shape) for w in weights]
            + [pl.BlockSpec(memory_space=pltpu.SMEM)],
            out_specs=[anywhere] * 6
            + [
                full(pairs, rows, 2 * HEAD),
                full(pairs, rows, 2 * HEAD),
                pl.BlockSpec(
                    (2, rows, 1), lambda s, *_: (jnp.clip(s - FIRST_PAIR, 0, pairs - 1), 0, 0)
                ),
                by_rows,
                by_rows,
                full(1, width),
                full(1, width),
            ],
            scratch_shapes=[
                pltpu.VMEM((rows, width), BF),
                pltpu.VMEM((rows, width), BF),
                pltpu.VMEM((2, pairs, keys, 2 * HEAD), BF),
                pltpu.VMEM((heads, BANDS, T, T), F32),
                pltpu.VMEM((chunks, *own), BF),
                pltpu.VMEM((2, *tile), BF),
                pltpu.VMEM((1, 2, 1, zs, Y, C * seq, shard, T), BF),
                sems(12),
                sems(2, 2, pairs),
                sems(count, 2, zs + 2),
                sems(count, 2, zs + 2),
                sems(1, 2, zs + 2),
                sems(1, 2, zs + 2),
            ],
        ),
        out_shape=[
            out((count, *tile), BF),
            out((chunks - 4, *own), BF),
            out((rows, width), BF),
            out((rows, width), BF),
            out((2, pairs, keys, 2 * HEAD), BF),
            out((heads, BANDS, T, T), F32),
            out((pairs, rows, 2 * HEAD), BF),
            out((pairs, rows, 2 * HEAD), BF),
            out((2 * pairs, rows, 1), F32),
            out((rows, width), F32),
            out((rows, width), BF),
            out((1, width), F32),
            out((1, width), F32),
        ],
        compiler_params=pltpu.CompilerParams(
            collective_id=collective_id, has_side_effects=True, vmem_limit_bytes=VMEM_LIMIT
        ),
    )(live, prompt_x, cont_x, own_gain, *weights, table)


SPAN = 4 * T
VECTOR_ROWS = 8


def turned(tile):
    row = lax.broadcasted_iota(jnp.int32, tile.shape, 0)
    for bit in range(7):
        moved = pltpu.roll(tile, SPAN - (1 << bit), 1)
        tile = jnp.where((row >> bit) & 1 == 1, moved, tile)
    return tile


def band_sums(d_bias, h):
    near = jnp.concatenate([d_bias[h, 1], d_bias[h, 2], d_bias[h, 3]], axis=1)
    near = jnp.concatenate([near, jnp.zeros((T, T), F32)], axis=1)
    diagonal = jnp.sum(turned(near), axis=0, keepdims=True)
    rows = [diagonal[:, i * T : (i + 1) * T] for i in range(4)]
    rows += [jnp.sum(d_bias[h, band], axis=0, keepdims=True) for band in (0, 4)]
    return jnp.concatenate(rows + [jnp.zeros((2, T), F32)], axis=0)


def put(i, first_blocks, targets, value):
    @pl.when(i < first_blocks)
    def _():
        targets[0][...] = value

    @pl.when(i >= first_blocks)
    def _():
        targets[1][...] = value


def two_parts(size, width, first_blocks, blocks, first_step):
    one = lambda s, *_: (jnp.clip(s - first_step, 0, first_blocks - 1), 0)
    two = lambda s, *_: (jnp.clip(s - first_step - first_blocks, 0, blocks - first_blocks - 1), 0)
    return [pl.BlockSpec((size, width), one), pl.BlockSpec((size, width), two)]


def rows_of(vector):
    return [vector[:, i * T : (i + 1) * T] for i in range(vector.shape[1] // T)]


class Combine:
    STAGES = 4

    def __init__(self, place, total, arrived, send, recv):
        self.p, self.total, self.arrived, self.send, self.recv = place, total, arrived, send, recv

    def copies(self, i):
        p = self.p
        if i < 3:
            peers = [(i, (p.device(c=1 - p.c), p.device(x=1 - p.x), p.device(y=1 - p.y))[i])]
        else:
            peers = [(3 + d, p.device(z=(p.z + d) % p.zs)) for d in range(1, p.zs)]
        return [
            remote(self.total.at[i], self.arrived.at[at], self.send.at[at], self.recv.at[at], peer)
            for at, peer in peers
        ]

    def start(self, i):
        for copy in self.copies(i):
            copy.start()

    def finish(self, i):
        p = self.p
        for copy in self.copies(i):
            copy.wait_recv()
            copy.wait_send()
        if i < 3:
            self.total[i + 1] = self.total[i] + self.arrived[i]
        else:
            self.arrived[3] = self.total[i]
            terms = [self.arrived[3 + (p.z - z + p.zs) % p.zs] for z in range(p.zs)]
            self.total[i + 1] = functools.reduce(jnp.add, terms)


def back_kernel(zs, xs, shape, width, kept, live, *refs):
    q, k, v, bias, grad, out, norm, attended, branch_hbm, normed_hbm, parts, weights_hbm = refs[:12]
    d_middle, x_low, gain, d_gain_two, kept_sums = refs[12:17]
    d_x, feed_out, attention_out, vector_out = refs[17:19], refs[19:22], refs[22:26], refs[26]
    refs = refs[7:]
    (stage, turn_buf, d_q, d_kv, back_kv, k_sum, v_sum, d_bias) = refs[20:28]
    (w_buf, held, vector, total, arrived, gain_sum) = refs[28:34]
    (local, loads, kv_sems, both_sems) = refs[34:38]
    bufs, scatter_sems = refs[38 : 38 + BUFFERS], refs[38 + BUFFERS :]
    place = Place(zs, xs)
    step = pl.program_id(0)
    rows, keys = shape.rows, shape.keys
    prompt = shape.local_tiles * T
    pairs = d_q.shape[0]
    last = 2 * pairs
    turns = rows // T
    first_kept, end_kept = kept
    fed = parts.shape[0] - (end_kept - first_kept)
    size = d_x[0].shape[0]
    blocks = rows // size

    def stage_load(source):
        return pltpu.make_async_copy(source, stage, local.at[0])

    def weights_load(i):
        return pltpu.make_async_copy(weights_hbm.at[(2, 0, 1)[i]], w_buf.at[i], local.at[1 + i])

    def turn():
        def one(i, carry):
            part = tile_rows(i)
            turn_buf[:, part] = stage[part, :].T
            return carry

        lax.fori_loop(0, turns, one, 0)

    def part_load(c):
        j = jnp.where(c < first_kept, c, c + end_kept - first_kept)
        return pltpu.make_async_copy(parts.at[j], held.at[c % 3], loads.at[c % 3])

    @pl.when(step == 0)
    def _():
        part_load(step).start()
        stage_load(branch_hbm).start()
        place.barrier()
        for i in range(3):
            weights_load(i).start()

    def feed_store(j, half, total):
        piece = 2 * j + half

        @pl.when(piece < feed_out[0].shape[1] // T)
        def _():
            part = pl.ds(pl.multiple_of(piece * T, T), T)
            for i in range(3):
                feed_out[i][:, part] = total[i]

    def keep(c, half, total):
        @pl.when(c < fed)
        def _():
            feed_store(jnp.where(c < first_kept, c, c + end_kept - first_kept), half, total)

        for m, matrix in enumerate((3, 0, 1, 2)):

            @pl.when(c == fed + m)
            def _(matrix=matrix):
                for i in range(3):
                    piece = 3 * half + i
                    attention_out[matrix][:, piece * T : (piece + 1) * T] = total[i]

    @pl.when(step == 1)
    def _():
        def one(k, carry):
            for half in range(2):
                feed_store(k + first_kept, half, kept_sums[k, half])
            return carry

        lax.fori_loop(0, end_kept - first_kept, one, 0)

    engine = Scatter(place, bufs, *scatter_sems, keep)

    def due(offset, action):
        at = step - offset
        chunk = jnp.where(at <= fed, at, at - last + fed)
        early = (at >= 0) & (at <= fed)
        late = (at > last) & (at < last + 4)

        @pl.when(early | late)
        def _():
            action(chunk)

    def first(c):
        @pl.when(c < fed)
        def _():
            part_load(c).wait()

        engine.start_first(c, held.at[c % 3])

    due(4, engine.finish)
    due(3, engine.start_fourth)
    due(2, engine.start_third)
    due(1, lambda c: engine.start_second(c, held.at[c % 3]))
    due(0, first)

    @pl.when(step + 1 < fed)
    def _():
        part_load(step + 1).start()

    @pl.when(step == 0)
    def _():
        stage_load(branch_hbm).wait()
        turn()
        stage_load(normed_hbm).start()

    def kv_send(p):
        src = d_kv.at[p, :, pl.ds(rows, keys - rows)]
        peer = place.device(x=1 - place.x)
        return remote(src, back_kv.at[p], kv_sems.at[0, p], kv_sems.at[1, p], peer)

    @pl.when(step < last)
    def _():
        p = step // 2
        half = step % 2

        @pl.when(half == 0)
        def _():
            k_sum[...] = jnp.zeros_like(k_sum)
            v_sum[...] = jnp.zeros_like(v_sum)
            d_bias[...] = jnp.zeros_like(d_bias)

        inputs = (q, k, v, bias, grad, out, norm, d_q.at[p], d_bias, k_sum, v_sum)
        base = place.x * shape.local_tiles
        action = lambda i, c: attend_back_tile(shape, i, c, live, base, *inputs)

        @pl.when(half == 0)
        def _():
            for_tiles(shape, False, action)

        @pl.when(half == 1)
        def _():
            for_tiles(shape, True, action)
            d_kv[p, 0] = k_sum[...].astype(BF)
            d_kv[p, 1] = v_sum[...].astype(BF)
            kv_send(p).start()
            for h in range(2):
                vector[2 * p + h] = band_sums(d_bias, h)

    def produce(c, right):
        slot = c % 3
        for m in range(3):
            operand = right(m)

            def one(z, carry, m=m, operand=operand):
                block = turn_buf.shape[0] // zs
                part = pl.ds(pl.multiple_of(z * block, block), block)
                result = nn(turn_buf[part, :], operand).astype(BF)
                for side in range(2):
                    index = 2 * m + side
                    value = result[:, side * T : (side + 1) * T]
                    held[slot, index // 3, index % 3, z] = value.reshape(held.shape[4:])
                return carry

            lax.fori_loop(0, zs, one, 0)

    @pl.when(step == fed - 1)
    def _():
        produce(fed, lambda m: jnp.concatenate([attended[2 * m], attended[2 * m + 1]], axis=1))

    @pl.when(step == last)
    def _():
        stage_load(normed_hbm).wait()
        turn()
        produce(fed + 1, lambda m: jnp.concatenate([d_q[2 * m], d_q[2 * m + 1]], axis=1))

        def join(p, carry):
            kv_send(p).wait_recv()
            kv_send(p).wait_send()
            for side in range(2):
                own = d_kv[p, side, 0:prompt, :].astype(F32)
                d_kv[p, side, 0:prompt, :] = (own + back_kv[p, side].astype(F32)).astype(BF)
            return carry

        lax.fori_loop(0, pairs, join, 0)
        for i in range(3):
            weights_load(i).wait()
        gain_sum[...] = jnp.zeros_like(gain_sum)

    for side in range(2):

        @pl.when(step == last + 1 + side)
        def _(side=side):
            pick = lambda p: d_kv[p, side, 0:rows, :]
            produce(fed + 2 + side, lambda m: jnp.concatenate([pick(2 * m), pick(2 * m + 1)], axis=1))

    @pl.when((step >= last) & (step < last + blocks))
    def _():
        part = pl.ds(pl.multiple_of((step - last) * size, size), size)
        d_normed = None
        for i in range(3):
            for m in range(pairs // 2):
                if i == 0:
                    left = [d_q[2 * m + e, part, :] for e in range(2)]
                else:
                    left = [d_kv[2 * m + e, i - 1, part, :] for e in range(2)]
                pieces = [2 * m, 2 * m + 1]
                right = [w_buf[i, j // 3, j % 3].reshape(width, T) for j in pieces]
                term = nt(jnp.concatenate(left, axis=1), jnp.concatenate(right, axis=1))
                d_normed = term if d_normed is None else d_normed + term
        x = x_low[...].astype(F32)
        scale = lax.rsqrt(jnp.mean(x * x, axis=-1, keepdims=True) + EPS)
        unit = x * scale
        gain_sum[...] += jnp.sum(d_normed * unit, axis=0, keepdims=True)
        d_unit = d_normed * gain[...]
        inner = jnp.mean(d_unit * unit, axis=-1, keepdims=True)
        value = (d_middle[...] + scale * (d_unit - unit * inner)).astype(BF)
        put(step - last, prompt // size, d_x, value)

    mix = Combine(place, total, arrived, both_sems.at[0], both_sems.at[1])
    start = last + blocks
    tiles = 2 * pairs

    @pl.when(step == start - 1)
    def _():
        total[0, 0:tiles] = vector[...]
        both = rows_of(gain_sum[...]) + rows_of(d_gain_two[...])
        for i in range(len(both) // VECTOR_ROWS):
            group = both[i * VECTOR_ROWS : (i + 1) * VECTOR_ROWS]
            total[0, tiles + i] = jnp.concatenate(group, axis=0)
        mix.start(0)

    for i in range(mix.STAGES):

        @pl.when(step == start + i)
        def _(i=i):
            mix.finish(i)
            if i + 1 < mix.STAGES:
                mix.start(i + 1)
            else:
                vector_out[...] = total[mix.STAGES]


def back(q, kv, bias, grad, out, norm, branch, normed, parts, weights, d_middle, x_low, gain,
         d_gain_two, kept_sums, hidden, live, shape, sizes, kept, collective_id):
    grp, seq = sizes
    rows, width = x_low.shape
    pairs = q.shape[0]
    zs = grp // (Y * C)
    keys = shape.keys
    chunks, _, n, _, _, _, shard, lanes = parts.shape
    assert 0 < chunks - (kept[1] - kept[0]) <= 2 * pairs
    assert (pairs, n) == (6, 3) and 2 * width // T % VECTOR_ROWS == 0
    last = 2 * pairs
    size = min(rows, 256)
    blocks = rows // size
    prompt = shape.local_tiles * T
    assert prompt % size == 0
    tile = (2, n, zs, Y, C * seq, shard, lanes)
    stages = Combine.STAGES
    steps = max(last + blocks + stages, last + 8)
    inner = pairs * 2 * HEAD
    vector = (2 * pairs + 2 * width // T // VECTOR_ROWS, VECTOR_ROWS, T)
    pair = lambda s: jnp.minimum(s // 2, pairs - 1)
    by_pair = lambda rows_: pl.BlockSpec((rows_, 2 * HEAD), lambda s, *_: (0, pair(s)))
    in_pair = pl.BlockSpec((None, rows, 2 * HEAD), lambda s, *_: (pair(s), 0, 0))
    of_keys = lambda side: pl.BlockSpec(
        (None, None, keys, 2 * HEAD), lambda s, *_: (side, pair(s), 0, 0)
    )
    row_block = lambda s: jnp.clip(s - last, 0, blocks - 1)
    by_rows = pl.BlockSpec((size, width), lambda s, *_: (row_block(s), 0))
    full = lambda *dims: pl.BlockSpec(
        dims, lambda s, *_: (0,) * len(dims), pipeline_mode=pl.Buffered(1)
    )
    anywhere = pl.BlockSpec(memory_space=pl.ANY)
    sems = lambda *dims: pltpu.SemaphoreType.DMA(dims)
    return pl.pallas_call(
        functools.partial(back_kernel, zs, seq, shape, width, kept),
        grid_spec=pltpu.PrefetchScalarGridSpec(
            num_scalar_prefetch=1,
            grid=(steps,),
            in_specs=[
                in_pair,
                of_keys(0),
                of_keys(1),
                pl.BlockSpec((2, BANDS, T, T), lambda s, *_: (pair(s), 0, 0, 0)),
                by_pair(rows),
                in_pair,
                pl.BlockSpec((2, rows, 1), lambda s, *_: (pair(s), 0, 0)),
                full(pairs, rows, 2 * HEAD),
                anywhere,
                anywhere,
                anywhere,
                anywhere,
                by_rows,
                by_rows,
                full(1, width),
                full(1, width),
                full(*kept_sums.shape),
            ],
            out_specs=two_parts(size, width, prompt // size, blocks, last)
            + [full(shard, hidden)] * 3
            + [full(shard, inner)] * 4
            + [full(*vector)],
            scratch_shapes=[
                pltpu.VMEM((rows, width), BF),
                pltpu.VMEM((width, rows), BF),
                pltpu.VMEM((pairs, rows, 2 * HEAD), BF),
                pltpu.VMEM((pairs, 2, keys, 2 * HEAD), BF),
                pltpu.VMEM((pairs, 2, keys - rows, 2 * HEAD), BF),
                pltpu.VMEM((keys, 2 * HEAD), F32),
                pltpu.VMEM((keys, 2 * HEAD), F32),
                pltpu.VMEM((2, BANDS, T, T), F32),
                pltpu.VMEM((3, *tile), BF),
                pltpu.VMEM((3, *tile), BF),
                pltpu.VMEM((2 * pairs, VECTOR_ROWS, T), F32),
                pltpu.VMEM((stages + 1, *vector), F32),
                pltpu.VMEM((3 + zs, *vector), F32),
                pltpu.VMEM((1, width), F32),
                sems(4),
                sems(3),
                sems(2, pairs),
                sems(2, 3 + zs),
            ]
            + scatter_buffers(n, zs, seq, shard, lanes)
            + [sems(2, 2, zs + 2), sems(2, 2, zs + 2)],
        ),
        out_shape=[
            jax.ShapeDtypeStruct((prompt, width), BF),
            jax.ShapeDtypeStruct((rows - prompt, width), BF),
        ]
        + [jax.ShapeDtypeStruct((shard, hidden), F32)] * 3
        + [jax.ShapeDtypeStruct((shard, inner), F32)] * 4
        + [
            jax.ShapeDtypeStruct(vector, F32),
        ],
        compiler_params=pltpu.CompilerParams(
            collective_id=collective_id, has_side_effects=True, vmem_limit_bytes=VMEM_LIMIT
        ),
    )(live, q, kv, kv, bias, grad, out, norm, out, branch, normed, parts, weights, d_middle,
      x_low, gain, d_gain_two, kept_sums)


GELU_SCALE = 0.7978845608028654
GELU_CUBIC = 0.044715


def gelu_and_slope(a):
    square = a * a
    tanh = jnp.tanh(GELU_SCALE * a * (1.0 + GELU_CUBIC * square))
    half = 0.5 * (1.0 + tanh)
    slope = half + 0.5 * a * (1.0 - tanh * tanh) * (
        GELU_SCALE * (1.0 + 3.0 * GELU_CUBIC * square)
    )
    return a * half, slope


def feed_load(x_hbm, dy_parts, x, x_t, dy, dy_t, sem):
    loads = [pltpu.make_async_copy(x_hbm, x, sem.at[0])]
    start = 0
    for i, part in enumerate(dy_parts):
        target = dy.at[pl.ds(start, part.shape[0])]
        loads.append(pltpu.make_async_copy(part, target, sem.at[1 + i]))
        start += part.shape[0]
    for load in loads:
        load.start()
    for load in loads:
        load.wait()

    def turn(i, carry):
        part = pl.ds(pl.multiple_of(i * T, T), T)
        x_t[:, part] = x[part, :].T
        dy_t[:, part] = dy[part, :].T
        return carry

    lax.fori_loop(0, x.shape[0] // T, turn, 0)


def feed_chunk(read, write, blocks, out, d_x, x, x_t, dy, dy_t, hidden, d_gate, d_up):
    rows, width = x.shape
    row_block = min(rows, 256)
    width_block = width // blocks
    w_gate, w_up, w_down = [jnp.concatenate([read(0, i), read(1, i)], axis=1) for i in range(3)]

    def by_rows(i, carry):
        part = pl.ds(pl.multiple_of(i * row_block, row_block), row_block)
        gate = nn(x[part, :], w_gate)
        up = nn(x[part, :], w_up)
        d_hidden = nn(dy[part, :], w_down)
        active, slope = gelu_and_slope(gate)
        hidden_low = (active * up).astype(BF)
        d_gate_low = (d_hidden * up * slope).astype(BF)
        d_up_low = (d_hidden * active).astype(BF)
        hidden[part, :] = hidden_low
        d_gate[part, :] = d_gate_low
        d_up[part, :] = d_up_low
        out[part, :] += nt(hidden_low, w_down)
        d_x[part, :] += nt(d_gate_low, w_gate) + nt(d_up_low, w_up)
        return carry

    lax.fori_loop(0, rows // row_block, by_rows, 0)

    def by_width(i, carry):
        part = pl.ds(pl.multiple_of(i * width_block, width_block), width_block)
        pairs = ((x_t, d_gate), (x_t, d_up), (dy_t, hidden))
        for index, (left, right) in enumerate(pairs):
            total = nn(left[part, :], right[...]).astype(BF)
            write(0, index, i, total[:, :T])
            write(1, index, i, total[:, T:])
        return carry

    lax.fori_loop(0, blocks, by_width, 0)


def feed_kernel(x_hbm, dy_hbm, weights, out, d_x, grads, x, x_t, dy, dy_t, *rest):
    *work, sem = rest
    width_block = 512

    @pl.when(pl.program_id(0) == 0)
    def _():
        feed_load(x_hbm, [dy_hbm], x, x_t, dy, dy_t, sem)
        out[...] = jnp.zeros_like(out)
        d_x[...] = jnp.zeros_like(d_x)

    def write(half, index, block, value):
        part = pl.ds(pl.multiple_of(block * width_block, width_block), width_block)
        grads[0, half, index, part, :] = value

    read = lambda half, index: weights[0, half, index]
    blocks = x.shape[1] // width_block
    feed_chunk(read, write, blocks, out, d_x, x, x_t, dy, dy_t, *work)


def feed_scratch(rows, width):
    return [
        pltpu.VMEM((rows, width), BF),
        pltpu.VMEM((width, rows), BF),
        pltpu.VMEM((rows, width), BF),
        pltpu.VMEM((width, rows), BF),
        pltpu.VMEM((rows, 2 * T), BF),
        pltpu.VMEM((rows, 2 * T), BF),
        pltpu.VMEM((rows, 2 * T), BF),
        pltpu.SemaphoreType.DMA((3,)),
    ]


def feed(x, dy, weights):
    rows, width = x.shape
    chunks = weights.shape[0]
    chunk = pl.BlockSpec((1, 2, 3, width, T), lambda j: (j, 0, 0, 0, 0))
    whole = pl.BlockSpec((rows, width), lambda j: (0, 0), pipeline_mode=pl.Buffered(1))
    return pl.pallas_call(
        feed_kernel,
        grid=(chunks,),
        in_specs=[pl.BlockSpec(memory_space=pl.ANY)] * 2 + [chunk],
        out_specs=[whole, whole, chunk],
        out_shape=[
            jax.ShapeDtypeStruct((rows, width), F32),
            jax.ShapeDtypeStruct((rows, width), F32),
            jax.ShapeDtypeStruct((chunks, 2, 3, width, T), BF),
        ],
        scratch_shapes=feed_scratch(rows, width),
        compiler_params=pltpu.CompilerParams(vmem_limit_bytes=VMEM_LIMIT),
    )(x, dy, weights)


def feed_moving_kernel(zs, xs, early, kept, *refs):
    x_hbm, dy_one, dy_two, own, ready, middle, gain, whole, parts, sums = refs[:10]
    final, (d_middle, d_branch, d_attended, d_gain) = refs[10:12], refs[12:16]
    x, x_t, dy, dy_t, hidden, d_gate, d_up, sem = refs[16:24]
    out, d_x, held, w_buf, g_buf, local = refs[24:30]
    gather_sems, bufs = refs[30:32], refs[32 : 32 + BUFFERS]
    scatter_sems = refs[32 + BUFFERS :]
    chunks = own.shape[0]
    place = Place(zs, xs)
    step = pl.program_id(0)
    lag = max(0, 5 - early)
    first_kept, end_kept = kept
    width = x.shape[1]

    @pl.when(step == 0)
    def _():
        place.barrier()

    fetch = Gather(place, own, whole, *gather_sems)
    fetch.tick(step, early, chunks)

    @pl.when(step == 0)
    def _():
        load = pltpu.make_async_copy(own, held, local.at[0])
        load.start()
        load.wait()
        mine = whole.at[:, :, :, place.z, place.y, place.c * place.xs + place.x]
        store = pltpu.make_async_copy(held, mine, local.at[1])
        store.start()
        store.wait()
        feed_load(x_hbm, [dy_one, dy_two], x, x_t, dy, dy_t, sem)
        out[...] = jnp.zeros_like(out)
        d_x[...] = jnp.zeros_like(d_x)

    skipped = ready.shape[0] - early

    def weight_load(j, source, first=0):
        return pltpu.make_async_copy(source.at[first + j], w_buf.at[j % 2], local.at[2 + j % 2])

    def start_load(j):
        if early > 0:

            @pl.when(j < early)
            def _():
                weight_load(j, ready, skipped).start()

        @pl.when(j >= early)
        def _():
            weight_load(j, whole).start()

    def part_store(j):
        return pltpu.make_async_copy(g_buf.at[j % 2], parts.at[j], local.at[4 + j % 2])

    def is_kept(j):
        return (j >= first_kept) & (j < end_kept)

    def keep(k, half, total):
        sums[k, half] = total

    engine = Scatter(place, bufs, *scatter_sems, keep)
    due = lag + first_kept
    number = end_kept - first_kept
    grads_of = lambda k: g_buf.at[(k + first_kept) % 2]

    def tick(at):
        staged(at, due + 5, number, engine.finish)
        staged(at, due + 4, number, engine.start_fourth)
        staged(at, due + 3, number, engine.start_third)
        staged(at, due + 2, number, lambda k: engine.start_second(k, grads_of(k)))
        staged(at, due + 1, number, lambda k: engine.start_first(k, grads_of(k)))

    tick(step)

    chunk = step - lag
    if lag == 0:

        @pl.when(step == 0)
        def _():
            start_load(0)

    @pl.when((chunk >= (0 if lag == 0 else -1)) & (chunk + 1 < chunks))
    def _():
        start_load(chunk + 1)

    @pl.when((chunk >= 2) & (chunk < chunks + 2) & ~is_kept(chunk - 2))
    def _():
        part_store(chunk - 2).wait()

    @pl.when((chunk >= 0) & (chunk < chunks))
    def _():
        weight_load(chunk, whole).wait()
        slot = chunk % 2

        def read(half, index):
            return w_buf[slot, half, index].reshape(width, T)

        def write(half, index, block, value):
            shape = g_buf.shape[4:]
            g_buf[slot, half, index, block] = value.reshape(shape)

        work = (hidden, d_gate, d_up)
        feed_chunk(read, write, zs, out, d_x, x, x_t, dy, dy_t, *work)

        @pl.when(~is_kept(chunk))
        def _():
            part_store(chunk).start()

    spare = chunks % 2
    rows, size = x.shape[0], middle.shape[0]
    blocks = rows // size

    def o_load():
        return pltpu.make_async_copy(ready.at[skipped - 1], w_buf.at[spare], local.at[6])

    @pl.when(chunk == chunks - 1)
    def _():
        o_load().start()
        d_gain[...] = jnp.zeros_like(d_gain)

    @pl.when(chunk == chunks)
    def _():
        o_load().wait()

    @pl.when((chunk >= chunks) & (chunk < chunks + blocks))
    def _():
        i = chunk - chunks
        part = pl.ds(pl.multiple_of(i * size, size), size)
        values = middle[...]
        put(i, dy_one.shape[0] // size, final, (values + out[part, :]).astype(BF))
        scale = rms_scale(values)
        unit = values * scale
        d_normed = d_x[part, :]
        d_gain[...] += jnp.sum(d_normed * unit, axis=0, keepdims=True)
        total = dy[part, :].astype(F32) + norm_back(d_normed, unit, scale, gain[...])
        d_middle[...] = total
        low = total.astype(BF)
        d_branch[...] = low
        for m in range(d_attended.shape[1] // (2 * T)):
            right = joined_pieces(w_buf, spare, m)
            d_attended[:, 2 * m * T : 2 * (m + 1) * T] = nn(low, right).astype(BF)


def feed_moving(x, dy_one, dy_two, own, ready, middle, gain, inner, sizes, early, kept, collective_id):
    grp, seq = sizes
    rows, width = x.shape
    chunks, _, n, shard, lanes = own.shape
    zs = grp // (Y * C)
    tile = (2, n, zs, Y, C * seq, shard, lanes)
    one = pl.BlockSpec((1, width), lambda j: (0, 0), pipeline_mode=pl.Buffered(1))
    number = kept[1] - kept[0]
    sums = pl.BlockSpec(
        (number, 2, n, shard, lanes), lambda j: (0,) * 5, pipeline_mode=pl.Buffered(1)
    )
    lag = max(0, 5 - early)
    size = min(rows, 256)
    blocks = rows // size
    assert dy_one.shape[0] % size == 0
    tail = lag + chunks
    steps = max(tail + max(2, blocks), lag + kept[1] + 5)
    by_rows = lambda columns: pl.BlockSpec(
        (size, columns), lambda j: (jnp.clip(j - tail, 0, blocks - 1), 0)
    )
    out = jax.ShapeDtypeStruct
    anywhere = pl.BlockSpec(memory_space=pl.ANY)
    sems = lambda *shape: pltpu.SemaphoreType.DMA(shape)
    return pl.pallas_call(
        functools.partial(feed_moving_kernel, zs, seq, early, kept),
        grid=(steps,),
        in_specs=[anywhere] * 5 + [by_rows(width), one],
        out_specs=[anywhere, anywhere, sums]
        + two_parts(size, width, dy_one.shape[0] // size, blocks, tail)
        + [by_rows(width), by_rows(width), by_rows(inner), one],
        out_shape=[
            out((chunks, *tile), BF),
            out((chunks, *tile), BF),
            out((number, 2, n, shard, lanes), F32),
            out(dy_one.shape, BF),
            out(dy_two.shape, BF),
            out((rows, width), F32),
            out((rows, width), BF),
            out((rows, inner), BF),
            out((1, width), F32),
        ],
        scratch_shapes=feed_scratch(rows, width)
        + [
            pltpu.VMEM((rows, width), F32),
            pltpu.VMEM((rows, width), F32),
            pltpu.VMEM(own.shape, BF),
            pltpu.VMEM((2, *tile), BF),
            pltpu.VMEM((2, *tile), BF),
            sems(7),
            sems(chunks, 2, zs + 2),
            sems(chunks, 2, zs + 2),
        ]
        + scatter_buffers(n, zs, seq, shard, lanes)
        + [sems(2, 2, zs + 2), sems(2, 2, zs + 2)],
        compiler_params=pltpu.CompilerParams(
            collective_id=collective_id, has_side_effects=True, vmem_limit_bytes=VMEM_LIMIT
        ),
    )(x, dy_one, dy_two, own, ready, middle, gain)


def settle_kernel(*refs):
    *refs, sem = refs
    count = len(refs) // 3
    sources, targets, held = refs[:count], refs[count : 2 * count], refs[2 * count :]
    loads = [pltpu.make_async_copy(sources[i], held[i], sem.at[i]) for i in range(count)]
    stores = [pltpu.make_async_copy(held[i], targets[i], sem.at[count + i]) for i in range(count)]
    for load in loads:
        load.start()
    for load, store in zip(loads, stores):
        load.wait()
        store.start()
    for store in stores:
        store.wait()


def settle(*arrays):
    anywhere = pl.BlockSpec(memory_space=pl.ANY)
    return pl.pallas_call(
        settle_kernel,
        in_specs=[anywhere] * len(arrays),
        out_specs=[anywhere] * len(arrays),
        out_shape=[jax.ShapeDtypeStruct(a.shape, a.dtype) for a in arrays],
        scratch_shapes=[pltpu.VMEM(a.shape, a.dtype) for a in arrays]
        + [pltpu.SemaphoreType.DMA((2 * len(arrays),))],
        compiler_params=pltpu.CompilerParams(vmem_limit_bytes=VMEM_LIMIT),
    )(*arrays)


def rms_scale(values):
    return lax.rsqrt(jnp.mean(values * values, axis=-1, keepdims=True) + EPS)


def norm_back(d_normed, unit, scale, gain):
    d_unit = d_normed * gain
    return scale * (d_unit - unit * jnp.mean(d_unit * unit, axis=-1, keepdims=True))


def pieces_of(matrix):
    rows, columns = matrix.shape
    return jnp.swapaxes(matrix.reshape(rows, columns // T, T), 0, 1)


def joined(pieces):
    count, rows, _ = pieces.shape
    return jnp.swapaxes(pieces, 0, 1).reshape(rows, count * T)


def attention_chunks(matrices):
    flat = jnp.concatenate([pieces_of(m) for m in matrices], axis=0)
    pad = -flat.shape[0] % 6
    flat = jnp.pad(flat, ((0, pad), (0, 0), (0, 0)))
    return flat.reshape(-1, 2, 3, *flat.shape[1:])


def feed_chunks(matrices):
    stacked = jnp.stack([pieces_of(m) for m in matrices], axis=1)
    pad = -stacked.shape[0] % 2
    stacked = jnp.pad(stacked, ((0, pad), (0, 0), (0, 0), (0, 0)))
    return stacked.reshape(-1, 2, *stacked.shape[1:])


def body(sizes, *args):
    (
        prompt_x,
        cont_x,
        cont_len,
        prompt_cot,
        cont_cot,
        norm1_gain,
        q_weight,
        k_weight,
        v_weight,
        o_weight,
        bucket_table,
        norm2_gain,
        gate_weight,
        up_weight,
        down_weight,
    ) = args
    _, local_prompt, width = prompt_x.shape
    conts, cont_rows = cont_x.shape[1], cont_x.shape[2]
    assert prompt_x.shape[0] == 1 and cont_rows == T and local_prompt % T == 0
    seq = sizes[1]
    num_buckets, heads = bucket_table.shape
    inner = q_weight.shape[1]
    assert inner == heads * HEAD
    shard = q_weight.shape[0]
    hidden_width = gate_weight.shape[1]
    local_tiles = local_prompt // T
    tiles = local_tiles * seq
    seq_index = lax.axis_index("seq")

    split = lambda parts: (parts[0][None], parts[1].reshape(1, conts, cont_rows, width))
    cut = lambda values: (values[:local_prompt], values[local_prompt:])
    shape = Shape(tiles, local_tiles, conts)
    count = inner // T
    if can_move(sizes, shard):
        early, kept = 7, (9, 15)
        own_gain = jnp.stack([norm1_gain, norm2_gain])[None, :, None, :, None]
        own_gain = jnp.broadcast_to(own_gain, (1, 2, 1, shard, T)).astype(BF)
        cont_dy = cont_cot[0].reshape(-1, width)
        matrices = (q_weight, k_weight, v_weight, o_weight, gate_weight, up_weight, down_weight)
        (whole, own_feed, x_low, normed_one, kv, bias, queries, attended, log_norm, middle,
         normed_two, *gains) = front(
            prompt_x[0], cont_x[0].reshape(-1, width), own_gain, matrices, bucket_table.T, cont_len,
            shape, sizes, early, 0,
        )
        _, feed_parts, kept_sums, *final, d_middle, d_branch, d_attended, d_gain_two = feed_moving(
            normed_two, prompt_cot[0], cont_dy, own_feed, whole, middle, gains[1], inner, sizes,
            early, kept, 1,
        )
        (*d_x, gate_grad, up_grad, down_grad, q_grad, k_grad, v_grad, o_grad, vector) = back(
            queries, kv, bias, d_attended, attended, log_norm, d_branch, normed_one, feed_parts,
            whole, d_middle, x_low, gains[0], d_gain_two, kept_sums, hidden_width, cont_len, shape,
            sizes, kept, 2,
        )
        settled = settle(
            *final, *d_x, gate_grad, up_grad, down_grad, q_grad, k_grad, v_grad, o_grad
        )
        final, d_x = settled[:2], settled[2:4]
        gate_grad, up_grad, down_grad, q_grad, k_grad, v_grad, o_grad = settled[4:]
        near = vector[:heads, :4].reshape(heads, SPAN)
        far = jnp.sum(vector[:heads, 4:6], axis=-1)
        relative = (jnp.arange(SPAN) + T) % SPAN - 2 * T
        ids = jnp.concatenate([bucket_ids(relative), bucket_ids(jnp.array([-T, T]))])
        hot = (ids[:, None] == jnp.arange(num_buckets)).astype(F32)
        both = jnp.concatenate([near, far], axis=1)
        table_grad = jnp.einsum("hr,rb->bh", both, hot, precision=lax.Precision.HIGHEST)
        gain_grads = vector[heads:].reshape(2, sizes[0] * seq, shard)
        me = lax.axis_index("grp") * seq + seq_index
        norm1_grad, norm2_grad = lax.dynamic_index_in_dim(gain_grads, me, 1, keepdims=False)
    else:
        x_low = jnp.concatenate([prompt_x[0], cont_x[0].reshape(-1, width)], axis=0)
        dy_low = jnp.concatenate([prompt_cot[0], cont_cot[0].reshape(-1, width)], axis=0)
        x = x_low.astype(F32)
        dy = dy_low.astype(F32)
        lanes = jnp.zeros((shard, T - 2), F32)
        gains = jnp.concatenate([norm1_gain[:, None], norm2_gain[:, None], lanes], axis=1)
        own_attention = attention_chunks([q_weight, k_weight, v_weight, o_weight, gains]).astype(BF)
        own_feed = feed_chunks([gate_weight, up_weight, down_weight]).astype(BF)
        attention_whole = gather(own_attention, sizes)
        flat = attention_whole.reshape(-1, width, T)
        q_full, k_full, v_full, o_full = [
            joined(flat[i * count : (i + 1) * count]) for i in range(4)
        ]
        gain_one = flat[4 * count, :, 0].astype(F32)
        gain_two = flat[4 * count, :, 1].astype(F32)
        scale_one = rms_scale(x)
        unit_one = x * scale_one
        normed_one = (unit_one * gain_one).astype(BF)
        kv = nn(normed_one, jnp.concatenate([k_full, v_full], axis=1)).astype(BF)
        queries = nn(normed_one, q_full).astype(BF)
        gathered = lax.all_gather(kv[:local_prompt], "seq", axis=0, tiled=True)
        others = jnp.roll(gathered, -seq_index * local_prompt, axis=0)[local_prompt:]
        every = jnp.concatenate([kv, others], axis=0)
        keys, values = every[:, :inner], every[:, inner:]
        base = (seq_index * local_tiles).reshape(1).astype(jnp.int32)
        one_hot = band_one_hot(num_buckets)
        bias = jnp.einsum("cqkb,bh->hcqk", one_hot, bucket_table, precision=lax.Precision.HIGHEST)
        attended, log_norm = attend(queries, keys, values, bias, cont_len, base, shape)
        middle = x + nt(attended, o_full)
        scale_two = rms_scale(middle)
        unit_two = middle * scale_two
        normed_two = (unit_two * gain_two).astype(BF)
        out_sum, d_normed_two, feed_grads = feed(normed_two, dy_low, gather(own_feed, sizes))
        feed_sums = scatter(feed_grads)
        final = cut((middle + out_sum).astype(BF))
        d_gain_two = jnp.sum(d_normed_two * unit_two, axis=0)
        d_middle = dy + norm_back(d_normed_two, unit_two, scale_two, gain_two)
        d_branch = d_middle.astype(BF)
        d_attended = nn(d_branch, o_full).astype(BF)
        d_o = tn(d_branch, attended)
        d_queries, d_keys, d_values, d_bias = attend_back(
            queries, keys, values, bias, d_attended, attended, log_norm, cont_len, base, shape
        )
        d_table = jnp.einsum("hcqk,cqkb->bh", d_bias, one_hot, precision=lax.Precision.HIGHEST)
        d_kv = jnp.concatenate([d_keys, d_values], axis=1)
        prompt_parts = jnp.concatenate([d_kv[:local_prompt], d_kv[shape.rows :]], axis=0)
        prompt_parts = jnp.roll(prompt_parts, seq_index * local_prompt, axis=0)
        d_prompt = lax.psum_scatter(prompt_parts, "seq", scatter_dimension=0, tiled=True)
        d_kv = jnp.concatenate([d_prompt, d_kv[local_prompt : shape.rows]], axis=0)
        d_normed_one = nt(d_queries, q_full) + nt(d_kv, jnp.concatenate([k_full, v_full], axis=1))
        d_q = tn(normed_one, d_queries)
        d_kv_weight = tn(normed_one, d_kv)
        d_gain_one = jnp.sum(d_normed_one * unit_one, axis=0)
        d_x = d_middle + norm_back(d_normed_one, unit_one, scale_one, gain_one)
        d_x = cut(d_x.astype(BF))
        attention_parts = attention_chunks([d_q, d_kv_weight, d_o]).astype(BF)
        attention_sums = scatter(attention_parts).reshape(-1, shard, T)
        norm1_grad = lax.psum_scatter(d_gain_one, ("grp", "seq"), scatter_dimension=0, tiled=True)
        norm2_grad = lax.psum_scatter(d_gain_two, ("grp", "seq"), scatter_dimension=0, tiled=True)
        table_grad = lax.psum(d_table, ("grp", "seq"))
        feed_sums = feed_sums.reshape(-1, 3, shard, T)[: hidden_width // T]
        gate_grad, up_grad, down_grad = [joined(feed_sums[:, i]) for i in range(3)]
        q_grad, k_grad, v_grad, o_grad = [
            joined(attention_sums[i * count : (i + 1) * count]) for i in range(4)
        ]
    return (
        *split(final),
        *split(d_x),
        norm1_grad,
        q_grad,
        k_grad,
        v_grad,
        o_grad,
        table_grad,
        norm2_grad,
        gate_grad,
        up_grad,
        down_grad,
    )


def solution(mesh):
    sizes = (mesh.shape["grp"], mesh.shape["seq"])
    rows = P("grp", "seq", None)
    conts = P("grp", "seq", None, None)
    shard = P(("grp", "seq"), None)
    gain = P(("grp", "seq"))
    in_specs = (rows, conts, P("grp", "seq"), rows, conts, gain, shard, shard, shard, shard)
    in_specs += (P(), gain, shard, shard, shard)
    out_specs = (rows, conts, rows, conts, gain, shard, shard, shard, shard, P(), gain)
    out_specs += (shard, shard, shard)
    return jax.shard_map(
        functools.partial(body, sizes),
        mesh=mesh,
        in_specs=in_specs,
        out_specs=out_specs,
        check_vma=False,
    )
```

```python
import functools

import jax
import jax.numpy as jnp
from jax import lax
from jax.experimental import pallas as pl
from jax.experimental.pallas import tpu as pltpu
from jax.sharding import PartitionSpec as P

EPS = 1e-06
LIMITS = (8, 12, 16, 23, 32, 46, 64, 91)
NEGATIVE = -1e30
MESH = pl.DeviceIdType.MESH
T = 128
HEAD = 64
BANDS = 5
BF = jnp.bfloat16
F32 = jnp.float32
VMEM_LIMIT = 63 * 2**20
Y = 2
C = 2


def nn(left, right):
    return jnp.dot(left, right, preferred_element_type=F32)


def nt(left, right):
    return lax.dot_general(left, right, (((1,), (1,)), ((), ())), preferred_element_type=F32)


def tn(left, right):
    return lax.dot_general(left, right, (((0,), (0,)), ((), ())), preferred_element_type=F32)


def bucket_ids(relative):
    distance = jnp.abs(relative)
    coarse = 7 + sum(((distance >= boundary).astype(jnp.int32) for boundary in LIMITS))
    return jnp.where(distance < 8, distance, coarse) + 16 * (relative > 0).astype(jnp.int32)


def band_one_hot(num_buckets):
    band = jnp.arange(BANDS)[:, None, None] - 2
    query = jnp.arange(T)[None, :, None]
    key = jnp.arange(T)[None, None, :]
    ids = bucket_ids(band * T + key - query)
    return (ids[..., None] == jnp.arange(num_buckets)).astype(F32)


def can_move(sizes, rows):
    zs = sizes[0] // (Y * C)
    return rows % 16 == 0 and sizes[1] == 2 and sizes[0] % (Y * C) == 0 and zs in (2, 4, 8, 16)


class Place:
    def __init__(self, zs, xs):
        grp = lax.axis_index("grp")
        self.zs, self.xs = zs, xs
        self.x = lax.axis_index("seq")
        self.z = grp // (Y * C)
        self.y = (grp // C) % Y
        self.c = grp % C

    def device(self, z=None, y=None, c=None, x=None):
        z = self.z if z is None else z
        y = self.y if y is None else y
        c = self.c if c is None else c
        x = self.x if x is None else x
        return (z * (Y * C) + y * C + c, x)

    def peers(self):
        around = [self.device(z=(self.z + d) % self.zs) for d in range(1, self.zs)]
        return around + [
            self.device(y=1 - self.y),
            self.device(x=1 - self.x),
            self.device(c=1 - self.c),
        ]

    def barrier(self):
        sem = pltpu.get_barrier_semaphore()
        peers = self.peers()
        for peer in peers:
            pl.semaphore_signal(sem, inc=1, device_id=peer, device_id_type=MESH)
        pl.semaphore_wait(sem, len(peers))


def remote(src, dst, send_sem, recv_sem, device):
    return pltpu.make_async_remote_copy(
        src_ref=src,
        dst_ref=dst,
        send_sem=send_sem,
        recv_sem=recv_sem,
        device_id=device,
        device_id_type=MESH,
    )


def staged(step, offset, count, action):
    @pl.when((step >= offset) & (step < count + offset))
    def _():
        action(step - offset)


class Gather:
    def __init__(self, place, own, whole, send, recv):
        self.p, self.own, self.whole, self.send, self.recv = place, own, whole, send, recv

    def copy(self, k, half, index, src, dst, device):
        return remote(src, dst, self.send.at[k, half, index], self.recv.at[k, half, index], device)

    def alone(self, k, half):
        p = self.p
        dst = self.whole.at[k, half, :, p.z, p.y, p.c * p.xs + p.x]
        src = self.own.at[k, half]
        if half == 0:
            return [self.copy(k, half, 0, src, dst, p.device(x=1 - p.x))]
        peers = [p.device(z=(p.z + d) % p.zs) for d in range(1, p.zs)]
        return [self.copy(k, half, i, src, dst, peer) for i, peer in enumerate(peers)]

    def second(self, k, half):
        p = self.p
        if half == 0:
            view = self.whole.at[k, half, :, p.z, p.y, pl.ds(p.c * p.xs, p.xs)]
            peers = [p.device(z=(p.z + d) % p.zs) for d in range(1, p.zs)]
            return [self.copy(k, half, 1 + i, view, view, peer) for i, peer in enumerate(peers)]
        view = self.whole.at[k, half, :, :, p.y, p.c * p.xs + p.x]
        return [self.copy(k, half, p.zs - 1, view, view, p.device(y=1 - p.y))]

    def third(self, k, half):
        p = self.p
        if half == 0:
            view = self.whole.at[k, half, :, :, p.y, pl.ds(p.c * p.xs, p.xs)]
            peer = p.device(y=1 - p.y)
        else:
            view = self.whole.at[k, half, :, :, :, p.c * p.xs + p.x]
            peer = p.device(x=1 - p.x)
        return [self.copy(k, half, p.zs, view, view, peer)]

    def fourth(self, k, half):
        p = self.p
        view = self.whole.at[k, half, :, :, :, pl.ds(p.c * p.xs, p.xs)]
        return [self.copy(k, half, p.zs + 1, view, view, p.device(c=1 - p.c))]

    def tick(self, step, first, end):
        stages = (self.alone, self.second, self.third, self.fourth)

        def advance(offset, k):
            for half in (0, 1):
                if offset > 0:
                    for copy in stages[offset - 1](k, half):
                        copy.wait_recv()
                if offset < 4:
                    for copy in stages[offset](k, half):
                        copy.start()
                else:
                    for stage in stages:
                        for copy in stage(k, half):
                            copy.wait_send()

        for offset in range(5):
            staged(step, offset, end - first, lambda k, offset=offset: advance(offset, first + k))


def gather(own, sizes):
    return lax.all_gather(own, ("grp", "seq"), axis=3, tiled=True)


class Scatter:
    def __init__(self, place, bufs, send, recv, out):
        self.p, self.send, self.recv, self.out = place, send, recv, out
        (self.in1, self.in2, self.sum1, self.sum2) = bufs[:4]
        self.in3, self.in4, self.sum3 = bufs[4:6], bufs[6:8], bufs[8:10]

    def copy(self, k, half, index, src, dst, device):
        slot = k % 2
        return remote(
            src, dst, self.send.at[slot, half, index], self.recv.at[slot, half, index], device
        )

    def first(self, k, half, part):
        p = self.p
        src = part.at[half, :, :, :, pl.ds((1 - p.c) * p.xs, p.xs)]
        return self.copy(k, half, 0, src, self.in1.at[k % 2, half], p.device(c=1 - p.c))

    def second(self, k, half):
        p = self.p
        if half == 0:
            src, peer = self.sum1.at[k % 2, half, :, :, 1 - p.y], p.device(y=1 - p.y)
        else:
            src, peer = self.sum1.at[k % 2, half, :, :, :, 1 - p.x], p.device(x=1 - p.x)
        return self.copy(k, half, 1, src, self.in2.at[k % 2, half], peer)

    def third(self, k, half):
        p, slot = self.p, k % 2
        if half == 1:
            src = self.sum2.at[slot, half, :, :, 1 - p.y]
            return [self.copy(k, half, 2, src, self.in3[1].at[slot], p.device(y=1 - p.y))]
        copies = []
        for d in range(1, p.zs):
            target = (p.z + d) % p.zs
            src = self.sum2.at[slot, half, :, target]
            dst = self.in3[0].at[slot, d - 1]
            copies.append(self.copy(k, half, 1 + d, src, dst, p.device(z=target)))
        return copies

    def fourth(self, k, half):
        p, slot = self.p, k % 2
        if half == 0:
            src = self.sum3[0].at[slot, :, 1 - p.x]
            return [self.copy(k, half, p.zs + 1, src, self.in4[0].at[slot, 0], p.device(x=1 - p.x))]
        copies = []
        for d in range(1, p.zs):
            target = (p.z + d) % p.zs
            src = self.sum3[1].at[slot, :, target]
            dst = self.in4[1].at[slot, d - 1]
            copies.append(self.copy(k, half, 2 + d, src, dst, p.device(z=target)))
        return copies

    def finish(self, k):
        p, slot = self.p, k % 2
        for half in (0, 1):
            total = self.sum3[half][slot, :, p.x if half == 0 else p.z].astype(F32)
            for i, copy in enumerate(self.fourth(k, half)):
                copy.wait_recv()
                copy.wait_send()
                total = total + self.in4[half][slot, i].astype(F32)
            self.out(k, half, total)

    def start_fourth(self, k):
        p, slot = self.p, k % 2
        for half in (0, 1):
            for copy in self.third(k, half):
                copy.wait_recv()
                copy.wait_send()
            for i in range(self.sum2.shape[2]):
                if half == 0:
                    total = self.sum2[slot, half, i, p.z].astype(F32)
                    for d in range(1, p.zs):
                        total = total + self.in3[0][slot, d - 1, i].astype(F32)
                else:
                    total = self.sum2[slot, half, i, :, p.y].astype(F32)
                    total = total + self.in3[1][slot, i].astype(F32)
                self.sum3[half][slot, i] = total.astype(BF)
            for copy in self.fourth(k, half):
                copy.start()

    def start_third(self, k):
        p, slot = self.p, k % 2
        for half in (0, 1):
            copy = self.second(k, half)
            copy.wait_recv()
            copy.wait_send()
            for i in range(self.sum2.shape[2]):
                if half == 0:
                    mine = self.sum1[slot, half, i, :, p.y]
                else:
                    mine = self.sum1[slot, half, i, :, :, p.x]
                total = mine.astype(F32) + self.in2[slot, half, i].astype(F32)
                self.sum2[slot, half, i] = total.astype(BF)
            for copy in self.third(k, half):
                copy.start()

    def start_second(self, k, part):
        p, slot = self.p, k % 2
        for half in (0, 1):
            copy = self.first(k, half, part)
            copy.wait_recv()
            copy.wait_send()

            def add(z, _, half=half):
                for i in range(self.sum1.shape[2]):
                    mine = part[half, i, z, :, pl.ds(p.c * p.xs, p.xs)]
                    total = mine.astype(F32) + self.in1[slot, half, i, z].astype(F32)
                    self.sum1[slot, half, i, z] = total.astype(BF)
                return 0

            lax.fori_loop(0, p.zs, add, 0)
            self.second(k, half).start()

    def start_first(self, k, part):
        for half in (0, 1):
            self.first(k, half, part).start()


BUFFERS = 10


def scatter_buffers(n, zs, xs, rows, lanes):
    block = (rows, lanes)
    shapes = [
        (2, 2, n, zs, Y, xs, *block),
        (2, 2, n, zs, 2, *block),
        (2, 2, n, zs, Y, xs, *block),
        (2, 2, n, zs, 2, *block),
        (2, zs - 1, n, 2, *block),
        (2, n, zs, *block),
        (2, 1, n, *block),
        (2, zs - 1, n, *block),
        (2, n, 2, *block),
        (2, n, zs, *block),
    ]
    return [pltpu.VMEM(shape, BF) for shape in shapes]


def scatter(parts):
    return lax.psum_scatter(parts, ("grp", "seq"), scatter_dimension=3, tiled=True).astype(F32)


class Shape:
    def __init__(self, tiles, local_tiles, conts):
        self.tiles, self.local_tiles, self.conts = tiles, local_tiles, conts
        self.rows = (local_tiles + conts) * T
        self.keys = self.rows + (tiles - local_tiles) * T
        self.parts = [(0, range(local_tiles)), (self.rows, range(local_tiles, tiles))]
        self.parts = [(start, js) for start, js in self.parts if len(js)]


def band_of(key_tile, query_tile):
    return jnp.clip(key_tile - query_tile, -2, 2) + 2


def tile_lanes():
    first_half = lax.broadcasted_iota(jnp.int32, (T, 2 * HEAD), 1) < HEAD
    place = lax.broadcasted_iota(jnp.int32, (T, T), 1)
    return first_half, place


def tile_rows(i):
    return pl.ds(pl.multiple_of(i * T, T), T)


def attend_tile(shape, i, is_cont, live, base, q, k, v, bias, out, norm):
    first_half, place = tile_lanes()
    rows = tile_rows(i)
    queries = q[rows, :]
    query_tile = shape.tiles if is_cont else base + i
    mixed = []
    for h in range(2):
        mine = first_half if h == 0 else ~first_half
        masked = jnp.where(mine, queries, jnp.zeros_like(queries))
        logits = []
        for start, js in shape.parts:
            scores = nt(masked, k[start : start + len(js) * T, :])
            for at, j in enumerate(js):
                band = band_of(lax.rem(base + j, shape.tiles), query_tile)
                logits.append(scores[:, at * T : (at + 1) * T] + bias[h, band])
        if is_cont:
            own = nt(masked, k[rows, :]) + bias[h, 2]
            logits.append(jnp.where(place < live[0, i - shape.local_tiles], own, NEGATIVE))
        top = jnp.max(functools.reduce(jnp.maximum, logits), axis=1, keepdims=True)
        weights = [jnp.exp(part - top) for part in logits]
        total = jnp.sum(functools.reduce(jnp.add, weights), axis=1, keepdims=True)
        inverse = 1.0 / total
        probs = [(weight * inverse).astype(BF) for weight in weights]
        result = None
        for start, js in shape.parts:
            left = jnp.concatenate([probs[j] for j in js], axis=1)
            term = nn(left, v[start : start + len(js) * T, :])
            result = term if result is None else result + term
        if is_cont:
            result = result + nn(probs[shape.tiles], v[rows, :])
        mixed.append(result)
        norm[h, rows, :] = top + jnp.log(total)
    out[rows, :] = jnp.where(first_half, mixed[0], mixed[1]).astype(BF)


def for_tiles(shape, conts, action):
    first, last = (shape.local_tiles, shape.local_tiles + shape.conts) if conts else (0, shape.local_tiles)

    def one(i, carry):
        action(i, conts)
        return carry

    lax.fori_loop(first, last, one, 0)


def attend_kernel(shape, live, base, q, k, v, bias, out, norm):
    for conts in (False, True):
        for_tiles(
            shape,
            conts,
            lambda i, c: attend_tile(shape, i, c, live, base[0], q, k, v, bias, out, norm),
        )


def pair_block(n):
    return pl.BlockSpec((n, 2 * HEAD), lambda h, *_: (0, h))


def attend(q, k, v, bias, live, base, shape):
    rows, width = q.shape
    pairs = width // (2 * HEAD)
    return pl.pallas_call(
        functools.partial(attend_kernel, shape),
        grid_spec=pltpu.PrefetchScalarGridSpec(
            num_scalar_prefetch=2,
            grid=(pairs,),
            in_specs=[
                pair_block(rows),
                pair_block(shape.keys),
                pair_block(shape.keys),
                pl.BlockSpec((2, BANDS, T, T), lambda h, *_: (h, 0, 0, 0)),
            ],
            out_specs=[pair_block(rows), pl.BlockSpec((2, rows, 1), lambda h, *_: (h, 0, 0))],
        ),
        out_shape=[
            jax.ShapeDtypeStruct((rows, width), BF),
            jax.ShapeDtypeStruct((2 * pairs, rows, 1), F32),
        ],
        compiler_params=pltpu.CompilerParams(vmem_limit_bytes=VMEM_LIMIT),
    )(live, base, q, k, v, bias)


def attend_back_tile(
    shape, i, is_cont, live, base, q, k, v, bias, grad, out, norm, d_q, d_bias, k_sum, v_sum
):
    first_half, place = tile_lanes()
    rows = tile_rows(i)
    queries = q[rows, :]
    grads = grad[rows, :]
    query_tile = shape.tiles if is_cont else base + i
    overlap = grads.astype(F32) * out[rows, :].astype(F32)
    mixed = []
    for h in range(2):
        mine = first_half if h == 0 else ~first_half
        masked = jnp.where(mine, queries, jnp.zeros_like(queries))
        masked_grad = jnp.where(mine, grads, jnp.zeros_like(grads))
        inner = jnp.sum(jnp.where(mine, overlap, 0.0), axis=1, keepdims=True)
        log_norm = norm[h, rows, :]

        def piece(keys, bands, allowed):
            scores = nt(masked, k[keys, :])
            d_probs = nt(masked_grad, v[keys, :])
            probs_low, scores_low = [], []
            for at, band in enumerate(bands):
                cols = slice(at * T, (at + 1) * T)
                logits = scores[:, cols] + bias[h, band]
                if allowed is not None:
                    logits = jnp.where(allowed, logits, NEGATIVE)
                probs = jnp.exp(logits - log_norm)
                d_scores = probs * (d_probs[:, cols] - inner)
                d_bias[h, band] += d_scores
                probs_low.append(probs.astype(BF))
                scores_low.append(d_scores.astype(BF))
            probs_low = jnp.concatenate(probs_low, axis=1)
            scores_low = jnp.concatenate(scores_low, axis=1)
            v_sum[keys, :] += tn(probs_low, masked_grad)
            k_sum[keys, :] += tn(scores_low, masked)
            return nn(scores_low, k[keys, :])

        result = None
        for start, js in shape.parts:
            bands = [band_of(lax.rem(base + j, shape.tiles), query_tile) for j in js]
            term = piece(pl.ds(start, len(js) * T), bands, None)
            result = term if result is None else result + term
        if is_cont:
            result = result + piece(rows, [2], place < live[0, i - shape.local_tiles])
        mixed.append(result)
    d_q[rows, :] = jnp.where(first_half, mixed[0], mixed[1]).astype(BF)


def attend_back_kernel(
    shape, live, base, q, k, v, bias, grad, out, norm, d_q, d_k, d_v, d_bias, k_sum, v_sum
):
    k_sum[...] = jnp.zeros_like(k_sum)
    v_sum[...] = jnp.zeros_like(v_sum)
    d_bias[...] = jnp.zeros_like(d_bias)
    refs = (q, k, v, bias, grad, out, norm, d_q, d_bias, k_sum, v_sum)
    for conts in (False, True):
        for_tiles(shape, conts, lambda i, c: attend_back_tile(shape, i, c, live, base[0], *refs))
    d_k[...] = k_sum[...].astype(BF)
    d_v[...] = v_sum[...].astype(BF)


def attend_back(q, k, v, bias, grad, out, norm, live, base, shape):
    rows, width = q.shape
    pairs = width // (2 * HEAD)
    keys = shape.keys
    bands = pl.BlockSpec((2, BANDS, T, T), lambda h, *_: (h, 0, 0, 0))
    return pl.pallas_call(
        functools.partial(attend_back_kernel, shape),
        grid_spec=pltpu.PrefetchScalarGridSpec(
            num_scalar_prefetch=2,
            grid=(pairs,),
            in_specs=[
                pair_block(rows),
                pair_block(keys),
                pair_block(keys),
                bands,
                pair_block(rows),
                pair_block(rows),
                pl.BlockSpec((2, rows, 1), lambda h, *_: (h, 0, 0)),
            ],
            out_specs=[pair_block(rows), pair_block(keys), pair_block(keys), bands],
            scratch_shapes=[pltpu.VMEM((keys, 2 * HEAD), F32), pltpu.VMEM((keys, 2 * HEAD), F32)],
        ),
        out_shape=[
            jax.ShapeDtypeStruct((rows, width), BF),
            jax.ShapeDtypeStruct((keys, width), BF),
            jax.ShapeDtypeStruct((keys, width), BF),
            jax.ShapeDtypeStruct((2 * pairs, BANDS, T, T), F32),
        ],
        compiler_params=pltpu.CompilerParams(vmem_limit_bytes=VMEM_LIMIT),
    )(live, base, q, k, v, bias, grad, out, norm)


ORDER = (1, 2, 0, 3)
FIRST_PAIR = 8


def joined_pieces(w_buf, slot, m):
    pieces = [w_buf[slot, j // 3, j % 3] for j in (2 * m, 2 * m + 1)]
    return jnp.concatenate([piece.reshape(-1, T) for piece in pieces], axis=1)


def front_kernel(zs, xs, shape, early, live, *refs):
    (prompt_x, cont_x, own_gain, *weights) = refs[:10]
    table = refs[10]
    (whole, own_out, x_out, normed_out, kv_out, bias_out) = refs[11:17]
    (q, attended, norm, middle, normed_two, *gains) = refs[17:24]
    (x, normed, kv, bias, held, w_buf, gain_whole) = refs[24:31]
    (local, kv_sems, send, recv, gain_send, gain_recv) = refs[31:37]
    place = Place(zs, xs)
    step = pl.program_id(0)
    rows, width = x.shape
    prompt = shape.local_tiles * T
    pairs = q.shape[0]
    size = middle.shape[0]
    blocks = rows // size
    last = FIRST_PAIR + pairs
    count = 4 + early
    feed_weights = weights[4:]
    columns = feed_weights[0].shape[1] // T

    def x_load(i):
        source, part = ((prompt_x, pl.ds(0, prompt)), (cont_x, pl.ds(prompt, rows - prompt)))[i]
        return pltpu.make_async_copy(source, x.at[part], local.at[i])

    def mine_store():
        mine = whole.at[:, :, :, place.z, place.y, place.c * place.xs + place.x]
        return pltpu.make_async_copy(held.at[pl.ds(0, count)], mine, local.at[2])

    feed_own = held.at[pl.ds(4, held.shape[0] - 4)]
    kept = ((feed_own, own_out), (x, x_out), (normed, normed_out), (bias, bias_out), (kv, kv_out))

    def result(i):
        return pltpu.make_async_copy(*kept[i], local.at[3 + i])

    def weight_load(k):
        return pltpu.make_async_copy(whole.at[k], w_buf.at[k % 2], local.at[8 + k])

    @pl.when(step == 0)
    def _():
        place.barrier()
        x_load(0).start()
        x_load(1).start()
        for c, matrix in enumerate(ORDER):
            for j in range(6):
                held[c, j // 3, j % 3] = weights[matrix][:, j * T : (j + 1) * T].astype(BF)
        gain_whole[0, :, :, place.z, place.y, place.c * place.xs + place.x] = own_gain[0]

    Gather(place, own_gain, gain_whole, gain_send, gain_recv).tick(step, 0, 1)
    Gather(place, held, whole, send, recv).tick(step, 0, count)

    @pl.when(step == 0)
    def _():
        def convert(j, carry):
            part = pl.ds(pl.multiple_of(j * T, T), T)
            for i in range(3):
                held[4 + j // 2, j % 2, i] = feed_weights[i][:, part].astype(BF)
            return carry

        lax.fori_loop(0, columns, convert, 0)
        if columns % 2:
            held[4 + columns // 2, 1] = jnp.zeros(held.shape[2:], BF)
        mine_store().start()
        mine_store().wait()
        result(0).start()
        x_load(0).wait()
        x_load(1).wait()
        result(1).start()

    @pl.when(step == 1)
    def _():
        query = lax.broadcasted_iota(jnp.int32, (T, T), 0)
        key = lax.broadcasted_iota(jnp.int32, (T, T), 1)
        half = table.shape[1] // 2
        ids = [bucket_ids(band * T + key - query) for band in (-1, 0, 1)]
        found = (range(1, half), [*range(half), *range(half + 1, 2 * half)], range(half + 1, 2 * half))

        def one(h, carry):
            bias[h, 0] = jnp.full((T, T), table[h, half - 1])
            bias[h, 4] = jnp.full((T, T), table[h, 2 * half - 1])
            for band in range(3):
                value = jnp.zeros((T, T), F32)
                for bucket in found[band]:
                    value = jnp.where(ids[band] == bucket, table[h, bucket], value)
                bias[h, 1 + band] = value
            return carry

        lax.fori_loop(0, bias.shape[0], one, 0)

    for k in range(4):

        @pl.when(step == 4 + k)
        def _(k=k):
            weight_load(k).start()

    def by_rows(action):
        def one(i, carry):
            action(pl.ds(pl.multiple_of(i * size, size), size))
            return carry

        lax.fori_loop(0, blocks, one, 0)

    @pl.when(step == 4)
    def _():
        result(3).start()
        eye = lax.broadcasted_iota(jnp.int32, (T, T), 0) == lax.broadcasted_iota(jnp.int32, (T, T), 1)
        for g in range(2):
            column = gain_whole[0, g, 0].reshape(width, T).astype(F32)
            for i in range(width // T):
                cols = slice(i * T, (i + 1) * T)
                gains[g][:, cols] = jnp.sum(jnp.where(eye, column[cols], 0.0), axis=0, keepdims=True)

        def norm_rows(part):
            values = x[part, :].astype(F32)
            scale = lax.rsqrt(jnp.mean(values * values, axis=-1, keepdims=True) + EPS)
            normed[part, :] = (values * scale * gains[0][...]).astype(BF)

        by_rows(norm_rows)
        result(2).start()

    def project(slot, target):
        for m in range(pairs // 2):
            right = joined_pieces(w_buf, slot, m)

            def rows_of_product(part, m=m, right=right):
                product = nn(normed[part, :], right).astype(BF)
                target[2 * m, part, :] = product[:, :T]
                target[2 * m + 1, part, :] = product[:, T:]

            by_rows(rows_of_product)

    def kv_send(side, p):
        src = kv.at[side, p, pl.ds(0, prompt)]
        dst = kv.at[side, p, pl.ds(rows, prompt)]
        peer = place.device(x=1 - place.x)
        return remote(src, dst, kv_sems.at[0, side, p], kv_sems.at[1, side, p], peer)

    for k in range(3):

        @pl.when(step == 5 + k)
        def _(k=k):
            weight_load(k).wait()
            project(k % 2, kv.at[k] if k < 2 else q)
            if k < 2:
                for p in range(pairs):
                    kv_send(k, p).start()

    @pl.when(step == FIRST_PAIR)
    def _():
        weight_load(3).wait()

    @pl.when((step >= FIRST_PAIR) & (step < last))
    def _():
        p = step - FIRST_PAIR
        for side in range(2):
            kv_send(side, p).wait_recv()
            kv_send(side, p).wait_send()
        base = place.x * shape.local_tiles
        inputs = (q.at[p], kv.at[0, p], kv.at[1, p], bias.at[pl.ds(2 * p, 2)], attended.at[p], norm)
        for conts in (False, True):
            for_tiles(shape, conts, lambda i, c: attend_tile(shape, i, c, live, base, *inputs))

    @pl.when(step == last)
    def _():
        result(4).start()

    @pl.when(step >= last)
    def _():
        part = pl.ds(pl.multiple_of((step - last) * size, size), size)
        branch = None
        for m in range(pairs // 2):
            left = jnp.concatenate([attended[2 * m + e, part, :] for e in range(2)], axis=1)
            term = nt(left, joined_pieces(w_buf, 1, m))
            branch = term if branch is None else branch + term
        total = x[part, :].astype(F32) + branch
        middle[...] = total
        scale = lax.rsqrt(jnp.mean(total * total, axis=-1, keepdims=True) + EPS)
        normed_two[...] = (total * scale * gains[1][...]).astype(BF)

    @pl.when(step == last + blocks - 1)
    def _():
        for i in range(len(kept)):
            result(i).wait()


def front(prompt_x, cont_x, own_gain, weights, table, live, shape, sizes, early, collective_id):
    grp, seq = sizes
    rows, width = shape.rows, prompt_x.shape[1]
    shard, inner = weights[0].shape
    feed_columns = weights[4].shape[1] // T
    pairs, keys, heads = inner // (2 * HEAD), shape.keys, table.shape[0]
    assert pairs == 6 and table.shape[1] == 32 and keys - rows == prompt_x.shape[0]
    zs = grp // (Y * C)
    chunks = 4 + (feed_columns + 1) // 2
    count = 4 + early
    own = (2, 3, shard, T)
    tile = (2, 3, zs, Y, C * seq, shard, T)
    size = min(rows, 256)
    blocks = rows // size
    last = FIRST_PAIR + pairs
    steps = last + blocks
    assert count + 4 <= steps and count <= chunks
    full = lambda *dims: pl.BlockSpec(
        dims, lambda s, *_: (0,) * len(dims), pipeline_mode=pl.Buffered(1)
    )
    by_rows = pl.BlockSpec((size, width), lambda s, *_: (jnp.clip(s - last, 0, blocks - 1), 0))
    anywhere = pl.BlockSpec(memory_space=pl.ANY)
    sems = lambda *dims: pltpu.SemaphoreType.DMA(dims)
    out = jax.ShapeDtypeStruct
    return pl.pallas_call(
        functools.partial(front_kernel, zs, seq, shape, early),
        grid_spec=pltpu.PrefetchScalarGridSpec(
            num_scalar_prefetch=1,
            grid=(steps,),
            in_specs=[anywhere, anywhere, full(*own_gain.shape)]
            + [full(*w.shape) for w in weights]
            + [pl.BlockSpec(memory_space=pltpu.SMEM)],
            out_specs=[anywhere] * 6
            + [
                full(pairs, rows, 2 * HEAD),
                full(pairs, rows, 2 * HEAD),
                pl.BlockSpec(
                    (2, rows, 1), lambda s, *_: (jnp.clip(s - FIRST_PAIR, 0, pairs - 1), 0, 0)
                ),
                by_rows,
                by_rows,
                full(1, width),
                full(1, width),
            ],
            scratch_shapes=[
                pltpu.VMEM((rows, width), BF),
                pltpu.VMEM((rows, width), BF),
                pltpu.VMEM((2, pairs, keys, 2 * HEAD), BF),
                pltpu.VMEM((heads, BANDS, T, T), F32),
                pltpu.VMEM((chunks, *own), BF),
                pltpu.VMEM((2, *tile), BF),
                pltpu.VMEM((1, 2, 1, zs, Y, C * seq, shard, T), BF),
                sems(12),
                sems(2, 2, pairs),
                sems(count, 2, zs + 2),
                sems(count, 2, zs + 2),
                sems(1, 2, zs + 2),
                sems(1, 2, zs + 2),
            ],
        ),
        out_shape=[
            out((count, *tile), BF),
            out((chunks - 4, *own), BF),
            out((rows, width), BF),
            out((rows, width), BF),
            out((2, pairs, keys, 2 * HEAD), BF),
            out((heads, BANDS, T, T), F32),
            out((pairs, rows, 2 * HEAD), BF),
            out((pairs, rows, 2 * HEAD), BF),
            out((2 * pairs, rows, 1), F32),
            out((rows, width), F32),
            out((rows, width), BF),
            out((1, width), F32),
            out((1, width), F32),
        ],
        compiler_params=pltpu.CompilerParams(
            collective_id=collective_id, has_side_effects=True, vmem_limit_bytes=VMEM_LIMIT
        ),
    )(live, prompt_x, cont_x, own_gain, *weights, table)


SPAN = 4 * T
VECTOR_ROWS = 8


def turned(tile):
    row = lax.broadcasted_iota(jnp.int32, tile.shape, 0)
    for bit in range(7):
        moved = pltpu.roll(tile, SPAN - (1 << bit), 1)
        tile = jnp.where((row >> bit) & 1 == 1, moved, tile)
    return tile


def band_sums(d_bias, h):
    near = jnp.concatenate([d_bias[h, 1], d_bias[h, 2], d_bias[h, 3]], axis=1)
    near = jnp.concatenate([near, jnp.zeros((T, T), F32)], axis=1)
    diagonal = jnp.sum(turned(near), axis=0, keepdims=True)
    rows = [diagonal[:, i * T : (i + 1) * T] for i in range(4)]
    rows += [jnp.sum(d_bias[h, band], axis=0, keepdims=True) for band in (0, 4)]
    return jnp.concatenate(rows + [jnp.zeros((2, T), F32)], axis=0)


def put(i, first_blocks, targets, value):
    @pl.when(i < first_blocks)
    def _():
        targets[0][...] = value

    @pl.when(i >= first_blocks)
    def _():
        targets[1][...] = value


def two_parts(size, width, first_blocks, blocks, first_step):
    one = lambda s, *_: (jnp.clip(s - first_step, 0, first_blocks - 1), 0)
    two = lambda s, *_: (jnp.clip(s - first_step - first_blocks, 0, blocks - first_blocks - 1), 0)
    return [pl.BlockSpec((size, width), one), pl.BlockSpec((size, width), two)]


def rows_of(vector):
    return [vector[:, i * T : (i + 1) * T] for i in range(vector.shape[1] // T)]


class Combine:
    STAGES = 4

    def __init__(self, place, total, arrived, send, recv):
        self.p, self.total, self.arrived, self.send, self.recv = place, total, arrived, send, recv

    def copies(self, i):
        p = self.p
        if i < 3:
            peers = [(i, (p.device(c=1 - p.c), p.device(x=1 - p.x), p.device(y=1 - p.y))[i])]
        else:
            peers = [(3 + d, p.device(z=(p.z + d) % p.zs)) for d in range(1, p.zs)]
        return [
            remote(self.total.at[i], self.arrived.at[at], self.send.at[at], self.recv.at[at], peer)
            for at, peer in peers
        ]

    def start(self, i):
        for copy in self.copies(i):
            copy.start()

    def finish(self, i):
        p = self.p
        for copy in self.copies(i):
            copy.wait_recv()
            copy.wait_send()
        if i < 3:
            self.total[i + 1] = self.total[i] + self.arrived[i]
        else:
            self.arrived[3] = self.total[i]
            terms = [self.arrived[3 + (p.z - z + p.zs) % p.zs] for z in range(p.zs)]
            self.total[i + 1] = functools.reduce(jnp.add, terms)


def back_kernel(zs, xs, shape, width, kept, live, *refs):
    q, k, v, bias, grad, out, norm, attended, branch_hbm, normed_hbm, parts, weights_hbm = refs[:12]
    d_middle, x_low, gain, d_gain_two, kept_sums = refs[12:17]
    d_x, feed_out, attention_out, vector_out = refs[17:19], refs[19:22], refs[22:26], refs[26]
    refs = refs[7:]
    (stage, turn_buf, d_q, d_kv, back_kv, k_sum, v_sum, d_bias) = refs[20:28]
    (w_buf, held, vector, total, arrived, gain_sum) = refs[28:34]
    (local, loads, kv_sems, both_sems) = refs[34:38]
    bufs, scatter_sems = refs[38 : 38 + BUFFERS], refs[38 + BUFFERS :]
    place = Place(zs, xs)
    step = pl.program_id(0)
    rows, keys = shape.rows, shape.keys
    prompt = shape.local_tiles * T
    pairs = d_q.shape[0]
    last = 2 * pairs
    turns = rows // T
    first_kept, end_kept = kept
    fed = parts.shape[0] - (end_kept - first_kept)
    size = d_x[0].shape[0]
    blocks = rows // size

    def stage_load(source):
        return pltpu.make_async_copy(source, stage, local.at[0])

    def weights_load(i):
        return pltpu.make_async_copy(weights_hbm.at[(2, 0, 1)[i]], w_buf.at[i], local.at[1 + i])

    def turn():
        def one(i, carry):
            part = tile_rows(i)
            turn_buf[:, part] = stage[part, :].T
            return carry

        lax.fori_loop(0, turns, one, 0)

    def part_load(c):
        j = jnp.where(c < first_kept, c, c + end_kept - first_kept)
        return pltpu.make_async_copy(parts.at[j], held.at[c % 3], loads.at[c % 3])

    @pl.when(step == 0)
    def _():
        part_load(step).start()
        stage_load(branch_hbm).start()
        place.barrier()
        for i in range(3):
            weights_load(i).start()

    def feed_store(j, half, total):
        piece = 2 * j + half

        @pl.when(piece < feed_out[0].shape[1] // T)
        def _():
            part = pl.ds(pl.multiple_of(piece * T, T), T)
            for i in range(3):
                feed_out[i][:, part] = total[i]

    def keep(c, half, total):
        @pl.when(c < fed)
        def _():
            feed_store(jnp.where(c < first_kept, c, c + end_kept - first_kept), half, total)

        for m, matrix in enumerate((3, 0, 1, 2)):

            @pl.when(c == fed + m)
            def _(matrix=matrix):
                for i in range(3):
                    piece = 3 * half + i
                    attention_out[matrix][:, piece * T : (piece + 1) * T] = total[i]

    @pl.when(step == 1)
    def _():
        def one(k, carry):
            for half in range(2):
                feed_store(k + first_kept, half, kept_sums[k, half])
            return carry

        lax.fori_loop(0, end_kept - first_kept, one, 0)

    engine = Scatter(place, bufs, *scatter_sems, keep)

    def due(offset, action):
        at = step - offset
        chunk = jnp.where(at <= fed, at, at - last + fed)
        early = (at >= 0) & (at <= fed)
        late = (at > last) & (at < last + 4)

        @pl.when(early | late)
        def _():
            action(chunk)

    def first(c):
        @pl.when(c < fed)
        def _():
            part_load(c).wait()

        engine.start_first(c, held.at[c % 3])

    due(4, engine.finish)
    due(3, engine.start_fourth)
    due(2, engine.start_third)
    due(1, lambda c: engine.start_second(c, held.at[c % 3]))
    due(0, first)

    @pl.when(step + 1 < fed)
    def _():
        part_load(step + 1).start()

    @pl.when(step == 0)
    def _():
        stage_load(branch_hbm).wait()
        turn()
        stage_load(normed_hbm).start()

    def kv_send(p):
        src = d_kv.at[p, :, pl.ds(rows, keys - rows)]
        peer = place.device(x=1 - place.x)
        return remote(src, back_kv.at[p], kv_sems.at[0, p], kv_sems.at[1, p], peer)

    @pl.when(step < last)
    def _():
        p = step // 2
        half = step % 2

        @pl.when(half == 0)
        def _():
            k_sum[...] = jnp.zeros_like(k_sum)
            v_sum[...] = jnp.zeros_like(v_sum)
            d_bias[...] = jnp.zeros_like(d_bias)

        inputs = (q, k, v, bias, grad, out, norm, d_q.at[p], d_bias, k_sum, v_sum)
        base = place.x * shape.local_tiles
        action = lambda i, c: attend_back_tile(shape, i, c, live, base, *inputs)

        @pl.when(half == 0)
        def _():
            for_tiles(shape, False, action)

        @pl.when(half == 1)
        def _():
            for_tiles(shape, True, action)
            d_kv[p, 0] = k_sum[...].astype(BF)
            d_kv[p, 1] = v_sum[...].astype(BF)
            kv_send(p).start()
            for h in range(2):
                vector[2 * p + h] = band_sums(d_bias, h)

    def produce(c, right):
        slot = c % 3
        for m in range(3):
            operand = right(m)

            def one(z, carry, m=m, operand=operand):
                block = turn_buf.shape[0] // zs
                part = pl.ds(pl.multiple_of(z * block, block), block)
                result = nn(turn_buf[part, :], operand).astype(BF)
                for side in range(2):
                    index = 2 * m + side
                    value = result[:, side * T : (side + 1) * T]
                    held[slot, index // 3, index % 3, z] = value.reshape(held.shape[4:])
                return carry

            lax.fori_loop(0, zs, one, 0)

    @pl.when(step == fed - 1)
    def _():
        produce(fed, lambda m: jnp.concatenate([attended[2 * m], attended[2 * m + 1]], axis=1))

    @pl.when(step == fed)
    def _():
        stage_load(normed_hbm).wait()
        turn()

    @pl.when(step == last)
    def _():
        produce(fed + 1, lambda m: jnp.concatenate([d_q[2 * m], d_q[2 * m + 1]], axis=1))

        def join(p, carry):
            kv_send(p).wait_recv()
            kv_send(p).wait_send()
            for side in range(2):
                own = d_kv[p, side, 0:prompt, :].astype(F32)
                d_kv[p, side, 0:prompt, :] = (own + back_kv[p, side].astype(F32)).astype(BF)
            return carry

        lax.fori_loop(0, pairs, join, 0)
        for i in range(3):
            weights_load(i).wait()
        gain_sum[...] = jnp.zeros_like(gain_sum)

    for side in range(2):

        @pl.when(step == last + 1 + side)
        def _(side=side):
            pick = lambda p: d_kv[p, side, 0:rows, :]
            produce(fed + 2 + side, lambda m: jnp.concatenate([pick(2 * m), pick(2 * m + 1)], axis=1))

    @pl.when((step >= last) & (step < last + blocks))
    def _():
        part = pl.ds(pl.multiple_of((step - last) * size, size), size)
        d_normed = None
        for i in range(3):
            for m in range(pairs // 2):
                if i == 0:
                    left = [d_q[2 * m + e, part, :] for e in range(2)]
                else:
                    left = [d_kv[2 * m + e, i - 1, part, :] for e in range(2)]
                pieces = [2 * m, 2 * m + 1]
                right = [w_buf[i, j // 3, j % 3].reshape(width, T) for j in pieces]
                term = nt(jnp.concatenate(left, axis=1), jnp.concatenate(right, axis=1))
                d_normed = term if d_normed is None else d_normed + term
        x = x_low[...].astype(F32)
        scale = lax.rsqrt(jnp.mean(x * x, axis=-1, keepdims=True) + EPS)
        unit = x * scale
        gain_sum[...] += jnp.sum(d_normed * unit, axis=0, keepdims=True)
        d_unit = d_normed * gain[...]
        inner = jnp.mean(d_unit * unit, axis=-1, keepdims=True)
        value = (d_middle[...] + scale * (d_unit - unit * inner)).astype(BF)
        put(step - last, prompt // size, d_x, value)

    mix = Combine(place, total, arrived, both_sems.at[0], both_sems.at[1])
    start = last + blocks
    tiles = 2 * pairs

    @pl.when(step == start - 1)
    def _():
        total[0, 0:tiles] = vector[...]
        both = rows_of(gain_sum[...]) + rows_of(d_gain_two[...])
        for i in range(len(both) // VECTOR_ROWS):
            group = both[i * VECTOR_ROWS : (i + 1) * VECTOR_ROWS]
            total[0, tiles + i] = jnp.concatenate(group, axis=0)
        mix.start(0)

    for i in range(mix.STAGES):

        @pl.when(step == start + i)
        def _(i=i):
            mix.finish(i)
            if i + 1 < mix.STAGES:
                mix.start(i + 1)
            else:
                vector_out[...] = total[mix.STAGES]


def back(q, kv, bias, grad, out, norm, branch, normed, parts, weights, d_middle, x_low, gain,
         d_gain_two, kept_sums, hidden, live, shape, sizes, kept, collective_id):
    grp, seq = sizes
    rows, width = x_low.shape
    pairs = q.shape[0]
    zs = grp // (Y * C)
    keys = shape.keys
    chunks, _, n, _, _, _, shard, lanes = parts.shape
    assert 0 < chunks - (kept[1] - kept[0]) <= 2 * pairs
    assert (pairs, n) == (6, 3) and 2 * width // T % VECTOR_ROWS == 0
    last = 2 * pairs
    size = min(rows, 256)
    blocks = rows // size
    prompt = shape.local_tiles * T
    assert prompt % size == 0
    tile = (2, n, zs, Y, C * seq, shard, lanes)
    stages = Combine.STAGES
    steps = max(last + blocks + stages, last + 8)
    inner = pairs * 2 * HEAD
    vector = (2 * pairs + 2 * width // T // VECTOR_ROWS, VECTOR_ROWS, T)
    pair = lambda s: jnp.minimum(s // 2, pairs - 1)
    by_pair = lambda rows_: pl.BlockSpec((rows_, 2 * HEAD), lambda s, *_: (0, pair(s)))
    in_pair = pl.BlockSpec((None, rows, 2 * HEAD), lambda s, *_: (pair(s), 0, 0))
    of_keys = lambda side: pl.BlockSpec(
        (None, None, keys, 2 * HEAD), lambda s, *_: (side, pair(s), 0, 0)
    )
    row_block = lambda s: jnp.clip(s - last, 0, blocks - 1)
    by_rows = pl.BlockSpec((size, width), lambda s, *_: (row_block(s), 0))
    full = lambda *dims: pl.BlockSpec(
        dims, lambda s, *_: (0,) * len(dims), pipeline_mode=pl.Buffered(1)
    )
    anywhere = pl.BlockSpec(memory_space=pl.ANY)
    sems = lambda *dims: pltpu.SemaphoreType.DMA(dims)
    return pl.pallas_call(
        functools.partial(back_kernel, zs, seq, shape, width, kept),
        grid_spec=pltpu.PrefetchScalarGridSpec(
            num_scalar_prefetch=1,
            grid=(steps,),
            in_specs=[
                in_pair,
                of_keys(0),
                of_keys(1),
                pl.BlockSpec((2, BANDS, T, T), lambda s, *_: (pair(s), 0, 0, 0)),
                by_pair(rows),
                in_pair,
                pl.BlockSpec((2, rows, 1), lambda s, *_: (pair(s), 0, 0)),
                full(pairs, rows, 2 * HEAD),
                anywhere,
                anywhere,
                anywhere,
                anywhere,
                by_rows,
                by_rows,
                full(1, width),
                full(1, width),
                full(*kept_sums.shape),
            ],
            out_specs=two_parts(size, width, prompt // size, blocks, last)
            + [full(shard, hidden)] * 3
            + [full(shard, inner)] * 4
            + [full(*vector)],
            scratch_shapes=[
                pltpu.VMEM((rows, width), BF),
                pltpu.VMEM((width, rows), BF),
                pltpu.VMEM((pairs, rows, 2 * HEAD), BF),
                pltpu.VMEM((pairs, 2, keys, 2 * HEAD), BF),
                pltpu.VMEM((pairs, 2, keys - rows, 2 * HEAD), BF),
                pltpu.VMEM((keys, 2 * HEAD), F32),
                pltpu.VMEM((keys, 2 * HEAD), F32),
                pltpu.VMEM((2, BANDS, T, T), F32),
                pltpu.VMEM((3, *tile), BF),
                pltpu.VMEM((3, *tile), BF),
                pltpu.VMEM((2 * pairs, VECTOR_ROWS, T), F32),
                pltpu.VMEM((stages + 1, *vector), F32),
                pltpu.VMEM((3 + zs, *vector), F32),
                pltpu.VMEM((1, width), F32),
                sems(4),
                sems(3),
                sems(2, pairs),
                sems(2, 3 + zs),
            ]
            + scatter_buffers(n, zs, seq, shard, lanes)
            + [sems(2, 2, zs + 2), sems(2, 2, zs + 2)],
        ),
        out_shape=[
            jax.ShapeDtypeStruct((prompt, width), BF),
            jax.ShapeDtypeStruct((rows - prompt, width), BF),
        ]
        + [jax.ShapeDtypeStruct((shard, hidden), F32)] * 3
        + [jax.ShapeDtypeStruct((shard, inner), F32)] * 4
        + [
            jax.ShapeDtypeStruct(vector, F32),
        ],
        compiler_params=pltpu.CompilerParams(
            collective_id=collective_id, has_side_effects=True, vmem_limit_bytes=VMEM_LIMIT
        ),
    )(live, q, kv, kv, bias, grad, out, norm, out, branch, normed, parts, weights, d_middle,
      x_low, gain, d_gain_two, kept_sums)


GELU_SCALE = 0.7978845608028654
GELU_CUBIC = 0.044715


def gelu_and_slope(a):
    square = a * a
    tanh = jnp.tanh(GELU_SCALE * a * (1.0 + GELU_CUBIC * square))
    half = 0.5 * (1.0 + tanh)
    slope = half + 0.5 * a * (1.0 - tanh * tanh) * (
        GELU_SCALE * (1.0 + 3.0 * GELU_CUBIC * square)
    )
    return a * half, slope


def feed_load(x_hbm, dy_parts, x, x_t, dy, dy_t, sem):
    loads = [pltpu.make_async_copy(x_hbm, x, sem.at[0])]
    start = 0
    for i, part in enumerate(dy_parts):
        target = dy.at[pl.ds(start, part.shape[0])]
        loads.append(pltpu.make_async_copy(part, target, sem.at[1 + i]))
        start += part.shape[0]
    for load in loads:
        load.start()
    for load in loads:
        load.wait()

    def turn(i, carry):
        part = pl.ds(pl.multiple_of(i * T, T), T)
        x_t[:, part] = x[part, :].T
        dy_t[:, part] = dy[part, :].T
        return carry

    lax.fori_loop(0, x.shape[0] // T, turn, 0)


def feed_chunk(read, write, blocks, out, d_x, x, x_t, dy, dy_t, hidden, d_gate, d_up):
    rows, width = x.shape
    row_block = min(rows, 256)
    width_block = width // blocks
    w_gate, w_up, w_down = [jnp.concatenate([read(0, i), read(1, i)], axis=1) for i in range(3)]

    def by_rows(i, carry):
        part = pl.ds(pl.multiple_of(i * row_block, row_block), row_block)
        gate = nn(x[part, :], w_gate)
        up = nn(x[part, :], w_up)
        d_hidden = nn(dy[part, :], w_down)
        active, slope = gelu_and_slope(gate)
        hidden_low = (active * up).astype(BF)
        d_gate_low = (d_hidden * up * slope).astype(BF)
        d_up_low = (d_hidden * active).astype(BF)
        hidden[part, :] = hidden_low
        d_gate[part, :] = d_gate_low
        d_up[part, :] = d_up_low
        out[part, :] += nt(hidden_low, w_down)
        d_x[part, :] += nt(d_gate_low, w_gate) + nt(d_up_low, w_up)
        return carry

    lax.fori_loop(0, rows // row_block, by_rows, 0)

    def by_width(i, carry):
        part = pl.ds(pl.multiple_of(i * width_block, width_block), width_block)
        pairs = ((x_t, d_gate), (x_t, d_up), (dy_t, hidden))
        for index, (left, right) in enumerate(pairs):
            total = nn(left[part, :], right[...]).astype(BF)
            write(0, index, i, total[:, :T])
            write(1, index, i, total[:, T:])
        return carry

    lax.fori_loop(0, blocks, by_width, 0)


def feed_kernel(x_hbm, dy_hbm, weights, out, d_x, grads, x, x_t, dy, dy_t, *rest):
    *work, sem = rest
    width_block = 512

    @pl.when(pl.program_id(0) == 0)
    def _():
        feed_load(x_hbm, [dy_hbm], x, x_t, dy, dy_t, sem)
        out[...] = jnp.zeros_like(out)
        d_x[...] = jnp.zeros_like(d_x)

    def write(half, index, block, value):
        part = pl.ds(pl.multiple_of(block * width_block, width_block), width_block)
        grads[0, half, index, part, :] = value

    read = lambda half, index: weights[0, half, index]
    blocks = x.shape[1] // width_block
    feed_chunk(read, write, blocks, out, d_x, x, x_t, dy, dy_t, *work)


def feed_scratch(rows, width):
    return [
        pltpu.VMEM((rows, width), BF),
        pltpu.VMEM((width, rows), BF),
        pltpu.VMEM((rows, width), BF),
        pltpu.VMEM((width, rows), BF),
        pltpu.VMEM((rows, 2 * T), BF),
        pltpu.VMEM((rows, 2 * T), BF),
        pltpu.VMEM((rows, 2 * T), BF),
        pltpu.SemaphoreType.DMA((3,)),
    ]


def feed(x, dy, weights):
    rows, width = x.shape
    chunks = weights.shape[0]
    chunk = pl.BlockSpec((1, 2, 3, width, T), lambda j: (j, 0, 0, 0, 0))
    whole = pl.BlockSpec((rows, width), lambda j: (0, 0), pipeline_mode=pl.Buffered(1))
    return pl.pallas_call(
        feed_kernel,
        grid=(chunks,),
        in_specs=[pl.BlockSpec(memory_space=pl.ANY)] * 2 + [chunk],
        out_specs=[whole, whole, chunk],
        out_shape=[
            jax.ShapeDtypeStruct((rows, width), F32),
            jax.ShapeDtypeStruct((rows, width), F32),
            jax.ShapeDtypeStruct((chunks, 2, 3, width, T), BF),
        ],
        scratch_shapes=feed_scratch(rows, width),
        compiler_params=pltpu.CompilerParams(vmem_limit_bytes=VMEM_LIMIT),
    )(x, dy, weights)


def feed_moving_kernel(zs, xs, early, kept, *refs):
    x_hbm, dy_one, dy_two, own, ready, middle, gain, whole, parts, sums = refs[:10]
    final, (d_middle, d_branch, d_attended, d_gain) = refs[10:12], refs[12:16]
    x, x_t, dy, dy_t, hidden, d_gate, d_up, sem = refs[16:24]
    out, d_x, held, w_buf, g_buf, local = refs[24:30]
    gather_sems, bufs = refs[30:32], refs[32 : 32 + BUFFERS]
    scatter_sems = refs[32 + BUFFERS :]
    chunks = own.shape[0]
    place = Place(zs, xs)
    step = pl.program_id(0)
    lag = max(0, 5 - early)
    first_kept, end_kept = kept
    width = x.shape[1]

    @pl.when(step == 0)
    def _():
        place.barrier()

    fetch = Gather(place, own, whole, *gather_sems)
    fetch.tick(step, early, chunks)

    @pl.when(step == 0)
    def _():
        load = pltpu.make_async_copy(own, held, local.at[0])
        load.start()
        load.wait()
        mine = whole.at[:, :, :, place.z, place.y, place.c * place.xs + place.x]
        store = pltpu.make_async_copy(held, mine, local.at[1])
        store.start()
        store.wait()
        feed_load(x_hbm, [dy_one, dy_two], x, x_t, dy, dy_t, sem)
        out[...] = jnp.zeros_like(out)
        d_x[...] = jnp.zeros_like(d_x)

    skipped = ready.shape[0] - early

    def weight_load(j, source, first=0):
        return pltpu.make_async_copy(source.at[first + j], w_buf.at[j % 2], local.at[2 + j % 2])

    def start_load(j):
        if early > 0:

            @pl.when(j < early)
            def _():
                weight_load(j, ready, skipped).start()

        @pl.when(j >= early)
        def _():
            weight_load(j, whole).start()

    def part_store(j):
        return pltpu.make_async_copy(g_buf.at[j % 2], parts.at[j], local.at[4 + j % 2])

    def is_kept(j):
        return (j >= first_kept) & (j < end_kept)

    def keep(k, half, total):
        sums[k, half] = total

    engine = Scatter(place, bufs, *scatter_sems, keep)
    due = lag + first_kept
    number = end_kept - first_kept
    grads_of = lambda k: g_buf.at[(k + first_kept) % 2]

    def tick(at):
        staged(at, due + 5, number, engine.finish)
        staged(at, due + 4, number, engine.start_fourth)
        staged(at, due + 3, number, engine.start_third)
        staged(at, due + 2, number, lambda k: engine.start_second(k, grads_of(k)))
        staged(at, due + 1, number, lambda k: engine.start_first(k, grads_of(k)))

    tick(step)

    chunk = step - lag
    if lag == 0:

        @pl.when(step == 0)
        def _():
            start_load(0)

    @pl.when((chunk >= (0 if lag == 0 else -1)) & (chunk + 1 < chunks))
    def _():
        start_load(chunk + 1)

    @pl.when((chunk >= 2) & (chunk < chunks + 2) & ~is_kept(chunk - 2))
    def _():
        part_store(chunk - 2).wait()

    @pl.when((chunk >= 0) & (chunk < chunks))
    def _():
        weight_load(chunk, whole).wait()
        slot = chunk % 2

        def read(half, index):
            return w_buf[slot, half, index].reshape(width, T)

        def write(half, index, block, value):
            shape = g_buf.shape[4:]
            g_buf[slot, half, index, block] = value.reshape(shape)

        work = (hidden, d_gate, d_up)
        feed_chunk(read, write, zs, out, d_x, x, x_t, dy, dy_t, *work)

        @pl.when(~is_kept(chunk))
        def _():
            part_store(chunk).start()

    spare = chunks % 2
    rows, size = x.shape[0], middle.shape[0]
    blocks = rows // size

    def o_load():
        return pltpu.make_async_copy(ready.at[skipped - 1], w_buf.at[spare], local.at[6])

    @pl.when(chunk == chunks - 1)
    def _():
        o_load().start()
        d_gain[...] = jnp.zeros_like(d_gain)

    @pl.when(chunk == chunks)
    def _():
        o_load().wait()

    @pl.when((chunk >= chunks) & (chunk < chunks + blocks))
    def _():
        i = chunk - chunks
        part = pl.ds(pl.multiple_of(i * size, size), size)
        values = middle[...]
        put(i, dy_one.shape[0] // size, final, (values + out[part, :]).astype(BF))
        scale = rms_scale(values)
        unit = values * scale
        d_normed = d_x[part, :]
        d_gain[...] += jnp.sum(d_normed * unit, axis=0, keepdims=True)
        total = dy[part, :].astype(F32) + norm_back(d_normed, unit, scale, gain[...])
        d_middle[...] = total
        low = total.astype(BF)
        d_branch[...] = low
        for m in range(d_attended.shape[1] // (2 * T)):
            right = joined_pieces(w_buf, spare, m)
            d_attended[:, 2 * m * T : 2 * (m + 1) * T] = nn(low, right).astype(BF)


def feed_moving(x, dy_one, dy_two, own, ready, middle, gain, inner, sizes, early, kept, collective_id):
    grp, seq = sizes
    rows, width = x.shape
    chunks, _, n, shard, lanes = own.shape
    zs = grp // (Y * C)
    tile = (2, n, zs, Y, C * seq, shard, lanes)
    one = pl.BlockSpec((1, width), lambda j: (0, 0), pipeline_mode=pl.Buffered(1))
    number = kept[1] - kept[0]
    sums = pl.BlockSpec(
        (number, 2, n, shard, lanes), lambda j: (0,) * 5, pipeline_mode=pl.Buffered(1)
    )
    lag = max(0, 5 - early)
    size = min(rows, 256)
    blocks = rows // size
    assert dy_one.shape[0] % size == 0
    tail = lag + chunks
    steps = max(tail + max(2, blocks), lag + kept[1] + 5)
    by_rows = lambda columns: pl.BlockSpec(
        (size, columns), lambda j: (jnp.clip(j - tail, 0, blocks - 1), 0)
    )
    out = jax.ShapeDtypeStruct
    anywhere = pl.BlockSpec(memory_space=pl.ANY)
    sems = lambda *shape: pltpu.SemaphoreType.DMA(shape)
    return pl.pallas_call(
        functools.partial(feed_moving_kernel, zs, seq, early, kept),
        grid=(steps,),
        in_specs=[anywhere] * 5 + [by_rows(width), one],
        out_specs=[anywhere, anywhere, sums]
        + two_parts(size, width, dy_one.shape[0] // size, blocks, tail)
        + [by_rows(width), by_rows(width), by_rows(inner), one],
        out_shape=[
            out((chunks, *tile), BF),
            out((chunks, *tile), BF),
            out((number, 2, n, shard, lanes), F32),
            out(dy_one.shape, BF),
            out(dy_two.shape, BF),
            out((rows, width), F32),
            out((rows, width), BF),
            out((rows, inner), BF),
            out((1, width), F32),
        ],
        scratch_shapes=feed_scratch(rows, width)
        + [
            pltpu.VMEM((rows, width), F32),
            pltpu.VMEM((rows, width), F32),
            pltpu.VMEM(own.shape, BF),
            pltpu.VMEM((2, *tile), BF),
            pltpu.VMEM((2, *tile), BF),
            sems(7),
            sems(chunks, 2, zs + 2),
            sems(chunks, 2, zs + 2),
        ]
        + scatter_buffers(n, zs, seq, shard, lanes)
        + [sems(2, 2, zs + 2), sems(2, 2, zs + 2)],
        compiler_params=pltpu.CompilerParams(
            collective_id=collective_id, has_side_effects=True, vmem_limit_bytes=VMEM_LIMIT
        ),
    )(x, dy_one, dy_two, own, ready, middle, gain)


def settle_kernel(*refs):
    *refs, sem = refs
    count = len(refs) // 3
    sources, targets, held = refs[:count], refs[count : 2 * count], refs[2 * count :]
    loads = [pltpu.make_async_copy(sources[i], held[i], sem.at[i]) for i in range(count)]
    stores = [pltpu.make_async_copy(held[i], targets[i], sem.at[count + i]) for i in range(count)]
    for load in loads:
        load.start()
    for load, store in zip(loads, stores):
        load.wait()
        store.start()
    for store in stores:
        store.wait()


def settle(*arrays):
    anywhere = pl.BlockSpec(memory_space=pl.ANY)
    return pl.pallas_call(
        settle_kernel,
        in_specs=[anywhere] * len(arrays),
        out_specs=[anywhere] * len(arrays),
        out_shape=[jax.ShapeDtypeStruct(a.shape, a.dtype) for a in arrays],
        scratch_shapes=[pltpu.VMEM(a.shape, a.dtype) for a in arrays]
        + [pltpu.SemaphoreType.DMA((2 * len(arrays),))],
        compiler_params=pltpu.CompilerParams(vmem_limit_bytes=VMEM_LIMIT),
    )(*arrays)


def rms_scale(values):
    return lax.rsqrt(jnp.mean(values * values, axis=-1, keepdims=True) + EPS)


def norm_back(d_normed, unit, scale, gain):
    d_unit = d_normed * gain
    return scale * (d_unit - unit * jnp.mean(d_unit * unit, axis=-1, keepdims=True))


def pieces_of(matrix):
    rows, columns = matrix.shape
    return jnp.swapaxes(matrix.reshape(rows, columns // T, T), 0, 1)


def joined(pieces):
    count, rows, _ = pieces.shape
    return jnp.swapaxes(pieces, 0, 1).reshape(rows, count * T)


def attention_chunks(matrices):
    flat = jnp.concatenate([pieces_of(m) for m in matrices], axis=0)
    pad = -flat.shape[0] % 6
    flat = jnp.pad(flat, ((0, pad), (0, 0), (0, 0)))
    return flat.reshape(-1, 2, 3, *flat.shape[1:])


def feed_chunks(matrices):
    stacked = jnp.stack([pieces_of(m) for m in matrices], axis=1)
    pad = -stacked.shape[0] % 2
    stacked = jnp.pad(stacked, ((0, pad), (0, 0), (0, 0), (0, 0)))
    return stacked.reshape(-1, 2, *stacked.shape[1:])


def body(sizes, *args):
    (
        prompt_x,
        cont_x,
        cont_len,
        prompt_cot,
        cont_cot,
        norm1_gain,
        q_weight,
        k_weight,
        v_weight,
        o_weight,
        bucket_table,
        norm2_gain,
        gate_weight,
        up_weight,
        down_weight,
    ) = args
    _, local_prompt, width = prompt_x.shape
    conts, cont_rows = cont_x.shape[1], cont_x.shape[2]
    assert prompt_x.shape[0] == 1 and cont_rows == T and local_prompt % T == 0
    seq = sizes[1]
    num_buckets, heads = bucket_table.shape
    inner = q_weight.shape[1]
    assert inner == heads * HEAD
    shard = q_weight.shape[0]
    hidden_width = gate_weight.shape[1]
    local_tiles = local_prompt // T
    tiles = local_tiles * seq
    seq_index = lax.axis_index("seq")

    split = lambda parts: (parts[0][None], parts[1].reshape(1, conts, cont_rows, width))
    cut = lambda values: (values[:local_prompt], values[local_prompt:])
    shape = Shape(tiles, local_tiles, conts)
    count = inner // T
    if can_move(sizes, shard):
        early, kept = 7, (8, 14)
        own_gain = jnp.stack([norm1_gain, norm2_gain])[None, :, None, :, None]
        own_gain = jnp.broadcast_to(own_gain, (1, 2, 1, shard, T)).astype(BF)
        cont_dy = cont_cot[0].reshape(-1, width)
        matrices = (q_weight, k_weight, v_weight, o_weight, gate_weight, up_weight, down_weight)
        (whole, own_feed, x_low, normed_one, kv, bias, queries, attended, log_norm, middle,
         normed_two, *gains) = front(
            prompt_x[0], cont_x[0].reshape(-1, width), own_gain, matrices, bucket_table.T, cont_len,
            shape, sizes, early, 0,
        )
        _, feed_parts, kept_sums, *final, d_middle, d_branch, d_attended, d_gain_two = feed_moving(
            normed_two, prompt_cot[0], cont_dy, own_feed, whole, middle, gains[1], inner, sizes,
            early, kept, 1,
        )
        (*d_x, gate_grad, up_grad, down_grad, q_grad, k_grad, v_grad, o_grad, vector) = back(
            queries, kv, bias, d_attended, attended, log_norm, d_branch, normed_one, feed_parts,
            whole, d_middle, x_low, gains[0], d_gain_two, kept_sums, hidden_width, cont_len, shape,
            sizes, kept, 2,
        )
        settled = settle(
            *final, *d_x, gate_grad, up_grad, down_grad, q_grad, k_grad, v_grad, o_grad
        )
        final, d_x = settled[:2], settled[2:4]
        gate_grad, up_grad, down_grad, q_grad, k_grad, v_grad, o_grad = settled[4:]
        near = vector[:heads, :4].reshape(heads, SPAN)
        far = jnp.sum(vector[:heads, 4:6], axis=-1)
        relative = (jnp.arange(SPAN) + T) % SPAN - 2 * T
        ids = jnp.concatenate([bucket_ids(relative), bucket_ids(jnp.array([-T, T]))])
        hot = (ids[:, None] == jnp.arange(num_buckets)).astype(F32)
        both = jnp.concatenate([near, far], axis=1)
        table_grad = jnp.einsum("hr,rb->bh", both, hot, precision=lax.Precision.HIGHEST)
        gain_grads = vector[heads:].reshape(2, sizes[0] * seq, shard)
        me = lax.axis_index("grp") * seq + seq_index
        norm1_grad, norm2_grad = lax.dynamic_index_in_dim(gain_grads, me, 1, keepdims=False)
    else:
        x_low = jnp.concatenate([prompt_x[0], cont_x[0].reshape(-1, width)], axis=0)
        dy_low = jnp.concatenate([prompt_cot[0], cont_cot[0].reshape(-1, width)], axis=0)
        x = x_low.astype(F32)
        dy = dy_low.astype(F32)
        lanes = jnp.zeros((shard, T - 2), F32)
        gains = jnp.concatenate([norm1_gain[:, None], norm2_gain[:, None], lanes], axis=1)
        own_attention = attention_chunks([q_weight, k_weight, v_weight, o_weight, gains]).astype(BF)
        own_feed = feed_chunks([gate_weight, up_weight, down_weight]).astype(BF)
        attention_whole = gather(own_attention, sizes)
        flat = attention_whole.reshape(-1, width, T)
        q_full, k_full, v_full, o_full = [
            joined(flat[i * count : (i + 1) * count]) for i in range(4)
        ]
        gain_one = flat[4 * count, :, 0].astype(F32)
        gain_two = flat[4 * count, :, 1].astype(F32)
        scale_one = rms_scale(x)
        unit_one = x * scale_one
        normed_one = (unit_one * gain_one).astype(BF)
        kv = nn(normed_one, jnp.concatenate([k_full, v_full], axis=1)).astype(BF)
        queries = nn(normed_one, q_full).astype(BF)
        gathered = lax.all_gather(kv[:local_prompt], "seq", axis=0, tiled=True)
        others = jnp.roll(gathered, -seq_index * local_prompt, axis=0)[local_prompt:]
        every = jnp.concatenate([kv, others], axis=0)
        keys, values = every[:, :inner], every[:, inner:]
        base = (seq_index * local_tiles).reshape(1).astype(jnp.int32)
        one_hot = band_one_hot(num_buckets)
        bias = jnp.einsum("cqkb,bh->hcqk", one_hot, bucket_table, precision=lax.Precision.HIGHEST)
        attended, log_norm = attend(queries, keys, values, bias, cont_len, base, shape)
        middle = x + nt(attended, o_full)
        scale_two = rms_scale(middle)
        unit_two = middle * scale_two
        normed_two = (unit_two * gain_two).astype(BF)
        out_sum, d_normed_two, feed_grads = feed(normed_two, dy_low, gather(own_feed, sizes))
        feed_sums = scatter(feed_grads)
        final = cut((middle + out_sum).astype(BF))
        d_gain_two = jnp.sum(d_normed_two * unit_two, axis=0)
        d_middle = dy + norm_back(d_normed_two, unit_two, scale_two, gain_two)
        d_branch = d_middle.astype(BF)
        d_attended = nn(d_branch, o_full).astype(BF)
        d_o = tn(d_branch, attended)
        d_queries, d_keys, d_values, d_bias = attend_back(
            queries, keys, values, bias, d_attended, attended, log_norm, cont_len, base, shape
        )
        d_table = jnp.einsum("hcqk,cqkb->bh", d_bias, one_hot, precision=lax.Precision.HIGHEST)
        d_kv = jnp.concatenate([d_keys, d_values], axis=1)
        prompt_parts = jnp.concatenate([d_kv[:local_prompt], d_kv[shape.rows :]], axis=0)
        prompt_parts = jnp.roll(prompt_parts, seq_index * local_prompt, axis=0)
        d_prompt = lax.psum_scatter(prompt_parts, "seq", scatter_dimension=0, tiled=True)
        d_kv = jnp.concatenate([d_prompt, d_kv[local_prompt : shape.rows]], axis=0)
        d_normed_one = nt(d_queries, q_full) + nt(d_kv, jnp.concatenate([k_full, v_full], axis=1))
        d_q = tn(normed_one, d_queries)
        d_kv_weight = tn(normed_one, d_kv)
        d_gain_one = jnp.sum(d_normed_one * unit_one, axis=0)
        d_x = d_middle + norm_back(d_normed_one, unit_one, scale_one, gain_one)
        d_x = cut(d_x.astype(BF))
        attention_parts = attention_chunks([d_q, d_kv_weight, d_o]).astype(BF)
        attention_sums = scatter(attention_parts).reshape(-1, shard, T)
        norm1_grad = lax.psum_scatter(d_gain_one, ("grp", "seq"), scatter_dimension=0, tiled=True)
        norm2_grad = lax.psum_scatter(d_gain_two, ("grp", "seq"), scatter_dimension=0, tiled=True)
        table_grad = lax.psum(d_table, ("grp", "seq"))
        feed_sums = feed_sums.reshape(-1, 3, shard, T)[: hidden_width // T]
        gate_grad, up_grad, down_grad = [joined(feed_sums[:, i]) for i in range(3)]
        q_grad, k_grad, v_grad, o_grad = [
            joined(attention_sums[i * count : (i + 1) * count]) for i in range(4)
        ]
    return (
        *split(final),
        *split(d_x),
        norm1_grad,
        q_grad,
        k_grad,
        v_grad,
        o_grad,
        table_grad,
        norm2_grad,
        gate_grad,
        up_grad,
        down_grad,
    )


def solution(mesh):
    sizes = (mesh.shape["grp"], mesh.shape["seq"])
    rows = P("grp", "seq", None)
    conts = P("grp", "seq", None, None)
    shard = P(("grp", "seq"), None)
    gain = P(("grp", "seq"))
    in_specs = (rows, conts, P("grp", "seq"), rows, conts, gain, shard, shard, shard, shard)
    in_specs += (P(), gain, shard, shard, shard)
    out_specs = (rows, conts, rows, conts, gain, shard, shard, shard, shard, P(), gain)
    out_specs += (shard, shard, shard)
    return jax.shard_map(
        functools.partial(body, sizes),
        mesh=mesh,
        in_specs=in_specs,
        out_specs=out_specs,
        check_vma=False,
    )
```
